32 devices in a mesh: dp: 8 (over y, x, core), mp: 4 (over z).
Axes of the slice: x: 2, y: 2, z: 4, core: 2. Of those that a mesh axis runs over, the one named last changes fastest.
Arguments:
- layer_input: bfloat16 [8192, 2048], P(('dp', 'mp')), may hold values from -6 to 6
- query_weight: bfloat16 [2048, 2048], P('dp', 'mp'), may hold values from -0.125 to 0.125
- key_weight: bfloat16 [2048, 2048], P('dp', 'mp'), may hold values from -0.125 to 0.125
- value_weight: bfloat16 [2048, 2048], P('dp', 'mp'), may hold values from -0.125 to 0.125
- out_weight: bfloat16 [2048, 2048], P('mp', 'dp'), may hold values from -0.125 to 0.125
- gate_weight: bfloat16 [2048, 8192], P('dp', 'mp'), may hold values from -0.125 to 0.125
- up_weight: bfloat16 [2048, 8192], P('dp', 'mp'), may hold values from -0.125 to 0.125
- down_weight: bfloat16 [8192, 2048], P('mp', 'dp'), may hold values from -0.0625 to 0.0625
- query_gain: bfloat16 [16, 128], P('mp', 'dp'), may hold values from 0.099609375 to 1.8984375
- key_gain: bfloat16 [16, 128], P('mp', 'dp'), may hold values from 0.099609375 to 1.8984375
- attn_gain: bfloat16 [2048], P('dp'), may hold values from 0.099609375 to 1.8984375
- mlp_gain: bfloat16 [2048], P('dp'), may hold values from 0.099609375 to 1.8984375
- seq_lens: int32 [8, 2], P('dp'), may hold values from 0 to 1024, as said below
- out_grad: bfloat16 [8192, 2048], P(('dp', 'mp')), may hold values from -6 to 6
Outputs:
- layer_output: bfloat16 [8192, 2048], P(('dp', 'mp'))
- input_grad: float32 [8192, 2048], P(('dp', 'mp'))
- query_weight_grad: float32 [2048, 2048], P('dp', 'mp')
- key_weight_grad: float32 [2048, 2048], P('dp', 'mp')
- value_weight_grad: float32 [2048, 2048], P('dp', 'mp')
- out_weight_grad: float32 [2048, 2048], P('mp', 'dp')
- gate_weight_grad: float32 [2048, 8192], P('dp', 'mp')
- up_weight_grad: float32 [2048, 8192], P('dp', 'mp')
- down_weight_grad: float32 [8192, 2048], P('mp', 'dp')
- query_gain_grad: float32 [16, 128], P('mp', 'dp')
- key_gain_grad: float32 [16, 128], P('mp', 'dp')
- attn_gain_grad: float32 [2048], P('dp')
- mlp_gain_grad: float32 [2048], P('dp')
The draws below stay inside these ranges and needn't reach their ends.
Inputs may be any that keep to these rules, and one draw needn't show every extreme that they name: `seq_lens`: row g lists the lengths of the sequences packed in order from the start of data group g's 1024 positions: each nonzero length is 512 or more, zeros follow the last sequence, and together they cover at most 1024 positions; the positions after them are padding. At least one group holds a single sequence of 1024.
All inputs are finite; a program needn't handle non-finite values.
Results may differ from the reference program's by a relative error of at most 0.022.
Values may be sent and summed in bfloat16 or wider, within the bound.
A program may use at most 192 MiB of HBM per device.

```python
import math
import jax
import jax.numpy as jnp
from jax import lax

D = 2048
HEADS = 16
HD = 128
FF = 8192
GROUP_TOK = 1024
MIN_LEN = 512
SLOTS = 2
TOKENS = 8192
N_DP = 8


def draw_seq_lens(key, part):
    split_keys = jax.random.split(key, 5)
    group_index = jnp.arange(N_DP, dtype=jnp.int32)
    chosen_group = jax.random.randint(split_keys[0], (), 0, N_DP)
    whole_flag = (group_index == chosen_group).astype(jnp.int32)
    seq_count = jax.random.randint(split_keys[1], (N_DP,), 1, SLOTS)
    seq_count = seq_count * (1 - whole_flag) + whole_flag
    pad_count = jax.random.randint(split_keys[2], (N_DP,), 0, MIN_LEN) * (1 - whole_flag)
    powers = jax.random.randint(split_keys[3], (N_DP, SLOTS), 0, 7)
    factors = jax.random.randint(split_keys[4], (N_DP, SLOTS), 1, 4)
    slot_index = jnp.arange(SLOTS, dtype=jnp.int32)
    live = (slot_index[None, :] < seq_count[:, None]).astype(jnp.int32)
    weights = jnp.left_shift(jnp.ones_like(powers), powers) * factors * live
    slack = GROUP_TOK - seq_count * MIN_LEN - pad_count
    weight_total = jnp.sum(weights, axis=1, dtype=jnp.int32)
    extras = slack[:, None] * weights // weight_total[:, None]
    return ((MIN_LEN + extras) * live).astype(jnp.int32)


def block_levels(key, extent, cuts, least, high):
    level = 1.0
    for axis_at, parts in cuts:
        draws = jax.random.uniform(jax.random.fold_in(jax.random.fold_in(key, 6), axis_at), (parts,), jnp.float32, least / len(cuts), high / len(cuts))
        level = level * jnp.repeat(jnp.exp(draws), extent[axis_at] // parts).reshape((-1,) + (1,) * (len(extent) - 1 - axis_at))
    return level


def bell_draw(own_key, extent, width, limit, cuts=(), held_as=jnp.bfloat16):
    values = jax.random.normal(own_key, extent, jnp.float32) * width
    if len(cuts) > 0:
        values = block_levels(own_key, extent, cuts, -0.22, 0.18) * values
    return jnp.clip(values, min=-limit, max=limit).astype(held_as)


def setup_inputs(seed: int = 0) -> dict:
    key_list = jax.random.split(jax.random.key(seed), 15)
    return {
        "layer_input": bell_draw(key_list[0], (TOKENS, D), 1.0, 6.0, ((0, 32),)),
        "query_weight": bell_draw(key_list[1], (D, D), D ** -0.5, 0.125, ((0, 8), (1, 4))),
        "key_weight": bell_draw(key_list[2], (D, D), D ** -0.5, 0.125, ((0, 8), (1, 4))),
        "value_weight": bell_draw(key_list[3], (D, D), D ** -0.5, 0.125, ((0, 8), (1, 4))),
        "out_weight": bell_draw(key_list[4], (D, D), D ** -0.5, 0.125, ((0, 4), (1, 8))),
        "gate_weight": bell_draw(key_list[5], (D, FF), D ** -0.5, 0.125, ((0, 8), (1, 4))),
        "up_weight": bell_draw(key_list[6], (D, FF), D ** -0.5, 0.125, ((0, 8), (1, 4))),
        "down_weight": bell_draw(key_list[7], (FF, D), FF ** -0.5, 0.0625, ((0, 4), (1, 8))),
        "query_gain": jnp.clip(1.0 + 0.18 * jax.random.normal(key_list[8], (HEADS, HD), jnp.float32), 0.099609375, 1.8984375).astype(jnp.bfloat16),
        "key_gain": jnp.clip(1.0 + 0.18 * jax.random.normal(key_list[9], (HEADS, HD), jnp.float32), 0.099609375, 1.8984375).astype(jnp.bfloat16),
        "attn_gain": jnp.clip(1.0 + 0.18 * jax.random.normal(key_list[10], (D,), jnp.float32), 0.099609375, 1.8984375).astype(jnp.bfloat16),
        "mlp_gain": jnp.clip(1.0 + 0.18 * jax.random.normal(key_list[11], (D,), jnp.float32), 0.099609375, 1.8984375).astype(jnp.bfloat16),
        "seq_lens": draw_seq_lens(jax.random.fold_in(key_list[14], 71), 0),
        "out_grad": bell_draw(key_list[13], (TOKENS, D), 1.0, 6.0, ((0, 32),)),
    }


@jax.custom_vjp
def low(v):
    return lax.optimization_barrier(v.astype(jnp.bfloat16)).astype(jnp.float32)

@jax.custom_vjp
def low_back(v):
    return v

def low_keep(v):
    return (low(v), None)

def low_pass(kept, grad):
    return (grad,)

def back_keep(v):
    return (v, None)

def back_low(kept, grad):
    return (low(grad),)
low.defvjp(low_keep, low_pass)
low_back.defvjp(back_keep, back_low)
EPS = 1e-06
THETA = 500000.0
MASKED = -1000000000.0

def product(former, latter):
    return jnp.dot(former, latter, precision=lax.Precision.HIGHEST)

def inverse_rms(values):
    return lax.rsqrt(lax.optimization_barrier(jnp.mean(values * values, axis=-1, keepdims=True)) + EPS)

def layout(lengths):
    seq_ends = jnp.cumsum(lengths, dtype=jnp.int32)
    starts = seq_ends - lengths
    places = jnp.arange(GROUP_TOK, dtype=jnp.int32)
    slot_ids = jnp.arange(SLOTS, dtype=jnp.int32)
    segment = lax.optimization_barrier(jnp.sum((places[:, None] >= seq_ends[None, :]).astype(jnp.int32), axis=1, dtype=jnp.int32))
    chosen = (segment[:, None] == slot_ids[None, :]).astype(jnp.int32)
    padded = (segment == SLOTS).astype(jnp.int32)
    begins = lax.optimization_barrier(jnp.sum(chosen * starts[None, :], axis=1, dtype=jnp.int32)) + padded * seq_ends[SLOTS - 1]
    return (segment, places - begins, places < seq_ends[SLOTS - 1])

def rotary_tables(positions):
    half_dim = HD // 2
    frequency = jnp.exp(jnp.arange(half_dim, dtype=jnp.float32) * (-2.0 * math.log(THETA) / HD))
    angles = positions.astype(jnp.float32)[:, None] * frequency[None, :]
    doubled = jnp.concatenate([angles, angles], axis=1)
    return (jnp.cos(doubled)[:, None, :], jnp.sin(doubled)[:, None, :])

def rotate(values, cos_table, sin_table):
    half_dim = values.shape[-1] // 2
    turned = jnp.concatenate([-values[..., half_dim:], values[..., :half_dim]], axis=-1)
    return values * cos_table + turned * sin_table

def group_forward(inputs, lengths, params):
    query_weight, key_weight, value_weight, out_weight, gate_weight, up_weight, down_weight, query_gain, key_gain, attn_gain, mlp_gain = params
    segment, positions, valid = layout(lengths)
    cos_table, sin_table = rotary_tables(positions)
    query_raw = low_back(product(inputs, query_weight))
    key_raw = low_back(product(inputs, key_weight))
    value_all = low(low_back(product(inputs, value_weight))).reshape(GROUP_TOK, HEADS, HD)
    query_normed = (query_raw * inverse_rms(query_raw) * query_gain.reshape(D)).reshape(GROUP_TOK, HEADS, HD)
    key_normed = (key_raw * inverse_rms(key_raw) * key_gain.reshape(D)).reshape(GROUP_TOK, HEADS, HD)
    query_all = low(rotate(query_normed, cos_table, sin_table))
    key_all = low(rotate(key_normed, cos_table, sin_table))
    block_rows = min(512, GROUP_TOK)
    block_count = GROUP_TOK // block_rows
    places = jnp.arange(GROUP_TOK, dtype=jnp.int32)
    score_scale = 1.0 / math.sqrt(HD)

    def attend(pieces):
        query_block, segment_block, place_block = pieces
        scores = jnp.einsum('qhd,khd->hqk', query_block, key_all, precision=lax.Precision.HIGHEST) * score_scale
        allowed = (segment_block[:, None] == segment[None, :]) & (place_block[:, None] >= places[None, :])
        scores = low_back(jnp.where(allowed[None], scores, MASKED))
        attn_probs = low(jax.nn.softmax(scores, axis=-1))
        return jnp.einsum('hqk,khd->qhd', attn_probs, value_all, precision=lax.Precision.HIGHEST)
    mixed = lax.map(jax.checkpoint(attend), (query_all.reshape(block_count, block_rows, HEADS, HD), segment.reshape(block_count, block_rows), places.reshape(block_count, block_rows)))
    attended = low(low_back(mixed.reshape(GROUP_TOK, D)))
    branch = low_back(product(attended, out_weight))
    middle = inputs + branch * inverse_rms(branch) * attn_gain
    middle_low = low(middle)
    gate_proj = low_back(product(middle_low, gate_weight))
    up_proj = low_back(product(middle_low, up_weight))
    hidden = low(jax.nn.silu(gate_proj) * up_proj)
    mlp_out = low_back(product(hidden, down_weight))
    return middle + mlp_out * inverse_rms(mlp_out) * mlp_gain

def reference(layer_input, query_weight, key_weight, value_weight, out_weight, gate_weight, up_weight, down_weight, query_gain, key_gain, attn_gain, mlp_gain, seq_lens, out_grad):
    params = (query_weight.astype(jnp.float32), key_weight.astype(jnp.float32), value_weight.astype(jnp.float32), out_weight.astype(jnp.float32), gate_weight.astype(jnp.float32), up_weight.astype(jnp.float32), down_weight.astype(jnp.float32), query_gain.astype(jnp.float32), key_gain.astype(jnp.float32), attn_gain.astype(jnp.float32), mlp_gain.astype(jnp.float32))
    inputs_all = layer_input.astype(jnp.float32).reshape(N_DP, GROUP_TOK, D)
    grads_all = out_grad.astype(jnp.float32).reshape(N_DP, GROUP_TOK, D)

    def one_group(running, pieces):
        inputs, lengths, cotangent = pieces
        valid = layout(lengths)[2]
        outputs, pullback = jax.vjp(lambda inputs_in, params_in: group_forward(inputs_in, lengths, params_in), inputs, params)
        input_part, param_grads = pullback(cotangent * valid[:, None].astype(jnp.float32))
        running = jax.tree.map(lambda before, extra_grad: before + extra_grad, running, param_grads)
        return (running, (outputs, input_part))
    zero_grads = jax.tree.map(jnp.zeros_like, params)
    totals, (outputs, input_parts) = lax.scan(one_group, zero_grads, (inputs_all, seq_lens, grads_all))
    return (outputs.reshape(TOKENS, D).astype(jnp.bfloat16), input_parts.reshape(TOKENS, D), totals[0], totals[1], totals[2], totals[3], totals[4], totals[5], totals[6], totals[7], totals[8], totals[9], totals[10])
```

```python
import functools
import math

import jax
import jax.numpy as jnp
from jax import lax
from jax.experimental import pallas as pl
from jax.experimental.pallas import tpu as pltpu
from jax.sharding import PartitionSpec as P

EPS = 1e-06
THETA = 500000.0
MASKED = -1000000000.0
CHUNKS = 4
STAGGER = 2
TILE = 256
QUERY_ROWS = 256
BF = jnp.bfloat16
F32 = jnp.float32
MIB = 1 << 20
HBM = pl.BlockSpec(memory_space=pl.ANY)
VMEM = pl.BlockSpec(memory_space=pltpu.VMEM)


def plain_dot(former, latter):
    return jnp.dot(former, latter, preferred_element_type=F32)


def inner_dot(former, latter):
    return lax.dot_general(
        former, latter, (((0,), (0,)), ((), ())), preferred_element_type=F32
    )


def outer_dot(former, latter):
    return lax.dot_general(
        former, latter, (((1,), (1,)), ((), ())), preferred_element_type=F32
    )


def layout(lengths, group_size):
    slot_count = lengths.shape[0]
    seq_ends = jnp.cumsum(lengths, dtype=jnp.int32)
    starts = seq_ends - lengths
    places = jnp.arange(group_size, dtype=jnp.int32)
    slot_ids = jnp.arange(slot_count, dtype=jnp.int32)
    segment = jnp.sum(
        (places[:, None] >= seq_ends[None, :]).astype(jnp.int32), axis=1, dtype=jnp.int32
    )
    chosen = (segment[:, None] == slot_ids[None, :]).astype(jnp.int32)
    padded = (segment == slot_count).astype(jnp.int32)
    begins = (
        jnp.sum(chosen * starts[None, :], axis=1, dtype=jnp.int32)
        + padded * seq_ends[slot_count - 1]
    )
    return (begins, places - begins, places < seq_ends[slot_count - 1])


def rotary_tables(positions, head_size):
    half_dim = head_size // 2
    frequency = jnp.exp(jnp.arange(half_dim, dtype=F32) * (-2.0 * math.log(THETA) / head_size))
    angles = positions.astype(F32)[:, None] * frequency[None, :]
    cos_half, sin_half = jnp.cos(angles), jnp.sin(angles)
    return (
        jnp.concatenate([cos_half, cos_half], axis=1),
        jnp.concatenate([-sin_half, sin_half], axis=1),
    )


def neighbour_barrier(me, n):
    barrier = pltpu.get_barrier_semaphore()

    @pl.when(me > 0)
    def _():
        pl.semaphore_signal(barrier, inc=1, device_id={"mp": me - 1})

    @pl.when(me < n - 1)
    def _():
        pl.semaphore_signal(barrier, inc=1, device_id={"mp": me + 1})

    pl.semaphore_wait(barrier, jnp.minimum(me, 1) + jnp.minimum(n - 1 - me, 1))


class LineGather:
    def __init__(self, n, me, own, full, send_sem, recv_sem, local_sem):
        self.n, self.me, self.own, self.full = n, me, own, full
        self.send_sem, self.recv_sem, self.local_sem = send_sem, recv_sem, local_sem

    def local_copy(self, c):
        return pltpu.make_async_copy(self.own(c), self.full(self.me, c), self.local_sem.at[c])

    def copy(self, c, step, way, block, src):
        return pltpu.make_async_remote_copy(
            src_ref=src,
            dst_ref=self.full(block, c),
            send_sem=self.send_sem.at[c, step - 1, way],
            recv_sem=self.recv_sem.at[c, step - 1, way],
            device_id={"mp": self.me + (1 if way == 0 else -1)},
        )

    def sides(self):
        return ((0, self.me), (1, self.n - 1 - self.me))

    def block_at(self, way, step):
        return self.me - step if way == 0 else self.me + step

    def step(self, c, step):
        n = self.n
        if step == 1:
            self.local_copy(c).start()
        for way, place in self.sides():
            if step > 1:

                @pl.when(place >= step - 1)
                def _(way=way):
                    block = self.block_at(way, step - 1)
                    self.copy(c, step - 1, way, block, self.own(c)).wait_recv()

            @pl.when((place >= step - 1) & (place < n - 1))
            def _(way=way):
                block = self.block_at(way, step - 1)
                src = self.own(c) if step == 1 else self.full(block, c)
                self.copy(c, step, way, block, src).start()

    def last(self, c):
        n = self.n
        for way, place in self.sides():

            @pl.when(place == n - 1)
            def _(way=way):
                block = self.block_at(way, n - 1)
                self.copy(c, n - 1, way, block, self.own(c)).wait_recv()

    def drain(self, c):
        self.local_copy(c).wait()
        for step in range(1, self.n):
            for way, place in self.sides():

                @pl.when((place >= step - 1) & (place < self.n - 1))
                def _(way=way):
                    self.copy(c, step, way, self.me, self.own(c)).wait_send()


class LineScatter:
    def __init__(self, n, me, rows, part, send, recv, send_sem, recv_sem):
        self.n, self.me, self.rows = n, me, rows
        self.part, self.send, self.recv = part, send, recv
        self.send_sem, self.recv_sem = send_sem, recv_sem

    def piece(self, c, owner):
        first = pl.multiple_of(owner * self.rows, self.rows)
        return self.part.at[c, pl.ds(first, self.rows)]

    def copy(self, c, step, way, src):
        return pltpu.make_async_remote_copy(
            src_ref=src,
            dst_ref=self.recv.at[c, step, way],
            send_sem=self.send_sem.at[c, step, way],
            recv_sem=self.recv_sem.at[c, step, way],
            device_id={"mp": self.me + (1 if way == 0 else -1)},
        )

    def sides(self):
        return ((0, self.me), (1, self.n - 1 - self.me))

    def step(self, c, step):
        n = self.n
        for way, place in self.sides():
            owner = n - 1 - step + self.me if way == 0 else step - (n - 1 - self.me)

            @pl.when(place == 0)
            def _(way=way, owner=owner):
                self.copy(c, step, way, self.piece(c, owner)).start()

            if step > 0:

                @pl.when((place > 0) & (place <= min(step, n - 2)))
                def _(way=way, owner=owner):
                    slot = self.send.at[c, step - 1, way]
                    self.copy(c, step - 1, way, slot).wait_recv()
                    slot[...] = (
                        self.piece(c, owner)[...].astype(F32)
                        + self.recv[c, step - 1, way].astype(F32)
                    ).astype(BF)
                    self.copy(c, step, way, slot).start()

    def total(self, c, out):
        n = self.n
        out[...] = self.piece(c, self.me)[...].astype(F32)
        for way, place in self.sides():

            @pl.when(place > 0)
            def _(way=way):
                self.copy(c, n - 2, way, self.recv.at[c, n - 2, way]).wait_recv()
                out[...] += self.recv[c, n - 2, way].astype(F32)

    def drain(self, c):
        n = self.n
        for step in range(n - 1):
            for way, place in self.sides():

                @pl.when(place <= min(step, n - 2))
                def _(way=way):
                    self.copy(c, step, way, self.recv.at[c, step, way]).wait_send()


def run_line(n, chunks, stagger, compute, scatter, row_work, gather):
    last_step = 2 * n - 2 if gather is not None else n - 1
    events = sorted(
        (step + stagger * c, c, step) for c in range(chunks) for step in range(last_step + 1)
    )
    for _, c, step in events:
        if step < n - 1:
            if step == 0:
                compute(c)
            scatter.step(c, step)
        elif step == n - 1:
            row_work(c)
            if gather is not None:
                gather.step(c, 1)
        elif step < 2 * n - 2:
            gather.step(c, step - n + 2)
        else:
            gather.last(c)
    for c in range(chunks):
        scatter.drain(c)
        if gather is not None:
            gather.drain(c)


def inverse_rms(rows):
    return lax.rsqrt(jnp.mean(rows * rows, axis=1, keepdims=True) + EPS)


def norm_back(values, inverse, gain_row, upstream):
    weighted = upstream * gain_row
    mean_term = jnp.mean(weighted * values, axis=1, keepdims=True)
    grad_values = inverse * weighted - values * (inverse * inverse * inverse) * mean_term
    return (grad_values, jnp.sum(upstream * values * inverse, axis=0, keepdims=True))


def scatter_scratch(n, rows, width):
    return [
        pltpu.VMEM((CHUNKS, n * rows, width), BF),
        pltpu.VMEM((CHUNKS, max(n - 2, 1), 2, rows, width), BF),
        pltpu.VMEM((CHUNKS, n - 1, 2, rows, width), BF),
        pltpu.SemaphoreType.DMA((CHUNKS, n - 1, 2)),
        pltpu.SemaphoreType.DMA((CHUNKS, n - 1, 2)),
        pltpu.VMEM((rows, width), F32),
    ]


def gather_scratch(n, rows, width):
    return [
        pltpu.VMEM((CHUNKS, rows, width), BF),
        pltpu.SemaphoreType.DMA((CHUNKS, n - 1, 2)),
        pltpu.SemaphoreType.DMA((CHUNKS, n - 1, 2)),
        pltpu.SemaphoreType.DMA((CHUNKS,)),
    ]


def chunk_span(c, rows):
    return pl.ds(c * rows, rows)


def make_gather(n, me, rows, own, full, send_sem, recv_sem, local_sem):
    return LineGather(
        n,
        me,
        lambda c: own.at[c],
        lambda block, c: full.at[block, chunk_span(c, rows)],
        send_sem,
        recv_sem,
        local_sem,
    )


def gather_rows_kernel(n, rows, block, full, send_sem, recv_sem, local_sem):
    me = lax.axis_index("mp")
    neighbour_barrier(me, n)
    gather = LineGather(
        n,
        me,
        lambda c: block.at[chunk_span(c, rows)],
        lambda index, c: full.at[index, chunk_span(c, rows)],
        send_sem,
        recv_sem,
        local_sem,
    )
    for step in range(1, n):
        for c in range(CHUNKS):
            gather.step(c, step)
    for c in range(CHUNKS):
        gather.last(c)
    for c in range(CHUNKS):
        gather.drain(c)


def gather_rows(n, block):
    rows = block.shape[0] // CHUNKS
    sems = gather_scratch(n, rows, block.shape[1])[1:]
    return pl.pallas_call(
        functools.partial(gather_rows_kernel, n, rows),
        out_shape=jax.ShapeDtypeStruct((n,) + block.shape, block.dtype),
        in_specs=[HBM],
        out_specs=HBM,
        scratch_shapes=sems,
        compiler_params=pltpu.CompilerParams(collective_id=0, has_side_effects=True),
        name="gather_rows",
    )(block)


def attn_out_kernel(
    n, rows, att, wo, x, scale, branch, middle, full,
    part, send, recv, rs_send_sem, rs_recv_sem, total, own, ag_send_sem, ag_recv_sem, local_sem,
    packed,
):
    me = lax.axis_index("mp")
    neighbour_barrier(me, n)
    width = wo.shape[1]
    block_rows = rows * CHUNKS

    def compute(c):
        for j in range(n):
            packed[j * rows : (j + 1) * rows] = att[
                j * block_rows + c * rows : j * block_rows + (c + 1) * rows
            ]

        @pl.loop(0, width // (2 * TILE))
        def _(tile):
            cols = pl.ds(pl.multiple_of(tile * 2 * TILE, 2 * TILE), 2 * TILE)
            part[c, :, cols] = plain_dot(packed[...], wo[:, cols]).astype(BF)

    scatter = LineScatter(n, me, rows, part, send, recv, rs_send_sem, rs_recv_sem)
    gather = make_gather(n, me, rows, own, full, ag_send_sem, ag_recv_sem, local_sem)

    def row_work(c):
        scatter.total(c, total)
        span = chunk_span(c, rows)
        value = total[...]
        branch[span] = value
        new = x[span].astype(F32) + value * inverse_rms(value) * scale[...]
        middle[span] = new
        own[c] = new.astype(BF)

    run_line(n, CHUNKS, STAGGER, compute, scatter, row_work, gather)


def attn_out(n, attended, full_out, layer_input, scale):
    row_count, width = layer_input.shape
    rows = row_count // CHUNKS
    return pl.pallas_call(
        functools.partial(attn_out_kernel, n, rows),
        out_shape=(
            jax.ShapeDtypeStruct((row_count, width), F32),
            jax.ShapeDtypeStruct((row_count, width), F32),
            jax.ShapeDtypeStruct((n, row_count, width), BF),
        ),
        in_specs=[VMEM] * 4,
        out_specs=(VMEM, VMEM, HBM),
        scratch_shapes=scatter_scratch(n, rows, width)
        + gather_scratch(n, rows, width)
        + [pltpu.VMEM((n * rows, attended.shape[1]), BF)],
        compiler_params=pltpu.CompilerParams(
            collective_id=1, has_side_effects=True, vmem_limit_bytes=56 * MIB
        ),
        name="attn_out",
    )(attended, full_out, layer_input, scale)


class WeightTiles:
    def __init__(self, source, held, sem, axis, size):
        self.source, self.held, self.sem, self.axis, self.size = source, held, sem, axis, size
        self.count = source.shape[axis] // size

    def at(self, ref, tile):
        span = pl.ds(pl.multiple_of(tile * self.size, self.size), self.size)
        return ref.at[:, span] if self.axis == 1 else ref.at[span]

    def copy(self, tile):
        return pltpu.make_async_copy(
            self.at(self.source, tile), self.at(self.held, tile), self.sem.at[tile]
        )

    def start(self):
        for tile in range(self.count):
            self.copy(tile).start()


def mlp_forward_kernel(
    n, rows, h_full, wg, wu, wd, middle, upstream_in, row_valid, scale,
    output, dm_full, gate_out, up_out, hidden_out, gain_out,
    part, send, recv, rs_send_sem, rs_recv_sem, total, own, ag_send_sem, ag_recv_sem, local_sem,
    vg, vu, vd, wsem, h_buf, h_sem, gate_buf, up_buf, hidden_buf, out_sem,
):
    me = lax.axis_index("mp")
    width, hidden_width = wg.shape

    def h_copy(c, j):
        return pltpu.make_async_copy(
            h_full.at[j, chunk_span(c, rows)],
            h_buf.at[c % 2, pl.ds(j * rows, rows)],
            h_sem.at[c % 2, j],
        )

    for j in range(n):
        h_copy(0, j).start()
    gate_tiles = WeightTiles(wg, vg, wsem.at[0], 1, TILE)
    up_tiles = WeightTiles(wu, vu, wsem.at[1], 1, TILE)
    down_tiles = WeightTiles(wd, vd, wsem.at[2], 1, TILE)
    for tile in range(gate_tiles.count):
        gate_tiles.copy(tile).start()
        up_tiles.copy(tile).start()
    down_tiles.start()
    neighbour_barrier(me, n)

    def save_copies(c, j):
        slot = c % 2
        span = pl.ds(j * rows, rows)
        return [
            pltpu.make_async_copy(
                buf.at[slot, span], out.at[j, chunk_span(c, rows)], out_sem.at[slot, k, j]
            )
            for k, (buf, out) in enumerate(
                ((gate_buf, gate_out), (up_buf, up_out), (hidden_buf, hidden_out))
            )
        ]

    def compute(c):
        slot = c % 2
        for j in range(n):
            h_copy(c, j).wait()
        if c + 1 < CHUNKS:
            for j in range(n):
                h_copy(c + 1, j).start()
        if c >= 2:
            for j in range(n):
                for copy in save_copies(c - 2, j):
                    copy.wait()

        @pl.loop(0, hidden_width // TILE)
        def _(tile):
            if c == 0:
                gate_tiles.copy(tile).wait()
                up_tiles.copy(tile).wait()
            cols = pl.ds(pl.multiple_of(tile * TILE, TILE), TILE)
            gate = plain_dot(h_buf[slot], vg[:, cols])
            up = plain_dot(h_buf[slot], vu[:, cols])
            gate_buf[slot, :, cols] = gate.astype(BF)
            up_buf[slot, :, cols] = up.astype(BF)
            hidden_buf[slot, :, cols] = (gate * jax.nn.sigmoid(gate) * up).astype(BF)

        for j in range(n):
            for copy in save_copies(c, j):
                copy.start()

        @pl.loop(0, width // TILE)
        def _(tile):
            if c == 0:
                down_tiles.copy(tile).wait()
            cols = pl.ds(pl.multiple_of(tile * TILE, TILE), TILE)
            part[c, :, cols] = plain_dot(hidden_buf[slot], vd[:, cols]).astype(BF)

    scatter = LineScatter(n, me, rows, part, send, recv, rs_send_sem, rs_recv_sem)
    gather = make_gather(n, me, rows, own, dm_full, ag_send_sem, ag_recv_sem, local_sem)

    def row_work(c):
        scatter.total(c, total)
        span = chunk_span(c, rows)
        value = total[...]
        inverse = inverse_rms(value)
        output[span] = (middle[span] + value * inverse * scale[...]).astype(BF)
        upstream = upstream_in[span].astype(F32) * row_valid[span]
        grad, gain = norm_back(value, inverse, scale[...], upstream)
        own[c] = grad.astype(BF)
        gain_out[...] = gain if c == 0 else gain_out[...] + gain

    run_line(n, CHUNKS, STAGGER, compute, scatter, row_work, gather)
    for c in range(max(CHUNKS - 2, 0), CHUNKS):
        for j in range(n):
            for copy in save_copies(c, j):
                copy.wait()


def mlp_forward(n, h_full, wg, wu, wd, middle, out_grad, row_valid, scale):
    row_count, width = middle.shape
    hidden_width = wg.shape[1]
    rows = row_count // CHUNKS
    saved = jax.ShapeDtypeStruct((n, row_count, hidden_width), BF)
    most = max(width, hidden_width) // TILE
    return pl.pallas_call(
        functools.partial(mlp_forward_kernel, n, rows),
        out_shape=(
            jax.ShapeDtypeStruct((row_count, width), BF),
            jax.ShapeDtypeStruct((n, row_count, width), BF),
            saved,
            saved,
            saved,
            jax.ShapeDtypeStruct((1, width), F32),
        ),
        in_specs=[HBM] * 4 + [VMEM] * 4,
        out_specs=(VMEM, HBM, HBM, HBM, HBM, VMEM),
        scratch_shapes=scatter_scratch(n, rows, width)
        + gather_scratch(n, rows, width)
        + [
            pltpu.VMEM(wg.shape, BF),
            pltpu.VMEM(wu.shape, BF),
            pltpu.VMEM(wd.shape, BF),
            pltpu.SemaphoreType.DMA((3, most)),
            pltpu.VMEM((2, n * rows, width), BF),
            pltpu.SemaphoreType.DMA((2, n)),
        ]
        + [pltpu.VMEM((2, n * rows, hidden_width), BF)] * 3
        + [pltpu.SemaphoreType.DMA((2, 3, n))],
        compiler_params=pltpu.CompilerParams(
            collective_id=2, has_side_effects=True, vmem_limit_bytes=60 * MIB
        ),
        name="mlp_forward",
    )(h_full, wg, wu, wd, middle, out_grad, row_valid, scale)


def mlp_backward_kernel(
    n, rows, dm_full, wg, wu, wd, gate_in, up_in, branch, upstream_in, row_valid, scale,
    middle_grad, da_full, gate_grad, up_grad, gain_out,
    part, send, recv, rs_send_sem, rs_recv_sem, total, own, ag_send_sem, ag_recv_sem, local_sem,
    vg, vu, vd, wsem, dm_buf, gate_buf, up_buf, in_sem, dgate_buf, dup_buf, out_sem,
):
    me = lax.axis_index("mp")
    width, hidden_width = wg.shape

    def in_copies(c, j):
        span = pl.ds(j * rows, rows)
        return [
            pltpu.make_async_copy(
                source.at[j, chunk_span(c, rows)], buf.at[span], in_sem.at[k, j]
            )
            for k, (source, buf) in enumerate(
                ((dm_full, dm_buf), (gate_in, gate_buf), (up_in, up_buf))
            )
        ]

    for j in range(n):
        for copy in in_copies(0, j):
            copy.start()
    down_tiles = WeightTiles(wd, vd, wsem.at[0], 0, TILE)
    gate_tiles = WeightTiles(wg, vg, wsem.at[1], 0, TILE)
    up_tiles = WeightTiles(wu, vu, wsem.at[2], 0, TILE)
    down_tiles.start()
    for tile in range(gate_tiles.count):
        gate_tiles.copy(tile).start()
        up_tiles.copy(tile).start()
    neighbour_barrier(me, n)

    def save_copies(c, j):
        slot = c % 2
        span = pl.ds(j * rows, rows)
        return [
            pltpu.make_async_copy(
                buf.at[slot, span], out.at[j, chunk_span(c, rows)], out_sem.at[slot, k, j]
            )
            for k, (buf, out) in enumerate(((dgate_buf, gate_grad), (dup_buf, up_grad)))
        ]

    def compute(c):
        slot = c % 2
        for j in range(n):
            for copy in in_copies(c, j):
                copy.wait()
        if c >= 2:
            for j in range(n):
                for copy in save_copies(c - 2, j):
                    copy.wait()

        @pl.loop(0, hidden_width // TILE)
        def _(tile):
            if c == 0:
                down_tiles.copy(tile).wait()
            cols = pl.ds(pl.multiple_of(tile * TILE, TILE), TILE)
            hidden_grad = outer_dot(dm_buf[...], vd[cols, :])
            gate = gate_buf[:, cols].astype(F32)
            up = up_buf[:, cols].astype(F32)
            sigmoid = jax.nn.sigmoid(gate)
            dgate_buf[slot, :, cols] = (
                hidden_grad * up * sigmoid * (1.0 + gate * (1.0 - sigmoid))
            ).astype(BF)
            dup_buf[slot, :, cols] = (hidden_grad * gate * sigmoid).astype(BF)

        if c + 1 < CHUNKS:
            for j in range(n):
                for copy in in_copies(c + 1, j):
                    copy.start()
        for j in range(n):
            for copy in save_copies(c, j):
                copy.start()

        @pl.loop(0, width // TILE)
        def _(tile):
            if c == 0:
                gate_tiles.copy(tile).wait()
                up_tiles.copy(tile).wait()
            cols = pl.ds(pl.multiple_of(tile * TILE, TILE), TILE)
            part[c, :, cols] = (
                outer_dot(dgate_buf[slot], vg[cols, :]) + outer_dot(dup_buf[slot], vu[cols, :])
            ).astype(BF)

    scatter = LineScatter(n, me, rows, part, send, recv, rs_send_sem, rs_recv_sem)
    gather = make_gather(n, me, rows, own, da_full, ag_send_sem, ag_recv_sem, local_sem)

    def row_work(c):
        scatter.total(c, total)
        span = chunk_span(c, rows)
        upstream = upstream_in[span].astype(F32) * row_valid[span] + total[...]
        middle_grad[span] = upstream
        value = branch[span]
        grad, gain = norm_back(value, inverse_rms(value), scale[...], upstream)
        own[c] = grad.astype(BF)
        gain_out[...] = gain if c == 0 else gain_out[...] + gain

    run_line(n, CHUNKS, STAGGER, compute, scatter, row_work, gather)
    for c in range(max(CHUNKS - 2, 0), CHUNKS):
        for j in range(n):
            for copy in save_copies(c, j):
                copy.wait()


def mlp_backward(n, dm_full, wg, wu, wd, gate, up, branch, out_grad, row_valid, scale):
    row_count, width = branch.shape
    hidden_width = wg.shape[1]
    rows = row_count // CHUNKS
    saved = jax.ShapeDtypeStruct((n, row_count, hidden_width), BF)
    most = max(width, hidden_width) // TILE
    return pl.pallas_call(
        functools.partial(mlp_backward_kernel, n, rows),
        out_shape=(
            jax.ShapeDtypeStruct((row_count, width), F32),
            jax.ShapeDtypeStruct((n, row_count, width), BF),
            saved,
            saved,
            jax.ShapeDtypeStruct((1, width), F32),
        ),
        in_specs=[HBM] * 6 + [VMEM] * 4,
        out_specs=(VMEM, HBM, HBM, HBM, VMEM),
        scratch_shapes=scatter_scratch(n, rows, width)
        + gather_scratch(n, rows, width)
        + [
            pltpu.VMEM(wg.shape, BF),
            pltpu.VMEM(wu.shape, BF),
            pltpu.VMEM(wd.shape, BF),
            pltpu.SemaphoreType.DMA((3, most)),
            pltpu.VMEM((n * rows, width), BF),
            pltpu.VMEM((n * rows, hidden_width), BF),
            pltpu.VMEM((n * rows, hidden_width), BF),
            pltpu.SemaphoreType.DMA((3, n)),
        ]
        + [pltpu.VMEM((2, n * rows, hidden_width), BF)] * 2
        + [pltpu.SemaphoreType.DMA((2, 2, n))],
        compiler_params=pltpu.CompilerParams(
            collective_id=3, has_side_effects=True, vmem_limit_bytes=60 * MIB
        ),
        name="mlp_backward",
    )(dm_full, wg, wu, wd, gate, up, branch, out_grad, row_valid, scale)


def input_grad_kernel(
    n, rows, grads, weight, base, out,
    part, send, recv, rs_send_sem, rs_recv_sem, total, packed,
):
    me = lax.axis_index("mp")
    neighbour_barrier(me, n)
    width = weight.shape[0]
    block_rows = rows * CHUNKS

    def compute(c):
        for j in range(n):
            packed[j * rows : (j + 1) * rows] = grads[
                j * block_rows + c * rows : j * block_rows + (c + 1) * rows
            ]

        @pl.loop(0, width // TILE)
        def _(tile):
            cols = pl.ds(pl.multiple_of(tile * TILE, TILE), TILE)
            part[c, :, cols] = outer_dot(packed[...], weight[cols, :]).astype(BF)

    scatter = LineScatter(n, me, rows, part, send, recv, rs_send_sem, rs_recv_sem)

    def row_work(c):
        scatter.total(c, total)
        span = chunk_span(c, rows)
        out[span] = base[span] + total[...]

    run_line(n, CHUNKS, 1, compute, scatter, row_work, None)


def input_gradient(n, grads, weight, base):
    row_count, width = base.shape
    rows = row_count // CHUNKS
    return pl.pallas_call(
        functools.partial(input_grad_kernel, n, rows),
        out_shape=jax.ShapeDtypeStruct((row_count, width), F32),
        in_specs=[VMEM] * 3,
        out_specs=VMEM,
        scratch_shapes=scatter_scratch(n, rows, width)
        + [pltpu.VMEM((n * rows, grads.shape[1]), BF)],
        compiler_params=pltpu.CompilerParams(
            collective_id=4, has_side_effects=True, vmem_limit_bytes=56 * MIB
        ),
        name="input_gradient",
    )(grads, weight, base)


def turn(values, cos, sin):
    return values * cos + pltpu.roll(values, values.shape[1] // 2, 1) * sin


def turn_back(values, cos, sin):
    return values * cos + pltpu.roll(values * sin, values.shape[1] // 2, 1)


def allowed_keys(starts, first_row, rows, key_end):
    places = first_row + lax.broadcasted_iota(jnp.int32, (rows, key_end), 0)
    keys = lax.broadcasted_iota(jnp.int32, (rows, key_end), 1)
    return (keys <= places) & (keys >= starts)


def attention_kernel(
    q_raw, k_raw, v_raw, q_inv, k_inv, q_gain, k_gain, cos, sin, starts,
    out, q_low, k_low, v_low, log_total,
):
    size, head = q_raw.shape
    score_scale = 1.0 / math.sqrt(head)
    q_low[...] = turn(q_raw[...] * q_inv[...] * q_gain[...], cos[...], sin[...]).astype(BF)
    k_low[...] = turn(k_raw[...] * k_inv[...] * k_gain[...], cos[...], sin[...]).astype(BF)
    v_low[...] = v_raw[...].astype(BF)
    rows = min(QUERY_ROWS, size)
    for first in range(0, size, rows):
        end = first + rows
        span = slice(first, end)
        scores = outer_dot(q_low[span], k_low[:end]) * score_scale
        scores = jnp.where(allowed_keys(starts[span], first, rows, end), scores, MASKED)
        row_max = jnp.max(scores, axis=1, keepdims=True)
        exponents = jnp.exp(scores - row_max)
        row_total = jnp.sum(exponents, axis=1, keepdims=True)
        probs = (exponents * (1.0 / row_total)).astype(BF)
        out[span] = plain_dot(probs, v_low[:end]).astype(BF)
        log_total[span] = row_max + jnp.log(row_total)


def head_specs(size, head, heads, count):
    return [pl.BlockSpec((size, head), lambda h, k=k: (0, k * heads + h)) for k in range(count)]


def attention(qkv_raw, q_inv, k_inv, q_gain, k_gain, cos, sin, starts, heads):
    size = qkv_raw.shape[0]
    head = cos.shape[1]
    column = pl.BlockSpec((size, 1), lambda h: (0, 0))
    table = pl.BlockSpec((size, head), lambda h: (0, 0))
    gain = pl.BlockSpec((1, head), lambda h: (0, h))
    by_head = pl.BlockSpec((size, head), lambda h: (0, h))
    low = jax.ShapeDtypeStruct((size, heads * head), BF)
    return pl.pallas_call(
        attention_kernel,
        grid=(heads,),
        out_shape=(low, low, low, low, jax.ShapeDtypeStruct((heads, size, 1), F32)),
        in_specs=head_specs(size, head, heads, 3)
        + [column, column, gain, gain, table, table, column],
        out_specs=(by_head,) * 4 + (pl.BlockSpec((None, size, 1), lambda h: (h, 0, 0)),),
        compiler_params=pltpu.CompilerParams(vmem_limit_bytes=48 * MIB),
        name="attention",
    )(qkv_raw, qkv_raw, qkv_raw, q_inv, k_inv, q_gain, k_gain, cos, sin, starts)


def attention_back_kernel(
    q_raw, k_raw, q_low, k_low, v_low, out_grad, log_total,
    q_inv, k_inv, q_gain, k_gain, cos, sin, starts,
    q_weighted, k_weighted, v_grad, q_dots, k_dots, q_gain_grad, k_gain_grad,
    q_grad, k_sum, v_sum,
):
    size, head = q_raw.shape
    score_scale = 1.0 / math.sqrt(head)
    rows = min(QUERY_ROWS, size)
    for first in reversed(range(0, size, rows)):
        end = first + rows
        span = slice(first, end)
        scores = outer_dot(q_low[span], k_low[:end]) * score_scale
        scores = jnp.where(allowed_keys(starts[span], first, rows, end), scores, MASKED)
        probs = jnp.exp(scores - log_total[span])
        prob_grad = outer_dot(out_grad[span], v_low[:end])
        probs_low = probs.astype(BF)
        weighted = probs * prob_grad
        score_grad = (
            weighted - probs * jnp.sum(weighted, axis=1, keepdims=True)
        ).astype(BF)
        q_grad[span] = plain_dot(score_grad, k_low[:end]) * score_scale
        k_extra = inner_dot(score_grad, q_low[span])
        v_extra = inner_dot(probs_low, out_grad[span])
        if end == size:
            k_sum[...] = k_extra
            v_sum[...] = v_extra
        else:
            k_sum[:end] += k_extra
            v_sum[:end] += v_extra
    first_head = pl.program_id(0) == 0
    for raw, inv, gain, grad, factor, weighted_out, dots, gain_grad in (
        (q_raw, q_inv, q_gain, q_grad, None, q_weighted, q_dots, q_gain_grad),
        (k_raw, k_inv, k_gain, k_sum, score_scale, k_weighted, k_dots, k_gain_grad),
    ):
        value = grad[...] if factor is None else grad[...] * factor
        normed = turn_back(value, cos[...], sin[...])
        weighted = normed * gain[...]
        weighted_out[...] = weighted
        gain_grad[...] = jnp.sum(normed * raw[...] * inv[...], axis=0, keepdims=True)
        dot = jnp.sum(weighted * raw[...], axis=1, keepdims=True)

        @pl.when(first_head)
        def _():
            dots[...] = dot

        @pl.when(jnp.logical_not(first_head))
        def _():
            dots[...] += dot

    v_grad[...] = v_sum[...].astype(BF)


def attention_back(
    qkv_raw, q_low, k_low, v_low, out_grad, log_total, q_inv, k_inv, q_gain, k_gain, cos, sin,
    starts, heads,
):
    size = qkv_raw.shape[0]
    head = cos.shape[1]
    column = pl.BlockSpec((size, 1), lambda h: (0, 0))
    table = pl.BlockSpec((size, head), lambda h: (0, 0))
    gain = pl.BlockSpec((1, head), lambda h: (0, h))
    by_head = pl.BlockSpec((size, head), lambda h: (0, h))
    wide = jax.ShapeDtypeStruct((size, heads * head), F32)
    dots = jax.ShapeDtypeStruct((size, 1), F32)
    gains = jax.ShapeDtypeStruct((1, heads * head), F32)
    return pl.pallas_call(
        attention_back_kernel,
        grid=(heads,),
        out_shape=(
            wide, wide, jax.ShapeDtypeStruct((size, heads * head), BF), dots, dots, gains, gains,
        ),
        in_specs=head_specs(size, head, heads, 2)
        + [by_head] * 4
        + [pl.BlockSpec((None, size, 1), lambda h: (h, 0, 0))]
        + [column, column, gain, gain, table, table, column],
        out_specs=(by_head, by_head, by_head, column, column, gain, gain),
        scratch_shapes=[pltpu.VMEM((size, head), F32)] * 3,
        compiler_params=pltpu.CompilerParams(vmem_limit_bytes=48 * MIB),
        name="attention_back",
    )(
        qkv_raw, qkv_raw, q_low, k_low, v_low, out_grad, log_total,
        q_inv, k_inv, q_gain, k_gain, cos, sin, starts,
    )


def local(
    layer_input,
    query_weight,
    key_weight,
    value_weight,
    out_weight,
    gate_weight,
    up_weight,
    down_weight,
    query_gain,
    key_gain,
    attn_gain,
    mlp_gain,
    seq_lens,
    out_grad,
):
    n = lax.axis_size("mp")
    n_dp = lax.axis_size("dp")
    me = lax.axis_index("mp")
    row_count, model_width = layer_input.shape
    group_size = row_count * n
    local_heads, gain_part = query_gain.shape
    head_size = gain_part * n_dp
    local_width = local_heads * head_size

    full_qkv = lax.all_gather(
        jnp.concatenate([query_weight, key_weight, value_weight], axis=1), "dp", axis=0, tiled=True
    )
    full_out = lax.all_gather(out_weight, "dp", axis=1, tiled=True)
    full_gate = lax.all_gather(gate_weight, "dp", axis=0, tiled=True)
    full_up = lax.all_gather(up_weight, "dp", axis=0, tiled=True)
    full_down = lax.all_gather(down_weight, "dp", axis=1, tiled=True)
    head_part = local_heads * gain_part
    gain_parts = lax.all_gather(
        jnp.concatenate(
            [query_gain.reshape(head_part), key_gain.reshape(head_part), attn_gain, mlp_gain]
        ),
        "dp",
        axis=0,
    ).astype(F32)
    width_part = attn_gain.shape[0]

    def head_gain(first):
        piece = gain_parts[:, first : first + head_part].reshape(n_dp, local_heads, gain_part)
        return piece.transpose(1, 0, 2).reshape(1, local_width)

    query_scale = head_gain(0)
    key_scale = head_gain(head_part)
    attn_scale = gain_parts[:, 2 * head_part : 2 * head_part + width_part].reshape(1, model_width)
    mlp_scale = gain_parts[:, 2 * head_part + width_part :].reshape(1, model_width)

    starts, positions, valid = layout(seq_lens[0], group_size)
    starts = starts[:, None]
    cos_table, sin_table = rotary_tables(positions, head_size)
    row_valid = lax.dynamic_slice_in_dim(valid, me * row_count, row_count, 0).astype(F32)[:, None]

    inputs_full = gather_rows(n, layer_input).reshape(group_size, model_width)
    qkv_raw = plain_dot(inputs_full, full_qkv)
    query_raw = qkv_raw[:, :local_width]
    key_raw = qkv_raw[:, local_width : 2 * local_width]
    query_sums, key_sums = lax.psum(
        (jnp.sum(query_raw * query_raw, axis=1), jnp.sum(key_raw * key_raw, axis=1)), "mp"
    )
    query_inv = lax.rsqrt(query_sums / model_width + EPS)[:, None]
    key_inv = lax.rsqrt(key_sums / model_width + EPS)[:, None]
    attended, query_low, key_low, value_low, log_total = attention(
        qkv_raw, query_inv, key_inv, query_scale, key_scale, cos_table, sin_table, starts,
        local_heads,
    )
    branch, middle, middle_full = attn_out(n, attended, full_out, layer_input, attn_scale)
    layer_output, mlp_grad_full, gate, up, hidden, mlp_gain_part = mlp_forward(
        n, middle_full, full_gate, full_up, full_down, middle, out_grad, row_valid, mlp_scale
    )
    middle_grad, branch_full, gate_grad, up_grad, attn_gain_part = mlp_backward(
        n, mlp_grad_full, full_gate, full_up, full_down, gate, up, branch, out_grad, row_valid,
        attn_scale,
    )

    def flat(rows):
        return rows.reshape(group_size, rows.shape[-1])

    def dp_scatter(part, dimension):
        return lax.psum_scatter(
            part.astype(BF), "dp", scatter_dimension=dimension, tiled=True
        ).astype(F32)

    grad_down = dp_scatter(inner_dot(flat(hidden), flat(mlp_grad_full)), 1)
    grad_gate = dp_scatter(inner_dot(flat(middle_full), flat(gate_grad)), 0)
    grad_up = dp_scatter(inner_dot(flat(middle_full), flat(up_grad)), 0)
    grad_out = dp_scatter(inner_dot(attended, flat(branch_full)), 1)

    mixed_grad = outer_dot(flat(branch_full), full_out).astype(BF)
    query_weighted, key_weighted, value_grad, query_dots, key_dots, query_gain_part, key_gain_part = (
        attention_back(
            qkv_raw, query_low, key_low, value_low, mixed_grad, log_total, query_inv, key_inv,
            query_scale, key_scale, cos_table, sin_table, starts, local_heads,
        )
    )
    query_dots, key_dots, attn_gain_sum, mlp_gain_sum = lax.psum(
        (query_dots[:, 0], key_dots[:, 0], attn_gain_part[0], mlp_gain_part[0]), "mp"
    )
    query_raw_grad = (
        query_inv * query_weighted - query_raw * query_inv**3 * (query_dots / model_width)[:, None]
    ).astype(BF)
    key_raw_grad = (
        key_inv * key_weighted - key_raw * key_inv**3 * (key_dots / model_width)[:, None]
    ).astype(BF)
    qkv_grad = jnp.concatenate([query_raw_grad, key_raw_grad, value_grad], axis=1)
    grad_qkv = dp_scatter(inner_dot(inputs_full, qkv_grad), 0)
    input_grad = input_gradient(n, qkv_grad, full_qkv, middle_grad)

    gain_sums = lax.psum(
        jnp.concatenate([attn_gain_sum, mlp_gain_sum, query_gain_part[0], key_gain_part[0]]), "dp"
    )
    at = lax.axis_index("dp")
    grad_attn_gain = lax.dynamic_slice_in_dim(gain_sums, at * width_part, width_part)
    grad_mlp_gain = lax.dynamic_slice_in_dim(gain_sums, model_width + at * width_part, width_part)

    def head_gain_grad(first):
        whole = gain_sums[first : first + local_width].reshape(local_heads, head_size)
        return lax.dynamic_slice_in_dim(whole, at * gain_part, gain_part, 1)

    return (
        layer_output,
        input_grad,
        grad_qkv[:, :local_width],
        grad_qkv[:, local_width : 2 * local_width],
        grad_qkv[:, 2 * local_width :],
        grad_out,
        grad_gate,
        grad_up,
        grad_down,
        head_gain_grad(2 * model_width),
        head_gain_grad(2 * model_width + local_width),
        grad_attn_gain,
        grad_mlp_gain,
    )


def solution(mesh):
    return jax.shard_map(
        local,
        mesh=mesh,
        in_specs=(
            P(("dp", "mp"), None),
            P("dp", "mp"),
            P("dp", "mp"),
            P("dp", "mp"),
            P("mp", "dp"),
            P("dp", "mp"),
            P("dp", "mp"),
            P("mp", "dp"),
            P("mp", "dp"),
            P("mp", "dp"),
            P("dp"),
            P("dp"),
            P("dp", None),
            P(("dp", "mp"), None),
        ),
        out_specs=(
            P(("dp", "mp"), None),
            P(("dp", "mp"), None),
            P("dp", "mp"),
            P("dp", "mp"),
            P("dp", "mp"),
            P("mp", "dp"),
            P("dp", "mp"),
            P("dp", "mp"),
            P("mp", "dp"),
            P("mp", "dp"),
            P("mp", "dp"),
            P("dp"),
            P("dp"),
        ),
        check_vma=False,
    )
```

```python
import functools
import math

import jax
import jax.numpy as jnp
from jax import lax
from jax.experimental import pallas as pl
from jax.experimental.pallas import tpu as pltpu
from jax.sharding import PartitionSpec as P

EPS = 1e-06
THETA = 500000.0
MASKED = -1000000000.0
CHUNKS = 4
STAGGER = 2
TILE = 256
QUERY_ROWS = 256
BF = jnp.bfloat16
F32 = jnp.float32
MIB = 1 << 20
HBM = pl.BlockSpec(memory_space=pl.ANY)
VMEM = pl.BlockSpec(memory_space=pltpu.VMEM)


def cost(micros):
    return pl.CostEstimate(
        flops=micros * 1_000_000_000, bytes_accessed=micros * 3_000_000, transcendentals=0
    )


def plain_dot(former, latter):
    return jnp.dot(former, latter, preferred_element_type=F32)


def inner_dot(former, latter):
    return lax.dot_general(
        former, latter, (((0,), (0,)), ((), ())), preferred_element_type=F32
    )


def outer_dot(former, latter):
    return lax.dot_general(
        former, latter, (((1,), (1,)), ((), ())), preferred_element_type=F32
    )


def layout(lengths, group_size):
    slot_count = lengths.shape[0]
    seq_ends = jnp.cumsum(lengths, dtype=jnp.int32)
    starts = seq_ends - lengths
    places = jnp.arange(group_size, dtype=jnp.int32)
    slot_ids = jnp.arange(slot_count, dtype=jnp.int32)
    segment = jnp.sum(
        (places[:, None] >= seq_ends[None, :]).astype(jnp.int32), axis=1, dtype=jnp.int32
    )
    chosen = (segment[:, None] == slot_ids[None, :]).astype(jnp.int32)
    padded = (segment == slot_count).astype(jnp.int32)
    begins = (
        jnp.sum(chosen * starts[None, :], axis=1, dtype=jnp.int32)
        + padded * seq_ends[slot_count - 1]
    )
    return (begins, places - begins, places < seq_ends[slot_count - 1])


def rotary_tables(positions, head_size):
    half_dim = head_size // 2
    frequency = jnp.exp(jnp.arange(half_dim, dtype=F32) * (-2.0 * math.log(THETA) / head_size))
    angles = positions.astype(F32)[:, None] * frequency[None, :]
    cos_half, sin_half = jnp.cos(angles), jnp.sin(angles)
    return (
        jnp.concatenate([cos_half, cos_half], axis=1),
        jnp.concatenate([-sin_half, sin_half], axis=1),
    )


def neighbour_barrier(me, n):
    barrier = pltpu.get_barrier_semaphore()

    @pl.when(me > 0)
    def _():
        pl.semaphore_signal(barrier, inc=1, device_id={"mp": me - 1})

    @pl.when(me < n - 1)
    def _():
        pl.semaphore_signal(barrier, inc=1, device_id={"mp": me + 1})

    pl.semaphore_wait(barrier, jnp.minimum(me, 1) + jnp.minimum(n - 1 - me, 1))


class LineGather:
    def __init__(self, n, me, own, full, send_sem, recv_sem, local_sem):
        self.n, self.me, self.own, self.full = n, me, own, full
        self.send_sem, self.recv_sem, self.local_sem = send_sem, recv_sem, local_sem

    def local_copy(self, c):
        return pltpu.make_async_copy(self.own(c), self.full(self.me, c), self.local_sem.at[c])

    def copy(self, c, step, way, block, src):
        return pltpu.make_async_remote_copy(
            src_ref=src,
            dst_ref=self.full(block, c),
            send_sem=self.send_sem.at[c, step - 1, way],
            recv_sem=self.recv_sem.at[c, step - 1, way],
            device_id={"mp": self.me + (1 if way == 0 else -1)},
        )

    def sides(self):
        return ((0, self.me), (1, self.n - 1 - self.me))

    def block_at(self, way, step):
        return self.me - step if way == 0 else self.me + step

    def step(self, c, step):
        n = self.n
        if step == 1:
            self.local_copy(c).start()
        for way, place in self.sides():
            if step > 1:

                @pl.when(place >= step - 1)
                def _(way=way):
                    block = self.block_at(way, step - 1)
                    self.copy(c, step - 1, way, block, self.own(c)).wait_recv()

            @pl.when((place >= step - 1) & (place < n - 1))
            def _(way=way):
                block = self.block_at(way, step - 1)
                src = self.own(c) if step == 1 else self.full(block, c)
                self.copy(c, step, way, block, src).start()

    def last(self, c):
        n = self.n
        for way, place in self.sides():

            @pl.when(place == n - 1)
            def _(way=way):
                block = self.block_at(way, n - 1)
                self.copy(c, n - 1, way, block, self.own(c)).wait_recv()

    def drain(self, c):
        self.local_copy(c).wait()
        for step in range(1, self.n):
            for way, place in self.sides():

                @pl.when((place >= step - 1) & (place < self.n - 1))
                def _(way=way):
                    self.copy(c, step, way, self.me, self.own(c)).wait_send()


class LineScatter:
    def __init__(self, n, me, rows, part, send, recv, send_sem, recv_sem):
        self.n, self.me, self.rows = n, me, rows
        self.part, self.send, self.recv = part, send, recv
        self.send_sem, self.recv_sem = send_sem, recv_sem

    def piece(self, c, owner):
        first = pl.multiple_of(owner * self.rows, self.rows)
        return self.part.at[c, pl.ds(first, self.rows)]

    def copy(self, c, step, way, src):
        return pltpu.make_async_remote_copy(
            src_ref=src,
            dst_ref=self.recv.at[c, step, way],
            send_sem=self.send_sem.at[c, step, way],
            recv_sem=self.recv_sem.at[c, step, way],
            device_id={"mp": self.me + (1 if way == 0 else -1)},
        )

    def sides(self):
        return ((0, self.me), (1, self.n - 1 - self.me))

    def step(self, c, step):
        n = self.n
        for way, place in self.sides():
            owner = n - 1 - step + self.me if way == 0 else step - (n - 1 - self.me)

            @pl.when(place == 0)
            def _(way=way, owner=owner):
                self.copy(c, step, way, self.piece(c, owner)).start()

            if step > 0:

                @pl.when((place > 0) & (place <= min(step, n - 2)))
                def _(way=way, owner=owner):
                    slot = self.send.at[c, step - 1, way]
                    self.copy(c, step - 1, way, slot).wait_recv()
                    slot[...] = (
                        self.piece(c, owner)[...].astype(F32)
                        + self.recv[c, step - 1, way].astype(F32)
                    ).astype(BF)
                    self.copy(c, step, way, slot).start()

    def total(self, c, out):
        n = self.n
        out[...] = self.piece(c, self.me)[...].astype(F32)
        for way, place in self.sides():

            @pl.when(place > 0)
            def _(way=way):
                self.copy(c, n - 2, way, self.recv.at[c, n - 2, way]).wait_recv()
                out[...] += self.recv[c, n - 2, way].astype(F32)

    def drain(self, c):
        n = self.n
        for step in range(n - 1):
            for way, place in self.sides():

                @pl.when(place <= min(step, n - 2))
                def _(way=way):
                    self.copy(c, step, way, self.recv.at[c, step, way]).wait_send()


def run_line(n, chunks, stagger, compute, scatter, row_work, gather):
    last_step = 2 * n - 2 if gather is not None else n - 1
    events = sorted(
        (step + stagger * c, c, step) for c in range(chunks) for step in range(last_step + 1)
    )
    for _, c, step in events:
        if step < n - 1:
            if step == 0:
                compute(c)
            scatter.step(c, step)
        elif step == n - 1:
            row_work(c)
            if gather is not None:
                gather.step(c, 1)
        elif step < 2 * n - 2:
            gather.step(c, step - n + 2)
        else:
            gather.last(c)
    for c in range(chunks):
        scatter.drain(c)
        if gather is not None:
            gather.drain(c)


def inverse_rms(rows):
    return lax.rsqrt(jnp.mean(rows * rows, axis=1, keepdims=True) + EPS)


def norm_back(values, inverse, gain_row, upstream):
    weighted = upstream * gain_row
    mean_term = jnp.mean(weighted * values, axis=1, keepdims=True)
    grad_values = inverse * weighted - values * (inverse * inverse * inverse) * mean_term
    return (grad_values, jnp.sum(upstream * values * inverse, axis=0, keepdims=True))


def scatter_scratch(n, rows, width):
    return [
        pltpu.VMEM((CHUNKS, n * rows, width), BF),
        pltpu.VMEM((CHUNKS, max(n - 2, 1), 2, rows, width), BF),
        pltpu.VMEM((CHUNKS, n - 1, 2, rows, width), BF),
        pltpu.SemaphoreType.DMA((CHUNKS, n - 1, 2)),
        pltpu.SemaphoreType.DMA((CHUNKS, n - 1, 2)),
        pltpu.VMEM((rows, width), F32),
    ]


def gather_scratch(n, rows, width):
    return [
        pltpu.VMEM((CHUNKS, rows, width), BF),
        pltpu.SemaphoreType.DMA((CHUNKS, n - 1, 2)),
        pltpu.SemaphoreType.DMA((CHUNKS, n - 1, 2)),
        pltpu.SemaphoreType.DMA((CHUNKS,)),
    ]


def chunk_span(c, rows):
    return pl.ds(c * rows, rows)


def make_gather(n, me, rows, own, full, send_sem, recv_sem, local_sem):
    return LineGather(
        n,
        me,
        lambda c: own.at[c],
        lambda block, c: full.at[block, chunk_span(c, rows)],
        send_sem,
        recv_sem,
        local_sem,
    )


def peer_barrier(axes):
    barrier = pltpu.get_barrier_semaphore()
    count = 0
    for name, index, size in axes:
        for shift in range(1, size):
            pl.semaphore_signal(barrier, inc=1, device_id={name: lax.rem(index + shift, size)})
            count += 1
    return lambda: pl.semaphore_wait(barrier, count)


def exchange(name, index, size, src, recv, send_sem, recv_sem):
    def copy(shift):
        peer = lax.rem(index + shift, size)
        return pltpu.make_async_remote_copy(
            src_ref=src(peer),
            dst_ref=recv.at[shift - 1],
            send_sem=send_sem.at[shift - 1],
            recv_sem=recv_sem.at[shift - 1],
            device_id={name: peer},
        )

    return [copy(shift) for shift in range(1, size)]


def gather_rows_kernel(
    n, n_dp, rows, block, gains, full, gain_parts,
    send_sem, recv_sem, local_sem, gain_recv, gain_send_sem, gain_recv_sem,
):
    me, at = lax.axis_index("mp"), lax.axis_index("dp")
    peer_barrier((("mp", me, n), ("dp", at, n_dp)))()
    gather = LineGather(
        n,
        me,
        lambda c: block.at[chunk_span(c, rows)],
        lambda index, c: full.at[index, chunk_span(c, rows)],
        send_sem,
        recv_sem,
        local_sem,
    )
    for c in range(CHUNKS):
        gather.step(c, 1)
    copies = exchange(
        "dp", at, n_dp, lambda peer: gains, gain_recv, gain_send_sem, gain_recv_sem
    )
    for copy in copies:
        copy.start()
    for step in range(2, n):
        for c in range(CHUNKS):
            gather.step(c, step)
    gain_parts[at] = gains[...]
    for shift, copy in enumerate(copies, 1):
        copy.wait_recv()
        gain_parts[lax.rem(at + n_dp - shift, n_dp)] = gain_recv[shift - 1]
    for c in range(CHUNKS):
        gather.last(c)
    for c in range(CHUNKS):
        gather.drain(c)
    for copy in copies:
        copy.wait_send()


def gather_rows(n, n_dp, block, gains):
    rows = block.shape[0] // CHUNKS
    sems = gather_scratch(n, rows, block.shape[1])[1:]
    return pl.pallas_call(
        functools.partial(gather_rows_kernel, n, n_dp, rows),
        out_shape=(
            jax.ShapeDtypeStruct((n,) + block.shape, block.dtype),
            jax.ShapeDtypeStruct((n_dp,) + gains.shape, F32),
        ),
        in_specs=[HBM, VMEM],
        out_specs=(HBM, VMEM),
        scratch_shapes=sems
        + [
            pltpu.VMEM((n_dp - 1,) + gains.shape, F32),
            pltpu.SemaphoreType.DMA((n_dp - 1,)),
            pltpu.SemaphoreType.DMA((n_dp - 1,)),
        ],
        compiler_params=pltpu.CompilerParams(collective_id=0, has_side_effects=True),
        name="gather_rows",
        cost_estimate=cost(75),
    )(block, gains)


def attn_out_kernel(
    n, rows, att, wo, x, scale, branch, middle, full,
    part, send, recv, rs_send_sem, rs_recv_sem, total, own, ag_send_sem, ag_recv_sem, local_sem,
    packed,
):
    me = lax.axis_index("mp")
    neighbour_barrier(me, n)
    width = wo.shape[1]
    block_rows = rows * CHUNKS

    def compute(c):
        for j in range(n):
            packed[j * rows : (j + 1) * rows] = att[
                j * block_rows + c * rows : j * block_rows + (c + 1) * rows
            ]

        @pl.loop(0, width // (2 * TILE))
        def _(tile):
            cols = pl.ds(pl.multiple_of(tile * 2 * TILE, 2 * TILE), 2 * TILE)
            part[c, :, cols] = plain_dot(packed[...], wo[:, cols]).astype(BF)

    scatter = LineScatter(n, me, rows, part, send, recv, rs_send_sem, rs_recv_sem)
    gather = make_gather(n, me, rows, own, full, ag_send_sem, ag_recv_sem, local_sem)

    def row_work(c):
        scatter.total(c, total)
        span = chunk_span(c, rows)
        value = total[...]
        branch[span] = value
        new = x[span].astype(F32) + value * inverse_rms(value) * scale[...]
        middle[span] = new
        own[c] = new.astype(BF)

    run_line(n, CHUNKS, STAGGER, compute, scatter, row_work, gather)


def attn_out(n, attended, full_out, layer_input, scale):
    row_count, width = layer_input.shape
    rows = row_count // CHUNKS
    return pl.pallas_call(
        functools.partial(attn_out_kernel, n, rows),
        out_shape=(
            jax.ShapeDtypeStruct((row_count, width), F32),
            jax.ShapeDtypeStruct((row_count, width), F32),
            jax.ShapeDtypeStruct((n, row_count, width), BF),
        ),
        in_specs=[VMEM] * 4,
        out_specs=(VMEM, VMEM, HBM),
        scratch_shapes=scatter_scratch(n, rows, width)
        + gather_scratch(n, rows, width)
        + [pltpu.VMEM((n * rows, attended.shape[1]), BF)],
        compiler_params=pltpu.CompilerParams(
            collective_id=1, has_side_effects=True, vmem_limit_bytes=56 * MIB
        ),
        name="attn_out",
        cost_estimate=cost(115),
    )(attended, full_out, layer_input, scale)


class WeightTiles:
    def __init__(self, source, held, sem, axis, size):
        self.source, self.held, self.sem, self.axis, self.size = source, held, sem, axis, size
        self.count = source.shape[axis] // size

    def at(self, ref, tile):
        span = pl.ds(pl.multiple_of(tile * self.size, self.size), self.size)
        return ref.at[:, span] if self.axis == 1 else ref.at[span]

    def copy(self, tile):
        return pltpu.make_async_copy(
            self.at(self.source, tile), self.at(self.held, tile), self.sem.at[tile]
        )

    def start(self):
        for tile in range(self.count):
            self.copy(tile).start()


def mlp_forward_kernel(
    n, rows, h_full, wg, wu, wd, middle, upstream_in, row_valid, scale,
    output, dm_full, gate_out, up_out, hidden_out, gain_out,
    part, send, recv, rs_send_sem, rs_recv_sem, total, own, ag_send_sem, ag_recv_sem, local_sem,
    vg, vu, vd, wsem, h_buf, h_sem, gate_buf, up_buf, hidden_buf, out_sem,
):
    me = lax.axis_index("mp")
    width, hidden_width = wg.shape

    def h_copy(c, j):
        return pltpu.make_async_copy(
            h_full.at[j, chunk_span(c, rows)],
            h_buf.at[c % 2, pl.ds(j * rows, rows)],
            h_sem.at[c % 2, j],
        )

    for j in range(n):
        h_copy(0, j).start()
    gate_tiles = WeightTiles(wg, vg, wsem.at[0], 1, TILE)
    up_tiles = WeightTiles(wu, vu, wsem.at[1], 1, TILE)
    down_tiles = WeightTiles(wd, vd, wsem.at[2], 1, TILE)
    for tile in range(gate_tiles.count):
        gate_tiles.copy(tile).start()
        up_tiles.copy(tile).start()
    down_tiles.start()
    neighbour_barrier(me, n)

    def save_copies(c, j):
        slot = c % 2
        span = pl.ds(j * rows, rows)
        return [
            pltpu.make_async_copy(
                buf.at[slot, span], out.at[j, chunk_span(c, rows)], out_sem.at[slot, k, j]
            )
            for k, (buf, out) in enumerate(
                ((gate_buf, gate_out), (up_buf, up_out), (hidden_buf, hidden_out))
            )
        ]

    def compute(c):
        slot = c % 2
        for j in range(n):
            h_copy(c, j).wait()
        if c + 1 < CHUNKS:
            for j in range(n):
                h_copy(c + 1, j).start()
        if c >= 2:
            for j in range(n):
                for copy in save_copies(c - 2, j):
                    copy.wait()

        @pl.loop(0, hidden_width // TILE)
        def _(tile):
            if c == 0:
                gate_tiles.copy(tile).wait()
                up_tiles.copy(tile).wait()
            cols = pl.ds(pl.multiple_of(tile * TILE, TILE), TILE)
            gate = plain_dot(h_buf[slot], vg[:, cols])
            up = plain_dot(h_buf[slot], vu[:, cols])
            gate_buf[slot, :, cols] = gate.astype(BF)
            up_buf[slot, :, cols] = up.astype(BF)
            hidden_buf[slot, :, cols] = (gate * jax.nn.sigmoid(gate) * up).astype(BF)

        for j in range(n):
            for copy in save_copies(c, j):
                copy.start()

        @pl.loop(0, width // TILE)
        def _(tile):
            if c == 0:
                down_tiles.copy(tile).wait()
            cols = pl.ds(pl.multiple_of(tile * TILE, TILE), TILE)
            part[c, :, cols] = plain_dot(hidden_buf[slot], vd[:, cols]).astype(BF)

    scatter = LineScatter(n, me, rows, part, send, recv, rs_send_sem, rs_recv_sem)
    gather = make_gather(n, me, rows, own, dm_full, ag_send_sem, ag_recv_sem, local_sem)

    def row_work(c):
        scatter.total(c, total)
        span = chunk_span(c, rows)
        value = total[...]
        inverse = inverse_rms(value)
        output[span] = (middle[span] + value * inverse * scale[...]).astype(BF)
        upstream = upstream_in[span].astype(F32) * row_valid[span]
        grad, gain = norm_back(value, inverse, scale[...], upstream)
        own[c] = grad.astype(BF)
        gain_out[...] = gain if c == 0 else gain_out[...] + gain

    run_line(n, CHUNKS, STAGGER, compute, scatter, row_work, gather)
    for c in range(max(CHUNKS - 2, 0), CHUNKS):
        for j in range(n):
            for copy in save_copies(c, j):
                copy.wait()


def mlp_forward(n, h_full, wg, wu, wd, middle, out_grad, row_valid, scale):
    row_count, width = middle.shape
    hidden_width = wg.shape[1]
    rows = row_count // CHUNKS
    saved = jax.ShapeDtypeStruct((n, row_count, hidden_width), BF)
    most = max(width, hidden_width) // TILE
    return pl.pallas_call(
        functools.partial(mlp_forward_kernel, n, rows),
        out_shape=(
            jax.ShapeDtypeStruct((row_count, width), BF),
            jax.ShapeDtypeStruct((n, row_count, width), BF),
            saved,
            saved,
            saved,
            jax.ShapeDtypeStruct((1, width), F32),
        ),
        in_specs=[HBM] * 4 + [VMEM] * 4,
        out_specs=(VMEM, HBM, HBM, HBM, HBM, VMEM),
        scratch_shapes=scatter_scratch(n, rows, width)
        + gather_scratch(n, rows, width)
        + [
            pltpu.VMEM(wg.shape, BF),
            pltpu.VMEM(wu.shape, BF),
            pltpu.VMEM(wd.shape, BF),
            pltpu.SemaphoreType.DMA((3, most)),
            pltpu.VMEM((2, n * rows, width), BF),
            pltpu.SemaphoreType.DMA((2, n)),
        ]
        + [pltpu.VMEM((2, n * rows, hidden_width), BF)] * 3
        + [pltpu.SemaphoreType.DMA((2, 3, n))],
        compiler_params=pltpu.CompilerParams(
            collective_id=2, has_side_effects=True, vmem_limit_bytes=60 * MIB
        ),
        name="mlp_forward",
        cost_estimate=cost(135),
    )(h_full, wg, wu, wd, middle, out_grad, row_valid, scale)


def mlp_backward_kernel(
    n, rows, dm_full, wg, wu, wd, gate_in, up_in, branch, upstream_in, row_valid, scale,
    middle_grad, da_full, gate_grad, up_grad, gain_out,
    part, send, recv, rs_send_sem, rs_recv_sem, total, own, ag_send_sem, ag_recv_sem, local_sem,
    vg, vu, vd, wsem, dm_buf, gate_buf, up_buf, in_sem, dgate_buf, dup_buf, out_sem,
):
    me = lax.axis_index("mp")
    width, hidden_width = wg.shape

    def in_copies(c, j):
        span = pl.ds(j * rows, rows)
        return [
            pltpu.make_async_copy(
                source.at[j, chunk_span(c, rows)], buf.at[span], in_sem.at[k, j]
            )
            for k, (source, buf) in enumerate(
                ((dm_full, dm_buf), (gate_in, gate_buf), (up_in, up_buf))
            )
        ]

    for j in range(n):
        for copy in in_copies(0, j):
            copy.start()
    down_tiles = WeightTiles(wd, vd, wsem.at[0], 0, TILE)
    gate_tiles = WeightTiles(wg, vg, wsem.at[1], 0, TILE)
    up_tiles = WeightTiles(wu, vu, wsem.at[2], 0, TILE)
    down_tiles.start()
    for tile in range(gate_tiles.count):
        gate_tiles.copy(tile).start()
        up_tiles.copy(tile).start()
    neighbour_barrier(me, n)

    def save_copies(c, j):
        slot = c % 2
        span = pl.ds(j * rows, rows)
        return [
            pltpu.make_async_copy(
                buf.at[slot, span], out.at[j, chunk_span(c, rows)], out_sem.at[slot, k, j]
            )
            for k, (buf, out) in enumerate(((dgate_buf, gate_grad), (dup_buf, up_grad)))
        ]

    def compute(c):
        slot = c % 2
        for j in range(n):
            for copy in in_copies(c, j):
                copy.wait()
        if c >= 2:
            for j in range(n):
                for copy in save_copies(c - 2, j):
                    copy.wait()

        @pl.loop(0, hidden_width // TILE)
        def _(tile):
            if c == 0:
                down_tiles.copy(tile).wait()
            cols = pl.ds(pl.multiple_of(tile * TILE, TILE), TILE)
            hidden_grad = outer_dot(dm_buf[...], vd[cols, :])
            gate = gate_buf[:, cols].astype(F32)
            up = up_buf[:, cols].astype(F32)
            sigmoid = jax.nn.sigmoid(gate)
            dgate_buf[slot, :, cols] = (
                hidden_grad * up * sigmoid * (1.0 + gate * (1.0 - sigmoid))
            ).astype(BF)
            dup_buf[slot, :, cols] = (hidden_grad * gate * sigmoid).astype(BF)

        if c + 1 < CHUNKS:
            for j in range(n):
                for copy in in_copies(c + 1, j):
                    copy.start()
        for j in range(n):
            for copy in save_copies(c, j):
                copy.start()

        @pl.loop(0, width // TILE)
        def _(tile):
            if c == 0:
                gate_tiles.copy(tile).wait()
                up_tiles.copy(tile).wait()
            cols = pl.ds(pl.multiple_of(tile * TILE, TILE), TILE)
            part[c, :, cols] = (
                outer_dot(dgate_buf[slot], vg[cols, :]) + outer_dot(dup_buf[slot], vu[cols, :])
            ).astype(BF)

    scatter = LineScatter(n, me, rows, part, send, recv, rs_send_sem, rs_recv_sem)
    gather = make_gather(n, me, rows, own, da_full, ag_send_sem, ag_recv_sem, local_sem)

    def row_work(c):
        scatter.total(c, total)
        span = chunk_span(c, rows)
        upstream = upstream_in[span].astype(F32) * row_valid[span] + total[...]
        middle_grad[span] = upstream
        value = branch[span]
        grad, gain = norm_back(value, inverse_rms(value), scale[...], upstream)
        own[c] = grad.astype(BF)
        gain_out[...] = gain if c == 0 else gain_out[...] + gain

    run_line(n, CHUNKS, STAGGER, compute, scatter, row_work, gather)
    for c in range(max(CHUNKS - 2, 0), CHUNKS):
        for j in range(n):
            for copy in save_copies(c, j):
                copy.wait()


def mlp_backward(n, dm_full, wg, wu, wd, gate, up, branch, out_grad, row_valid, scale):
    row_count, width = branch.shape
    hidden_width = wg.shape[1]
    rows = row_count // CHUNKS
    saved = jax.ShapeDtypeStruct((n, row_count, hidden_width), BF)
    most = max(width, hidden_width) // TILE
    return pl.pallas_call(
        functools.partial(mlp_backward_kernel, n, rows),
        out_shape=(
            jax.ShapeDtypeStruct((row_count, width), F32),
            jax.ShapeDtypeStruct((n, row_count, width), BF),
            saved,
            saved,
            jax.ShapeDtypeStruct((1, width), F32),
        ),
        in_specs=[HBM] * 6 + [VMEM] * 4,
        out_specs=(VMEM, HBM, HBM, HBM, VMEM),
        scratch_shapes=scatter_scratch(n, rows, width)
        + gather_scratch(n, rows, width)
        + [
            pltpu.VMEM(wg.shape, BF),
            pltpu.VMEM(wu.shape, BF),
            pltpu.VMEM(wd.shape, BF),
            pltpu.SemaphoreType.DMA((3, most)),
            pltpu.VMEM((n * rows, width), BF),
            pltpu.VMEM((n * rows, hidden_width), BF),
            pltpu.VMEM((n * rows, hidden_width), BF),
            pltpu.SemaphoreType.DMA((3, n)),
        ]
        + [pltpu.VMEM((2, n * rows, hidden_width), BF)] * 2
        + [pltpu.SemaphoreType.DMA((2, 2, n))],
        compiler_params=pltpu.CompilerParams(
            collective_id=3, has_side_effects=True, vmem_limit_bytes=60 * MIB
        ),
        name="mlp_backward",
        cost_estimate=cost(137),
    )(dm_full, wg, wu, wd, gate, up, branch, out_grad, row_valid, scale)


def last_grads_kernel(
    n, n_dp, rows, grads, weight, base, inputs, att, da, gains,
    input_grad, qkv_out, out_out, gain_out,
    part, send, recv, rs_send_sem, rs_recv_sem, total, packed,
    x_buf, da_buf, load_sem,
    core_send_qkv, core_send_out, core_recv_qkv, core_recv_out, core_send_sem, core_recv_sem,
    chip_send_qkv, chip_send_out, chip_recv_qkv, chip_recv_out, chip_send_sem, chip_recv_sem,
    gain_recv, gain_send_sem, gain_recv_sem, mp_recv, mp_send_sem, mp_recv_sem, own_qkv, own_out,
):
    me, at = lax.axis_index("mp"), lax.axis_index("dp")
    entered = peer_barrier((("mp", me, n), ("dp", at, n_dp)))
    width = weight.shape[0]
    block_rows = rows * CHUNKS
    local_width = att.shape[1]
    chips = n_dp // 2
    chip, core = at // 2, lax.rem(at, 2)
    part_width = width // n_dp

    def place(k):
        target = lax.rem(chip + 1 + k % chips, chips)
        return 2 * target + (1 - core if k < chips else core)

    def loads(k):
        cols = pl.ds(pl.multiple_of(place(k) * part_width, part_width), part_width)
        return [
            pltpu.make_async_copy(inputs.at[:, cols], x_buf.at[k % 2], load_sem.at[k % 2, 0]),
            pltpu.make_async_copy(da.at[:, cols], da_buf.at[k % 2], load_sem.at[k % 2, 1]),
        ]

    for copy in loads(0):
        copy.start()

    def compute(c):
        for j in range(n):
            packed[j * rows : (j + 1) * rows] = grads[
                j * block_rows + c * rows : j * block_rows + (c + 1) * rows
            ]

        @pl.loop(0, width // TILE)
        def _(tile):
            cols = pl.ds(pl.multiple_of(tile * TILE, TILE), TILE)
            part[c, :, cols] = outer_dot(packed[...], weight[cols, :]).astype(BF)

    scatter = LineScatter(n, me, rows, part, send, recv, rs_send_sem, rs_recv_sem)

    def row_work(c):
        scatter.total(c, total)
        span = chunk_span(c, rows)
        input_grad[span] = base[span] + total[...]

    def core_copies(k):
        other = 2 * chip + 1 - core
        return [
            pltpu.make_async_remote_copy(
                src_ref=src.at[k],
                dst_ref=dst.at[k],
                send_sem=core_send_sem.at[k, which],
                recv_sem=core_recv_sem.at[k, which],
                device_id={"dp": other},
            )
            for which, (src, dst) in enumerate(
                ((core_send_qkv, core_recv_qkv), (core_send_out, core_recv_out))
            )
        ]

    def chip_copies(k):
        other = 2 * lax.rem(chip + 1 + k, chips) + core
        return [
            pltpu.make_async_remote_copy(
                src_ref=src.at[k],
                dst_ref=dst.at[k],
                send_sem=chip_send_sem.at[k, which],
                recv_sem=chip_recv_sem.at[k, which],
                device_id={"dp": other},
            )
            for which, (src, dst) in enumerate(
                ((chip_send_qkv, chip_recv_qkv), (chip_send_out, chip_recv_out))
            )
        ]

    def weight_block(k):
        slot = k % 2
        for copy in loads(k):
            copy.wait()
        if k + 1 < 2 * chips:
            for copy in loads(k + 1):
                copy.start()
        if k >= chips:
            for copy in core_copies(k - chips):
                copy.wait_recv()

        @pl.loop(0, 3)
        def _(tile):
            cols = pl.ds(pl.multiple_of(tile * local_width, local_width), local_width)
            block = inner_dot(x_buf[slot], grads[:, cols])
            if k < chips:
                core_send_qkv[k, :, cols] = block.astype(BF)
            else:
                block = block + core_recv_qkv[k - chips, :, cols].astype(F32)
                if k < 2 * chips - 1:
                    chip_send_qkv[k - chips, :, cols] = block.astype(BF)
                else:
                    own_qkv[:, cols] = block

        block = inner_dot(att[...], da_buf[slot])
        if k < chips:
            core_send_out[k] = block.astype(BF)
            for copy in core_copies(k):
                copy.start()
        else:
            block = block + core_recv_out[k - chips].astype(F32)
            if k < 2 * chips - 1:
                chip_send_out[k - chips] = block.astype(BF)
                for copy in chip_copies(k - chips):
                    copy.start()
            else:
                own_out[...] = block

    gain_copies = exchange(
        "dp", at, n_dp, lambda peer: gains.at[peer], gain_recv, gain_send_sem, gain_recv_sem
    )
    mp_copies = exchange("mp", me, n, lambda peer: gain_out, mp_recv, mp_send_sem, mp_recv_sem)

    compute(0)
    entered()
    scatter.step(0, 0)
    for copy in gain_copies:
        copy.start()
    for c in range(1, CHUNKS):
        compute(c)
        scatter.step(c, 0)
    for k in range(chips):
        weight_block(k)
    line = [(step, c) for step in range(1, n) for c in range(CHUNKS)]
    done = 0
    for k in range(chips, 2 * chips + 1):
        if k < 2 * chips:
            weight_block(k)
        until = len(line) if k == 2 * chips else (k - chips + 1) * CHUNKS // 2
        for step, c in line[done:until]:
            if step < n - 1:
                scatter.step(c, step)
            else:
                row_work(c)
        done = until
        if k == chips:
            gain_out[...] = gains[at]
            for shift, copy in enumerate(gain_copies, 1):
                copy.wait_recv()
                gain_out[...] += gain_recv[shift - 1]
            for copy in mp_copies:
                copy.start()
    for k in range(chips - 1):
        for copy in chip_copies(k):
            copy.wait_recv()
    qkv_out[...] = own_qkv[...]
    out_out[...] = own_out[...]
    for k in range(chips - 1):
        qkv_out[...] += chip_recv_qkv[k].astype(F32)
        out_out[...] += chip_recv_out[k].astype(F32)
    for copy in mp_copies:
        copy.wait_recv()
        copy.wait_send()
    lanes = lax.broadcasted_iota(jnp.int32, gain_out.shape, 1)
    shared = gain_out[...]
    for shift in range(1, n):
        shared = shared + mp_recv[shift - 1]
    gain_out[...] = jnp.where(lanes < 2 * part_width, shared, gain_out[...])
    for copy in gain_copies:
        copy.wait_send()
    for c in range(CHUNKS):
        scatter.drain(c)
    for k in range(chips):
        for copy in core_copies(k):
            copy.wait_send()
    for k in range(chips - 1):
        for copy in chip_copies(k):
            copy.wait_send()


def last_grads(n, n_dp, grads, weight, base, inputs, attended, da_full, gains):
    row_count, width = base.shape
    rows = row_count // CHUNKS
    size, local_width = attended.shape
    part_width = width // n_dp
    chips = n_dp // 2
    qkv_block = (part_width, 3 * local_width)
    out_block = (local_width, part_width)
    gain_block = gains.shape[1:]
    return pl.pallas_call(
        functools.partial(last_grads_kernel, n, n_dp, rows),
        out_shape=(
            jax.ShapeDtypeStruct((row_count, width), F32),
            jax.ShapeDtypeStruct(qkv_block, F32),
            jax.ShapeDtypeStruct(out_block, F32),
            jax.ShapeDtypeStruct(gain_block, F32),
        ),
        in_specs=[VMEM, VMEM, VMEM, HBM, VMEM, HBM, VMEM],
        out_specs=(VMEM,) * 4,
        scratch_shapes=scatter_scratch(n, rows, width)
        + [
            pltpu.VMEM((n * rows, 3 * local_width), BF),
            pltpu.VMEM((2, size, part_width), BF),
            pltpu.VMEM((2, size, part_width), BF),
            pltpu.SemaphoreType.DMA((2, 2)),
        ]
        + [pltpu.VMEM((chips,) + block, BF) for block in (qkv_block, out_block) * 2]
        + [pltpu.SemaphoreType.DMA((chips, 2))] * 2
        + [pltpu.VMEM((chips - 1,) + block, BF) for block in (qkv_block, out_block) * 2]
        + [pltpu.SemaphoreType.DMA((chips - 1, 2))] * 2
        + [pltpu.VMEM((n_dp - 1,) + gain_block, F32)]
        + [pltpu.SemaphoreType.DMA((n_dp - 1,))] * 2
        + [pltpu.VMEM((n - 1,) + gain_block, F32)]
        + [pltpu.SemaphoreType.DMA((n - 1,))] * 2
        + [pltpu.VMEM(qkv_block, F32), pltpu.VMEM(out_block, F32)],
        compiler_params=pltpu.CompilerParams(
            collective_id=4, has_side_effects=True, vmem_limit_bytes=60 * MIB
        ),
        name="last_grads",
        cost_estimate=cost(90),
    )(grads, weight, base, inputs, attended, da_full, gains)


def turn(values, cos, sin):
    return values * cos + pltpu.roll(values, values.shape[1] // 2, 1) * sin


def turn_back(values, cos, sin):
    return values * cos + pltpu.roll(values * sin, values.shape[1] // 2, 1)


def allowed_keys(starts, first_row, rows, key_end):
    places = first_row + lax.broadcasted_iota(jnp.int32, (rows, key_end), 0)
    keys = lax.broadcasted_iota(jnp.int32, (rows, key_end), 1)
    return (keys <= places) & (keys >= starts)


def columns_to_rows(first, second):
    lanes = lax.broadcasted_iota(jnp.int32, (first.shape[0], 128), 1)
    return jnp.transpose(jnp.where(lanes == 0, first, second))[:8]


def sum_columns(n, me, first, second, entered, held, recv, turned, send_sem, recv_sem):
    held[...] = columns_to_rows(first, second)
    copies = exchange("mp", me, n, lambda peer: held, recv, send_sem, recv_sem)
    entered()
    for copy in copies:
        copy.start()
    total = held[...]
    for shift, copy in enumerate(copies, 1):
        copy.wait_recv()
        total = total + recv[shift - 1]
    for copy in copies:
        copy.wait_send()
    turned[...] = jnp.zeros_like(turned)
    turned[:8] = total
    back = jnp.transpose(turned[...])
    return back[:, 0:1], back[:, 1:2]


def sum_scratch(n, size):
    return [
        pltpu.VMEM((8, size), F32),
        pltpu.VMEM((n - 1, 8, size), F32),
        pltpu.VMEM((128, size), F32),
        pltpu.SemaphoreType.DMA((n - 1,)),
        pltpu.SemaphoreType.DMA((n - 1,)),
    ]


def attention_kernel(
    n, heads, model_width, qkv, q_gain, k_gain, cos, sin, starts,
    out, q_low, k_low, v_low, log_total, q_inv, k_inv, *sums,
):
    me = lax.axis_index("mp")
    entered = peer_barrier((("mp", me, n),))
    size = qkv.shape[0]
    width = qkv.shape[1] // 3
    head = width // heads
    score_scale = 1.0 / math.sqrt(head)

    def squares(first):
        return jnp.sum(jnp.square(qkv[:, first : first + width]), axis=1, keepdims=True)

    q_sum, k_sum = sum_columns(n, me, squares(0), squares(width), entered, *sums)
    q_inv[...] = lax.rsqrt(q_sum / model_width + EPS)
    k_inv[...] = lax.rsqrt(k_sum / model_width + EPS)
    rows = min(QUERY_ROWS, size)

    @pl.loop(0, heads)
    def _(h):
        def cols(first):
            return pl.ds(pl.multiple_of(first + h * head, head), head)

        here = cols(0)
        q_low[:, here] = turn(
            qkv[:, here] * q_inv[...] * q_gain[:, here], cos[...], sin[...]
        ).astype(BF)
        k_low[:, here] = turn(
            qkv[:, cols(width)] * k_inv[...] * k_gain[:, here], cos[...], sin[...]
        ).astype(BF)
        v_low[:, here] = qkv[:, cols(2 * width)].astype(BF)
        for first in range(0, size, rows):
            end = first + rows
            span = slice(first, end)
            scores = outer_dot(q_low[span, here], k_low[:end, here]) * score_scale
            scores = jnp.where(allowed_keys(starts[span], first, rows, end), scores, MASKED)
            row_max = jnp.max(scores, axis=1, keepdims=True)
            exponents = jnp.exp(scores - row_max)
            row_total = jnp.sum(exponents, axis=1, keepdims=True)
            probs = (exponents * (1.0 / row_total)).astype(BF)
            out[span, here] = plain_dot(probs, v_low[:end, here]).astype(BF)
            log_total[h, span] = row_max + jnp.log(row_total)


def attention(n, heads, model_width, qkv_raw, q_gain, k_gain, cos, sin, starts):
    size = qkv_raw.shape[0]
    low = jax.ShapeDtypeStruct((size, qkv_raw.shape[1] // 3), BF)
    column = jax.ShapeDtypeStruct((size, 1), F32)
    return pl.pallas_call(
        functools.partial(attention_kernel, n, heads, model_width),
        out_shape=(low,) * 4 + (jax.ShapeDtypeStruct((heads, size, 1), F32), column, column),
        in_specs=[VMEM] * 6,
        out_specs=(VMEM,) * 7,
        scratch_shapes=sum_scratch(n, size),
        compiler_params=pltpu.CompilerParams(
            collective_id=5, has_side_effects=True, vmem_limit_bytes=56 * MIB
        ),
        name="attention",
        cost_estimate=cost(25),
    )(qkv_raw, q_gain, k_gain, cos, sin, starts)


def attention_back_kernel(
    n, heads, model_width, qkv, q_low, k_low, v_low, out_grad, log_total,
    q_inv, k_inv, q_gain, k_gain, cos, sin, starts,
    grads, q_gain_grad, k_gain_grad,
    q_weighted, k_weighted, q_grad, k_sum, v_sum, q_dots, k_dots, *sums,
):
    me = lax.axis_index("mp")
    entered = peer_barrier((("mp", me, n),))
    size = qkv.shape[0]
    width = qkv.shape[1] // 3
    head = width // heads
    score_scale = 1.0 / math.sqrt(head)
    rows = min(QUERY_ROWS, size)
    q_dots[...] = jnp.zeros_like(q_dots)
    k_dots[...] = jnp.zeros_like(k_dots)

    @pl.loop(0, heads)
    def _(h):
        def cols(first):
            return pl.ds(pl.multiple_of(first + h * head, head), head)

        here = cols(0)
        for first in reversed(range(0, size, rows)):
            end = first + rows
            span = slice(first, end)
            scores = outer_dot(q_low[span, here], k_low[:end, here]) * score_scale
            scores = jnp.where(allowed_keys(starts[span], first, rows, end), scores, MASKED)
            probs = jnp.exp(scores - log_total[h, span])
            prob_grad = outer_dot(out_grad[span, here], v_low[:end, here])
            probs_low = probs.astype(BF)
            weighted = probs * prob_grad
            score_grad = (
                weighted - probs * jnp.sum(weighted, axis=1, keepdims=True)
            ).astype(BF)
            q_grad[span] = plain_dot(score_grad, k_low[:end, here]) * score_scale
            k_extra = inner_dot(score_grad, q_low[span, here])
            v_extra = inner_dot(probs_low, out_grad[span, here])
            if end == size:
                k_sum[...] = k_extra
                v_sum[...] = v_extra
            else:
                k_sum[:end] += k_extra
                v_sum[:end] += v_extra
        for first, inv, gain, grad, factor, weighted_out, dots, gain_grad in (
            (0, q_inv, q_gain, q_grad, None, q_weighted, q_dots, q_gain_grad),
            (width, k_inv, k_gain, k_sum, score_scale, k_weighted, k_dots, k_gain_grad),
        ):
            raw = qkv[:, cols(first)]
            value = grad[...] if factor is None else grad[...] * factor
            normed = turn_back(value, cos[...], sin[...])
            weighted = normed * gain[:, here]
            weighted_out[:, here] = weighted
            gain_grad[:, here] = jnp.sum(normed * raw * inv[...], axis=0, keepdims=True)
            dots[...] += jnp.sum(weighted * raw, axis=1, keepdims=True)
        grads[:, cols(2 * width)] = v_sum[...].astype(BF)

    q_total, k_total = sum_columns(n, me, q_dots[...], k_dots[...], entered, *sums)
    for first, inv, weighted, dots in (
        (0, q_inv, q_weighted, q_total),
        (width, k_inv, k_weighted, k_total),
    ):
        scale = inv[...]
        factor = scale * scale * scale * (dots / model_width)
        grads[:, first : first + width] = (
            scale * weighted[...] - qkv[:, first : first + width] * factor
        ).astype(BF)


def attention_back(
    n, heads, model_width, qkv_raw, q_low, k_low, v_low, out_grad, log_total, q_inv, k_inv,
    q_gain, k_gain, cos, sin, starts,
):
    size, width = q_low.shape
    head = width // heads
    gains = jax.ShapeDtypeStruct((1, width), F32)
    return pl.pallas_call(
        functools.partial(attention_back_kernel, n, heads, model_width),
        out_shape=(jax.ShapeDtypeStruct((size, 3 * width), BF), gains, gains),
        in_specs=[VMEM] * 13,
        out_specs=(VMEM,) * 3,
        scratch_shapes=[pltpu.VMEM((size, width), F32)] * 2
        + [pltpu.VMEM((size, head), F32)] * 3
        + [pltpu.VMEM((size, 1), F32)] * 2
        + sum_scratch(n, size),
        compiler_params=pltpu.CompilerParams(
            collective_id=6, has_side_effects=True, vmem_limit_bytes=56 * MIB
        ),
        name="attention_back",
        cost_estimate=cost(30),
    )(
        qkv_raw, q_low, k_low, v_low, out_grad, log_total, q_inv, k_inv, q_gain, k_gain,
        cos, sin, starts,
    )


def local(
    layer_input,
    query_weight,
    key_weight,
    value_weight,
    out_weight,
    gate_weight,
    up_weight,
    down_weight,
    query_gain,
    key_gain,
    attn_gain,
    mlp_gain,
    seq_lens,
    out_grad,
):
    n = lax.axis_size("mp")
    n_dp = lax.axis_size("dp")
    me = lax.axis_index("mp")
    row_count, model_width = layer_input.shape
    group_size = row_count * n
    local_heads, gain_part = query_gain.shape
    head_size = gain_part * n_dp
    local_width = local_heads * head_size

    full_qkv = lax.all_gather(
        jnp.concatenate([query_weight, key_weight, value_weight], axis=1), "dp", axis=0, tiled=True
    )
    full_out = lax.all_gather(out_weight, "dp", axis=1, tiled=True)
    full_gate = lax.all_gather(gate_weight, "dp", axis=0, tiled=True)
    full_up = lax.all_gather(up_weight, "dp", axis=0, tiled=True)
    full_down = lax.all_gather(down_weight, "dp", axis=1, tiled=True)
    head_part = local_heads * gain_part
    width_part = attn_gain.shape[0]
    own_gains = jnp.concatenate(
        [attn_gain, mlp_gain, query_gain.reshape(head_part), key_gain.reshape(head_part)]
    ).astype(F32)[None]
    inputs_full, gain_parts = gather_rows(n, n_dp, layer_input, own_gains)
    inputs_full = inputs_full.reshape(group_size, model_width)
    gain_parts = gain_parts[:, 0]

    def head_gain(first):
        piece = gain_parts[:, first : first + head_part].reshape(n_dp, local_heads, gain_part)
        return piece.transpose(1, 0, 2).reshape(1, local_width)

    query_scale = head_gain(2 * width_part)
    key_scale = head_gain(2 * width_part + head_part)
    attn_scale = gain_parts[:, :width_part].reshape(1, model_width)
    mlp_scale = gain_parts[:, width_part : 2 * width_part].reshape(1, model_width)

    starts, positions, valid = layout(seq_lens[0], group_size)
    starts = starts[:, None]
    cos_table, sin_table = rotary_tables(positions, head_size)
    row_valid = lax.dynamic_slice_in_dim(valid, me * row_count, row_count, 0).astype(F32)[:, None]

    qkv_raw = plain_dot(inputs_full, full_qkv)
    attended, query_low, key_low, value_low, log_total, query_inv, key_inv = attention(
        n, local_heads, model_width, qkv_raw, query_scale, key_scale, cos_table, sin_table, starts
    )
    branch, middle, middle_full = attn_out(n, attended, full_out, layer_input, attn_scale)
    layer_output, mlp_grad_full, gate, up, hidden, mlp_gain_part = mlp_forward(
        n, middle_full, full_gate, full_up, full_down, middle, out_grad, row_valid, mlp_scale
    )

    def flat(rows):
        return rows.reshape(group_size, rows.shape[-1])

    def dp_scatter(part, dimension):
        return lax.psum_scatter(part, "dp", scatter_dimension=dimension, tiled=True)

    down_part = inner_dot(flat(hidden), flat(mlp_grad_full)).astype(BF)
    mlp_grad_full, down_part = lax.optimization_barrier((mlp_grad_full, down_part))
    grad_down = dp_scatter(down_part, 1)
    middle_grad, branch_full, gate_grad, up_grad, attn_gain_part = mlp_backward(
        n, mlp_grad_full, full_gate, full_up, full_down, gate, up, branch, out_grad, row_valid,
        attn_scale,
    )
    branch_full = flat(branch_full)
    gate_part = inner_dot(flat(middle_full), flat(gate_grad)).astype(BF)
    branch_full, gate_part, grad_down = lax.optimization_barrier(
        (branch_full, gate_part, grad_down)
    )
    grad_gate = dp_scatter(gate_part, 0)

    mixed_grad = outer_dot(branch_full, full_out).astype(BF)
    qkv_grad, query_gain_part, key_gain_part = attention_back(
        n, local_heads, model_width, qkv_raw, query_low, key_low, value_low, mixed_grad, log_total,
        query_inv, key_inv, query_scale, key_scale, cos_table, sin_table, starts,
    )
    up_part = inner_dot(flat(middle_full), flat(up_grad)).astype(BF)
    qkv_grad, up_part, grad_gate = lax.optimization_barrier((qkv_grad, up_part, grad_gate))
    grad_up = dp_scatter(up_part, 0)

    def by_part(row):
        return row.reshape(n_dp, -1)

    def by_head_part(row):
        pieces = row.reshape(local_heads, n_dp, gain_part).transpose(1, 0, 2)
        return pieces.reshape(n_dp, head_part)

    gain_grads = jnp.concatenate(
        [
            by_part(attn_gain_part),
            by_part(mlp_gain_part),
            by_head_part(query_gain_part),
            by_head_part(key_gain_part),
        ],
        axis=1,
    )[:, None]
    input_grad, grad_qkv, grad_out, gain_sums = last_grads(
        n, n_dp, qkv_grad, full_qkv, middle_grad, inputs_full, attended, branch_full, gain_grads
    )
    gain_sums = gain_sums[0]
    heads_at = 2 * width_part
    return (
        layer_output,
        input_grad,
        grad_qkv[:, :local_width],
        grad_qkv[:, local_width : 2 * local_width],
        grad_qkv[:, 2 * local_width :],
        grad_out,
        grad_gate.astype(F32),
        grad_up.astype(F32),
        grad_down.astype(F32),
        gain_sums[heads_at : heads_at + head_part].reshape(local_heads, gain_part),
        gain_sums[heads_at + head_part :].reshape(local_heads, gain_part),
        gain_sums[:width_part],
        gain_sums[width_part:heads_at],
    )


def solution(mesh):
    return jax.shard_map(
        local,
        mesh=mesh,
        in_specs=(
            P(("dp", "mp"), None),
            P("dp", "mp"),
            P("dp", "mp"),
            P("dp", "mp"),
            P("mp", "dp"),
            P("dp", "mp"),
            P("dp", "mp"),
            P("mp", "dp"),
            P("mp", "dp"),
            P("mp", "dp"),
            P("dp"),
            P("dp"),
            P("dp", None),
            P(("dp", "mp"), None),
        ),
        out_specs=(
            P(("dp", "mp"), None),
            P(("dp", "mp"), None),
            P("dp", "mp"),
            P("dp", "mp"),
            P("dp", "mp"),
            P("mp", "dp"),
            P("dp", "mp"),
            P("dp", "mp"),
            P("mp", "dp"),
            P("mp", "dp"),
            P("mp", "dp"),
            P("dp"),
            P("dp"),
        ),
        check_vma=False,
    )
```

```python
import functools
import math

import jax
import jax.numpy as jnp
from jax import lax
from jax.experimental import pallas as pl
from jax.experimental.pallas import tpu as pltpu
from jax.sharding import PartitionSpec as P

EPS = 1e-06
THETA = 500000.0
MASKED = -1000000000.0
CHUNKS = 4
STAGGER = 2
EDGES = False
FILL = 2
TILE = 512
QUERY_ROWS = 256
BF = jnp.bfloat16
F32 = jnp.float32
MIB = 1 << 20
HBM = pl.BlockSpec(memory_space=pl.ANY)
VMEM = pl.BlockSpec(memory_space=pltpu.VMEM)


def cost(micros):
    return pl.CostEstimate(
        flops=micros * 1_000_000_000, bytes_accessed=micros * 3_000_000, transcendentals=0
    )


def plain_dot(former, latter):
    return jnp.dot(former, latter, preferred_element_type=F32)


def inner_dot(former, latter):
    return lax.dot_general(
        former, latter, (((0,), (0,)), ((), ())), preferred_element_type=F32
    )


def outer_dot(former, latter):
    return lax.dot_general(
        former, latter, (((1,), (1,)), ((), ())), preferred_element_type=F32
    )


def layout(lengths, group_size):
    slot_count = lengths.shape[0]
    seq_ends = jnp.cumsum(lengths, dtype=jnp.int32)
    starts = seq_ends - lengths
    places = jnp.arange(group_size, dtype=jnp.int32)
    slot_ids = jnp.arange(slot_count, dtype=jnp.int32)
    segment = jnp.sum(
        (places[:, None] >= seq_ends[None, :]).astype(jnp.int32), axis=1, dtype=jnp.int32
    )
    chosen = (segment[:, None] == slot_ids[None, :]).astype(jnp.int32)
    padded = (segment == slot_count).astype(jnp.int32)
    begins = (
        jnp.sum(chosen * starts[None, :], axis=1, dtype=jnp.int32)
        + padded * seq_ends[slot_count - 1]
    )
    return (begins, places - begins, places < seq_ends[slot_count - 1])


def rotary_tables(positions, head_size):
    half_dim = head_size // 2
    frequency = jnp.exp(jnp.arange(half_dim, dtype=F32) * (-2.0 * math.log(THETA) / head_size))
    angles = positions.astype(F32)[:, None] * frequency[None, :]
    cos_half, sin_half = jnp.cos(angles), jnp.sin(angles)
    return (
        jnp.concatenate([cos_half, cos_half], axis=1),
        jnp.concatenate([-sin_half, sin_half], axis=1),
    )


def neighbour_barrier(me, n):
    barrier = pltpu.get_barrier_semaphore()

    @pl.when(me > 0)
    def _():
        pl.semaphore_signal(barrier, inc=1, device_id={"mp": me - 1})

    @pl.when(me < n - 1)
    def _():
        pl.semaphore_signal(barrier, inc=1, device_id={"mp": me + 1})

    pl.semaphore_wait(barrier, jnp.minimum(me, 1) + jnp.minimum(n - 1 - me, 1))


class LineGather:
    def __init__(self, n, me, own, full, send_sem, recv_sem, local_sem):
        self.n, self.me, self.own, self.full = n, me, own, full
        self.send_sem, self.recv_sem, self.local_sem = send_sem, recv_sem, local_sem

    def local_copy(self, c):
        return pltpu.make_async_copy(self.own(c), self.full(self.me, c), self.local_sem.at[c])

    def copy(self, c, step, way, block, src):
        return pltpu.make_async_remote_copy(
            src_ref=src,
            dst_ref=self.full(block, c),
            send_sem=self.send_sem.at[c, step - 1, way],
            recv_sem=self.recv_sem.at[c, step - 1, way],
            device_id={"mp": self.me + (1 if way == 0 else -1)},
        )

    def sides(self):
        return ((0, self.me), (1, self.n - 1 - self.me))

    def block_at(self, way, step):
        return self.me - step if way == 0 else self.me + step

    def step(self, c, step):
        n = self.n
        if step == 1:
            self.local_copy(c).start()
        for way, place in self.sides():
            if step > 1:

                @pl.when(place >= step - 1)
                def _(way=way):
                    block = self.block_at(way, step - 1)
                    self.copy(c, step - 1, way, block, self.own(c)).wait_recv()

            @pl.when((place >= step - 1) & (place < n - 1))
            def _(way=way):
                block = self.block_at(way, step - 1)
                src = self.own(c) if step == 1 else self.full(block, c)
                self.copy(c, step, way, block, src).start()

    def last(self, c):
        n = self.n
        for way, place in self.sides():

            @pl.when(place == n - 1)
            def _(way=way):
                block = self.block_at(way, n - 1)
                self.copy(c, n - 1, way, block, self.own(c)).wait_recv()

    def drain(self, c):
        self.local_copy(c).wait()
        for step in range(1, self.n):
            for way, place in self.sides():

                @pl.when((place >= step - 1) & (place < self.n - 1))
                def _(way=way):
                    self.copy(c, step, way, self.me, self.own(c)).wait_send()


class LineScatter:
    def __init__(self, n, me, rows, part, recv, send_sem, recv_sem):
        self.n, self.me, self.rows = n, me, rows
        self.part, self.recv = part, recv
        self.send_sem, self.recv_sem = send_sem, recv_sem

    def piece(self, c, owner):
        first = pl.multiple_of(owner * self.rows, self.rows)
        return self.part.at[c, pl.ds(first, self.rows)]

    def copy(self, c, step, way, src):
        return pltpu.make_async_remote_copy(
            src_ref=src,
            dst_ref=self.recv.at[c, step, way],
            send_sem=self.send_sem.at[c, step, way],
            recv_sem=self.recv_sem.at[c, step, way],
            device_id={"mp": self.me + (1 if way == 0 else -1)},
        )

    def sides(self):
        return ((0, self.me), (1, self.n - 1 - self.me))

    def owner(self, way, step):
        return self.n - 1 - step + self.me if way == 0 else step - (self.n - 1 - self.me)

    def edge(self, c, step):
        for way, place in self.sides():

            @pl.when(place == 0)
            def _(way=way):
                self.copy(c, step, way, self.piece(c, self.owner(way, step))).start()

    def step(self, c, step):
        for way, place in self.sides():

            @pl.when((place > 0) & (place <= min(step, self.n - 2)))
            def _(way=way):
                piece = self.piece(c, self.owner(way, step))
                self.copy(c, step - 1, way, piece).wait_recv()
                piece[...] = (
                    piece[...].astype(F32) + self.recv[c, step - 1, way].astype(F32)
                ).astype(BF)
                self.copy(c, step, way, piece).start()

    def total(self, c, out):
        n = self.n
        out[...] = self.piece(c, self.me)[...].astype(F32)
        for way, place in self.sides():

            @pl.when(place > 0)
            def _(way=way):
                self.copy(c, n - 2, way, self.recv.at[c, n - 2, way]).wait_recv()
                out[...] += self.recv[c, n - 2, way].astype(F32)

    def drain(self, c):
        n = self.n
        for step in range(n - 1):
            for way, place in self.sides():

                @pl.when(place <= min(step, n - 2))
                def _(way=way):
                    self.copy(c, step, way, self.recv.at[c, step, way]).wait_send()


def run_line(n, chunks, stagger, compute, scatter, row_work, gather, filler=None):
    last_step = 2 * n - 2 if gather is not None else n - 1
    events = sorted(
        (step + stagger * c - (0.5 if step == 0 else 0), c, step)
        for c in range(chunks)
        for step in range(last_step + 1)
    )
    computed = 0
    for _, c, step in events:
        if step == 0:
            compute(c)
            for ahead in range(n - 1 if EDGES else 1):
                scatter.edge(c, ahead)
            computed += 1
        elif step < n - 1:
            if not EDGES:
                scatter.edge(c, step)
            scatter.step(c, step)
        elif step == n - 1:
            row_work(c)
            if gather is not None:
                gather.step(c, 1)
        elif step < 2 * n - 2:
            gather.step(c, step - n + 2)
        else:
            gather.last(c)
        if filler is not None and computed == chunks:
            filler()
    for c in range(chunks):
        scatter.drain(c)
        if gather is not None:
            gather.drain(c)


def flipped(chip, bit):
    return chip + bit - 2 * bit * lax.rem(chip // bit, 2)


def bits_of(number):
    return [1 << k for k in range(number.bit_length()) if number >> k & 1]


def relative_chip(chip, relative):
    for bit in bits_of(relative):
        chip = flipped(chip, bit)
    return chip


def relative_order(chips):
    return sorted(range(chips), key=lambda r: (-len(bits_of(r)), r))


class PlaneReduce:
    def __init__(self, at, chips, rows, views, sems, out):
        self.chip, self.core = at // 2, lax.rem(at, 2)
        self.chips, self.rows, self.out = chips, rows, out
        self.core_send, self.core_recv, self.held, self.message = views
        self.core_send_sem, self.core_recv_sem, self.send_sem, self.recv_sem = sems

    def first_bit(self, relative, half):
        bits = bits_of(relative)
        return bits[0] if half == 0 else bits[-1]

    def before(self, relative, half):
        return [
            r for r in range(1, self.chips) if r - self.first_bit(r, half) == relative
        ]

    def owner(self, relative, same_core):
        return 2 * relative_chip(self.chip, relative) + (
            self.core if same_core else 1 - self.core
        )

    def half_rows(self, half):
        return pl.ds(half * (self.rows // 2), self.rows // 2)

    def core_copy(self, relative):
        return pltpu.make_async_remote_copy(
            src_ref=self.core_send(relative),
            dst_ref=self.core_recv(relative),
            send_sem=self.core_send_sem.at[relative],
            recv_sem=self.core_recv_sem.at[relative],
            device_id={"dp": 2 * self.chip + 1 - self.core},
        )

    def message_copy(self, relative, half):
        span = self.half_rows(half)
        target = flipped(self.chip, self.first_bit(relative, half))
        return pltpu.make_async_remote_copy(
            src_ref=self.held(relative).at[span],
            dst_ref=self.message(relative).at[span],
            send_sem=self.send_sem.at[relative, half],
            recv_sem=self.recv_sem.at[relative, half],
            device_id={"dp": 2 * target + self.core},
        )

    def push(self, relative, half):
        span = self.half_rows(half)
        for r in self.before(relative, half):
            self.message_copy(r, half).wait_recv()
            held = self.held(relative)
            held[span] = (
                held[span].astype(F32) + self.message(r)[span].astype(F32)
            ).astype(BF)
        self.message_copy(relative, half).start()

    def finish(self):
        for half in range(2):
            span = self.half_rows(half)
            for r in self.before(0, half):
                self.message_copy(r, half).wait_recv()
                self.out[span] += self.message(r)[span].astype(F32)

    def drain_core(self, relative):
        self.core_copy(relative).wait_send()

    def drain(self):
        for r in range(1, self.chips):
            for half in range(2):
                self.message_copy(r, half).wait_send()


def plane_sems(chips):
    return [pltpu.SemaphoreType.DMA((chips,))] * 2 + [pltpu.SemaphoreType.DMA((chips, 2))] * 2


def stage_barrier(me, n, at, chips):
    barrier = pltpu.get_barrier_semaphore()

    @pl.when(me > 0)
    def _():
        pl.semaphore_signal(barrier, inc=1, device_id={"mp": me - 1})

    @pl.when(me < n - 1)
    def _():
        pl.semaphore_signal(barrier, inc=1, device_id={"mp": me + 1})

    count = signal_partners(barrier, at, chips)
    pl.semaphore_wait(barrier, count + jnp.minimum(me, 1) + jnp.minimum(n - 1 - me, 1))


def signal_partners(sem, at, chips):
    chip, core = at // 2, lax.rem(at, 2)
    pl.semaphore_signal(sem, inc=1, device_id={"dp": 2 * chip + 1 - core})
    bits = [1 << k for k in range(chips.bit_length() - 1)]
    for bit in bits:
        pl.semaphore_signal(sem, inc=1, device_id={"dp": 2 * flipped(chip, bit) + core})
    return 1 + len(bits)


def inverse_rms(rows):
    return lax.rsqrt(jnp.mean(rows * rows, axis=1, keepdims=True) + EPS)


def norm_back(values, inverse, gain_row, upstream):
    weighted = upstream * gain_row
    mean_term = jnp.mean(weighted * values, axis=1, keepdims=True)
    grad_values = inverse * weighted - values * (inverse * inverse * inverse) * mean_term
    return (grad_values, jnp.sum(upstream * values * inverse, axis=0, keepdims=True))


def scatter_scratch(n, rows, width):
    return [
        pltpu.VMEM((CHUNKS, n * rows, width), BF),
        pltpu.VMEM((CHUNKS, n - 1, 2, rows, width), BF),
        pltpu.SemaphoreType.DMA((CHUNKS, n - 1, 2)),
        pltpu.SemaphoreType.DMA((CHUNKS, n - 1, 2)),
        pltpu.VMEM((rows, width), F32),
    ]


def gather_scratch(n, rows, width):
    return [
        pltpu.VMEM((CHUNKS, rows, width), BF),
        pltpu.SemaphoreType.DMA((CHUNKS, n - 1, 2)),
        pltpu.SemaphoreType.DMA((CHUNKS, n - 1, 2)),
        pltpu.SemaphoreType.DMA((CHUNKS,)),
    ]


def chunk_span(c, rows):
    return pl.ds(c * rows, rows)


def make_gather(n, me, rows, own, full, send_sem, recv_sem, local_sem):
    return LineGather(
        n,
        me,
        lambda c: own.at[c],
        lambda block, c: full.at[block, chunk_span(c, rows)],
        send_sem,
        recv_sem,
        local_sem,
    )


def peer_barrier(axes):
    barrier = pltpu.get_barrier_semaphore()
    count = 0
    for name, index, size in axes:
        for shift in range(1, size):
            pl.semaphore_signal(barrier, inc=1, device_id={name: lax.rem(index + shift, size)})
            count += 1
    return lambda: pl.semaphore_wait(barrier, count)


def exchange(name, index, size, src, recv, send_sem, recv_sem):
    def copy(shift):
        peer = lax.rem(index + shift, size)
        return pltpu.make_async_remote_copy(
            src_ref=src(peer),
            dst_ref=recv.at[shift - 1],
            send_sem=send_sem.at[shift - 1],
            recv_sem=recv_sem.at[shift - 1],
            device_id={name: peer},
        )

    return [copy(shift) for shift in range(1, size)]


def gather_rows_kernel(
    n, n_dp, rows, block, gains, full, gain_parts,
    send_sem, recv_sem, local_sem, gain_recv, gain_send_sem, gain_recv_sem,
):
    me, at = lax.axis_index("mp"), lax.axis_index("dp")
    peer_barrier((("mp", me, n), ("dp", at, n_dp)))()
    gather = LineGather(
        n,
        me,
        lambda c: block.at[chunk_span(c, rows)],
        lambda index, c: full.at[index, chunk_span(c, rows)],
        send_sem,
        recv_sem,
        local_sem,
    )
    for c in range(CHUNKS):
        gather.step(c, 1)
    copies = exchange(
        "dp", at, n_dp, lambda peer: gains, gain_recv, gain_send_sem, gain_recv_sem
    )
    for copy in copies:
        copy.start()
    for step in range(2, n):
        for c in range(CHUNKS):
            gather.step(c, step)
    gain_parts[at] = gains[...]
    for shift, copy in enumerate(copies, 1):
        copy.wait_recv()
        gain_parts[lax.rem(at + n_dp - shift, n_dp)] = gain_recv[shift - 1]
    for c in range(CHUNKS):
        gather.last(c)
    for c in range(CHUNKS):
        gather.drain(c)
    for copy in copies:
        copy.wait_send()


def gather_rows(n, n_dp, block, gains):
    rows = block.shape[0] // CHUNKS
    sems = gather_scratch(n, rows, block.shape[1])[1:]
    return pl.pallas_call(
        functools.partial(gather_rows_kernel, n, n_dp, rows),
        out_shape=(
            jax.ShapeDtypeStruct((n,) + block.shape, block.dtype),
            jax.ShapeDtypeStruct((n_dp,) + gains.shape, F32),
        ),
        in_specs=[HBM, VMEM],
        out_specs=(HBM, VMEM),
        scratch_shapes=sems
        + [
            pltpu.VMEM((n_dp - 1,) + gains.shape, F32),
            pltpu.SemaphoreType.DMA((n_dp - 1,)),
            pltpu.SemaphoreType.DMA((n_dp - 1,)),
        ],
        compiler_params=pltpu.CompilerParams(collective_id=0, has_side_effects=True),
        name="gather_rows",
        cost_estimate=cost(75),
    )(block, gains)


def attn_out_kernel(
    n, rows, att, wo, x, scale, branch, middle, full,
    part, recv, rs_send_sem, rs_recv_sem, total, own, ag_send_sem, ag_recv_sem, local_sem,
    packed,
):
    me = lax.axis_index("mp")
    neighbour_barrier(me, n)
    width = wo.shape[1]
    block_rows = rows * CHUNKS

    def compute(c):
        for j in range(n):
            packed[j * rows : (j + 1) * rows] = att[
                j * block_rows + c * rows : j * block_rows + (c + 1) * rows
            ]

        @pl.loop(0, width // TILE)
        def _(tile):
            cols = pl.ds(pl.multiple_of(tile * TILE, TILE), TILE)
            part[c, :, cols] = plain_dot(packed[...], wo[:, cols]).astype(BF)

    scatter = LineScatter(n, me, rows, part, recv, rs_send_sem, rs_recv_sem)
    gather = make_gather(n, me, rows, own, full, ag_send_sem, ag_recv_sem, local_sem)

    def row_work(c):
        scatter.total(c, total)
        span = chunk_span(c, rows)
        value = total[...]
        branch[span] = value
        new = x[span].astype(F32) + value * inverse_rms(value) * scale[...]
        middle[span] = new
        own[c] = new.astype(BF)

    run_line(n, CHUNKS, STAGGER, compute, scatter, row_work, gather)


def attn_out(n, attended, full_out, layer_input, scale):
    row_count, width = layer_input.shape
    rows = row_count // CHUNKS
    return pl.pallas_call(
        functools.partial(attn_out_kernel, n, rows),
        out_shape=(
            jax.ShapeDtypeStruct((row_count, width), F32),
            jax.ShapeDtypeStruct((row_count, width), F32),
            jax.ShapeDtypeStruct((n, row_count, width), BF),
        ),
        in_specs=[VMEM] * 4,
        out_specs=(VMEM, VMEM, HBM),
        scratch_shapes=scatter_scratch(n, rows, width)
        + gather_scratch(n, rows, width)
        + [pltpu.VMEM((n * rows, attended.shape[1]), BF)],
        compiler_params=pltpu.CompilerParams(
            collective_id=1, has_side_effects=True, vmem_limit_bytes=56 * MIB
        ),
        name="attn_out",
        cost_estimate=cost(115),
    )(attended, full_out, layer_input, scale)


class WeightTiles:
    def __init__(self, source, held, sem, axis, size):
        self.source, self.held, self.sem, self.axis, self.size = source, held, sem, axis, size
        self.count = source.shape[axis] // size

    def at(self, ref, tile):
        span = pl.ds(pl.multiple_of(tile * self.size, self.size), self.size)
        return ref.at[:, span] if self.axis == 1 else ref.at[span]

    def copy(self, tile):
        return pltpu.make_async_copy(
            self.at(self.source, tile), self.at(self.held, tile), self.sem.at[tile]
        )

    def start(self):
        for tile in range(self.count):
            self.copy(tile).start()


def mlp_forward_kernel(
    n, rows, h_full, wg, wu, wd, middle, upstream_in, row_valid, scale,
    output, dm_full, gate_out, up_out, hidden_out, gain_out,
    part, recv, rs_send_sem, rs_recv_sem, total, own, ag_send_sem, ag_recv_sem, local_sem,
    vg, vu, vd, wsem, h_buf, h_sem, gate_buf, up_buf, hidden_buf, out_sem,
):
    me = lax.axis_index("mp")
    width, hidden_width = wg.shape

    def h_copy(c, j):
        return pltpu.make_async_copy(
            h_full.at[j, chunk_span(c, rows)],
            h_buf.at[c % 2, pl.ds(j * rows, rows)],
            h_sem.at[c % 2, j],
        )

    for j in range(n):
        h_copy(0, j).start()
    gate_tiles = WeightTiles(wg, vg, wsem.at[0], 1, TILE)
    up_tiles = WeightTiles(wu, vu, wsem.at[1], 1, TILE)
    down_tiles = WeightTiles(wd, vd, wsem.at[2], 1, TILE)
    for tile in range(gate_tiles.count):
        gate_tiles.copy(tile).start()
        up_tiles.copy(tile).start()
    down_tiles.start()
    neighbour_barrier(me, n)

    def save_copies(c, j):
        slot = c % 2
        span = pl.ds(j * rows, rows)
        return [
            pltpu.make_async_copy(
                buf.at[slot, span], out.at[j, chunk_span(c, rows)], out_sem.at[slot, k, j]
            )
            for k, (buf, out) in enumerate(
                ((gate_buf, gate_out), (up_buf, up_out), (hidden_buf, hidden_out))
            )
        ]

    def compute(c):
        slot = c % 2
        for j in range(n):
            h_copy(c, j).wait()
        if c + 1 < CHUNKS:
            for j in range(n):
                h_copy(c + 1, j).start()
        if c >= 2:
            for j in range(n):
                for copy in save_copies(c - 2, j):
                    copy.wait()

        @pl.loop(0, hidden_width // TILE)
        def _(tile):
            if c == 0:
                gate_tiles.copy(tile).wait()
                up_tiles.copy(tile).wait()
            cols = pl.ds(pl.multiple_of(tile * TILE, TILE), TILE)
            gate = plain_dot(h_buf[slot], vg[:, cols])
            up = plain_dot(h_buf[slot], vu[:, cols])
            gate_buf[slot, :, cols] = gate.astype(BF)
            up_buf[slot, :, cols] = up.astype(BF)
            hidden_buf[slot, :, cols] = (gate * jax.nn.sigmoid(gate) * up).astype(BF)

        for j in range(n):
            for copy in save_copies(c, j):
                copy.start()

        @pl.loop(0, width // TILE)
        def _(tile):
            if c == 0:
                down_tiles.copy(tile).wait()
            cols = pl.ds(pl.multiple_of(tile * TILE, TILE), TILE)
            part[c, :, cols] = plain_dot(hidden_buf[slot], vd[:, cols]).astype(BF)

    scatter = LineScatter(n, me, rows, part, recv, rs_send_sem, rs_recv_sem)
    gather = make_gather(n, me, rows, own, dm_full, ag_send_sem, ag_recv_sem, local_sem)

    def row_work(c):
        scatter.total(c, total)
        span = chunk_span(c, rows)
        value = total[...]
        inverse = inverse_rms(value)
        output[span] = (middle[span] + value * inverse * scale[...]).astype(BF)
        upstream = upstream_in[span].astype(F32) * row_valid[span]
        grad, gain = norm_back(value, inverse, scale[...], upstream)
        own[c] = grad.astype(BF)
        gain_out[...] = gain if c == 0 else gain_out[...] + gain

    run_line(n, CHUNKS, STAGGER, compute, scatter, row_work, gather)
    for c in range(max(CHUNKS - 2, 0), CHUNKS):
        for j in range(n):
            for copy in save_copies(c, j):
                copy.wait()


def mlp_forward(n, h_full, wg, wu, wd, middle, out_grad, row_valid, scale):
    row_count, width = middle.shape
    hidden_width = wg.shape[1]
    rows = row_count // CHUNKS
    saved = jax.ShapeDtypeStruct((n, row_count, hidden_width), BF)
    most = max(width, hidden_width) // TILE
    return pl.pallas_call(
        functools.partial(mlp_forward_kernel, n, rows),
        out_shape=(
            jax.ShapeDtypeStruct((row_count, width), BF),
            jax.ShapeDtypeStruct((n, row_count, width), BF),
            saved,
            saved,
            saved,
            jax.ShapeDtypeStruct((1, width), F32),
        ),
        in_specs=[HBM] * 4 + [VMEM] * 4,
        out_specs=(VMEM, HBM, HBM, HBM, HBM, VMEM),
        scratch_shapes=scatter_scratch(n, rows, width)
        + gather_scratch(n, rows, width)
        + [
            pltpu.VMEM(wg.shape, BF),
            pltpu.VMEM(wu.shape, BF),
            pltpu.VMEM(wd.shape, BF),
            pltpu.SemaphoreType.DMA((3, most)),
            pltpu.VMEM((2, n * rows, width), BF),
            pltpu.SemaphoreType.DMA((2, n)),
        ]
        + [pltpu.VMEM((2, n * rows, hidden_width), BF)] * 3
        + [pltpu.SemaphoreType.DMA((2, 3, n))],
        compiler_params=pltpu.CompilerParams(
            collective_id=2, has_side_effects=True, vmem_limit_bytes=60 * MIB
        ),
        name="mlp_forward",
        cost_estimate=cost(135),
    )(h_full, wg, wu, wd, middle, out_grad, row_valid, scale)


def mlp_backward_kernel(
    n, n_dp, rows, dm_full, h_full, wg, wu, wd, gate_in, up_in, branch, upstream_in, row_valid,
    scale,
    middle_grad, da_full, gain_out, gate_out, up_out,
    part, recv, rs_send_sem, rs_recv_sem, total, own, ag_send_sem, ag_recv_sem, local_sem,
    vg, vu, vd, wsem, dm_buf, gate_buf, up_buf, in_sem, dgate, dup, mg_buf, mg_sem,
    h_buf, h_sem, extra, ready, *plane,
):
    me, at = lax.axis_index("mp"), lax.axis_index("dp")
    width, hidden_width = wg.shape
    chips = n_dp // 2
    part_width = width // n_dp
    size = n * rows * CHUNKS

    def in_copies(c, j):
        span = pl.ds(j * rows, rows)
        return [
            pltpu.make_async_copy(
                source.at[j, chunk_span(c, rows)], buf.at[span], in_sem.at[k, j]
            )
            for k, (source, buf) in enumerate(
                ((dm_full, dm_buf), (gate_in, gate_buf), (up_in, up_buf))
            )
        ]

    for j in range(n):
        for copy in in_copies(0, j):
            copy.start()
    down_tiles = WeightTiles(wd, vd, wsem.at[0], 0, TILE)
    gate_tiles = WeightTiles(wg, vg, wsem.at[1], 0, TILE)
    up_tiles = WeightTiles(wu, vu, wsem.at[2], 0, TILE)
    down_tiles.start()
    for tile in range(gate_tiles.count):
        gate_tiles.copy(tile).start()
        up_tiles.copy(tile).start()
    stage_barrier(me, n, at, chips)

    def compute(c):
        here = pl.ds(c * n * rows, n * rows)
        for j in range(n):
            for copy in in_copies(c, j):
                copy.wait()

        @pl.loop(0, hidden_width // TILE)
        def _(tile):
            if c == 0:
                down_tiles.copy(tile).wait()
            cols = pl.ds(pl.multiple_of(tile * TILE, TILE), TILE)
            hidden_grad = outer_dot(dm_buf[...], vd[cols, :])
            gate = gate_buf[:, cols].astype(F32)
            up = up_buf[:, cols].astype(F32)
            sigmoid = jax.nn.sigmoid(gate)
            dgate[here, cols] = (
                hidden_grad * up * sigmoid * (1.0 + gate * (1.0 - sigmoid))
            ).astype(BF)
            dup[here, cols] = (hidden_grad * gate * sigmoid).astype(BF)

        if c + 1 < CHUNKS:
            for j in range(n):
                for copy in in_copies(c + 1, j):
                    copy.start()

        @pl.loop(0, width // TILE)
        def _(tile):
            if c == 0:
                gate_tiles.copy(tile).wait()
                up_tiles.copy(tile).wait()
            cols = pl.ds(pl.multiple_of(tile * TILE, TILE), TILE)
            part[c, :, cols] = (
                outer_dot(dgate[here], vg[cols, :]) + outer_dot(dup[here], vu[cols, :])
            ).astype(BF)

        if c + 1 == CHUNKS:
            for copy in h_copies(0):
                copy.start()
            signal_partners(ready, at, chips)

    scatter = LineScatter(n, me, rows, part, recv, rs_send_sem, rs_recv_sem)
    gather = make_gather(n, me, rows, own, da_full, ag_send_sem, ag_recv_sem, local_sem)

    def mg_copy(c):
        return pltpu.make_async_copy(
            mg_buf.at[c % 2], middle_grad.at[chunk_span(c, rows)], mg_sem.at[c % 2]
        )

    def row_work(c):
        scatter.total(c, total)
        span = chunk_span(c, rows)
        upstream = upstream_in[span].astype(F32) * row_valid[span] + total[...]
        if c >= 2:
            mg_copy(c - 2).wait()
        mg_buf[c % 2] = upstream
        mg_copy(c).start()
        value = branch[span]
        grad, gain = norm_back(value, inverse_rms(value), scale[...], upstream)
        own[c] = grad.astype(BF)
        gain_out[...] = gain if c == 0 else gain_out[...] + gain

    block_width = pl.ds(0, hidden_width)

    def slot(index):
        for ref in (vg, vu, vd):
            count = ref.shape[0] // part_width
            if index < count:
                return ref.at[pl.ds(index * part_width, part_width), block_width]
            index -= count
        return extra.at[index]

    base = [chips, chips + 3 * chips]
    reduces = []
    for which, out in enumerate((gate_out, up_out)):
        first = base[which]
        views = (
            lambda r: slot(r),
            lambda r, first=first: slot(first + r),
            lambda r, first=first: slot(first + chips + r),
            lambda r, first=first: slot(first + 2 * chips + r - 1),
        )
        reduces.append(
            PlaneReduce(at, chips, part_width, views, plane[4 * which : 4 * which + 4], out)
        )
    order = relative_order(chips)
    jobs = [
        (which, same_core, r)
        for which in range(2)
        for same_core in (False, True)
        for r in order
    ]

    def h_copies(index):
        which, same_core, r = jobs[index]
        first = reduces[which].owner(r, same_core) * part_width
        cols = pl.ds(pl.multiple_of(first, part_width), part_width)
        return [
            pltpu.make_async_copy(
                h_full.at[j, :, cols],
                h_buf.at[index % 2, j],
                h_sem.at[index % 2, j],
            )
            for j in range(n)
        ]

    def weight_block(index):
        which, same_core, r = jobs[index]
        reduce = reduces[which]
        grad = (dgate, dup)[which]
        if index == 0:
            pl.semaphore_wait(ready, 1 + len(bits_of(chips - 1)))
        for copy in h_copies(index):
            copy.wait()
        if index + 1 < len(jobs):
            for copy in h_copies(index + 1):
                copy.start()
        if same_core:
            reduce.core_copy(r).wait_recv()
        elif which == 1:
            reduces[0].drain_core(r)
        left = jnp.concatenate(
            [
                h_buf[index % 2, j, c * rows : (c + 1) * rows]
                for c in range(CHUNKS)
                for j in range(n)
            ],
            axis=0,
        )

        @pl.loop(0, hidden_width // TILE)
        def _(tile):
            cols = pl.ds(pl.multiple_of(tile * TILE, TILE), TILE)
            block = inner_dot(left, grad[:, cols])
            if not same_core:
                reduce.core_send(r)[:, cols] = block.astype(BF)
            else:
                block = block + reduce.core_recv(r)[:, cols].astype(F32)
                if r > 0:
                    reduce.held(r)[:, cols] = block.astype(BF)
                else:
                    reduce.out[:, cols] = block

        if not same_core:
            reduce.core_copy(r).start()

    work = []
    for index, (which, same_core, r) in enumerate(jobs):
        work.append(lambda index=index: weight_block(index))
        if same_core and r > 0:
            for half in range(2):
                if not reduces[which].before(r, half):
                    work.append(lambda w=which, r=r, half=half: reduces[w].push(r, half))
                    work[-2:] = [lambda f=work[-2], g=work[-1]: (f(), g())]
        if same_core and r == order[-1]:
            for late in order:
                for half in range(2):
                    if late > 0 and reduces[which].before(late, half):
                        work.append(lambda w=which, r=late, half=half: reduces[w].push(r, half))
    pending = iter(work)

    def filler():
        for _ in range(FILL):
            job = next(pending, None)
            if job is not None:
                job()

    run_line(n, CHUNKS, STAGGER, compute, scatter, row_work, gather, filler)
    for job in pending:
        job()
    for reduce in reduces:
        reduce.finish()
        reduce.drain()
    for r in range(chips):
        reduces[1].drain_core(r)
    for c in range(max(CHUNKS - 2, 0), CHUNKS):
        mg_copy(c).wait()


def mlp_backward(n, n_dp, dm_full, h_full, wg, wu, wd, gate, up, branch, out_grad, row_valid, scale):
    row_count, width = branch.shape
    hidden_width = wg.shape[1]
    rows = row_count // CHUNKS
    size = n * row_count
    chips = n_dp // 2
    part_width = width // n_dp
    block = (part_width, hidden_width)
    most = max(width, hidden_width) // TILE
    slots = (2 * width + hidden_width) // part_width
    extra = max(7 * chips - 1 - slots, 1)
    return pl.pallas_call(
        functools.partial(mlp_backward_kernel, n, n_dp, rows),
        out_shape=(
            jax.ShapeDtypeStruct((row_count, width), F32),
            jax.ShapeDtypeStruct((n, row_count, width), BF),
            jax.ShapeDtypeStruct((1, width), F32),
            jax.ShapeDtypeStruct(block, F32),
            jax.ShapeDtypeStruct(block, F32),
        ),
        in_specs=[HBM] * 7 + [VMEM] * 4,
        out_specs=(HBM, HBM, VMEM, VMEM, VMEM),
        scratch_shapes=scatter_scratch(n, rows, width)
        + gather_scratch(n, rows, width)
        + [
            pltpu.VMEM(wg.shape, BF),
            pltpu.VMEM(wu.shape, BF),
            pltpu.VMEM(wd.shape, BF),
            pltpu.SemaphoreType.DMA((3, most)),
            pltpu.VMEM((n * rows, width), BF),
            pltpu.VMEM((n * rows, hidden_width), BF),
            pltpu.VMEM((n * rows, hidden_width), BF),
            pltpu.SemaphoreType.DMA((3, n)),
        ]
        + [pltpu.VMEM((size, hidden_width), BF)] * 2
        + [
            pltpu.VMEM((2, rows, width), F32),
            pltpu.SemaphoreType.DMA((2,)),
            pltpu.VMEM((2, n, row_count, part_width), BF),
            pltpu.SemaphoreType.DMA((2, n)),
            pltpu.VMEM((extra,) + block, BF),
            pltpu.SemaphoreType.REGULAR,
        ]
        + plane_sems(chips) * 2,
        compiler_params=pltpu.CompilerParams(
            collective_id=3, has_side_effects=True, vmem_limit_bytes=63 * MIB
        ),
        name="mlp_backward",
        cost_estimate=cost(145),
    )(dm_full, h_full, wg, wu, wd, gate, up, branch, out_grad, row_valid, scale)


def last_grads_kernel(
    n, n_dp, rows, grads, weight, base, inputs, att, da, gains,
    input_grad, qkv_out, out_out, gain_out,
    part, recv, rs_send_sem, rs_recv_sem, total, packed,
    x_buf, da_buf, load_sem,
    send_qkv, recv_qkv, held_qkv, message_qkv, send_out, recv_out, held_out, message_out,
    gain_recv, gain_send_sem, gain_recv_sem, mp_recv, mp_send_sem, mp_recv_sem, *plane,
):
    me, at = lax.axis_index("mp"), lax.axis_index("dp")
    entered = peer_barrier((("mp", me, n), ("dp", at, n_dp)))
    width = weight.shape[0]
    block_rows = rows * CHUNKS
    local_width = att.shape[1]
    chips = n_dp // 2
    part_width = width // n_dp
    order = relative_order(chips)
    jobs = [(same_core, r) for same_core in (False, True) for r in order]

    def views(send, recv, held, message):
        return (
            lambda r: send.at[r],
            lambda r: recv.at[r],
            lambda r: held.at[r - 1],
            lambda r: message.at[r - 1],
        )

    by_qkv = PlaneReduce(
        at, chips, part_width, views(send_qkv, recv_qkv, held_qkv, message_qkv), plane[:4], qkv_out
    )
    by_out = PlaneReduce(
        at, chips, local_width, views(send_out, recv_out, held_out, message_out), plane[4:], out_out
    )

    def loads(k):
        same_core, r = jobs[k]
        first = by_qkv.owner(r, same_core) * part_width
        cols = pl.ds(pl.multiple_of(first, part_width), part_width)
        return [
            pltpu.make_async_copy(inputs.at[:, cols], x_buf.at[k % 2], load_sem.at[k % 2, 0]),
            pltpu.make_async_copy(da.at[:, cols], da_buf.at[k % 2], load_sem.at[k % 2, 1]),
        ]

    for copy in loads(0):
        copy.start()

    def compute(c):
        for j in range(n):
            packed[j * rows : (j + 1) * rows] = grads[
                j * block_rows + c * rows : j * block_rows + (c + 1) * rows
            ]

        @pl.loop(0, width // TILE)
        def _(tile):
            cols = pl.ds(pl.multiple_of(tile * TILE, TILE), TILE)
            part[c, :, cols] = outer_dot(packed[...], weight[cols, :]).astype(BF)

    scatter = LineScatter(n, me, rows, part, recv, rs_send_sem, rs_recv_sem)

    def row_work(c):
        scatter.total(c, total)
        span = chunk_span(c, rows)
        input_grad[span] = base[span] + total[...]

    def weight_block(k):
        same_core, r = jobs[k]
        slot = k % 2
        for copy in loads(k):
            copy.wait()
        if k + 1 < len(jobs):
            for copy in loads(k + 1):
                copy.start()
        if same_core:
            by_qkv.core_copy(r).wait_recv()
            by_out.core_copy(r).wait_recv()

        def keep(reduce, block, cols):
            if not same_core:
                reduce.core_send(r)[:, cols] = block.astype(BF)
                return
            block = block + reduce.core_recv(r)[:, cols].astype(F32)
            if r > 0:
                reduce.held(r)[:, cols] = block.astype(BF)
            else:
                reduce.out[:, cols] = block

        @pl.loop(0, 3)
        def _(tile):
            cols = pl.ds(pl.multiple_of(tile * local_width, local_width), local_width)
            keep(by_qkv, inner_dot(x_buf[slot], grads[:, cols]), cols)

        keep(by_out, inner_dot(att[...], da_buf[slot]), slice(None))
        for reduce in (by_qkv, by_out):
            if not same_core:
                reduce.core_copy(r).start()
            elif r > 0:
                for half in range(2):
                    if not reduce.before(r, half):
                        reduce.push(r, half)

    gain_copies = exchange(
        "dp", at, n_dp, lambda peer: gains.at[peer], gain_recv, gain_send_sem, gain_recv_sem
    )
    mp_copies = exchange("mp", me, n, lambda peer: gain_out, mp_recv, mp_send_sem, mp_recv_sem)
    line = iter([(step, c) for c in range(CHUNKS) for step in range(1, n)])

    def line_steps(count):
        for _ in range(count):
            step, c = next(line, (None, None))
            if step is None:
                return
            if step < n - 1:
                scatter.step(c, step)
            else:
                row_work(c)

    def send_edges(c):
        for step in range(n - 1):
            scatter.edge(c, step)

    compute(0)
    entered()
    send_edges(0)
    for copy in gain_copies:
        copy.start()
    blocks = iter(range(len(jobs)))
    for c in range(1, CHUNKS):
        weight_block(next(blocks))
        compute(c)
        send_edges(c)
    for k in blocks:
        weight_block(k)
        line_steps(2)
    late = [(r, half) for r in order for half in range(2) if r > 0 and by_qkv.before(r, half)]
    for r, half in late:
        for reduce in (by_qkv, by_out):
            reduce.push(r, half)
        line_steps(1)
    gain_out[...] = gains[at]
    for shift, copy in enumerate(gain_copies, 1):
        copy.wait_recv()
        gain_out[...] += gain_recv[shift - 1]
    for copy in mp_copies:
        copy.start()
    line_steps(n * CHUNKS)
    for reduce in (by_qkv, by_out):
        reduce.finish()
    for copy in mp_copies:
        copy.wait_recv()
        copy.wait_send()
    lanes = lax.broadcasted_iota(jnp.int32, gain_out.shape, 1)
    shared = gain_out[...]
    for shift in range(1, n):
        shared = shared + mp_recv[shift - 1]
    gain_out[...] = jnp.where(lanes < 2 * part_width, shared, gain_out[...])
    for copy in gain_copies:
        copy.wait_send()
    for c in range(CHUNKS):
        scatter.drain(c)
    for reduce in (by_qkv, by_out):
        for r in range(chips):
            reduce.drain_core(r)
        reduce.drain()


def last_grads(n, n_dp, grads, weight, base, inputs, attended, da_full, gains):
    row_count, width = base.shape
    rows = row_count // CHUNKS
    size, local_width = attended.shape
    part_width = width // n_dp
    chips = n_dp // 2
    qkv_block = (part_width, 3 * local_width)
    out_block = (local_width, part_width)
    gain_block = gains.shape[1:]
    return pl.pallas_call(
        functools.partial(last_grads_kernel, n, n_dp, rows),
        out_shape=(
            jax.ShapeDtypeStruct((row_count, width), F32),
            jax.ShapeDtypeStruct(qkv_block, F32),
            jax.ShapeDtypeStruct(out_block, F32),
            jax.ShapeDtypeStruct(gain_block, F32),
        ),
        in_specs=[VMEM, VMEM, VMEM, HBM, VMEM, HBM, VMEM],
        out_specs=(VMEM,) * 4,
        scratch_shapes=scatter_scratch(n, rows, width)
        + [
            pltpu.VMEM((n * rows, 3 * local_width), BF),
            pltpu.VMEM((2, size, part_width), BF),
            pltpu.VMEM((2, size, part_width), BF),
            pltpu.SemaphoreType.DMA((2, 2)),
        ]
        + [
            pltpu.VMEM((count,) + block, BF)
            for block in (qkv_block, out_block)
            for count in (chips, chips, chips - 1, chips - 1)
        ]
        + [pltpu.VMEM((n_dp - 1,) + gain_block, F32)]
        + [pltpu.SemaphoreType.DMA((n_dp - 1,))] * 2
        + [pltpu.VMEM((n - 1,) + gain_block, F32)]
        + [pltpu.SemaphoreType.DMA((n - 1,))] * 2
        + plane_sems(chips) * 2,
        compiler_params=pltpu.CompilerParams(
            collective_id=4, has_side_effects=True, vmem_limit_bytes=60 * MIB
        ),
        name="last_grads",
        cost_estimate=cost(80),
    )(grads, weight, base, inputs, attended, da_full, gains)


def turn(values, cos, sin):
    return values * cos + pltpu.roll(values, values.shape[1] // 2, 1) * sin


def turn_back(values, cos, sin):
    return values * cos + pltpu.roll(values * sin, values.shape[1] // 2, 1)


def allowed_keys(starts, first_row, rows, key_end):
    places = first_row + lax.broadcasted_iota(jnp.int32, (rows, key_end), 0)
    keys = lax.broadcasted_iota(jnp.int32, (rows, key_end), 1)
    return (keys <= places) & (keys >= starts)


def columns_to_rows(first, second):
    lanes = lax.broadcasted_iota(jnp.int32, (first.shape[0], 128), 1)
    return jnp.transpose(jnp.where(lanes == 0, first, second))[:8]


def sum_columns(n, me, first, second, entered, held, recv, turned, send_sem, recv_sem):
    held[...] = columns_to_rows(first, second)
    copies = exchange("mp", me, n, lambda peer: held, recv, send_sem, recv_sem)
    entered()
    for copy in copies:
        copy.start()
    total = held[...]
    for shift, copy in enumerate(copies, 1):
        copy.wait_recv()
        total = total + recv[shift - 1]
    for copy in copies:
        copy.wait_send()
    turned[...] = jnp.zeros_like(turned)
    turned[:8] = total
    back = jnp.transpose(turned[...])
    return back[:, 0:1], back[:, 1:2]


def sum_scratch(n, size):
    return [
        pltpu.VMEM((8, size), F32),
        pltpu.VMEM((n - 1, 8, size), F32),
        pltpu.VMEM((128, size), F32),
        pltpu.SemaphoreType.DMA((n - 1,)),
        pltpu.SemaphoreType.DMA((n - 1,)),
    ]


def attention_kernel(
    n, heads, model_width, qkv, q_gain, k_gain, cos, sin, starts,
    out, q_low, k_low, v_low, log_total, q_inv, k_inv, *sums,
):
    me = lax.axis_index("mp")
    entered = peer_barrier((("mp", me, n),))
    size = qkv.shape[0]
    width = qkv.shape[1] // 3
    head = width // heads
    score_scale = 1.0 / math.sqrt(head)

    def squares(first):
        return jnp.sum(jnp.square(qkv[:, first : first + width]), axis=1, keepdims=True)

    q_sum, k_sum = sum_columns(n, me, squares(0), squares(width), entered, *sums)
    q_inv[...] = lax.rsqrt(q_sum / model_width + EPS)
    k_inv[...] = lax.rsqrt(k_sum / model_width + EPS)
    rows = min(QUERY_ROWS, size)

    @pl.loop(0, heads)
    def _(h):
        def cols(first):
            return pl.ds(pl.multiple_of(first + h * head, head), head)

        here = cols(0)
        q_low[:, here] = turn(
            qkv[:, here] * q_inv[...] * q_gain[:, here], cos[...], sin[...]
        ).astype(BF)
        k_low[:, here] = turn(
            qkv[:, cols(width)] * k_inv[...] * k_gain[:, here], cos[...], sin[...]
        ).astype(BF)
        v_low[:, here] = qkv[:, cols(2 * width)].astype(BF)
        for first in range(0, size, rows):
            end = first + rows
            span = slice(first, end)
            scores = outer_dot(q_low[span, here], k_low[:end, here]) * score_scale
            scores = jnp.where(allowed_keys(starts[span], first, rows, end), scores, MASKED)
            row_max = jnp.max(scores, axis=1, keepdims=True)
            exponents = jnp.exp(scores - row_max)
            row_total = jnp.sum(exponents, axis=1, keepdims=True)
            probs = (exponents * (1.0 / row_total)).astype(BF)
            out[span, here] = plain_dot(probs, v_low[:end, here]).astype(BF)
            log_total[h, span] = row_max + jnp.log(row_total)


def attention(n, heads, model_width, qkv_raw, q_gain, k_gain, cos, sin, starts):
    size = qkv_raw.shape[0]
    low = jax.ShapeDtypeStruct((size, qkv_raw.shape[1] // 3), BF)
    column = jax.ShapeDtypeStruct((size, 1), F32)
    return pl.pallas_call(
        functools.partial(attention_kernel, n, heads, model_width),
        out_shape=(low,) * 4 + (jax.ShapeDtypeStruct((heads, size, 1), F32), column, column),
        in_specs=[VMEM] * 6,
        out_specs=(VMEM,) * 7,
        scratch_shapes=sum_scratch(n, size),
        compiler_params=pltpu.CompilerParams(
            collective_id=5, has_side_effects=True, vmem_limit_bytes=56 * MIB
        ),
        name="attention",
        cost_estimate=cost(25),
    )(qkv_raw, q_gain, k_gain, cos, sin, starts)


def attention_back_kernel(
    n, heads, model_width, qkv, q_low, k_low, v_low, out_grad, log_total,
    q_inv, k_inv, q_gain, k_gain, cos, sin, starts,
    grads, q_gain_grad, k_gain_grad,
    q_weighted, k_weighted, q_grad, k_sum, v_sum, q_dots, k_dots, *sums,
):
    me = lax.axis_index("mp")
    entered = peer_barrier((("mp", me, n),))
    size = qkv.shape[0]
    width = qkv.shape[1] // 3
    head = width // heads
    score_scale = 1.0 / math.sqrt(head)
    rows = min(QUERY_ROWS, size)
    q_dots[...] = jnp.zeros_like(q_dots)
    k_dots[...] = jnp.zeros_like(k_dots)

    @pl.loop(0, heads)
    def _(h):
        def cols(first):
            return pl.ds(pl.multiple_of(first + h * head, head), head)

        here = cols(0)
        for first in reversed(range(0, size, rows)):
            end = first + rows
            span = slice(first, end)
            scores = outer_dot(q_low[span, here], k_low[:end, here]) * score_scale
            scores = jnp.where(allowed_keys(starts[span], first, rows, end), scores, MASKED)
            probs = jnp.exp(scores - log_total[h, span])
            prob_grad = outer_dot(out_grad[span, here], v_low[:end, here])
            probs_low = probs.astype(BF)
            weighted = probs * prob_grad
            score_grad = (
                weighted - probs * jnp.sum(weighted, axis=1, keepdims=True)
            ).astype(BF)
            q_grad[span] = plain_dot(score_grad, k_low[:end, here]) * score_scale
            k_extra = inner_dot(score_grad, q_low[span, here])
            v_extra = inner_dot(probs_low, out_grad[span, here])
            if end == size:
                k_sum[...] = k_extra
                v_sum[...] = v_extra
            else:
                k_sum[:end] += k_extra
                v_sum[:end] += v_extra
        for first, inv, gain, grad, factor, weighted_out, dots, gain_grad in (
            (0, q_inv, q_gain, q_grad, None, q_weighted, q_dots, q_gain_grad),
            (width, k_inv, k_gain, k_sum, score_scale, k_weighted, k_dots, k_gain_grad),
        ):
            raw = qkv[:, cols(first)]
            value = grad[...] if factor is None else grad[...] * factor
            normed = turn_back(value, cos[...], sin[...])
            weighted = normed * gain[:, here]
            weighted_out[:, here] = weighted
            gain_grad[:, here] = jnp.sum(normed * raw * inv[...], axis=0, keepdims=True)
            dots[...] += jnp.sum(weighted * raw, axis=1, keepdims=True)
        grads[:, cols(2 * width)] = v_sum[...].astype(BF)

    q_total, k_total = sum_columns(n, me, q_dots[...], k_dots[...], entered, *sums)
    for first, inv, weighted, dots in (
        (0, q_inv, q_weighted, q_total),
        (width, k_inv, k_weighted, k_total),
    ):
        scale = inv[...]
        factor = scale * scale * scale * (dots / model_width)
        grads[:, first : first + width] = (
            scale * weighted[...] - qkv[:, first : first + width] * factor
        ).astype(BF)


def attention_back(
    n, heads, model_width, qkv_raw, q_low, k_low, v_low, out_grad, log_total, q_inv, k_inv,
    q_gain, k_gain, cos, sin, starts,
):
    size, width = q_low.shape
    head = width // heads
    gains = jax.ShapeDtypeStruct((1, width), F32)
    return pl.pallas_call(
        functools.partial(attention_back_kernel, n, heads, model_width),
        out_shape=(jax.ShapeDtypeStruct((size, 3 * width), BF), gains, gains),
        in_specs=[VMEM] * 13,
        out_specs=(VMEM,) * 3,
        scratch_shapes=[pltpu.VMEM((size, width), F32)] * 2
        + [pltpu.VMEM((size, head), F32)] * 3
        + [pltpu.VMEM((size, 1), F32)] * 2
        + sum_scratch(n, size),
        compiler_params=pltpu.CompilerParams(
            collective_id=6, has_side_effects=True, vmem_limit_bytes=56 * MIB
        ),
        name="attention_back",
        cost_estimate=cost(30),
    )(
        qkv_raw, q_low, k_low, v_low, out_grad, log_total, q_inv, k_inv, q_gain, k_gain,
        cos, sin, starts,
    )


def local(
    layer_input,
    query_weight,
    key_weight,
    value_weight,
    out_weight,
    gate_weight,
    up_weight,
    down_weight,
    query_gain,
    key_gain,
    attn_gain,
    mlp_gain,
    seq_lens,
    out_grad,
):
    n = lax.axis_size("mp")
    n_dp = lax.axis_size("dp")
    me = lax.axis_index("mp")
    row_count, model_width = layer_input.shape
    group_size = row_count * n
    local_heads, gain_part = query_gain.shape
    head_size = gain_part * n_dp
    local_width = local_heads * head_size

    full_qkv = lax.all_gather(
        jnp.concatenate([query_weight, key_weight, value_weight], axis=1), "dp", axis=0, tiled=True
    )
    full_out = lax.all_gather(out_weight, "dp", axis=1, tiled=True)
    full_gate = lax.all_gather(gate_weight, "dp", axis=0, tiled=True)
    full_up = lax.all_gather(up_weight, "dp", axis=0, tiled=True)
    full_down = lax.all_gather(down_weight, "dp", axis=1, tiled=True)
    head_part = local_heads * gain_part
    width_part = attn_gain.shape[0]
    own_gains = jnp.concatenate(
        [attn_gain, mlp_gain, query_gain.reshape(head_part), key_gain.reshape(head_part)]
    ).astype(F32)[None]
    inputs_full, gain_parts = gather_rows(n, n_dp, layer_input, own_gains)
    inputs_full = inputs_full.reshape(group_size, model_width)
    gain_parts = gain_parts[:, 0]

    def head_gain(first):
        piece = gain_parts[:, first : first + head_part].reshape(n_dp, local_heads, gain_part)
        return piece.transpose(1, 0, 2).reshape(1, local_width)

    query_scale = head_gain(2 * width_part)
    key_scale = head_gain(2 * width_part + head_part)
    attn_scale = gain_parts[:, :width_part].reshape(1, model_width)
    mlp_scale = gain_parts[:, width_part : 2 * width_part].reshape(1, model_width)

    starts, positions, valid = layout(seq_lens[0], group_size)
    starts = starts[:, None]
    cos_table, sin_table = rotary_tables(positions, head_size)
    row_valid = lax.dynamic_slice_in_dim(valid, me * row_count, row_count, 0).astype(F32)[:, None]

    qkv_raw = plain_dot(inputs_full, full_qkv)
    attended, query_low, key_low, value_low, log_total, query_inv, key_inv = attention(
        n, local_heads, model_width, qkv_raw, query_scale, key_scale, cos_table, sin_table, starts
    )
    branch, middle, middle_full = attn_out(n, attended, full_out, layer_input, attn_scale)
    layer_output, mlp_grad_full, gate, up, hidden, mlp_gain_part = mlp_forward(
        n, middle_full, full_gate, full_up, full_down, middle, out_grad, row_valid, mlp_scale
    )

    def flat(rows):
        return rows.reshape(group_size, rows.shape[-1])

    def dp_scatter(part, dimension):
        return lax.psum_scatter(part, "dp", scatter_dimension=dimension, tiled=True)

    down_part = inner_dot(flat(hidden), flat(mlp_grad_full)).astype(BF)
    mlp_grad_full, down_part = lax.optimization_barrier((mlp_grad_full, down_part))
    grad_down = dp_scatter(down_part, 1)
    middle_grad, branch_full, attn_gain_part, grad_gate, grad_up = mlp_backward(
        n, n_dp, mlp_grad_full, middle_full, full_gate, full_up, full_down, gate, up, branch,
        out_grad, row_valid, attn_scale,
    )
    branch_full = flat(branch_full)
    branch_full, grad_down = lax.optimization_barrier((branch_full, grad_down))

    mixed_grad = outer_dot(branch_full, full_out).astype(BF)
    qkv_grad, query_gain_part, key_gain_part = attention_back(
        n, local_heads, model_width, qkv_raw, query_low, key_low, value_low, mixed_grad, log_total,
        query_inv, key_inv, query_scale, key_scale, cos_table, sin_table, starts,
    )

    def by_part(row):
        return row.reshape(n_dp, -1)

    def by_head_part(row):
        pieces = row.reshape(local_heads, n_dp, gain_part).transpose(1, 0, 2)
        return pieces.reshape(n_dp, head_part)

    gain_grads = jnp.concatenate(
        [
            by_part(attn_gain_part),
            by_part(mlp_gain_part),
            by_head_part(query_gain_part),
            by_head_part(key_gain_part),
        ],
        axis=1,
    )[:, None]
    input_grad, grad_qkv, grad_out, gain_sums = last_grads(
        n, n_dp, qkv_grad, full_qkv, middle_grad, inputs_full, attended, branch_full, gain_grads
    )
    gain_sums = gain_sums[0]
    heads_at = 2 * width_part
    return (
        layer_output,
        input_grad,
        grad_qkv[:, :local_width],
        grad_qkv[:, local_width : 2 * local_width],
        grad_qkv[:, 2 * local_width :],
        grad_out,
        grad_gate,
        grad_up,
        grad_down.astype(F32),
        gain_sums[heads_at : heads_at + head_part].reshape(local_heads, gain_part),
        gain_sums[heads_at + head_part :].reshape(local_heads, gain_part),
        gain_sums[:width_part],
        gain_sums[width_part:heads_at],
    )


def solution(mesh):
    return jax.shard_map(
        local,
        mesh=mesh,
        in_specs=(
            P(("dp", "mp"), None),
            P("dp", "mp"),
            P("dp", "mp"),
            P("dp", "mp"),
            P("mp", "dp"),
            P("dp", "mp"),
            P("dp", "mp"),
            P("mp", "dp"),
            P("mp", "dp"),
            P("mp", "dp"),
            P("dp"),
            P("dp"),
            P("dp", None),
            P(("dp", "mp"), None),
        ),
        out_specs=(
            P(("dp", "mp"), None),
            P(("dp", "mp"), None),
            P("dp", "mp"),
            P("dp", "mp"),
            P("dp", "mp"),
            P("mp", "dp"),
            P("dp", "mp"),
            P("dp", "mp"),
            P("mp", "dp"),
            P("mp", "dp"),
            P("mp", "dp"),
            P("dp"),
            P("dp"),
        ),
        check_vma=False,
    )
```

```python
import functools
import math

import jax
import jax.numpy as jnp
from jax import lax
from jax.experimental import pallas as pl
from jax.experimental.pallas import tpu as pltpu
from jax.sharding import PartitionSpec as P

EPS = 1e-06
THETA = 500000.0
MASKED = -1000000000.0
CHUNKS = 4
STAGGER = 2
EDGES = False
FILL = 2
PERIOD = 8
TILE = 512
QUERY_ROWS = 256
BF = jnp.bfloat16
F32 = jnp.float32
MIB = 1 << 20
HBM = pl.BlockSpec(memory_space=pl.ANY)
VMEM = pl.BlockSpec(memory_space=pltpu.VMEM)


def cost(micros):
    return pl.CostEstimate(
        flops=micros * 1_000_000_000, bytes_accessed=micros * 3_000_000, transcendentals=0
    )


def plain_dot(former, latter):
    return jnp.dot(former, latter, preferred_element_type=F32)


def inner_dot(former, latter):
    return lax.dot_general(
        former, latter, (((0,), (0,)), ((), ())), preferred_element_type=F32
    )


def outer_dot(former, latter):
    return lax.dot_general(
        former, latter, (((1,), (1,)), ((), ())), preferred_element_type=F32
    )


def layout(lengths, group_size):
    slot_count = lengths.shape[0]
    seq_ends = jnp.cumsum(lengths, dtype=jnp.int32)
    starts = seq_ends - lengths
    places = jnp.arange(group_size, dtype=jnp.int32)
    slot_ids = jnp.arange(slot_count, dtype=jnp.int32)
    segment = jnp.sum(
        (places[:, None] >= seq_ends[None, :]).astype(jnp.int32), axis=1, dtype=jnp.int32
    )
    chosen = (segment[:, None] == slot_ids[None, :]).astype(jnp.int32)
    padded = (segment == slot_count).astype(jnp.int32)
    begins = (
        jnp.sum(chosen * starts[None, :], axis=1, dtype=jnp.int32)
        + padded * seq_ends[slot_count - 1]
    )
    return (begins, places - begins, places < seq_ends[slot_count - 1])


def rotary_tables(positions, head_size):
    half_dim = head_size // 2
    frequency = jnp.exp(jnp.arange(half_dim, dtype=F32) * (-2.0 * math.log(THETA) / head_size))
    angles = positions.astype(F32)[:, None] * frequency[None, :]
    cos_half, sin_half = jnp.cos(angles), jnp.sin(angles)
    return (
        jnp.concatenate([cos_half, cos_half], axis=1),
        jnp.concatenate([-sin_half, sin_half], axis=1),
    )


def neighbour_barrier(me, n):
    barrier = pltpu.get_barrier_semaphore()

    @pl.when(me > 0)
    def _():
        pl.semaphore_signal(barrier, inc=1, device_id={"mp": me - 1})

    @pl.when(me < n - 1)
    def _():
        pl.semaphore_signal(barrier, inc=1, device_id={"mp": me + 1})

    pl.semaphore_wait(barrier, jnp.minimum(me, 1) + jnp.minimum(n - 1 - me, 1))


class LineGather:
    def __init__(self, n, me, own, full, send_sem, recv_sem, local_sem):
        self.n, self.me, self.own, self.full = n, me, own, full
        self.send_sem, self.recv_sem, self.local_sem = send_sem, recv_sem, local_sem

    def local_copy(self, c):
        return pltpu.make_async_copy(self.own(c), self.full(self.me, c), self.local_sem.at[c])

    def copy(self, c, step, way, block, src):
        return pltpu.make_async_remote_copy(
            src_ref=src,
            dst_ref=self.full(block, c),
            send_sem=self.send_sem.at[c, step - 1, way],
            recv_sem=self.recv_sem.at[c, step - 1, way],
            device_id={"mp": self.me + (1 if way == 0 else -1)},
        )

    def sides(self):
        return ((0, self.me), (1, self.n - 1 - self.me))

    def block_at(self, way, step):
        return self.me - step if way == 0 else self.me + step

    def step(self, c, step):
        n = self.n
        if step == 1:
            self.local_copy(c).start()
        for way, place in self.sides():
            if step > 1:

                @pl.when(place >= step - 1)
                def _(way=way):
                    block = self.block_at(way, step - 1)
                    self.copy(c, step - 1, way, block, self.own(c)).wait_recv()

            @pl.when((place >= step - 1) & (place < n - 1))
            def _(way=way):
                block = self.block_at(way, step - 1)
                src = self.own(c) if step == 1 else self.full(block, c)
                self.copy(c, step, way, block, src).start()

    def last(self, c):
        n = self.n
        for way, place in self.sides():

            @pl.when(place == n - 1)
            def _(way=way):
                block = self.block_at(way, n - 1)
                self.copy(c, n - 1, way, block, self.own(c)).wait_recv()

    def drain(self, c):
        self.local_copy(c).wait()
        self.drain_sends(c)

    def drain_sends(self, c):
        for step in range(1, self.n):
            for way, place in self.sides():

                @pl.when((place >= step - 1) & (place < self.n - 1))
                def _(way=way):
                    self.copy(c, step, way, self.me, self.own(c)).wait_send()


class LineScatter:
    def __init__(self, n, me, rows, part, recv, send_sem, recv_sem):
        self.n, self.me, self.rows = n, me, rows
        self.part, self.recv = part, recv
        self.send_sem, self.recv_sem = send_sem, recv_sem

    def piece(self, c, owner):
        first = pl.multiple_of(owner * self.rows, self.rows)
        return self.part.at[c, pl.ds(first, self.rows)]

    def copy(self, c, step, way, src):
        return pltpu.make_async_remote_copy(
            src_ref=src,
            dst_ref=self.recv.at[c, step, way],
            send_sem=self.send_sem.at[c, step, way],
            recv_sem=self.recv_sem.at[c, step, way],
            device_id={"mp": self.me + (1 if way == 0 else -1)},
        )

    def sides(self):
        return ((0, self.me), (1, self.n - 1 - self.me))

    def owner(self, way, step):
        return self.n - 1 - step + self.me if way == 0 else step - (self.n - 1 - self.me)

    def edge(self, c, step):
        for way, place in self.sides():

            @pl.when(place == 0)
            def _(way=way):
                self.copy(c, step, way, self.piece(c, self.owner(way, step))).start()

    def step(self, c, step):
        for way, place in self.sides():

            @pl.when((place > 0) & (place <= min(step, self.n - 2)))
            def _(way=way):
                piece = self.piece(c, self.owner(way, step))
                self.copy(c, step - 1, way, piece).wait_recv()
                piece[...] = (
                    piece[...].astype(F32) + self.recv[c, step - 1, way].astype(F32)
                ).astype(BF)
                self.copy(c, step, way, piece).start()

    def total(self, c, out):
        n = self.n
        out[...] = self.piece(c, self.me)[...].astype(F32)
        for way, place in self.sides():

            @pl.when(place > 0)
            def _(way=way):
                self.copy(c, n - 2, way, self.recv.at[c, n - 2, way]).wait_recv()
                out[...] += self.recv[c, n - 2, way].astype(F32)

    def drain(self, c):
        n = self.n
        for step in range(n - 1):
            for way, place in self.sides():

                @pl.when(place <= min(step, n - 2))
                def _(way=way):
                    self.copy(c, step, way, self.recv.at[c, step, way]).wait_send()


def run_line(n, chunks, stagger, compute, scatter, row_work, gather, filler=None):
    last_step = 2 * n - 2 if gather is not None else n - 1
    events = sorted(
        (step + stagger * c - (0.5 if step == 0 else 0), c, step)
        for c in range(chunks)
        for step in range(last_step + 1)
    )
    computed = 0
    for _, c, step in events:
        if step == 0:
            compute(c)
            for ahead in range(n - 1 if EDGES else 1):
                scatter.edge(c, ahead)
            computed += 1
        elif step < n - 1:
            if not EDGES:
                scatter.edge(c, step)
            scatter.step(c, step)
        elif step == n - 1:
            row_work(c)
            if gather is not None:
                gather.step(c, 1)
        elif step < 2 * n - 2:
            gather.step(c, step - n + 2)
        else:
            gather.last(c)
        if filler is not None and computed == chunks:
            filler()
    for c in range(chunks):
        scatter.drain(c)
        if gather is not None:
            gather.drain(c)


def flipped(chip, bit):
    return chip + bit - 2 * bit * lax.rem(chip // bit, 2)


def bits_of(number):
    return [1 << k for k in range(number.bit_length()) if number >> k & 1]


def relative_chip(chip, relative):
    for bit in bits_of(relative):
        chip = flipped(chip, bit)
    return chip


def relative_order(chips):
    return sorted(range(chips), key=lambda r: (-len(bits_of(r)), r))


class PlaneReduce:
    def __init__(self, at, chips, rows, views, sems, out):
        self.chip, self.core = at // 2, lax.rem(at, 2)
        self.chips, self.rows, self.out = chips, rows, out
        self.core_send, self.core_recv, self.held, self.message = views
        self.core_send_sem, self.core_recv_sem, self.send_sem, self.recv_sem = sems

    def first_bit(self, relative, half):
        bits = bits_of(relative)
        return bits[0] if half == 0 else bits[-1]

    def before(self, relative, half):
        return [
            r for r in range(1, self.chips) if r - self.first_bit(r, half) == relative
        ]

    def owner(self, relative, same_core):
        return 2 * relative_chip(self.chip, relative) + (
            self.core if same_core else 1 - self.core
        )

    def half_rows(self, half):
        return pl.ds(half * (self.rows // 2), self.rows // 2)

    def core_copy(self, relative):
        return pltpu.make_async_remote_copy(
            src_ref=self.core_send(relative),
            dst_ref=self.core_recv(relative),
            send_sem=self.core_send_sem.at[relative],
            recv_sem=self.core_recv_sem.at[relative],
            device_id={"dp": 2 * self.chip + 1 - self.core},
        )

    def message_copy(self, relative, half):
        span = self.half_rows(half)
        target = flipped(self.chip, self.first_bit(relative, half))
        return pltpu.make_async_remote_copy(
            src_ref=self.held(relative).at[span],
            dst_ref=self.message(relative).at[span],
            send_sem=self.send_sem.at[relative, half],
            recv_sem=self.recv_sem.at[relative, half],
            device_id={"dp": 2 * target + self.core},
        )

    def push(self, relative, half):
        span = self.half_rows(half)
        for r in self.before(relative, half):
            self.message_copy(r, half).wait_recv()
            held = self.held(relative)
            held[span] = (
                held[span].astype(F32) + self.message(r)[span].astype(F32)
            ).astype(BF)
        self.message_copy(relative, half).start()

    def finish(self):
        for half in range(2):
            span = self.half_rows(half)
            for r in self.before(0, half):
                self.message_copy(r, half).wait_recv()
                self.out[span] += self.message(r)[span].astype(F32)

    def drain_core(self, relative):
        self.core_copy(relative).wait_send()

    def drain(self):
        for r in range(1, self.chips):
            for half in range(2):
                self.message_copy(r, half).wait_send()


def plane_sems(chips):
    return [pltpu.SemaphoreType.DMA((chips,))] * 2 + [pltpu.SemaphoreType.DMA((chips, 2))] * 2


def stage_barrier(me, n, at, chips):
    barrier = pltpu.get_barrier_semaphore()

    @pl.when(me > 0)
    def _():
        pl.semaphore_signal(barrier, inc=1, device_id={"mp": me - 1})

    @pl.when(me < n - 1)
    def _():
        pl.semaphore_signal(barrier, inc=1, device_id={"mp": me + 1})

    count = signal_partners(barrier, at, chips)
    pl.semaphore_wait(barrier, count + jnp.minimum(me, 1) + jnp.minimum(n - 1 - me, 1))


def signal_partners(sem, at, chips):
    chip, core = at // 2, lax.rem(at, 2)
    pl.semaphore_signal(sem, inc=1, device_id={"dp": 2 * chip + 1 - core})
    bits = [1 << k for k in range(chips.bit_length() - 1)]
    for bit in bits:
        pl.semaphore_signal(sem, inc=1, device_id={"dp": 2 * flipped(chip, bit) + core})
    return 1 + len(bits)


def inverse_rms(rows):
    return lax.rsqrt(jnp.mean(rows * rows, axis=1, keepdims=True) + EPS)


def norm_back(values, inverse, gain_row, upstream):
    weighted = upstream * gain_row
    mean_term = jnp.mean(weighted * values, axis=1, keepdims=True)
    grad_values = inverse * weighted - values * (inverse * inverse * inverse) * mean_term
    return (grad_values, jnp.sum(upstream * values * inverse, axis=0, keepdims=True))


def scatter_scratch(n, rows, width):
    return [
        pltpu.VMEM((CHUNKS, n * rows, width), BF),
        pltpu.VMEM((CHUNKS, n - 1, 2, rows, width), BF),
        pltpu.SemaphoreType.DMA((CHUNKS, n - 1, 2)),
        pltpu.SemaphoreType.DMA((CHUNKS, n - 1, 2)),
        pltpu.VMEM((rows, width), F32),
    ]


def gather_scratch(n, rows, width):
    return [
        pltpu.VMEM((CHUNKS, rows, width), BF),
        pltpu.SemaphoreType.DMA((CHUNKS, n - 1, 2)),
        pltpu.SemaphoreType.DMA((CHUNKS, n - 1, 2)),
        pltpu.SemaphoreType.DMA((CHUNKS,)),
    ]


def chunk_span(c, rows):
    return pl.ds(c * rows, rows)


def make_gather(n, me, rows, own, full, send_sem, recv_sem, local_sem):
    return LineGather(
        n,
        me,
        lambda c: own.at[c],
        lambda block, c: full.at[block, chunk_span(c, rows)],
        send_sem,
        recv_sem,
        local_sem,
    )


def peer_barrier(axes):
    barrier = pltpu.get_barrier_semaphore()
    count = 0
    for name, index, size in axes:
        for shift in range(1, size):
            pl.semaphore_signal(barrier, inc=1, device_id={name: lax.rem(index + shift, size)})
            count += 1
    return lambda: pl.semaphore_wait(barrier, count)


def exchange(name, index, size, src, recv, send_sem, recv_sem):
    def copy(shift):
        peer = lax.rem(index + shift, size)
        return pltpu.make_async_remote_copy(
            src_ref=src(peer),
            dst_ref=recv.at[shift - 1],
            send_sem=send_sem.at[shift - 1],
            recv_sem=recv_sem.at[shift - 1],
            device_id={name: peer},
        )

    return [copy(shift) for shift in range(1, size)]


def gather_rows_kernel(
    n, n_dp, rows, block, gains, full, gain_parts,
    send_sem, recv_sem, local_sem, gain_recv, gain_send_sem, gain_recv_sem,
):
    me, at = lax.axis_index("mp"), lax.axis_index("dp")
    peer_barrier((("mp", me, n), ("dp", at, n_dp)))()
    gather = LineGather(
        n,
        me,
        lambda c: block.at[chunk_span(c, rows)],
        lambda index, c: full.at[index, chunk_span(c, rows)],
        send_sem,
        recv_sem,
        local_sem,
    )
    for c in range(CHUNKS):
        gather.step(c, 1)
    copies = exchange(
        "dp", at, n_dp, lambda peer: gains, gain_recv, gain_send_sem, gain_recv_sem
    )
    for copy in copies:
        copy.start()
    for step in range(2, n):
        for c in range(CHUNKS):
            gather.step(c, step)
    gain_parts[at] = gains[...]
    for shift, copy in enumerate(copies, 1):
        copy.wait_recv()
        gain_parts[lax.rem(at + n_dp - shift, n_dp)] = gain_recv[shift - 1]
    for c in range(CHUNKS):
        gather.last(c)
    for c in range(CHUNKS):
        gather.drain(c)
    for copy in copies:
        copy.wait_send()


def gather_rows(n, n_dp, block, gains):
    rows = block.shape[0] // CHUNKS
    sems = gather_scratch(n, rows, block.shape[1])[1:]
    return pl.pallas_call(
        functools.partial(gather_rows_kernel, n, n_dp, rows),
        out_shape=(
            jax.ShapeDtypeStruct((n,) + block.shape, block.dtype),
            jax.ShapeDtypeStruct((n_dp,) + gains.shape, F32),
        ),
        in_specs=[HBM, VMEM],
        out_specs=(HBM, VMEM),
        scratch_shapes=sems
        + [
            pltpu.VMEM((n_dp - 1,) + gains.shape, F32),
            pltpu.SemaphoreType.DMA((n_dp - 1,)),
            pltpu.SemaphoreType.DMA((n_dp - 1,)),
        ],
        compiler_params=pltpu.CompilerParams(collective_id=0, has_side_effects=True),
        name="gather_rows",
        cost_estimate=cost(75),
    )(block, gains)


def attn_out_kernel(
    n, rows, att, wo, x, scale, branch, middle, full,
    part, recv, rs_send_sem, rs_recv_sem, total, own, ag_send_sem, ag_recv_sem, local_sem,
    packed,
):
    me = lax.axis_index("mp")
    neighbour_barrier(me, n)
    width = wo.shape[1]
    block_rows = rows * CHUNKS

    def compute(c):
        for j in range(n):
            packed[j * rows : (j + 1) * rows] = att[
                j * block_rows + c * rows : j * block_rows + (c + 1) * rows
            ]

        @pl.loop(0, width // TILE)
        def _(tile):
            cols = pl.ds(pl.multiple_of(tile * TILE, TILE), TILE)
            part[c, :, cols] = plain_dot(packed[...], wo[:, cols]).astype(BF)

    scatter = LineScatter(n, me, rows, part, recv, rs_send_sem, rs_recv_sem)
    gather = make_gather(n, me, rows, own, full, ag_send_sem, ag_recv_sem, local_sem)

    def row_work(c):
        scatter.total(c, total)
        span = chunk_span(c, rows)
        value = total[...]
        branch[span] = value
        new = x[span].astype(F32) + value * inverse_rms(value) * scale[...]
        middle[span] = new
        own[c] = new.astype(BF)

    run_line(n, CHUNKS, STAGGER, compute, scatter, row_work, gather)


def attn_out(n, attended, full_out, layer_input, scale):
    row_count, width = layer_input.shape
    rows = row_count // CHUNKS
    return pl.pallas_call(
        functools.partial(attn_out_kernel, n, rows),
        out_shape=(
            jax.ShapeDtypeStruct((row_count, width), F32),
            jax.ShapeDtypeStruct((row_count, width), F32),
            jax.ShapeDtypeStruct((n, row_count, width), BF),
        ),
        in_specs=[VMEM] * 4,
        out_specs=(VMEM, VMEM, HBM),
        scratch_shapes=scatter_scratch(n, rows, width)
        + gather_scratch(n, rows, width)
        + [pltpu.VMEM((n * rows, attended.shape[1]), BF)],
        compiler_params=pltpu.CompilerParams(
            collective_id=1, has_side_effects=True, vmem_limit_bytes=56 * MIB
        ),
        name="attn_out",
        cost_estimate=cost(115),
    )(attended, full_out, layer_input, scale)


class WeightTiles:
    def __init__(self, source, held, sem, axis, size):
        self.source, self.held, self.sem, self.axis, self.size = source, held, sem, axis, size
        self.count = source.shape[axis] // size

    def at(self, ref, tile):
        span = pl.ds(pl.multiple_of(tile * self.size, self.size), self.size)
        return ref.at[:, span] if self.axis == 1 else ref.at[span]

    def copy(self, tile):
        return pltpu.make_async_copy(
            self.at(self.source, tile), self.at(self.held, tile), self.sem.at[tile]
        )

    def start(self):
        for tile in range(self.count):
            self.copy(tile).start()


def mlp_kernel(
    n, n_dp, rows, h_full, wg, wu, wd, middle, branch, upstream_in, row_valid, mlp_scale, attn_scale,
    output, dm_full, hidden_out, mlp_gain, middle_grad, da_full, attn_gain, gate_out, up_out,
    part, recv, rs_send_sem, rs_recv_sem, total, own, ag_send_sem, ag_recv_sem, local_sem,
    vg, vu, vd, wsem, in_buf, in_sem, gate_all, up_all, hidden_buf, hidden_sem,
    row_buf, row_sem, mg_buf, mg_sem, h_buf, h_sem, extra, ready, *plane,
):
    me, at = lax.axis_index("mp"), lax.axis_index("dp")
    width, hidden_width = wg.shape
    chips = n_dp // 2
    part_width = width // n_dp

    def in_copies(phase, c):
        source = h_full if phase == 0 else dm_full
        return [
            pltpu.make_async_copy(
                source.at[j, chunk_span(c, rows)],
                in_buf.at[c % 2, pl.ds(j * rows, rows)],
                in_sem.at[c % 2, j],
            )
            for j in range(n)
        ]

    def start(copies):
        for copy in copies:
            copy.start()

    def wait(copies):
        for copy in copies:
            copy.wait()

    def row_copy(phase, c):
        source = middle if phase == 0 else branch
        return pltpu.make_async_copy(
            source.at[chunk_span(c, rows)], row_buf.at[c % 2], row_sem.at[c % 2]
        )

    start(in_copies(0, 0))
    gate_tiles = WeightTiles(wg, vg, wsem.at[0], 1, TILE)
    up_tiles = WeightTiles(wu, vu, wsem.at[1], 1, TILE)
    down_tiles = WeightTiles(wd, vd, wsem.at[2], 1, TILE)
    for tile in range(gate_tiles.count):
        gate_tiles.copy(tile).start()
        up_tiles.copy(tile).start()
    down_tiles.start()
    row_copy(0, 0).start()
    stage_barrier(me, n, at, chips)

    scatter = LineScatter(n, me, rows, part, recv, rs_send_sem, rs_recv_sem)
    gathers = [
        make_gather(n, me, rows, own, full, ag_send_sem, ag_recv_sem, local_sem)
        for full in (dm_full, da_full)
    ]

    def hidden_copies(c):
        return [
            pltpu.make_async_copy(
                hidden_buf.at[c % 2, pl.ds(j * rows, rows)],
                hidden_out.at[j, chunk_span(c, rows)],
                hidden_sem.at[c % 2, j],
            )
            for j in range(n)
        ]

    def forward(c):
        here = pl.ds(c * n * rows, n * rows)
        slot = c % 2
        wait(in_copies(0, c))
        if c + 1 < CHUNKS:
            start(in_copies(0, c + 1))
        if c >= 2:
            wait(hidden_copies(c - 2))

        @pl.loop(0, hidden_width // TILE)
        def _(tile):
            if c == 0:
                gate_tiles.copy(tile).wait()
                up_tiles.copy(tile).wait()
            cols = pl.ds(pl.multiple_of(tile * TILE, TILE), TILE)
            gate = plain_dot(in_buf[slot], vg[:, cols])
            up = plain_dot(in_buf[slot], vu[:, cols])
            gate_all[here, cols] = gate.astype(BF)
            up_all[here, cols] = up.astype(BF)
            hidden_buf[slot, :, cols] = (gate * jax.nn.sigmoid(gate) * up).astype(BF)

        start(hidden_copies(c))

        @pl.loop(0, width // TILE)
        def _(tile):
            if c == 0:
                down_tiles.copy(tile).wait()
            cols = pl.ds(pl.multiple_of(tile * TILE, TILE), TILE)
            part[c, :, cols] = plain_dot(hidden_buf[slot], vd[:, cols]).astype(BF)

    def backward(c):
        here = pl.ds(c * n * rows, n * rows)
        scatter.drain(c)
        gathers[0].drain_sends(c)
        wait(in_copies(1, c))

        @pl.loop(0, hidden_width // TILE)
        def _(tile):
            cols = pl.ds(pl.multiple_of(tile * TILE, TILE), TILE)
            hidden_grad = outer_dot(in_buf[c % 2], vd[cols, :])
            gate = gate_all[here, cols].astype(F32)
            up = up_all[here, cols].astype(F32)
            sigmoid = jax.nn.sigmoid(gate)
            gate_all[here, cols] = (
                hidden_grad * up * sigmoid * (1.0 + gate * (1.0 - sigmoid))
            ).astype(BF)
            up_all[here, cols] = (hidden_grad * gate * sigmoid).astype(BF)

        @pl.loop(0, width // TILE)
        def _(tile):
            cols = pl.ds(pl.multiple_of(tile * TILE, TILE), TILE)
            part[c, :, cols] = (
                outer_dot(gate_all[here], vg[cols, :]) + outer_dot(up_all[here], vu[cols, :])
            ).astype(BF)

        if c + 1 == CHUNKS:
            start(h_copies(0))
            signal_partners(ready, at, chips)

    def mg_copy(c):
        return pltpu.make_async_copy(
            mg_buf.at[c % 2], middle_grad.at[chunk_span(c, rows)], mg_sem.at[c % 2]
        )

    def next_row_copy(phase, c):
        if c + 1 < CHUNKS:
            row_copy(phase, c + 1).start()
        elif phase == 0:
            row_copy(1, 0).start()

    def forward_rows(c):
        scatter.total(c, total)
        span = chunk_span(c, rows)
        row_copy(0, c).wait()
        next_row_copy(0, c)
        value = total[...]
        inverse = inverse_rms(value)
        output[span] = (row_buf[c % 2] + value * inverse * mlp_scale[...]).astype(BF)
        upstream = upstream_in[span].astype(F32) * row_valid[span]
        grad, gain = norm_back(value, inverse, mlp_scale[...], upstream)
        own[c] = grad.astype(BF)
        mlp_gain[...] = gain if c == 0 else mlp_gain[...] + gain

    def backward_rows(c):
        scatter.total(c, total)
        span = chunk_span(c, rows)
        row_copy(1, c).wait()
        next_row_copy(1, c)
        upstream = upstream_in[span].astype(F32) * row_valid[span] + total[...]
        if c >= 2:
            mg_copy(c - 2).wait()
        mg_buf[c % 2] = upstream
        mg_copy(c).start()
        value = row_buf[c % 2]
        grad, gain = norm_back(value, inverse_rms(value), attn_scale[...], upstream)
        own[c] = grad.astype(BF)
        attn_gain[...] = gain if c == 0 else attn_gain[...] + gain

    block_width = pl.ds(0, hidden_width)

    def slot_at(index):
        for ref in (vg, vu, vd):
            count = ref.shape[0] // part_width
            if index < count:
                return ref.at[pl.ds(index * part_width, part_width), block_width]
            index -= count
        return extra.at[index]

    reduces = []
    for which, out in enumerate((gate_out, up_out)):
        first = chips + 3 * chips * which
        views = (
            lambda r: slot_at(r),
            lambda r, first=first: slot_at(first + r),
            lambda r, first=first: slot_at(first + chips + r),
            lambda r, first=first: slot_at(first + 2 * chips + r - 1),
        )
        reduces.append(
            PlaneReduce(at, chips, part_width, views, plane[4 * which : 4 * which + 4], out)
        )
    order = relative_order(chips)
    jobs = [
        (which, same_core, r)
        for which in range(2)
        for same_core in (False, True)
        for r in order
    ]

    def h_copies(index):
        which, same_core, r = jobs[index]
        first = reduces[which].owner(r, same_core) * part_width
        cols = pl.ds(pl.multiple_of(first, part_width), part_width)
        return [
            pltpu.make_async_copy(
                h_full.at[j, :, cols], h_buf.at[index % 2, j], h_sem.at[index % 2, j]
            )
            for j in range(n)
        ]

    def weight_block(index):
        which, same_core, r = jobs[index]
        reduce = reduces[which]
        grad = (gate_all, up_all)[which]
        if index == 0:
            pl.semaphore_wait(ready, 1 + len(bits_of(chips - 1)))
        wait(h_copies(index))
        if index + 1 < len(jobs):
            start(h_copies(index + 1))
        if same_core:
            reduce.core_copy(r).wait_recv()
        elif which == 1:
            reduces[0].drain_core(r)
        left = jnp.concatenate(
            [
                h_buf[index % 2, j, c * rows : (c + 1) * rows]
                for c in range(CHUNKS)
                for j in range(n)
            ],
            axis=0,
        )

        @pl.loop(0, hidden_width // TILE)
        def _(tile):
            cols = pl.ds(pl.multiple_of(tile * TILE, TILE), TILE)
            block = inner_dot(left, grad[:, cols])
            if not same_core:
                reduce.core_send(r)[:, cols] = block.astype(BF)
            else:
                block = block + reduce.core_recv(r)[:, cols].astype(F32)
                if r > 0:
                    reduce.held(r)[:, cols] = block.astype(BF)
                else:
                    reduce.out[:, cols] = block

        if not same_core:
            reduce.core_copy(r).start()
        elif r > 0:
            for half in range(2):
                if not reduce.before(r, half):
                    reduce.push(r, half)

    work = []
    for index, (which, same_core, r) in enumerate(jobs):
        work.append(functools.partial(weight_block, index))
        if same_core and r == order[-1]:
            for late in order:
                for half in range(2):
                    if late > 0 and reduces[which].before(late, half):
                        work.append(functools.partial(reduces[which].push, late, half))
    pending = iter(work)

    last_step = 2 * n - 2
    events = sorted(
        (max(PERIOD, last_step + 1) * phase + step + STAGGER * c - (0.5 if step == 0 else 0), phase, c, step)
        for phase in range(2)
        for c in range(CHUNKS)
        for step in range(last_step + 1)
    )
    filling = False
    for _, phase, c, step in events:
        gather = gathers[phase]
        if step == 0:
            (forward, backward)[phase](c)
            filling = filling or (phase == 1 and c + 1 == CHUNKS)
        if step < n - 1:
            scatter.edge(c, step)
            if step > 0:
                scatter.step(c, step)
        elif step == n - 1:
            (forward_rows, backward_rows)[phase](c)
            gather.step(c, 1)
        elif step < last_step:
            gather.step(c, step - n + 2)
        else:
            gather.last(c)
            if phase == 0:
                gather.local_copy(c).wait()
                start(in_copies(1, c))
        if filling:
            for _ in range(FILL):
                job = next(pending, None)
                if job is not None:
                    job()
    for job in pending:
        job()
    for c in range(CHUNKS):
        scatter.drain(c)
        gathers[1].drain(c)
    for reduce in reduces:
        reduce.finish()
        reduce.drain()
    for r in range(chips):
        reduces[1].drain_core(r)
    for c in range(max(CHUNKS - 2, 0), CHUNKS):
        mg_copy(c).wait()
        wait(hidden_copies(c))


def mlp(n, n_dp, h_full, wg, wu, wd, middle, branch, out_grad, row_valid, mlp_scale, attn_scale):
    row_count, width = branch.shape
    hidden_width = wg.shape[1]
    rows = row_count // CHUNKS
    size = n * row_count
    chips = n_dp // 2
    part_width = width // n_dp
    block = (part_width, hidden_width)
    most = max(width, hidden_width) // TILE
    slots = (2 * width + hidden_width) // part_width
    extra = 7 * chips - 1 - slots
    return pl.pallas_call(
        functools.partial(mlp_kernel, n, n_dp, rows),
        out_shape=(
            jax.ShapeDtypeStruct((row_count, width), BF),
            jax.ShapeDtypeStruct((n, row_count, width), BF),
            jax.ShapeDtypeStruct((n, row_count, hidden_width), BF),
            jax.ShapeDtypeStruct((1, width), F32),
            jax.ShapeDtypeStruct((row_count, width), F32),
            jax.ShapeDtypeStruct((n, row_count, width), BF),
            jax.ShapeDtypeStruct((1, width), F32),
            jax.ShapeDtypeStruct(block, F32),
            jax.ShapeDtypeStruct(block, F32),
        ),
        in_specs=[HBM] * 6 + [VMEM] * 4,
        out_specs=(VMEM, HBM, HBM, VMEM, HBM, HBM, VMEM, VMEM, VMEM),
        scratch_shapes=scatter_scratch(n, rows, width)
        + gather_scratch(n, rows, width)
        + [
            pltpu.VMEM(wg.shape, BF),
            pltpu.VMEM(wu.shape, BF),
            pltpu.VMEM(wd.shape, BF),
            pltpu.SemaphoreType.DMA((3, most)),
            pltpu.VMEM((2, n * rows, width), BF),
            pltpu.SemaphoreType.DMA((2, n)),
            pltpu.VMEM((size, hidden_width), BF),
            pltpu.VMEM((size, hidden_width), BF),
            pltpu.VMEM((2, n * rows, hidden_width), BF),
            pltpu.SemaphoreType.DMA((2, n)),
            pltpu.VMEM((2, rows, width), F32),
            pltpu.SemaphoreType.DMA((2,)),
            pltpu.VMEM((2, rows, width), F32),
            pltpu.SemaphoreType.DMA((2,)),
            pltpu.VMEM((2, n, row_count, part_width), BF),
            pltpu.SemaphoreType.DMA((2, n)),
            pltpu.VMEM((extra,) + block if extra > 0 else (1, 16, 128), BF),
            pltpu.SemaphoreType.REGULAR,
        ]
        + plane_sems(chips) * 2,
        compiler_params=pltpu.CompilerParams(
            collective_id=2, has_side_effects=True, vmem_limit_bytes=63 * MIB
        ),
        name="mlp",
        cost_estimate=cost(260),
    )(h_full, wg, wu, wd, middle, branch, out_grad, row_valid, mlp_scale, attn_scale)


def last_grads_kernel(
    n, n_dp, rows, grads, weight, base, inputs, att, da, gains,
    input_grad, qkv_out, out_out, gain_out,
    part, recv, rs_send_sem, rs_recv_sem, total, packed,
    x_buf, da_buf, load_sem,
    send_qkv, recv_qkv, held_qkv, message_qkv, send_out, recv_out, held_out, message_out,
    gain_recv, gain_send_sem, gain_recv_sem, mp_recv, mp_send_sem, mp_recv_sem, *plane,
):
    me, at = lax.axis_index("mp"), lax.axis_index("dp")
    entered = peer_barrier((("mp", me, n), ("dp", at, n_dp)))
    width = weight.shape[0]
    block_rows = rows * CHUNKS
    local_width = att.shape[1]
    chips = n_dp // 2
    part_width = width // n_dp
    order = relative_order(chips)
    jobs = [(same_core, r) for same_core in (False, True) for r in order]

    def views(send, recv, held, message):
        return (
            lambda r: send.at[r],
            lambda r: recv.at[r],
            lambda r: held.at[r - 1],
            lambda r: message.at[r - 1],
        )

    by_qkv = PlaneReduce(
        at, chips, part_width, views(send_qkv, recv_qkv, held_qkv, message_qkv), plane[:4], qkv_out
    )
    by_out = PlaneReduce(
        at, chips, local_width, views(send_out, recv_out, held_out, message_out), plane[4:], out_out
    )

    def loads(k):
        same_core, r = jobs[k]
        first = by_qkv.owner(r, same_core) * part_width
        cols = pl.ds(pl.multiple_of(first, part_width), part_width)
        return [
            pltpu.make_async_copy(inputs.at[:, cols], x_buf.at[k % 2], load_sem.at[k % 2, 0]),
            pltpu.make_async_copy(da.at[:, cols], da_buf.at[k % 2], load_sem.at[k % 2, 1]),
        ]

    for copy in loads(0):
        copy.start()

    def compute(c):
        for j in range(n):
            packed[j * rows : (j + 1) * rows] = grads[
                j * block_rows + c * rows : j * block_rows + (c + 1) * rows
            ]

        @pl.loop(0, width // TILE)
        def _(tile):
            cols = pl.ds(pl.multiple_of(tile * TILE, TILE), TILE)
            part[c, :, cols] = outer_dot(packed[...], weight[cols, :]).astype(BF)

    scatter = LineScatter(n, me, rows, part, recv, rs_send_sem, rs_recv_sem)

    def row_work(c):
        scatter.total(c, total)
        span = chunk_span(c, rows)
        input_grad[span] = base[span] + total[...]

    def weight_block(k):
        same_core, r = jobs[k]
        slot = k % 2
        for copy in loads(k):
            copy.wait()
        if k + 1 < len(jobs):
            for copy in loads(k + 1):
                copy.start()
        if same_core:
            by_qkv.core_copy(r).wait_recv()
            by_out.core_copy(r).wait_recv()

        def keep(reduce, block, cols):
            if not same_core:
                reduce.core_send(r)[:, cols] = block.astype(BF)
                return
            block = block + reduce.core_recv(r)[:, cols].astype(F32)
            if r > 0:
                reduce.held(r)[:, cols] = block.astype(BF)
            else:
                reduce.out[:, cols] = block

        @pl.loop(0, 3)
        def _(tile):
            cols = pl.ds(pl.multiple_of(tile * local_width, local_width), local_width)
            keep(by_qkv, inner_dot(x_buf[slot], grads[:, cols]), cols)

        keep(by_out, inner_dot(att[...], da_buf[slot]), slice(None))
        for reduce in (by_qkv, by_out):
            if not same_core:
                reduce.core_copy(r).start()
            elif r > 0:
                for half in range(2):
                    if not reduce.before(r, half):
                        reduce.push(r, half)

    gain_copies = exchange(
        "dp", at, n_dp, lambda peer: gains.at[peer], gain_recv, gain_send_sem, gain_recv_sem
    )
    mp_copies = exchange("mp", me, n, lambda peer: gain_out, mp_recv, mp_send_sem, mp_recv_sem)
    line = iter([(step, c) for c in range(CHUNKS) for step in range(1, n)])

    def line_steps(count):
        for _ in range(count):
            step, c = next(line, (None, None))
            if step is None:
                return
            if step < n - 1:
                scatter.step(c, step)
            else:
                row_work(c)

    def send_edges(c):
        for step in range(n - 1):
            scatter.edge(c, step)

    compute(0)
    entered()
    send_edges(0)
    for copy in gain_copies:
        copy.start()
    blocks = iter(range(len(jobs)))
    for c in range(1, CHUNKS):
        weight_block(next(blocks))
        compute(c)
        send_edges(c)
    for k in blocks:
        weight_block(k)
        line_steps(2)
    late = [(r, half) for r in order for half in range(2) if r > 0 and by_qkv.before(r, half)]
    for r, half in late:
        for reduce in (by_qkv, by_out):
            reduce.push(r, half)
        line_steps(1)
    gain_out[...] = gains[at]
    for shift, copy in enumerate(gain_copies, 1):
        copy.wait_recv()
        gain_out[...] += gain_recv[shift - 1]
    for copy in mp_copies:
        copy.start()
    line_steps(n * CHUNKS)
    for reduce in (by_qkv, by_out):
        reduce.finish()
    for copy in mp_copies:
        copy.wait_recv()
        copy.wait_send()
    lanes = lax.broadcasted_iota(jnp.int32, gain_out.shape, 1)
    shared = gain_out[...]
    for shift in range(1, n):
        shared = shared + mp_recv[shift - 1]
    gain_out[...] = jnp.where(lanes < 2 * part_width, shared, gain_out[...])
    for copy in gain_copies:
        copy.wait_send()
    for c in range(CHUNKS):
        scatter.drain(c)
    for reduce in (by_qkv, by_out):
        for r in range(chips):
            reduce.drain_core(r)
        reduce.drain()


def last_grads(n, n_dp, grads, weight, base, inputs, attended, da_full, gains):
    row_count, width = base.shape
    rows = row_count // CHUNKS
    size, local_width = attended.shape
    part_width = width // n_dp
    chips = n_dp // 2
    qkv_block = (part_width, 3 * local_width)
    out_block = (local_width, part_width)
    gain_block = gains.shape[1:]
    return pl.pallas_call(
        functools.partial(last_grads_kernel, n, n_dp, rows),
        out_shape=(
            jax.ShapeDtypeStruct((row_count, width), F32),
            jax.ShapeDtypeStruct(qkv_block, F32),
            jax.ShapeDtypeStruct(out_block, F32),
            jax.ShapeDtypeStruct(gain_block, F32),
        ),
        in_specs=[VMEM, VMEM, VMEM, HBM, VMEM, HBM, VMEM],
        out_specs=(VMEM,) * 4,
        scratch_shapes=scatter_scratch(n, rows, width)
        + [
            pltpu.VMEM((n * rows, 3 * local_width), BF),
            pltpu.VMEM((2, size, part_width), BF),
            pltpu.VMEM((2, size, part_width), BF),
            pltpu.SemaphoreType.DMA((2, 2)),
        ]
        + [
            pltpu.VMEM((count,) + block, BF)
            for block in (qkv_block, out_block)
            for count in (chips, chips, chips - 1, chips - 1)
        ]
        + [pltpu.VMEM((n_dp - 1,) + gain_block, F32)]
        + [pltpu.SemaphoreType.DMA((n_dp - 1,))] * 2
        + [pltpu.VMEM((n - 1,) + gain_block, F32)]
        + [pltpu.SemaphoreType.DMA((n - 1,))] * 2
        + plane_sems(chips) * 2,
        compiler_params=pltpu.CompilerParams(
            collective_id=4, has_side_effects=True, vmem_limit_bytes=60 * MIB
        ),
        name="last_grads",
        cost_estimate=cost(80),
    )(grads, weight, base, inputs, attended, da_full, gains)


def turn(values, cos, sin):
    return values * cos + pltpu.roll(values, values.shape[1] // 2, 1) * sin


def turn_back(values, cos, sin):
    return values * cos + pltpu.roll(values * sin, values.shape[1] // 2, 1)


def allowed_keys(starts, first_row, rows, key_end):
    places = first_row + lax.broadcasted_iota(jnp.int32, (rows, key_end), 0)
    keys = lax.broadcasted_iota(jnp.int32, (rows, key_end), 1)
    return (keys <= places) & (keys >= starts)


def columns_to_rows(first, second):
    lanes = lax.broadcasted_iota(jnp.int32, (first.shape[0], 128), 1)
    return jnp.transpose(jnp.where(lanes == 0, first, second))[:8]


def sum_columns(n, me, first, second, entered, held, recv, turned, send_sem, recv_sem):
    held[...] = columns_to_rows(first, second)
    copies = exchange("mp", me, n, lambda peer: held, recv, send_sem, recv_sem)
    entered()
    for copy in copies:
        copy.start()
    total = held[...]
    for shift, copy in enumerate(copies, 1):
        copy.wait_recv()
        total = total + recv[shift - 1]
    for copy in copies:
        copy.wait_send()
    turned[...] = jnp.zeros_like(turned)
    turned[:8] = total
    back = jnp.transpose(turned[...])
    return back[:, 0:1], back[:, 1:2]


def sum_scratch(n, size):
    return [
        pltpu.VMEM((8, size), F32),
        pltpu.VMEM((n - 1, 8, size), F32),
        pltpu.VMEM((128, size), F32),
        pltpu.SemaphoreType.DMA((n - 1,)),
        pltpu.SemaphoreType.DMA((n - 1,)),
    ]


def attention_kernel(
    n, heads, model_width, qkv, q_gain, k_gain, cos, sin, starts,
    out, q_low, k_low, v_low, log_total, q_inv, k_inv, *sums,
):
    me = lax.axis_index("mp")
    entered = peer_barrier((("mp", me, n),))
    size = qkv.shape[0]
    width = qkv.shape[1] // 3
    head = width // heads
    score_scale = 1.0 / math.sqrt(head)

    def squares(first):
        return jnp.sum(jnp.square(qkv[:, first : first + width]), axis=1, keepdims=True)

    q_sum, k_sum = sum_columns(n, me, squares(0), squares(width), entered, *sums)
    q_inv[...] = lax.rsqrt(q_sum / model_width + EPS)
    k_inv[...] = lax.rsqrt(k_sum / model_width + EPS)
    rows = min(QUERY_ROWS, size)

    @pl.loop(0, heads)
    def _(h):
        def cols(first):
            return pl.ds(pl.multiple_of(first + h * head, head), head)

        here = cols(0)
        q_low[:, here] = turn(
            qkv[:, here] * q_inv[...] * q_gain[:, here], cos[...], sin[...]
        ).astype(BF)
        k_low[:, here] = turn(
            qkv[:, cols(width)] * k_inv[...] * k_gain[:, here], cos[...], sin[...]
        ).astype(BF)
        v_low[:, here] = qkv[:, cols(2 * width)].astype(BF)
        for first in range(0, size, rows):
            end = first + rows
            span = slice(first, end)
            scores = outer_dot(q_low[span, here], k_low[:end, here]) * score_scale
            scores = jnp.where(allowed_keys(starts[span], first, rows, end), scores, MASKED)
            row_max = jnp.max(scores, axis=1, keepdims=True)
            exponents = jnp.exp(scores - row_max)
            row_total = jnp.sum(exponents, axis=1, keepdims=True)
            probs = (exponents * (1.0 / row_total)).astype(BF)
            out[span, here] = plain_dot(probs, v_low[:end, here]).astype(BF)
            log_total[h, span] = row_max + jnp.log(row_total)


def attention(n, heads, model_width, qkv_raw, q_gain, k_gain, cos, sin, starts):
    size = qkv_raw.shape[0]
    low = jax.ShapeDtypeStruct((size, qkv_raw.shape[1] // 3), BF)
    column = jax.ShapeDtypeStruct((size, 1), F32)
    return pl.pallas_call(
        functools.partial(attention_kernel, n, heads, model_width),
        out_shape=(low,) * 4 + (jax.ShapeDtypeStruct((heads, size, 1), F32), column, column),
        in_specs=[VMEM] * 6,
        out_specs=(VMEM,) * 7,
        scratch_shapes=sum_scratch(n, size),
        compiler_params=pltpu.CompilerParams(
            collective_id=5, has_side_effects=True, vmem_limit_bytes=56 * MIB
        ),
        name="attention",
        cost_estimate=cost(25),
    )(qkv_raw, q_gain, k_gain, cos, sin, starts)


def attention_back_kernel(
    n, heads, model_width, qkv, q_low, k_low, v_low, out_grad, log_total,
    q_inv, k_inv, q_gain, k_gain, cos, sin, starts,
    grads, q_gain_grad, k_gain_grad,
    q_weighted, k_weighted, q_grad, k_sum, v_sum, q_dots, k_dots, *sums,
):
    me = lax.axis_index("mp")
    entered = peer_barrier((("mp", me, n),))
    size = qkv.shape[0]
    width = qkv.shape[1] // 3
    head = width // heads
    score_scale = 1.0 / math.sqrt(head)
    rows = min(QUERY_ROWS, size)
    q_dots[...] = jnp.zeros_like(q_dots)
    k_dots[...] = jnp.zeros_like(k_dots)

    @pl.loop(0, heads)
    def _(h):
        def cols(first):
            return pl.ds(pl.multiple_of(first + h * head, head), head)

        here = cols(0)
        for first in reversed(range(0, size, rows)):
            end = first + rows
            span = slice(first, end)
            scores = outer_dot(q_low[span, here], k_low[:end, here]) * score_scale
            scores = jnp.where(allowed_keys(starts[span], first, rows, end), scores, MASKED)
            probs = jnp.exp(scores - log_total[h, span])
            prob_grad = outer_dot(out_grad[span, here], v_low[:end, here])
            probs_low = probs.astype(BF)
            weighted = probs * prob_grad
            score_grad = (
                weighted - probs * jnp.sum(weighted, axis=1, keepdims=True)
            ).astype(BF)
            q_grad[span] = plain_dot(score_grad, k_low[:end, here]) * score_scale
            k_extra = inner_dot(score_grad, q_low[span, here])
            v_extra = inner_dot(probs_low, out_grad[span, here])
            if end == size:
                k_sum[...] = k_extra
                v_sum[...] = v_extra
            else:
                k_sum[:end] += k_extra
                v_sum[:end] += v_extra
        for first, inv, gain, grad, factor, weighted_out, dots, gain_grad in (
            (0, q_inv, q_gain, q_grad, None, q_weighted, q_dots, q_gain_grad),
            (width, k_inv, k_gain, k_sum, score_scale, k_weighted, k_dots, k_gain_grad),
        ):
            raw = qkv[:, cols(first)]
            value = grad[...] if factor is None else grad[...] * factor
            normed = turn_back(value, cos[...], sin[...])
            weighted = normed * gain[:, here]
            weighted_out[:, here] = weighted
            gain_grad[:, here] = jnp.sum(normed * raw * inv[...], axis=0, keepdims=True)
            dots[...] += jnp.sum(weighted * raw, axis=1, keepdims=True)
        grads[:, cols(2 * width)] = v_sum[...].astype(BF)

    q_total, k_total = sum_columns(n, me, q_dots[...], k_dots[...], entered, *sums)
    for first, inv, weighted, dots in (
        (0, q_inv, q_weighted, q_total),
        (width, k_inv, k_weighted, k_total),
    ):
        scale = inv[...]
        factor = scale * scale * scale * (dots / model_width)
        grads[:, first : first + width] = (
            scale * weighted[...] - qkv[:, first : first + width] * factor
        ).astype(BF)


def attention_back(
    n, heads, model_width, qkv_raw, q_low, k_low, v_low, out_grad, log_total, q_inv, k_inv,
    q_gain, k_gain, cos, sin, starts,
):
    size, width = q_low.shape
    head = width // heads
    gains = jax.ShapeDtypeStruct((1, width), F32)
    return pl.pallas_call(
        functools.partial(attention_back_kernel, n, heads, model_width),
        out_shape=(jax.ShapeDtypeStruct((size, 3 * width), BF), gains, gains),
        in_specs=[VMEM] * 13,
        out_specs=(VMEM,) * 3,
        scratch_shapes=[pltpu.VMEM((size, width), F32)] * 2
        + [pltpu.VMEM((size, head), F32)] * 3
        + [pltpu.VMEM((size, 1), F32)] * 2
        + sum_scratch(n, size),
        compiler_params=pltpu.CompilerParams(
            collective_id=6, has_side_effects=True, vmem_limit_bytes=56 * MIB
        ),
        name="attention_back",
        cost_estimate=cost(30),
    )(
        qkv_raw, q_low, k_low, v_low, out_grad, log_total, q_inv, k_inv, q_gain, k_gain,
        cos, sin, starts,
    )


def local(
    layer_input,
    query_weight,
    key_weight,
    value_weight,
    out_weight,
    gate_weight,
    up_weight,
    down_weight,
    query_gain,
    key_gain,
    attn_gain,
    mlp_gain,
    seq_lens,
    out_grad,
):
    n = lax.axis_size("mp")
    n_dp = lax.axis_size("dp")
    me = lax.axis_index("mp")
    row_count, model_width = layer_input.shape
    group_size = row_count * n
    local_heads, gain_part = query_gain.shape
    head_size = gain_part * n_dp
    local_width = local_heads * head_size

    full_qkv = lax.all_gather(
        jnp.concatenate([query_weight, key_weight, value_weight], axis=1), "dp", axis=0, tiled=True
    )
    full_out = lax.all_gather(out_weight, "dp", axis=1, tiled=True)
    full_gate = lax.all_gather(gate_weight, "dp", axis=0, tiled=True)
    full_up = lax.all_gather(up_weight, "dp", axis=0, tiled=True)
    full_down = lax.all_gather(down_weight, "dp", axis=1, tiled=True)
    head_part = local_heads * gain_part
    width_part = attn_gain.shape[0]
    own_gains = jnp.concatenate(
        [attn_gain, mlp_gain, query_gain.reshape(head_part), key_gain.reshape(head_part)]
    ).astype(F32)[None]
    inputs_full, gain_parts = gather_rows(n, n_dp, layer_input, own_gains)
    inputs_full = inputs_full.reshape(group_size, model_width)
    gain_parts = gain_parts[:, 0]

    def head_gain(first):
        piece = gain_parts[:, first : first + head_part].reshape(n_dp, local_heads, gain_part)
        return piece.transpose(1, 0, 2).reshape(1, local_width)

    query_scale = head_gain(2 * width_part)
    key_scale = head_gain(2 * width_part + head_part)
    attn_scale = gain_parts[:, :width_part].reshape(1, model_width)
    mlp_scale = gain_parts[:, width_part : 2 * width_part].reshape(1, model_width)

    starts, positions, valid = layout(seq_lens[0], group_size)
    starts = starts[:, None]
    cos_table, sin_table = rotary_tables(positions, head_size)
    row_valid = lax.dynamic_slice_in_dim(valid, me * row_count, row_count, 0).astype(F32)[:, None]

    qkv_raw = plain_dot(inputs_full, full_qkv)
    attended, query_low, key_low, value_low, log_total, query_inv, key_inv = attention(
        n, local_heads, model_width, qkv_raw, query_scale, key_scale, cos_table, sin_table, starts
    )
    branch, middle, middle_full = attn_out(n, attended, full_out, layer_input, attn_scale)
    (
        layer_output, mlp_grad_full, hidden, mlp_gain_part, middle_grad, branch_full,
        attn_gain_part, grad_gate, grad_up,
    ) = mlp(
        n, n_dp, middle_full, full_gate, full_up, full_down, middle, branch, out_grad, row_valid,
        mlp_scale, attn_scale,
    )

    def flat(rows):
        return rows.reshape(group_size, rows.shape[-1])

    branch_full = flat(branch_full)
    down_part = inner_dot(flat(hidden), flat(mlp_grad_full)).astype(BF)
    branch_full, down_part = lax.optimization_barrier((branch_full, down_part))
    grad_down = lax.psum_scatter(down_part, "dp", scatter_dimension=1, tiled=True)

    mixed_grad = outer_dot(branch_full, full_out).astype(BF)
    qkv_grad, query_gain_part, key_gain_part = attention_back(
        n, local_heads, model_width, qkv_raw, query_low, key_low, value_low, mixed_grad, log_total,
        query_inv, key_inv, query_scale, key_scale, cos_table, sin_table, starts,
    )

    def by_part(row):
        return row.reshape(n_dp, -1)

    def by_head_part(row):
        pieces = row.reshape(local_heads, n_dp, gain_part).transpose(1, 0, 2)
        return pieces.reshape(n_dp, head_part)

    gain_grads = jnp.concatenate(
        [
            by_part(attn_gain_part),
            by_part(mlp_gain_part),
            by_head_part(query_gain_part),
            by_head_part(key_gain_part),
        ],
        axis=1,
    )[:, None]
    input_grad, grad_qkv, grad_out, gain_sums = last_grads(
        n, n_dp, qkv_grad, full_qkv, middle_grad, inputs_full, attended, branch_full, gain_grads
    )
    gain_sums = gain_sums[0]
    heads_at = 2 * width_part
    return (
        layer_output,
        input_grad,
        grad_qkv[:, :local_width],
        grad_qkv[:, local_width : 2 * local_width],
        grad_qkv[:, 2 * local_width :],
        grad_out,
        grad_gate,
        grad_up,
        grad_down.astype(F32),
        gain_sums[heads_at : heads_at + head_part].reshape(local_heads, gain_part),
        gain_sums[heads_at + head_part :].reshape(local_heads, gain_part),
        gain_sums[:width_part],
        gain_sums[width_part:heads_at],
    )


def solution(mesh):
    return jax.shard_map(
        local,
        mesh=mesh,
        in_specs=(
            P(("dp", "mp"), None),
            P("dp", "mp"),
            P("dp", "mp"),
            P("dp", "mp"),
            P("mp", "dp"),
            P("dp", "mp"),
            P("dp", "mp"),
            P("mp", "dp"),
            P("mp", "dp"),
            P("mp", "dp"),
            P("dp"),
            P("dp"),
            P("dp", None),
            P(("dp", "mp"), None),
        ),
        out_specs=(
            P(("dp", "mp"), None),
            P(("dp", "mp"), None),
            P("dp", "mp"),
            P("dp", "mp"),
            P("dp", "mp"),
            P("mp", "dp"),
            P("dp", "mp"),
            P("dp", "mp"),
            P("mp", "dp"),
            P("mp", "dp"),
            P("mp", "dp"),
            P("dp"),
            P("dp"),
        ),
        check_vma=False,
    )
```

```python
import functools
import math

import jax
import jax.numpy as jnp
from jax import lax
from jax.experimental import pallas as pl
from jax.experimental.pallas import tpu as pltpu
from jax.sharding import PartitionSpec as P

EPS = 1e-06
THETA = 500000.0
MASKED = -1000000000.0
CHUNKS = 4
STAGGER = 2
EDGES = False
FILL = 2
PERIOD = 8
TILE = 512
QUERY_ROWS = 256
BF = jnp.bfloat16
F32 = jnp.float32
MIB = 1 << 20
HBM = pl.BlockSpec(memory_space=pl.ANY)
VMEM = pl.BlockSpec(memory_space=pltpu.VMEM)


def cost(micros):
    return pl.CostEstimate(
        flops=micros * 1_000_000_000, bytes_accessed=micros * 3_000_000, transcendentals=0
    )


def plain_dot(former, latter):
    return jnp.dot(former, latter, preferred_element_type=F32)


def inner_dot(former, latter):
    return lax.dot_general(
        former, latter, (((0,), (0,)), ((), ())), preferred_element_type=F32
    )


def outer_dot(former, latter):
    return lax.dot_general(
        former, latter, (((1,), (1,)), ((), ())), preferred_element_type=F32
    )


def layout(lengths, group_size):
    slot_count = lengths.shape[0]
    seq_ends = jnp.cumsum(lengths, dtype=jnp.int32)
    starts = seq_ends - lengths
    places = jnp.arange(group_size, dtype=jnp.int32)
    slot_ids = jnp.arange(slot_count, dtype=jnp.int32)
    segment = jnp.sum(
        (places[:, None] >= seq_ends[None, :]).astype(jnp.int32), axis=1, dtype=jnp.int32
    )
    chosen = (segment[:, None] == slot_ids[None, :]).astype(jnp.int32)
    padded = (segment == slot_count).astype(jnp.int32)
    begins = (
        jnp.sum(chosen * starts[None, :], axis=1, dtype=jnp.int32)
        + padded * seq_ends[slot_count - 1]
    )
    return (begins, places - begins, places < seq_ends[slot_count - 1])


def rotary_tables(positions, head_size):
    half_dim = head_size // 2
    frequency = jnp.exp(jnp.arange(half_dim, dtype=F32) * (-2.0 * math.log(THETA) / head_size))
    angles = positions.astype(F32)[:, None] * frequency[None, :]
    cos_half, sin_half = jnp.cos(angles), jnp.sin(angles)
    return (
        jnp.concatenate([cos_half, cos_half], axis=1),
        jnp.concatenate([-sin_half, sin_half], axis=1),
    )


def neighbour_barrier(me, n):
    barrier = pltpu.get_barrier_semaphore()

    @pl.when(me > 0)
    def _():
        pl.semaphore_signal(barrier, inc=1, device_id={"mp": me - 1})

    @pl.when(me < n - 1)
    def _():
        pl.semaphore_signal(barrier, inc=1, device_id={"mp": me + 1})

    pl.semaphore_wait(barrier, jnp.minimum(me, 1) + jnp.minimum(n - 1 - me, 1))


class LineGather:
    def __init__(self, n, me, own, full, send_sem, recv_sem, local_sem):
        self.n, self.me, self.own, self.full = n, me, own, full
        self.send_sem, self.recv_sem, self.local_sem = send_sem, recv_sem, local_sem

    def local_copy(self, c):
        return pltpu.make_async_copy(self.own(c), self.full(self.me, c), self.local_sem.at[c])

    def copy(self, c, step, way, block, src):
        return pltpu.make_async_remote_copy(
            src_ref=src,
            dst_ref=self.full(block, c),
            send_sem=self.send_sem.at[c, step - 1, way],
            recv_sem=self.recv_sem.at[c, step - 1, way],
            device_id={"mp": self.me + (1 if way == 0 else -1)},
        )

    def sides(self):
        return ((0, self.me), (1, self.n - 1 - self.me))

    def block_at(self, way, step):
        return self.me - step if way == 0 else self.me + step

    def step(self, c, step):
        n = self.n
        if step == 1:
            self.local_copy(c).start()
        for way, place in self.sides():
            if step > 1:

                @pl.when(place >= step - 1)
                def _(way=way):
                    block = self.block_at(way, step - 1)
                    self.copy(c, step - 1, way, block, self.own(c)).wait_recv()

            @pl.when((place >= step - 1) & (place < n - 1))
            def _(way=way):
                block = self.block_at(way, step - 1)
                src = self.own(c) if step == 1 else self.full(block, c)
                self.copy(c, step, way, block, src).start()

    def last(self, c):
        n = self.n
        for way, place in self.sides():

            @pl.when(place == n - 1)
            def _(way=way):
                block = self.block_at(way, n - 1)
                self.copy(c, n - 1, way, block, self.own(c)).wait_recv()

    def drain(self, c):
        self.local_copy(c).wait()
        self.drain_sends(c)

    def drain_sends(self, c):
        for step in range(1, self.n):
            for way, place in self.sides():

                @pl.when((place >= step - 1) & (place < self.n - 1))
                def _(way=way):
                    self.copy(c, step, way, self.me, self.own(c)).wait_send()


class LineScatter:
    def __init__(self, n, me, rows, part, recv, send_sem, recv_sem):
        self.n, self.me, self.rows = n, me, rows
        self.part, self.recv = part, recv
        self.send_sem, self.recv_sem = send_sem, recv_sem

    def piece(self, c, owner):
        first = pl.multiple_of(owner * self.rows, self.rows)
        return self.part.at[c, pl.ds(first, self.rows)]

    def copy(self, c, step, way, src):
        return pltpu.make_async_remote_copy(
            src_ref=src,
            dst_ref=self.recv.at[c, step, way],
            send_sem=self.send_sem.at[c, step, way],
            recv_sem=self.recv_sem.at[c, step, way],
            device_id={"mp": self.me + (1 if way == 0 else -1)},
        )

    def sides(self):
        return ((0, self.me), (1, self.n - 1 - self.me))

    def owner(self, way, step):
        return self.n - 1 - step + self.me if way == 0 else step - (self.n - 1 - self.me)

    def edge(self, c, step):
        for way, place in self.sides():

            @pl.when(place == 0)
            def _(way=way):
                self.copy(c, step, way, self.piece(c, self.owner(way, step))).start()

    def step(self, c, step):
        for way, place in self.sides():

            @pl.when((place > 0) & (place <= min(step, self.n - 2)))
            def _(way=way):
                piece = self.piece(c, self.owner(way, step))
                self.copy(c, step - 1, way, piece).wait_recv()
                piece[...] = (
                    piece[...].astype(F32) + self.recv[c, step - 1, way].astype(F32)
                ).astype(BF)
                self.copy(c, step, way, piece).start()

    def total(self, c, out):
        n = self.n
        out[...] = self.piece(c, self.me)[...].astype(F32)
        for way, place in self.sides():

            @pl.when(place > 0)
            def _(way=way):
                self.copy(c, n - 2, way, self.recv.at[c, n - 2, way]).wait_recv()
                out[...] += self.recv[c, n - 2, way].astype(F32)

    def drain(self, c):
        n = self.n
        for step in range(n - 1):
            for way, place in self.sides():

                @pl.when(place <= min(step, n - 2))
                def _(way=way):
                    self.copy(c, step, way, self.recv.at[c, step, way]).wait_send()


def run_line(n, chunks, stagger, compute, scatter, row_work, gather, filler=None):
    last_step = 2 * n - 2 if gather is not None else n - 1
    events = sorted(
        (step + stagger * c - (0.5 if step == 0 else 0), c, step)
        for c in range(chunks)
        for step in range(last_step + 1)
    )
    computed = 0
    for _, c, step in events:
        if step == 0:
            compute(c)
            for ahead in range(n - 1 if EDGES else 1):
                scatter.edge(c, ahead)
            computed += 1
        elif step < n - 1:
            if not EDGES:
                scatter.edge(c, step)
            scatter.step(c, step)
        elif step == n - 1:
            row_work(c)
            if gather is not None:
                gather.step(c, 1)
        elif step < 2 * n - 2:
            gather.step(c, step - n + 2)
        else:
            gather.last(c)
        if filler is not None and computed == chunks:
            filler()
    for c in range(chunks):
        scatter.drain(c)
        if gather is not None:
            gather.drain(c)


def flipped(chip, bit):
    return chip + bit - 2 * bit * lax.rem(chip // bit, 2)


def bits_of(number):
    return [1 << k for k in range(number.bit_length()) if number >> k & 1]


def relative_chip(chip, relative):
    for bit in bits_of(relative):
        chip = flipped(chip, bit)
    return chip


def relative_order(chips):
    return sorted(range(chips), key=lambda r: (-len(bits_of(r)), r))


class PlaneReduce:
    def __init__(self, at, chips, rows, views, sems, out):
        self.chip, self.core = at // 2, lax.rem(at, 2)
        self.chips, self.rows, self.out = chips, rows, out
        self.core_send, self.core_recv, self.held, self.message = views
        self.core_send_sem, self.core_recv_sem, self.send_sem, self.recv_sem = sems

    def first_bit(self, relative, half):
        bits = bits_of(relative)
        return bits[0] if half == 0 else bits[-1]

    def before(self, relative, half):
        return [
            r for r in range(1, self.chips) if r - self.first_bit(r, half) == relative
        ]

    def owner(self, relative, same_core):
        return 2 * relative_chip(self.chip, relative) + (
            self.core if same_core else 1 - self.core
        )

    def half_rows(self, half):
        return pl.ds(half * (self.rows // 2), self.rows // 2)

    def core_copy(self, relative):
        return pltpu.make_async_remote_copy(
            src_ref=self.core_send(relative),
            dst_ref=self.core_recv(relative),
            send_sem=self.core_send_sem.at[relative],
            recv_sem=self.core_recv_sem.at[relative],
            device_id={"dp": 2 * self.chip + 1 - self.core},
        )

    def message_copy(self, relative, half):
        span = self.half_rows(half)
        target = flipped(self.chip, self.first_bit(relative, half))
        return pltpu.make_async_remote_copy(
            src_ref=self.held(relative).at[span],
            dst_ref=self.message(relative).at[span],
            send_sem=self.send_sem.at[relative, half],
            recv_sem=self.recv_sem.at[relative, half],
            device_id={"dp": 2 * target + self.core},
        )

    def push(self, relative, half):
        span = self.half_rows(half)
        for r in self.before(relative, half):
            self.message_copy(r, half).wait_recv()
            held = self.held(relative)
            held[span] = (
                held[span].astype(F32) + self.message(r)[span].astype(F32)
            ).astype(BF)
        self.message_copy(relative, half).start()

    def finish(self):
        for half in range(2):
            span = self.half_rows(half)
            for r in self.before(0, half):
                self.message_copy(r, half).wait_recv()
                self.out[span] += self.message(r)[span].astype(F32)

    def drain_core(self, relative):
        self.core_copy(relative).wait_send()

    def drain(self):
        for r in range(1, self.chips):
            for half in range(2):
                self.message_copy(r, half).wait_send()


def plane_sems(chips):
    return [pltpu.SemaphoreType.DMA((chips,))] * 2 + [pltpu.SemaphoreType.DMA((chips, 2))] * 2


def stage_barrier(me, n, at, chips):
    barrier = pltpu.get_barrier_semaphore()

    @pl.when(me > 0)
    def _():
        pl.semaphore_signal(barrier, inc=1, device_id={"mp": me - 1})

    @pl.when(me < n - 1)
    def _():
        pl.semaphore_signal(barrier, inc=1, device_id={"mp": me + 1})

    count = signal_partners(barrier, at, chips)
    pl.semaphore_wait(barrier, count + jnp.minimum(me, 1) + jnp.minimum(n - 1 - me, 1))


def signal_partners(sem, at, chips):
    chip, core = at // 2, lax.rem(at, 2)
    pl.semaphore_signal(sem, inc=1, device_id={"dp": 2 * chip + 1 - core})
    bits = [1 << k for k in range(chips.bit_length() - 1)]
    for bit in bits:
        pl.semaphore_signal(sem, inc=1, device_id={"dp": 2 * flipped(chip, bit) + core})
    return 1 + len(bits)


def inverse_rms(rows):
    return lax.rsqrt(jnp.mean(rows * rows, axis=1, keepdims=True) + EPS)


def norm_back(values, inverse, gain_row, upstream):
    weighted = upstream * gain_row
    mean_term = jnp.mean(weighted * values, axis=1, keepdims=True)
    grad_values = inverse * weighted - values * (inverse * inverse * inverse) * mean_term
    return (grad_values, jnp.sum(upstream * values * inverse, axis=0, keepdims=True))


def scatter_scratch(n, rows, width):
    return [
        pltpu.VMEM((CHUNKS, n * rows, width), BF),
        pltpu.VMEM((CHUNKS, n - 1, 2, rows, width), BF),
        pltpu.SemaphoreType.DMA((CHUNKS, n - 1, 2)),
        pltpu.SemaphoreType.DMA((CHUNKS, n - 1, 2)),
        pltpu.VMEM((rows, width), F32),
    ]


def gather_scratch(n, rows, width):
    return [
        pltpu.VMEM((CHUNKS, rows, width), BF),
        pltpu.SemaphoreType.DMA((CHUNKS, n - 1, 2)),
        pltpu.SemaphoreType.DMA((CHUNKS, n - 1, 2)),
        pltpu.SemaphoreType.DMA((CHUNKS,)),
    ]


def chunk_span(c, rows):
    return pl.ds(c * rows, rows)


def make_gather(n, me, rows, own, full, send_sem, recv_sem, local_sem):
    return LineGather(
        n,
        me,
        lambda c: own.at[c],
        lambda block, c: full.at[block, chunk_span(c, rows)],
        send_sem,
        recv_sem,
        local_sem,
    )


def peer_barrier(axes):
    barrier = pltpu.get_barrier_semaphore()
    count = 0
    for name, index, size in axes:
        for shift in range(1, size):
            pl.semaphore_signal(barrier, inc=1, device_id={name: lax.rem(index + shift, size)})
            count += 1
    return lambda: pl.semaphore_wait(barrier, count)


def exchange(name, index, size, src, recv, send_sem, recv_sem):
    def copy(shift):
        peer = lax.rem(index + shift, size)
        return pltpu.make_async_remote_copy(
            src_ref=src(peer),
            dst_ref=recv.at[shift - 1],
            send_sem=send_sem.at[shift - 1],
            recv_sem=recv_sem.at[shift - 1],
            device_id={name: peer},
        )

    return [copy(shift) for shift in range(1, size)]


class PlaneGather:
    def __init__(self, at, chips, rows, slot, sems):
        self.chip, self.core = at // 2, lax.rem(at, 2)
        self.chips, self.rows, self.slot = chips, rows, slot
        self.core_send_sem, self.core_recv_sem, self.send_sem, self.recv_sem = sems
        self.arrived = set()

    def last_bit(self, relative, half):
        bits = bits_of(relative)
        return bits[-1] if half == 0 else bits[0]

    def place(self, relative, same_core=True):
        return self.slot(
            2 * relative_chip(self.chip, relative) + (self.core if same_core else 1 - self.core)
        )

    def copy(self, relative, half):
        bit = self.last_bit(relative, half)
        view = self.place(relative - bit).at[pl.ds(half * (self.rows // 2), self.rows // 2)]
        return pltpu.make_async_remote_copy(
            src_ref=view,
            dst_ref=view,
            send_sem=self.send_sem.at[relative, half],
            recv_sem=self.recv_sem.at[relative, half],
            device_id={"dp": 2 * flipped(self.chip, bit) + self.core},
        )

    def core_copy(self, relative, same_core):
        view = self.place(relative, same_core)
        return pltpu.make_async_remote_copy(
            src_ref=view,
            dst_ref=view,
            send_sem=self.core_send_sem.at[relative],
            recv_sem=self.core_recv_sem.at[relative],
            device_id={"dp": 2 * self.chip + 1 - self.core},
        )

    def ensure(self, relative, half):
        if relative > 0 and (relative, half) not in self.arrived:
            self.arrived.add((relative, half))
            self.copy(relative, half).wait_recv()

    def send(self, passed_on):
        for count in range(1, self.chips.bit_length()):
            for r in range(1, self.chips):
                for half in range(2):
                    if len(bits_of(r)) == count and (count > 1) == passed_on:
                        self.ensure(r - self.last_bit(r, half), half)
                        self.copy(r, half).start()
        if not passed_on:
            self.core_copy(0, True).start()

    def swap(self, relatives):
        for r in relatives:
            for half in range(2):
                self.ensure(r, half)
            self.core_copy(r, True).start()

    def finish(self):
        for r in range(self.chips):
            self.core_copy(r, False).wait_recv()

    def drain(self):
        for r in range(self.chips):
            self.core_copy(r, True).wait_send()
            for half in range(2):
                if r > 0:
                    self.copy(r, half).wait_send()


def front_kernel(
    n, n_dp, rows, model_width, x, wq, wk, wv, wo, gains,
    full, qkv, full_qkv, full_out, gain_parts, q_inv, k_inv,
    send_sem, recv_sem, local_sem, gain_recv, gain_send_sem, gain_recv_sem,
    vqkv, vout, save_sem, x_buf, x_sem, squares,
    held, sum_recv, turned, sum_send_sem, sum_recv_sem, *plane,
):
    me, at = lax.axis_index("mp"), lax.axis_index("dp")
    peer_barrier((("mp", me, n), ("dp", at, n_dp)))()
    gather = LineGather(
        n,
        me,
        lambda c: x.at[chunk_span(c, rows)],
        lambda index, c: full.at[index, chunk_span(c, rows)],
        send_sem,
        recv_sem,
        local_sem,
    )
    for c in range(CHUNKS):
        gather.step(c, 1)
    chips = n_dp // 2
    part_width, width = wq.shape
    row_count = rows * CHUNKS

    def part(owner):
        return pl.ds(pl.multiple_of(owner * part_width, part_width), part_width)

    by_qkv = PlaneGather(at, chips, part_width, lambda owner: vqkv.at[part(owner)], plane[:4])
    by_out = PlaneGather(at, chips, width, lambda owner: vout.at[:, part(owner)], plane[4:])
    for k, weight in enumerate((wq, wk, wv)):
        vqkv[part(at), k * width : (k + 1) * width] = weight[...]
    by_qkv.send(False)
    vout[:, part(at)] = wo[...]
    by_out.send(False)
    copies = exchange(
        "dp", at, n_dp, lambda peer: gains, gain_recv, gain_send_sem, gain_recv_sem
    )
    for copy in copies:
        copy.start()

    def block(index, source):
        load = pltpu.make_async_copy(source, x_buf, x_sem)
        load.start()
        load.wait()
        here = pl.ds(pl.multiple_of(index * row_count, row_count), row_count)

        @pl.loop(0, 3)
        def _(tile):
            cols = pl.ds(pl.multiple_of(tile * width, width), width)
            value = plain_dot(x_buf[...], vqkv[:, cols])
            qkv[here, cols] = value
            squares[tile] = jnp.sum(value * value, axis=1, keepdims=True)

        held[:, here] = columns_to_rows(squares[0], squares[1])

    def blocks_at(step):
        @pl.loop(0, 2)
        def _(side):
            index = me - step + 2 * step * side

            @pl.when((index >= 0) & (index < n))
            def _():
                block(index, full.at[index])

    saves = [
        pltpu.make_async_copy(vqkv, full_qkv, save_sem.at[0]),
        pltpu.make_async_copy(vout, full_out, save_sem.at[1]),
    ]
    early = [r for r in range(1, chips) if len(bits_of(r)) == 1]
    late = [r for r in range(1, chips) if len(bits_of(r)) > 1]

    def weights_here():
        by_qkv.finish()
        saves[0].start()
        block(me, x)

    hooks = [
        lambda: by_qkv.send(True),
        None,
        None,
        lambda: by_qkv.swap(early),
        lambda: (by_qkv.swap(late), by_out.send(True)),
        lambda: by_out.swap(early + late),
        weights_here,
    ]
    ready = 1
    for step in range(2, n):
        for c in range(CHUNKS):
            gather.step(c, step)
            if hooks:
                hook = hooks.pop(0)
                if hook is not None:
                    hook()
        if not hooks:
            while ready < step:
                blocks_at(ready)
                ready += 1
    for hook in hooks:
        if hook is not None:
            hook()
    while ready < n - 1:
        blocks_at(ready)
        ready += 1
    gain_parts[at] = gains[...]
    for shift, copy in enumerate(copies, 1):
        copy.wait_recv()
        gain_parts[lax.rem(at + n_dp - shift, n_dp)] = gain_recv[shift - 1]
    by_out.finish()
    saves[1].start()
    for c in range(CHUNKS):
        gather.last(c)
    blocks_at(n - 1)
    q_sum, k_sum = sum_held(n, me, held, sum_recv, turned, sum_send_sem, sum_recv_sem)
    q_inv[...] = lax.rsqrt(q_sum / model_width + EPS)
    k_inv[...] = lax.rsqrt(k_sum / model_width + EPS)
    for c in range(CHUNKS):
        gather.drain(c)
    for copy in copies:
        copy.wait_send()
    for gathered in (by_qkv, by_out):
        gathered.drain()
    for copy in saves:
        copy.wait()


def front(n, n_dp, block, wq, wk, wv, wo, gains):
    row_count, model_width = block.shape
    rows = row_count // CHUNKS
    size = n * row_count
    width = wq.shape[1]
    chips = n_dp // 2
    column = jax.ShapeDtypeStruct((size, 1), F32)
    return pl.pallas_call(
        functools.partial(front_kernel, n, n_dp, rows, model_width),
        out_shape=(
            jax.ShapeDtypeStruct((n,) + block.shape, block.dtype),
            jax.ShapeDtypeStruct((size, 3 * width), F32),
            jax.ShapeDtypeStruct((model_width, 3 * width), BF),
            jax.ShapeDtypeStruct((width, model_width), BF),
            jax.ShapeDtypeStruct((n_dp,) + gains.shape, F32),
            column,
            column,
        ),
        in_specs=[HBM] + [VMEM] * 5,
        out_specs=(HBM, VMEM, HBM, HBM, VMEM, VMEM, VMEM),
        scratch_shapes=gather_scratch(n, rows, model_width)[1:]
        + [
            pltpu.VMEM((n_dp - 1,) + gains.shape, F32),
            pltpu.SemaphoreType.DMA((n_dp - 1,)),
            pltpu.SemaphoreType.DMA((n_dp - 1,)),
            pltpu.VMEM((model_width, 3 * width), BF),
            pltpu.VMEM((width, model_width), BF),
            pltpu.SemaphoreType.DMA((2,)),
            pltpu.VMEM((row_count, model_width), BF),
            pltpu.SemaphoreType.DMA,
            pltpu.VMEM((3, row_count, 1), F32),
        ]
        + sum_scratch(n, size)
        + plane_sems(chips) * 2,
        compiler_params=pltpu.CompilerParams(
            collective_id=0, has_side_effects=True, vmem_limit_bytes=48 * MIB
        ),
        name="front",
        cost_estimate=cost(80),
    )(block, wq, wk, wv, wo, gains)


def attn_out_kernel(
    n, rows, att, wo, x, scale, branch, middle, full,
    part, recv, rs_send_sem, rs_recv_sem, total, own, ag_send_sem, ag_recv_sem, local_sem,
    packed,
):
    me = lax.axis_index("mp")
    neighbour_barrier(me, n)
    width = wo.shape[1]
    block_rows = rows * CHUNKS

    def compute(c):
        for j in range(n):
            packed[j * rows : (j + 1) * rows] = att[
                j * block_rows + c * rows : j * block_rows + (c + 1) * rows
            ]

        @pl.loop(0, width // TILE)
        def _(tile):
            cols = pl.ds(pl.multiple_of(tile * TILE, TILE), TILE)
            part[c, :, cols] = plain_dot(packed[...], wo[:, cols]).astype(BF)

    scatter = LineScatter(n, me, rows, part, recv, rs_send_sem, rs_recv_sem)
    gather = make_gather(n, me, rows, own, full, ag_send_sem, ag_recv_sem, local_sem)

    def row_work(c):
        scatter.total(c, total)
        span = chunk_span(c, rows)
        value = total[...]
        branch[span] = value
        new = x[span].astype(F32) + value * inverse_rms(value) * scale[...]
        middle[span] = new
        own[c] = new.astype(BF)

    run_line(n, CHUNKS, STAGGER, compute, scatter, row_work, gather)


def attn_out(n, attended, full_out, layer_input, scale):
    row_count, width = layer_input.shape
    rows = row_count // CHUNKS
    return pl.pallas_call(
        functools.partial(attn_out_kernel, n, rows),
        out_shape=(
            jax.ShapeDtypeStruct((row_count, width), F32),
            jax.ShapeDtypeStruct((row_count, width), F32),
            jax.ShapeDtypeStruct((n, row_count, width), BF),
        ),
        in_specs=[VMEM] * 4,
        out_specs=(VMEM, VMEM, HBM),
        scratch_shapes=scatter_scratch(n, rows, width)
        + gather_scratch(n, rows, width)
        + [pltpu.VMEM((n * rows, attended.shape[1]), BF)],
        compiler_params=pltpu.CompilerParams(
            collective_id=1, has_side_effects=True, vmem_limit_bytes=56 * MIB
        ),
        name="attn_out",
        cost_estimate=cost(115),
    )(attended, full_out, layer_input, scale)


class WeightTiles:
    def __init__(self, source, held, sem, axis, size):
        self.source, self.held, self.sem, self.axis, self.size = source, held, sem, axis, size
        self.count = source.shape[axis] // size

    def at(self, ref, tile):
        span = pl.ds(pl.multiple_of(tile * self.size, self.size), self.size)
        return ref.at[:, span] if self.axis == 1 else ref.at[span]

    def copy(self, tile):
        return pltpu.make_async_copy(
            self.at(self.source, tile), self.at(self.held, tile), self.sem.at[tile]
        )

    def start(self):
        for tile in range(self.count):
            self.copy(tile).start()


def mlp_kernel(
    n, n_dp, rows, h_full, wg, wu, wd, middle, branch, upstream_in, row_valid, mlp_scale, attn_scale,
    output, dm_full, hidden_out, mlp_gain, middle_grad, da_full, attn_gain, gate_out, up_out,
    part, recv, rs_send_sem, rs_recv_sem, total, own, ag_send_sem, ag_recv_sem, local_sem,
    vg, vu, vd, wsem, in_buf, in_sem, gate_all, up_all, hidden_buf, hidden_sem,
    row_buf, row_sem, mg_buf, mg_sem, h_buf, h_sem, extra, ready, *plane,
):
    me, at = lax.axis_index("mp"), lax.axis_index("dp")
    width, hidden_width = wg.shape
    chips = n_dp // 2
    part_width = width // n_dp

    def in_copies(phase, c):
        source = h_full if phase == 0 else dm_full
        return [
            pltpu.make_async_copy(
                source.at[j, chunk_span(c, rows)],
                in_buf.at[c % 2, pl.ds(j * rows, rows)],
                in_sem.at[c % 2, j],
            )
            for j in range(n)
        ]

    def start(copies):
        for copy in copies:
            copy.start()

    def wait(copies):
        for copy in copies:
            copy.wait()

    def row_copy(phase, c):
        source = middle if phase == 0 else branch
        return pltpu.make_async_copy(
            source.at[chunk_span(c, rows)], row_buf.at[c % 2], row_sem.at[c % 2]
        )

    start(in_copies(0, 0))
    gate_tiles = WeightTiles(wg, vg, wsem.at[0], 1, TILE)
    up_tiles = WeightTiles(wu, vu, wsem.at[1], 1, TILE)
    down_tiles = WeightTiles(wd, vd, wsem.at[2], 1, TILE)
    for tile in range(gate_tiles.count):
        gate_tiles.copy(tile).start()
        up_tiles.copy(tile).start()
    down_tiles.start()
    row_copy(0, 0).start()
    stage_barrier(me, n, at, chips)

    scatter = LineScatter(n, me, rows, part, recv, rs_send_sem, rs_recv_sem)
    gathers = [
        make_gather(n, me, rows, own, full, ag_send_sem, ag_recv_sem, local_sem)
        for full in (dm_full, da_full)
    ]

    def hidden_copies(c):
        return [
            pltpu.make_async_copy(
                hidden_buf.at[c % 2, pl.ds(j * rows, rows)],
                hidden_out.at[j, chunk_span(c, rows)],
                hidden_sem.at[c % 2, j],
            )
            for j in range(n)
        ]

    def forward(c):
        here = pl.ds(c * n * rows, n * rows)
        slot = c % 2
        wait(in_copies(0, c))
        if c + 1 < CHUNKS:
            start(in_copies(0, c + 1))
        if c >= 2:
            wait(hidden_copies(c - 2))

        @pl.loop(0, hidden_width // TILE)
        def _(tile):
            if c == 0:
                gate_tiles.copy(tile).wait()
                up_tiles.copy(tile).wait()
            cols = pl.ds(pl.multiple_of(tile * TILE, TILE), TILE)
            gate = plain_dot(in_buf[slot], vg[:, cols])
            up = plain_dot(in_buf[slot], vu[:, cols])
            gate_all[here, cols] = gate.astype(BF)
            up_all[here, cols] = up.astype(BF)
            hidden_buf[slot, :, cols] = (gate * jax.nn.sigmoid(gate) * up).astype(BF)

        start(hidden_copies(c))

        @pl.loop(0, width // TILE)
        def _(tile):
            if c == 0:
                down_tiles.copy(tile).wait()
            cols = pl.ds(pl.multiple_of(tile * TILE, TILE), TILE)
            part[c, :, cols] = plain_dot(hidden_buf[slot], vd[:, cols]).astype(BF)

    def backward(c):
        here = pl.ds(c * n * rows, n * rows)
        scatter.drain(c)
        gathers[0].drain_sends(c)
        wait(in_copies(1, c))

        @pl.loop(0, hidden_width // TILE)
        def _(tile):
            cols = pl.ds(pl.multiple_of(tile * TILE, TILE), TILE)
            hidden_grad = outer_dot(in_buf[c % 2], vd[cols, :])
            gate = gate_all[here, cols].astype(F32)
            up = up_all[here, cols].astype(F32)
            sigmoid = jax.nn.sigmoid(gate)
            gate_all[here, cols] = (
                hidden_grad * up * sigmoid * (1.0 + gate * (1.0 - sigmoid))
            ).astype(BF)
            up_all[here, cols] = (hidden_grad * gate * sigmoid).astype(BF)

        @pl.loop(0, width // TILE)
        def _(tile):
            cols = pl.ds(pl.multiple_of(tile * TILE, TILE), TILE)
            part[c, :, cols] = (
                outer_dot(gate_all[here], vg[cols, :]) + outer_dot(up_all[here], vu[cols, :])
            ).astype(BF)

        if c + 1 == CHUNKS:
            start(h_copies(0))
            signal_partners(ready, at, chips)

    def mg_copy(c):
        return pltpu.make_async_copy(
            mg_buf.at[c % 2], middle_grad.at[chunk_span(c, rows)], mg_sem.at[c % 2]
        )

    def next_row_copy(phase, c):
        if c + 1 < CHUNKS:
            row_copy(phase, c + 1).start()
        elif phase == 0:
            row_copy(1, 0).start()

    def forward_rows(c):
        scatter.total(c, total)
        span = chunk_span(c, rows)
        row_copy(0, c).wait()
        next_row_copy(0, c)
        value = total[...]
        inverse = inverse_rms(value)
        output[span] = (row_buf[c % 2] + value * inverse * mlp_scale[...]).astype(BF)
        upstream = upstream_in[span].astype(F32) * row_valid[span]
        grad, gain = norm_back(value, inverse, mlp_scale[...], upstream)
        own[c] = grad.astype(BF)
        mlp_gain[...] = gain if c == 0 else mlp_gain[...] + gain

    def backward_rows(c):
        scatter.total(c, total)
        span = chunk_span(c, rows)
        row_copy(1, c).wait()
        next_row_copy(1, c)
        upstream = upstream_in[span].astype(F32) * row_valid[span] + total[...]
        if c >= 2:
            mg_copy(c - 2).wait()
        mg_buf[c % 2] = upstream
        mg_copy(c).start()
        value = row_buf[c % 2]
        grad, gain = norm_back(value, inverse_rms(value), attn_scale[...], upstream)
        own[c] = grad.astype(BF)
        attn_gain[...] = gain if c == 0 else attn_gain[...] + gain

    block_width = pl.ds(0, hidden_width)

    def slot_at(index):
        for ref in (vg, vu, vd):
            count = ref.shape[0] // part_width
            if index < count:
                return ref.at[pl.ds(index * part_width, part_width), block_width]
            index -= count
        return extra.at[index]

    reduces = []
    for which, out in enumerate((gate_out, up_out)):
        first = chips + 3 * chips * which
        views = (
            lambda r: slot_at(r),
            lambda r, first=first: slot_at(first + r),
            lambda r, first=first: slot_at(first + chips + r),
            lambda r, first=first: slot_at(first + 2 * chips + r - 1),
        )
        reduces.append(
            PlaneReduce(at, chips, part_width, views, plane[4 * which : 4 * which + 4], out)
        )
    order = relative_order(chips)
    jobs = [
        (which, same_core, r)
        for which in range(2)
        for same_core in (False, True)
        for r in order
    ]

    def h_copies(index):
        which, same_core, r = jobs[index]
        first = reduces[which].owner(r, same_core) * part_width
        cols = pl.ds(pl.multiple_of(first, part_width), part_width)
        return [
            pltpu.make_async_copy(
                h_full.at[j, :, cols], h_buf.at[index % 2, j], h_sem.at[index % 2, j]
            )
            for j in range(n)
        ]

    def weight_block(index):
        which, same_core, r = jobs[index]
        reduce = reduces[which]
        grad = (gate_all, up_all)[which]
        if index == 0:
            pl.semaphore_wait(ready, 1 + len(bits_of(chips - 1)))
        wait(h_copies(index))
        if index + 1 < len(jobs):
            start(h_copies(index + 1))
        if same_core:
            reduce.core_copy(r).wait_recv()
        elif which == 1:
            reduces[0].drain_core(r)
        left = jnp.concatenate(
            [
                h_buf[index % 2, j, c * rows : (c + 1) * rows]
                for c in range(CHUNKS)
                for j in range(n)
            ],
            axis=0,
        )

        @pl.loop(0, hidden_width // TILE)
        def _(tile):
            cols = pl.ds(pl.multiple_of(tile * TILE, TILE), TILE)
            block = inner_dot(left, grad[:, cols])
            if not same_core:
                reduce.core_send(r)[:, cols] = block.astype(BF)
            else:
                block = block + reduce.core_recv(r)[:, cols].astype(F32)
                if r > 0:
                    reduce.held(r)[:, cols] = block.astype(BF)
                else:
                    reduce.out[:, cols] = block

        if not same_core:
            reduce.core_copy(r).start()
        elif r > 0:
            for half in range(2):
                if not reduce.before(r, half):
                    reduce.push(r, half)

    work = []
    for index, (which, same_core, r) in enumerate(jobs):
        work.append(functools.partial(weight_block, index))
        if same_core and r == order[-1]:
            for late in order:
                for half in range(2):
                    if late > 0 and reduces[which].before(late, half):
                        work.append(functools.partial(reduces[which].push, late, half))
    pending = iter(work)

    last_step = 2 * n - 2
    events = sorted(
        (max(PERIOD, last_step + 1) * phase + step + STAGGER * c - (0.5 if step == 0 else 0), phase, c, step)
        for phase in range(2)
        for c in range(CHUNKS)
        for step in range(last_step + 1)
    )
    filling = False
    for _, phase, c, step in events:
        gather = gathers[phase]
        if step == 0:
            (forward, backward)[phase](c)
            filling = filling or (phase == 1 and c + 1 == CHUNKS)
        if step < n - 1:
            scatter.edge(c, step)
            if step > 0:
                scatter.step(c, step)
        elif step == n - 1:
            (forward_rows, backward_rows)[phase](c)
            gather.step(c, 1)
        elif step < last_step:
            gather.step(c, step - n + 2)
        else:
            gather.last(c)
            if phase == 0:
                gather.local_copy(c).wait()
                start(in_copies(1, c))
        if filling:
            for _ in range(FILL):
                job = next(pending, None)
                if job is not None:
                    job()
    for job in pending:
        job()
    for c in range(CHUNKS):
        scatter.drain(c)
        gathers[1].drain(c)
    for reduce in reduces:
        reduce.finish()
        reduce.drain()
    for r in range(chips):
        reduces[1].drain_core(r)
    for c in range(max(CHUNKS - 2, 0), CHUNKS):
        mg_copy(c).wait()
        wait(hidden_copies(c))


def mlp(n, n_dp, h_full, wg, wu, wd, middle, branch, out_grad, row_valid, mlp_scale, attn_scale):
    row_count, width = branch.shape
    hidden_width = wg.shape[1]
    rows = row_count // CHUNKS
    size = n * row_count
    chips = n_dp // 2
    part_width = width // n_dp
    block = (part_width, hidden_width)
    most = max(width, hidden_width) // TILE
    slots = (2 * width + hidden_width) // part_width
    extra = 7 * chips - 1 - slots
    return pl.pallas_call(
        functools.partial(mlp_kernel, n, n_dp, rows),
        out_shape=(
            jax.ShapeDtypeStruct((row_count, width), BF),
            jax.ShapeDtypeStruct((n, row_count, width), BF),
            jax.ShapeDtypeStruct((n, row_count, hidden_width), BF),
            jax.ShapeDtypeStruct((1, width), F32),
            jax.ShapeDtypeStruct((row_count, width), F32),
            jax.ShapeDtypeStruct((n, row_count, width), BF),
            jax.ShapeDtypeStruct((1, width), F32),
            jax.ShapeDtypeStruct(block, F32),
            jax.ShapeDtypeStruct(block, F32),
        ),
        in_specs=[HBM] * 6 + [VMEM] * 4,
        out_specs=(VMEM, HBM, HBM, VMEM, HBM, HBM, VMEM, VMEM, VMEM),
        scratch_shapes=scatter_scratch(n, rows, width)
        + gather_scratch(n, rows, width)
        + [
            pltpu.VMEM(wg.shape, BF),
            pltpu.VMEM(wu.shape, BF),
            pltpu.VMEM(wd.shape, BF),
            pltpu.SemaphoreType.DMA((3, most)),
            pltpu.VMEM((2, n * rows, width), BF),
            pltpu.SemaphoreType.DMA((2, n)),
            pltpu.VMEM((size, hidden_width), BF),
            pltpu.VMEM((size, hidden_width), BF),
            pltpu.VMEM((2, n * rows, hidden_width), BF),
            pltpu.SemaphoreType.DMA((2, n)),
            pltpu.VMEM((2, rows, width), F32),
            pltpu.SemaphoreType.DMA((2,)),
            pltpu.VMEM((2, rows, width), F32),
            pltpu.SemaphoreType.DMA((2,)),
            pltpu.VMEM((2, n, row_count, part_width), BF),
            pltpu.SemaphoreType.DMA((2, n)),
            pltpu.VMEM((extra,) + block if extra > 0 else (1, 16, 128), BF),
            pltpu.SemaphoreType.REGULAR,
        ]
        + plane_sems(chips) * 2,
        compiler_params=pltpu.CompilerParams(
            collective_id=2, has_side_effects=True, vmem_limit_bytes=63 * MIB
        ),
        name="mlp",
        cost_estimate=cost(260),
    )(h_full, wg, wu, wd, middle, branch, out_grad, row_valid, mlp_scale, attn_scale)


def last_grads_kernel(
    n, n_dp, rows, grads, weight, base, inputs, att, da, gains,
    input_grad, qkv_out, out_out, gain_out,
    part, recv, rs_send_sem, rs_recv_sem, total, packed,
    x_buf, da_buf, load_sem,
    send_qkv, recv_qkv, held_qkv, message_qkv, send_out, recv_out, held_out, message_out,
    gain_recv, gain_send_sem, gain_recv_sem, mp_recv, mp_send_sem, mp_recv_sem, *plane,
):
    me, at = lax.axis_index("mp"), lax.axis_index("dp")
    entered = peer_barrier((("mp", me, n), ("dp", at, n_dp)))
    width = weight.shape[0]
    block_rows = rows * CHUNKS
    local_width = att.shape[1]
    chips = n_dp // 2
    part_width = width // n_dp
    order = relative_order(chips)
    jobs = [(same_core, r) for same_core in (False, True) for r in order]

    def views(send, recv, held, message):
        return (
            lambda r: send.at[r],
            lambda r: recv.at[r],
            lambda r: held.at[r - 1],
            lambda r: message.at[r - 1],
        )

    by_qkv = PlaneReduce(
        at, chips, part_width, views(send_qkv, recv_qkv, held_qkv, message_qkv), plane[:4], qkv_out
    )
    by_out = PlaneReduce(
        at, chips, local_width, views(send_out, recv_out, held_out, message_out), plane[4:], out_out
    )

    def loads(k):
        same_core, r = jobs[k]
        first = by_qkv.owner(r, same_core) * part_width
        cols = pl.ds(pl.multiple_of(first, part_width), part_width)
        return [
            pltpu.make_async_copy(inputs.at[:, cols], x_buf.at[k % 2], load_sem.at[k % 2, 0]),
            pltpu.make_async_copy(da.at[:, cols], da_buf.at[k % 2], load_sem.at[k % 2, 1]),
        ]

    for copy in loads(0):
        copy.start()

    def compute(c):
        for j in range(n):
            packed[j * rows : (j + 1) * rows] = grads[
                j * block_rows + c * rows : j * block_rows + (c + 1) * rows
            ]

        @pl.loop(0, width // TILE)
        def _(tile):
            cols = pl.ds(pl.multiple_of(tile * TILE, TILE), TILE)
            part[c, :, cols] = outer_dot(packed[...], weight[cols, :]).astype(BF)

    scatter = LineScatter(n, me, rows, part, recv, rs_send_sem, rs_recv_sem)

    def row_work(c):
        scatter.total(c, total)
        span = chunk_span(c, rows)
        input_grad[span] = base[span] + total[...]

    def weight_block(k):
        same_core, r = jobs[k]
        slot = k % 2
        for copy in loads(k):
            copy.wait()
        if k + 1 < len(jobs):
            for copy in loads(k + 1):
                copy.start()
        if same_core:
            by_qkv.core_copy(r).wait_recv()
            by_out.core_copy(r).wait_recv()

        def keep(reduce, block, cols):
            if not same_core:
                reduce.core_send(r)[:, cols] = block.astype(BF)
                return
            block = block + reduce.core_recv(r)[:, cols].astype(F32)
            if r > 0:
                reduce.held(r)[:, cols] = block.astype(BF)
            else:
                reduce.out[:, cols] = block

        @pl.loop(0, 3)
        def _(tile):
            cols = pl.ds(pl.multiple_of(tile * local_width, local_width), local_width)
            keep(by_qkv, inner_dot(x_buf[slot], grads[:, cols]), cols)

        keep(by_out, inner_dot(att[...], da_buf[slot]), slice(None))
        for reduce in (by_qkv, by_out):
            if not same_core:
                reduce.core_copy(r).start()
            elif r > 0:
                for half in range(2):
                    if not reduce.before(r, half):
                        reduce.push(r, half)

    gain_copies = exchange(
        "dp", at, n_dp, lambda peer: gains.at[peer], gain_recv, gain_send_sem, gain_recv_sem
    )
    mp_copies = exchange("mp", me, n, lambda peer: gain_out, mp_recv, mp_send_sem, mp_recv_sem)
    line = iter([(step, c) for c in range(CHUNKS) for step in range(1, n)])

    def line_steps(count):
        for _ in range(count):
            step, c = next(line, (None, None))
            if step is None:
                return
            if step < n - 1:
                scatter.step(c, step)
            else:
                row_work(c)

    def send_edges(c):
        for step in range(n - 1):
            scatter.edge(c, step)

    compute(0)
    entered()
    send_edges(0)
    for copy in gain_copies:
        copy.start()
    blocks = iter(range(len(jobs)))
    for c in range(1, CHUNKS):
        weight_block(next(blocks))
        compute(c)
        send_edges(c)
    for k in blocks:
        weight_block(k)
        line_steps(2)
    late = [(r, half) for r in order for half in range(2) if r > 0 and by_qkv.before(r, half)]
    for r, half in late:
        for reduce in (by_qkv, by_out):
            reduce.push(r, half)
        line_steps(1)
    gain_out[...] = gains[at]
    for shift, copy in enumerate(gain_copies, 1):
        copy.wait_recv()
        gain_out[...] += gain_recv[shift - 1]
    for copy in mp_copies:
        copy.start()
    line_steps(n * CHUNKS)
    for reduce in (by_qkv, by_out):
        reduce.finish()
    for copy in mp_copies:
        copy.wait_recv()
        copy.wait_send()
    lanes = lax.broadcasted_iota(jnp.int32, gain_out.shape, 1)
    shared = gain_out[...]
    for shift in range(1, n):
        shared = shared + mp_recv[shift - 1]
    gain_out[...] = jnp.where(lanes < 2 * part_width, shared, gain_out[...])
    for copy in gain_copies:
        copy.wait_send()
    for c in range(CHUNKS):
        scatter.drain(c)
    for reduce in (by_qkv, by_out):
        for r in range(chips):
            reduce.drain_core(r)
        reduce.drain()


def last_grads(n, n_dp, grads, weight, base, inputs, attended, da_full, gains):
    row_count, width = base.shape
    rows = row_count // CHUNKS
    size, local_width = attended.shape
    part_width = width // n_dp
    chips = n_dp // 2
    qkv_block = (part_width, 3 * local_width)
    out_block = (local_width, part_width)
    gain_block = gains.shape[1:]
    return pl.pallas_call(
        functools.partial(last_grads_kernel, n, n_dp, rows),
        out_shape=(
            jax.ShapeDtypeStruct((row_count, width), F32),
            jax.ShapeDtypeStruct(qkv_block, F32),
            jax.ShapeDtypeStruct(out_block, F32),
            jax.ShapeDtypeStruct(gain_block, F32),
        ),
        in_specs=[VMEM, VMEM, VMEM, HBM, VMEM, HBM, VMEM],
        out_specs=(VMEM,) * 4,
        scratch_shapes=scatter_scratch(n, rows, width)
        + [
            pltpu.VMEM((n * rows, 3 * local_width), BF),
            pltpu.VMEM((2, size, part_width), BF),
            pltpu.VMEM((2, size, part_width), BF),
            pltpu.SemaphoreType.DMA((2, 2)),
        ]
        + [
            pltpu.VMEM((count,) + block, BF)
            for block in (qkv_block, out_block)
            for count in (chips, chips, chips - 1, chips - 1)
        ]
        + [pltpu.VMEM((n_dp - 1,) + gain_block, F32)]
        + [pltpu.SemaphoreType.DMA((n_dp - 1,))] * 2
        + [pltpu.VMEM((n - 1,) + gain_block, F32)]
        + [pltpu.SemaphoreType.DMA((n - 1,))] * 2
        + plane_sems(chips) * 2,
        compiler_params=pltpu.CompilerParams(
            collective_id=4, has_side_effects=True, vmem_limit_bytes=60 * MIB
        ),
        name="last_grads",
        cost_estimate=cost(80),
    )(grads, weight, base, inputs, attended, da_full, gains)


def turn(values, cos, sin):
    return values * cos + pltpu.roll(values, values.shape[1] // 2, 1) * sin


def turn_back(values, cos, sin):
    return values * cos + pltpu.roll(values * sin, values.shape[1] // 2, 1)


def allowed_keys(starts, first_row, rows, key_end):
    places = first_row + lax.broadcasted_iota(jnp.int32, (rows, key_end), 0)
    keys = lax.broadcasted_iota(jnp.int32, (rows, key_end), 1)
    return (keys <= places) & (keys >= starts)


def columns_to_rows(first, second):
    lanes = lax.broadcasted_iota(jnp.int32, (first.shape[0], 128), 1)
    return jnp.transpose(jnp.where(lanes == 0, first, second))[:8]


def sum_held(n, me, held, recv, turned, send_sem, recv_sem):
    copies = exchange("mp", me, n, lambda peer: held, recv, send_sem, recv_sem)
    for copy in copies:
        copy.start()
    total = held[...]
    for shift, copy in enumerate(copies, 1):
        copy.wait_recv()
        total = total + recv[shift - 1]
    for copy in copies:
        copy.wait_send()
    turned[...] = jnp.zeros_like(turned)
    turned[:8] = total
    back = jnp.transpose(turned[...])
    return back[:, 0:1], back[:, 1:2]


def sum_scratch(n, size):
    return [
        pltpu.VMEM((8, size), F32),
        pltpu.VMEM((n - 1, 8, size), F32),
        pltpu.VMEM((128, size), F32),
        pltpu.SemaphoreType.DMA((n - 1,)),
        pltpu.SemaphoreType.DMA((n - 1,)),
    ]


def attention_kernel(
    q_raw, k_raw, v_raw, q_inv, k_inv, q_gain, k_gain, cos, sin, starts,
    out, q_low, k_low, v_low, log_total,
):
    size, head = q_raw.shape
    score_scale = 1.0 / math.sqrt(head)
    q_low[...] = turn(q_raw[...] * q_inv[...] * q_gain[...], cos[...], sin[...]).astype(BF)
    k_low[...] = turn(k_raw[...] * k_inv[...] * k_gain[...], cos[...], sin[...]).astype(BF)
    v_low[...] = v_raw[...].astype(BF)
    rows = min(QUERY_ROWS, size)
    for first in range(0, size, rows):
        end = first + rows
        span = slice(first, end)
        scores = outer_dot(q_low[span], k_low[:end]) * score_scale
        scores = jnp.where(allowed_keys(starts[span], first, rows, end), scores, MASKED)
        row_max = jnp.max(scores, axis=1, keepdims=True)
        exponents = jnp.exp(scores - row_max)
        row_total = jnp.sum(exponents, axis=1, keepdims=True)
        probs = (exponents * (1.0 / row_total)).astype(BF)
        out[span] = plain_dot(probs, v_low[:end]).astype(BF)
        log_total[span] = row_max + jnp.log(row_total)


def head_specs(size, head, heads, count):
    return [pl.BlockSpec((size, head), lambda h, k=k: (0, k * heads + h)) for k in range(count)]


def attention(qkv_raw, q_inv, k_inv, q_gain, k_gain, cos, sin, starts, heads):
    size = qkv_raw.shape[0]
    head = cos.shape[1]
    column = pl.BlockSpec((size, 1), lambda h: (0, 0))
    table = pl.BlockSpec((size, head), lambda h: (0, 0))
    gain = pl.BlockSpec((1, head), lambda h: (0, h))
    by_head = pl.BlockSpec((size, head), lambda h: (0, h))
    low = jax.ShapeDtypeStruct((size, heads * head), BF)
    return pl.pallas_call(
        attention_kernel,
        grid=(heads,),
        out_shape=(low, low, low, low, jax.ShapeDtypeStruct((heads, size, 1), F32)),
        in_specs=head_specs(size, head, heads, 3)
        + [column, column, gain, gain, table, table, column],
        out_specs=(by_head,) * 4 + (pl.BlockSpec((None, size, 1), lambda h: (h, 0, 0)),),
        compiler_params=pltpu.CompilerParams(vmem_limit_bytes=48 * MIB),
        name="attention",
        cost_estimate=cost(18),
    )(qkv_raw, qkv_raw, qkv_raw, q_inv, k_inv, q_gain, k_gain, cos, sin, starts)


def attention_back_kernel(
    n, heads, model_width, qkv, q_low, k_low, v_low, out_grad, log_total,
    q_inv, k_inv, q_gain, k_gain, cos, sin, starts,
    grads, q_gain_grad, k_gain_grad,
    q_weighted, k_weighted, q_grad, k_sum, v_sum, q_dots, k_dots, *sums,
):
    me = lax.axis_index("mp")
    entered = peer_barrier((("mp", me, n),))
    size = qkv.shape[0]
    width = qkv.shape[1] // 3
    head = width // heads
    score_scale = 1.0 / math.sqrt(head)
    rows = min(QUERY_ROWS, size)
    q_dots[...] = jnp.zeros_like(q_dots)
    k_dots[...] = jnp.zeros_like(k_dots)

    @pl.loop(0, heads)
    def _(h):
        def cols(first):
            return pl.ds(pl.multiple_of(first + h * head, head), head)

        here = cols(0)
        for first in reversed(range(0, size, rows)):
            end = first + rows
            span = slice(first, end)
            scores = outer_dot(q_low[span, here], k_low[:end, here]) * score_scale
            scores = jnp.where(allowed_keys(starts[span], first, rows, end), scores, MASKED)
            probs = jnp.exp(scores - log_total[h, span])
            prob_grad = outer_dot(out_grad[span, here], v_low[:end, here])
            probs_low = probs.astype(BF)
            weighted = probs * prob_grad
            score_grad = (
                weighted - probs * jnp.sum(weighted, axis=1, keepdims=True)
            ).astype(BF)
            q_grad[span] = plain_dot(score_grad, k_low[:end, here]) * score_scale
            k_extra = inner_dot(score_grad, q_low[span, here])
            v_extra = inner_dot(probs_low, out_grad[span, here])
            if end == size:
                k_sum[...] = k_extra
                v_sum[...] = v_extra
            else:
                k_sum[:end] += k_extra
                v_sum[:end] += v_extra
        for first, inv, gain, grad, factor, weighted_out, dots, gain_grad in (
            (0, q_inv, q_gain, q_grad, None, q_weighted, q_dots, q_gain_grad),
            (width, k_inv, k_gain, k_sum, score_scale, k_weighted, k_dots, k_gain_grad),
        ):
            raw = qkv[:, cols(first)]
            value = grad[...] if factor is None else grad[...] * factor
            normed = turn_back(value, cos[...], sin[...])
            weighted = normed * gain[:, here]
            weighted_out[:, here] = weighted
            gain_grad[:, here] = jnp.sum(normed * raw * inv[...], axis=0, keepdims=True)
            dots[...] += jnp.sum(weighted * raw, axis=1, keepdims=True)
        grads[:, cols(2 * width)] = v_sum[...].astype(BF)

    held = sums[0]
    held[...] = columns_to_rows(q_dots[...], k_dots[...])
    entered()
    q_total, k_total = sum_held(n, me, *sums)
    for first, inv, weighted, dots in (
        (0, q_inv, q_weighted, q_total),
        (width, k_inv, k_weighted, k_total),
    ):
        scale = inv[...]
        factor = scale * scale * scale * (dots / model_width)
        grads[:, first : first + width] = (
            scale * weighted[...] - qkv[:, first : first + width] * factor
        ).astype(BF)


def attention_back(
    n, heads, model_width, qkv_raw, q_low, k_low, v_low, out_grad, log_total, q_inv, k_inv,
    q_gain, k_gain, cos, sin, starts,
):
    size, width = q_low.shape
    head = width // heads
    gains = jax.ShapeDtypeStruct((1, width), F32)
    return pl.pallas_call(
        functools.partial(attention_back_kernel, n, heads, model_width),
        out_shape=(jax.ShapeDtypeStruct((size, 3 * width), BF), gains, gains),
        in_specs=[VMEM] * 13,
        out_specs=(VMEM,) * 3,
        scratch_shapes=[pltpu.VMEM((size, width), F32)] * 2
        + [pltpu.VMEM((size, head), F32)] * 3
        + [pltpu.VMEM((size, 1), F32)] * 2
        + sum_scratch(n, size),
        compiler_params=pltpu.CompilerParams(
            collective_id=6, has_side_effects=True, vmem_limit_bytes=56 * MIB
        ),
        name="attention_back",
        cost_estimate=cost(30),
    )(
        qkv_raw, q_low, k_low, v_low, out_grad, log_total, q_inv, k_inv, q_gain, k_gain,
        cos, sin, starts,
    )


def local(
    layer_input,
    query_weight,
    key_weight,
    value_weight,
    out_weight,
    gate_weight,
    up_weight,
    down_weight,
    query_gain,
    key_gain,
    attn_gain,
    mlp_gain,
    seq_lens,
    out_grad,
):
    n = lax.axis_size("mp")
    n_dp = lax.axis_size("dp")
    me = lax.axis_index("mp")
    row_count, model_width = layer_input.shape
    group_size = row_count * n
    local_heads, gain_part = query_gain.shape
    head_size = gain_part * n_dp
    local_width = local_heads * head_size

    full_gate = lax.all_gather(gate_weight, "dp", axis=0, tiled=True)
    full_up = lax.all_gather(up_weight, "dp", axis=0, tiled=True)
    full_down = lax.all_gather(down_weight, "dp", axis=1, tiled=True)
    head_part = local_heads * gain_part
    width_part = attn_gain.shape[0]
    own_gains = jnp.concatenate(
        [attn_gain, mlp_gain, query_gain.reshape(head_part), key_gain.reshape(head_part)]
    ).astype(F32)[None]
    inputs_full, qkv_raw, full_qkv, full_out, gain_parts, query_inv, key_inv = front(
        n, n_dp, layer_input, query_weight, key_weight, value_weight, out_weight, own_gains
    )
    inputs_full = inputs_full.reshape(group_size, model_width)
    gain_parts = gain_parts[:, 0]

    def head_gain(first):
        piece = gain_parts[:, first : first + head_part].reshape(n_dp, local_heads, gain_part)
        return piece.transpose(1, 0, 2).reshape(1, local_width)

    query_scale = head_gain(2 * width_part)
    key_scale = head_gain(2 * width_part + head_part)
    attn_scale = gain_parts[:, :width_part].reshape(1, model_width)
    mlp_scale = gain_parts[:, width_part : 2 * width_part].reshape(1, model_width)

    starts, positions, valid = layout(seq_lens[0], group_size)
    starts = starts[:, None]
    cos_table, sin_table = rotary_tables(positions, head_size)
    row_valid = lax.dynamic_slice_in_dim(valid, me * row_count, row_count, 0).astype(F32)[:, None]

    attended, query_low, key_low, value_low, log_total = attention(
        qkv_raw, query_inv, key_inv, query_scale, key_scale, cos_table, sin_table, starts,
        local_heads,
    )
    branch, middle, middle_full = attn_out(n, attended, full_out, layer_input, attn_scale)
    (
        layer_output, mlp_grad_full, hidden, mlp_gain_part, middle_grad, branch_full,
        attn_gain_part, grad_gate, grad_up,
    ) = mlp(
        n, n_dp, middle_full, full_gate, full_up, full_down, middle, branch, out_grad, row_valid,
        mlp_scale, attn_scale,
    )

    def flat(rows):
        return rows.reshape(group_size, rows.shape[-1])

    branch_full = flat(branch_full)
    down_part = inner_dot(flat(hidden), flat(mlp_grad_full)).astype(BF)
    branch_full, down_part = lax.optimization_barrier((branch_full, down_part))
    grad_down = lax.psum_scatter(down_part, "dp", scatter_dimension=1, tiled=True)

    mixed_grad = outer_dot(branch_full, full_out).astype(BF)
    qkv_grad, query_gain_part, key_gain_part = attention_back(
        n, local_heads, model_width, qkv_raw, query_low, key_low, value_low, mixed_grad, log_total,
        query_inv, key_inv, query_scale, key_scale, cos_table, sin_table, starts,
    )

    def by_part(row):
        return row.reshape(n_dp, -1)

    def by_head_part(row):
        pieces = row.reshape(local_heads, n_dp, gain_part).transpose(1, 0, 2)
        return pieces.reshape(n_dp, head_part)

    gain_grads = jnp.concatenate(
        [
            by_part(attn_gain_part),
            by_part(mlp_gain_part),
            by_head_part(query_gain_part),
            by_head_part(key_gain_part),
        ],
        axis=1,
    )[:, None]
    input_grad, grad_qkv, grad_out, gain_sums = last_grads(
        n, n_dp, qkv_grad, full_qkv, middle_grad, inputs_full, attended, branch_full, gain_grads
    )
    gain_sums = gain_sums[0]
    heads_at = 2 * width_part
    return (
        layer_output,
        input_grad,
        grad_qkv[:, :local_width],
        grad_qkv[:, local_width : 2 * local_width],
        grad_qkv[:, 2 * local_width :],
        grad_out,
        grad_gate,
        grad_up,
        grad_down.astype(F32),
        gain_sums[heads_at : heads_at + head_part].reshape(local_heads, gain_part),
        gain_sums[heads_at + head_part :].reshape(local_heads, gain_part),
        gain_sums[:width_part],
        gain_sums[width_part:heads_at],
    )


def solution(mesh):
    return jax.shard_map(
        local,
        mesh=mesh,
        in_specs=(
            P(("dp", "mp"), None),
            P("dp", "mp"),
            P("dp", "mp"),
            P("dp", "mp"),
            P("mp", "dp"),
            P("dp", "mp"),
            P("dp", "mp"),
            P("mp", "dp"),
            P("mp", "dp"),
            P("mp", "dp"),
            P("dp"),
            P("dp"),
            P("dp", None),
            P(("dp", "mp"), None),
        ),
        out_specs=(
            P(("dp", "mp"), None),
            P(("dp", "mp"), None),
            P("dp", "mp"),
            P("dp", "mp"),
            P("dp", "mp"),
            P("mp", "dp"),
            P("dp", "mp"),
            P("dp", "mp"),
            P("mp", "dp"),
            P("mp", "dp"),
            P("mp", "dp"),
            P("dp"),
            P("dp"),
        ),
        check_vma=False,
    )
```

```python
import functools
import math

import jax
import jax.numpy as jnp
from jax import lax
from jax.experimental import pallas as pl
from jax.experimental.pallas import tpu as pltpu
from jax.sharding import PartitionSpec as P

EPS = 1e-06
THETA = 500000.0
MASKED = -1000000000.0
CHUNKS = 4
STAGGER = 2
EDGES = False
FILL = 2
PERIOD = 8
HOOKS = (3, 7, 10, 13, 16)
TILE = 512
QUERY_ROWS = 256
BF = jnp.bfloat16
F32 = jnp.float32
MIB = 1 << 20
HBM = pl.BlockSpec(memory_space=pl.ANY)
VMEM = pl.BlockSpec(memory_space=pltpu.VMEM)


def cost(micros):
    return pl.CostEstimate(
        flops=micros * 1_000_000_000, bytes_accessed=micros * 3_000_000, transcendentals=0
    )


def plain_dot(former, latter):
    return jnp.dot(former, latter, preferred_element_type=F32)


def inner_dot(former, latter):
    return lax.dot_general(
        former, latter, (((0,), (0,)), ((), ())), preferred_element_type=F32
    )


def outer_dot(former, latter):
    return lax.dot_general(
        former, latter, (((1,), (1,)), ((), ())), preferred_element_type=F32
    )


def layout(lengths, group_size):
    slot_count = lengths.shape[0]
    seq_ends = jnp.cumsum(lengths, dtype=jnp.int32)
    starts = seq_ends - lengths
    places = jnp.arange(group_size, dtype=jnp.int32)
    slot_ids = jnp.arange(slot_count, dtype=jnp.int32)
    segment = jnp.sum(
        (places[:, None] >= seq_ends[None, :]).astype(jnp.int32), axis=1, dtype=jnp.int32
    )
    chosen = (segment[:, None] == slot_ids[None, :]).astype(jnp.int32)
    padded = (segment == slot_count).astype(jnp.int32)
    begins = (
        jnp.sum(chosen * starts[None, :], axis=1, dtype=jnp.int32)
        + padded * seq_ends[slot_count - 1]
    )
    return (begins, places - begins, places < seq_ends[slot_count - 1])


def rotary_tables(positions, head_size):
    half_dim = head_size // 2
    frequency = jnp.exp(jnp.arange(half_dim, dtype=F32) * (-2.0 * math.log(THETA) / head_size))
    angles = positions.astype(F32)[:, None] * frequency[None, :]
    cos_half, sin_half = jnp.cos(angles), jnp.sin(angles)
    return (
        jnp.concatenate([cos_half, cos_half], axis=1),
        jnp.concatenate([-sin_half, sin_half], axis=1),
    )


def neighbour_barrier(me, n):
    barrier = pltpu.get_barrier_semaphore()

    @pl.when(me > 0)
    def _():
        pl.semaphore_signal(barrier, inc=1, device_id={"mp": me - 1})

    @pl.when(me < n - 1)
    def _():
        pl.semaphore_signal(barrier, inc=1, device_id={"mp": me + 1})

    pl.semaphore_wait(barrier, jnp.minimum(me, 1) + jnp.minimum(n - 1 - me, 1))


class LineGather:
    def __init__(self, n, me, own, full, send_sem, recv_sem, local_sem):
        self.n, self.me, self.own, self.full = n, me, own, full
        self.send_sem, self.recv_sem, self.local_sem = send_sem, recv_sem, local_sem

    def local_copy(self, c):
        return pltpu.make_async_copy(self.own(c), self.full(self.me, c), self.local_sem.at[c])

    def copy(self, c, step, way, block, src):
        return pltpu.make_async_remote_copy(
            src_ref=src,
            dst_ref=self.full(block, c),
            send_sem=self.send_sem.at[c, step - 1, way],
            recv_sem=self.recv_sem.at[c, step - 1, way],
            device_id={"mp": self.me + (1 if way == 0 else -1)},
        )

    def sides(self):
        return ((0, self.me), (1, self.n - 1 - self.me))

    def block_at(self, way, step):
        return self.me - step if way == 0 else self.me + step

    def step(self, c, step):
        n = self.n
        if step == 1:
            self.local_copy(c).start()
        for way, place in self.sides():
            if step > 1:

                @pl.when(place >= step - 1)
                def _(way=way):
                    block = self.block_at(way, step - 1)
                    self.copy(c, step - 1, way, block, self.own(c)).wait_recv()

            @pl.when((place >= step - 1) & (place < n - 1))
            def _(way=way):
                block = self.block_at(way, step - 1)
                src = self.own(c) if step == 1 else self.full(block, c)
                self.copy(c, step, way, block, src).start()

    def last(self, c):
        n = self.n
        for way, place in self.sides():

            @pl.when(place == n - 1)
            def _(way=way):
                block = self.block_at(way, n - 1)
                self.copy(c, n - 1, way, block, self.own(c)).wait_recv()

    def drain(self, c):
        self.local_copy(c).wait()
        self.drain_sends(c)

    def drain_sends(self, c):
        for step in range(1, self.n):
            for way, place in self.sides():

                @pl.when((place >= step - 1) & (place < self.n - 1))
                def _(way=way):
                    self.copy(c, step, way, self.me, self.own(c)).wait_send()


class LineScatter:
    def __init__(self, n, me, rows, part, recv, send_sem, recv_sem):
        self.n, self.me, self.rows = n, me, rows
        self.part, self.recv = part, recv
        self.send_sem, self.recv_sem = send_sem, recv_sem

    def piece(self, c, owner):
        first = pl.multiple_of(owner * self.rows, self.rows)
        return self.part.at[c, pl.ds(first, self.rows)]

    def copy(self, c, step, way, src):
        return pltpu.make_async_remote_copy(
            src_ref=src,
            dst_ref=self.recv.at[c, step, way],
            send_sem=self.send_sem.at[c, step, way],
            recv_sem=self.recv_sem.at[c, step, way],
            device_id={"mp": self.me + (1 if way == 0 else -1)},
        )

    def sides(self):
        return ((0, self.me), (1, self.n - 1 - self.me))

    def owner(self, way, step):
        return self.n - 1 - step + self.me if way == 0 else step - (self.n - 1 - self.me)

    def edge(self, c, step):
        for way, place in self.sides():

            @pl.when(place == 0)
            def _(way=way):
                self.copy(c, step, way, self.piece(c, self.owner(way, step))).start()

    def step(self, c, step):
        for way, place in self.sides():

            @pl.when((place > 0) & (place <= min(step, self.n - 2)))
            def _(way=way):
                piece = self.piece(c, self.owner(way, step))
                self.copy(c, step - 1, way, piece).wait_recv()
                piece[...] = (
                    piece[...].astype(F32) + self.recv[c, step - 1, way].astype(F32)
                ).astype(BF)
                self.copy(c, step, way, piece).start()

    def total(self, c, out):
        n = self.n
        out[...] = self.piece(c, self.me)[...].astype(F32)
        for way, place in self.sides():

            @pl.when(place > 0)
            def _(way=way):
                self.copy(c, n - 2, way, self.recv.at[c, n - 2, way]).wait_recv()
                out[...] += self.recv[c, n - 2, way].astype(F32)

    def drain(self, c):
        n = self.n
        for step in range(n - 1):
            for way, place in self.sides():

                @pl.when(place <= min(step, n - 2))
                def _(way=way):
                    self.copy(c, step, way, self.recv.at[c, step, way]).wait_send()


def run_line(n, chunks, stagger, compute, scatter, row_work, gather, filler=None):
    last_step = 2 * n - 2 if gather is not None else n - 1
    events = sorted(
        (step + stagger * c - (0.5 if step == 0 else 0), c, step)
        for c in range(chunks)
        for step in range(last_step + 1)
    )
    computed = 0
    for _, c, step in events:
        if step == 0:
            compute(c)
            for ahead in range(n - 1 if EDGES else 1):
                scatter.edge(c, ahead)
            computed += 1
        elif step < n - 1:
            if not EDGES:
                scatter.edge(c, step)
            scatter.step(c, step)
        elif step == n - 1:
            row_work(c)
            if gather is not None:
                gather.step(c, 1)
        elif step < 2 * n - 2:
            gather.step(c, step - n + 2)
        else:
            gather.last(c)
        if filler is not None and computed == chunks:
            filler()
    for c in range(chunks):
        scatter.drain(c)
        if gather is not None:
            gather.drain(c)


def flipped(chip, bit):
    return chip + bit - 2 * bit * lax.rem(chip // bit, 2)


def bits_of(number):
    return [1 << k for k in range(number.bit_length()) if number >> k & 1]


def relative_chip(chip, relative):
    for bit in bits_of(relative):
        chip = flipped(chip, bit)
    return chip


def relative_order(chips):
    return sorted(range(chips), key=lambda r: (-len(bits_of(r)), r))


class PlaneReduce:
    def __init__(self, at, chips, rows, views, sems, out):
        self.chip, self.core = at // 2, lax.rem(at, 2)
        self.chips, self.rows, self.out = chips, rows, out
        self.core_send, self.core_recv, self.held, self.message = views
        self.core_send_sem, self.core_recv_sem, self.send_sem, self.recv_sem = sems

    def first_bit(self, relative, half):
        bits = bits_of(relative)
        return bits[0] if half == 0 else bits[-1]

    def before(self, relative, half):
        return [
            r for r in range(1, self.chips) if r - self.first_bit(r, half) == relative
        ]

    def owner(self, relative, same_core):
        return 2 * relative_chip(self.chip, relative) + (
            self.core if same_core else 1 - self.core
        )

    def half_rows(self, half):
        return pl.ds(half * (self.rows // 2), self.rows // 2)

    def core_copy(self, relative):
        return pltpu.make_async_remote_copy(
            src_ref=self.core_send(relative),
            dst_ref=self.core_recv(relative),
            send_sem=self.core_send_sem.at[relative],
            recv_sem=self.core_recv_sem.at[relative],
            device_id={"dp": 2 * self.chip + 1 - self.core},
        )

    def message_copy(self, relative, half):
        span = self.half_rows(half)
        target = flipped(self.chip, self.first_bit(relative, half))
        return pltpu.make_async_remote_copy(
            src_ref=self.held(relative).at[span],
            dst_ref=self.message(relative).at[span],
            send_sem=self.send_sem.at[relative, half],
            recv_sem=self.recv_sem.at[relative, half],
            device_id={"dp": 2 * target + self.core},
        )

    def push(self, relative, half):
        span = self.half_rows(half)
        for r in self.before(relative, half):
            self.message_copy(r, half).wait_recv()
            held = self.held(relative)
            held[span] = (
                held[span].astype(F32) + self.message(r)[span].astype(F32)
            ).astype(BF)
        self.message_copy(relative, half).start()

    def finish(self):
        for half in range(2):
            span = self.half_rows(half)
            for r in self.before(0, half):
                self.message_copy(r, half).wait_recv()
                self.out[span] += self.message(r)[span].astype(F32)

    def drain_core(self, relative):
        self.core_copy(relative).wait_send()

    def drain(self):
        for r in range(1, self.chips):
            for half in range(2):
                self.message_copy(r, half).wait_send()


def plane_sems(chips):
    return [pltpu.SemaphoreType.DMA((chips,))] * 2 + [pltpu.SemaphoreType.DMA((chips, 2))] * 2


def stage_barrier(me, n, at, chips):
    barrier = pltpu.get_barrier_semaphore()

    @pl.when(me > 0)
    def _():
        pl.semaphore_signal(barrier, inc=1, device_id={"mp": me - 1})

    @pl.when(me < n - 1)
    def _():
        pl.semaphore_signal(barrier, inc=1, device_id={"mp": me + 1})

    count = signal_partners(barrier, at, chips)
    pl.semaphore_wait(barrier, count + jnp.minimum(me, 1) + jnp.minimum(n - 1 - me, 1))


def signal_partners(sem, at, chips):
    chip, core = at // 2, lax.rem(at, 2)
    pl.semaphore_signal(sem, inc=1, device_id={"dp": 2 * chip + 1 - core})
    bits = [1 << k for k in range(chips.bit_length() - 1)]
    for bit in bits:
        pl.semaphore_signal(sem, inc=1, device_id={"dp": 2 * flipped(chip, bit) + core})
    return 1 + len(bits)


def inverse_rms(rows):
    return lax.rsqrt(jnp.mean(rows * rows, axis=1, keepdims=True) + EPS)


def norm_back(values, inverse, gain_row, upstream):
    weighted = upstream * gain_row
    mean_term = jnp.mean(weighted * values, axis=1, keepdims=True)
    grad_values = inverse * weighted - values * (inverse * inverse * inverse) * mean_term
    return (grad_values, jnp.sum(upstream * values * inverse, axis=0, keepdims=True))


def scatter_scratch(n, rows, width):
    return [
        pltpu.VMEM((CHUNKS, n * rows, width), BF),
        pltpu.VMEM((CHUNKS, n - 1, 2, rows, width), BF),
        pltpu.SemaphoreType.DMA((CHUNKS, n - 1, 2)),
        pltpu.SemaphoreType.DMA((CHUNKS, n - 1, 2)),
        pltpu.VMEM((rows, width), F32),
    ]


def gather_scratch(n, rows, width):
    return [
        pltpu.VMEM((CHUNKS, rows, width), BF),
        pltpu.SemaphoreType.DMA((CHUNKS, n - 1, 2)),
        pltpu.SemaphoreType.DMA((CHUNKS, n - 1, 2)),
        pltpu.SemaphoreType.DMA((CHUNKS,)),
    ]


def chunk_span(c, rows):
    return pl.ds(c * rows, rows)


def make_gather(n, me, rows, own, full, send_sem, recv_sem, local_sem):
    return LineGather(
        n,
        me,
        lambda c: own.at[c],
        lambda block, c: full.at[block, chunk_span(c, rows)],
        send_sem,
        recv_sem,
        local_sem,
    )


def peer_barrier(axes):
    barrier = pltpu.get_barrier_semaphore()
    count = 0
    for name, index, size in axes:
        for shift in range(1, size):
            pl.semaphore_signal(barrier, inc=1, device_id={name: lax.rem(index + shift, size)})
            count += 1
    return lambda: pl.semaphore_wait(barrier, count)


def exchange(name, index, size, src, recv, send_sem, recv_sem):
    def copy(shift):
        peer = lax.rem(index + shift, size)
        return pltpu.make_async_remote_copy(
            src_ref=src(peer),
            dst_ref=recv.at[shift - 1],
            send_sem=send_sem.at[shift - 1],
            recv_sem=recv_sem.at[shift - 1],
            device_id={name: peer},
        )

    return [copy(shift) for shift in range(1, size)]


class PlaneGather:
    def __init__(self, at, chips, rows, slot, sems):
        self.chip, self.core = at // 2, lax.rem(at, 2)
        self.chips, self.rows, self.slot = chips, rows, slot
        self.core_send_sem, self.core_recv_sem, self.send_sem, self.recv_sem = sems
        self.arrived = set()

    def last_bit(self, relative, half):
        bits = bits_of(relative)
        return bits[-1] if half == 0 else bits[0]

    def place(self, relative, same_core=True):
        return self.slot(
            2 * relative_chip(self.chip, relative) + (self.core if same_core else 1 - self.core)
        )

    def copy(self, relative, half):
        bit = self.last_bit(relative, half)
        view = self.place(relative - bit).at[pl.ds(half * (self.rows // 2), self.rows // 2)]
        return pltpu.make_async_remote_copy(
            src_ref=view,
            dst_ref=view,
            send_sem=self.send_sem.at[relative, half],
            recv_sem=self.recv_sem.at[relative, half],
            device_id={"dp": 2 * flipped(self.chip, bit) + self.core},
        )

    def core_copy(self, relative, same_core):
        view = self.place(relative, same_core)
        return pltpu.make_async_remote_copy(
            src_ref=view,
            dst_ref=view,
            send_sem=self.core_send_sem.at[relative],
            recv_sem=self.core_recv_sem.at[relative],
            device_id={"dp": 2 * self.chip + 1 - self.core},
        )

    def ensure(self, relative, half):
        if relative > 0 and (relative, half) not in self.arrived:
            self.arrived.add((relative, half))
            self.copy(relative, half).wait_recv()

    def send(self, passed_on):
        for count in range(1, self.chips.bit_length()):
            for r in range(1, self.chips):
                for half in range(2):
                    if len(bits_of(r)) == count and (count > 1) == passed_on:
                        self.ensure(r - self.last_bit(r, half), half)
                        self.copy(r, half).start()
        if not passed_on:
            self.core_copy(0, True).start()

    def swap(self, relatives):
        for r in relatives:
            for half in range(2):
                self.ensure(r, half)
            self.core_copy(r, True).start()

    def finish(self):
        for r in range(self.chips):
            self.core_copy(r, False).wait_recv()

    def drain(self):
        for r in range(self.chips):
            self.core_copy(r, True).wait_send()
            for half in range(2):
                if r > 0:
                    self.copy(r, half).wait_send()


def front_kernel(
    n, n_dp, rows, model_width, x, wq, wk, wv, wo, gains, wg,
    full, qkv, full_qkv, full_out, gain_parts, q_inv, k_inv, full_gate,
    send_sem, recv_sem, local_sem, gain_recv, gain_send_sem, gain_recv_sem,
    vqkv, vout, save_sem, x_buf, x_sem, squares,
    held, sum_recv, turned, sum_send_sem, sum_recv_sem, gate_sem, *plane,
):
    me, at = lax.axis_index("mp"), lax.axis_index("dp")
    peer_barrier((("mp", me, n), ("dp", at, n_dp)))()
    gather = LineGather(
        n,
        me,
        lambda c: x.at[chunk_span(c, rows)],
        lambda index, c: full.at[index, chunk_span(c, rows)],
        send_sem,
        recv_sem,
        local_sem,
    )
    for c in range(CHUNKS):
        gather.step(c, 1)
    chips = n_dp // 2
    part_width, width = wq.shape
    row_count = rows * CHUNKS

    def part(owner):
        return pl.ds(pl.multiple_of(owner * part_width, part_width), part_width)

    by_qkv = PlaneGather(at, chips, part_width, lambda owner: vqkv.at[part(owner)], plane[:4])
    by_out = PlaneGather(at, chips, width, lambda owner: vout.at[:, part(owner)], plane[4:8])
    by_gate = PlaneGather(
        at, chips, part_width, lambda owner: full_gate.at[part(owner)], plane[8:]
    )
    gate_copy = pltpu.make_async_copy(wg, full_gate.at[part(at)], gate_sem)
    gate_copy.start()
    for k, weight in enumerate((wq, wk, wv)):
        vqkv[part(at), k * width : (k + 1) * width] = weight[...]
    by_qkv.send(False)
    vout[:, part(at)] = wo[...]
    copies = exchange(
        "dp", at, n_dp, lambda peer: gains, gain_recv, gain_send_sem, gain_recv_sem
    )
    for copy in copies:
        copy.start()

    def block(index, source):
        load = pltpu.make_async_copy(source, x_buf, x_sem)
        load.start()
        load.wait()
        here = pl.ds(pl.multiple_of(index * row_count, row_count), row_count)

        @pl.loop(0, 3)
        def _(tile):
            cols = pl.ds(pl.multiple_of(tile * width, width), width)
            value = plain_dot(x_buf[...], vqkv[:, cols])
            qkv[here, cols] = value
            squares[tile] = jnp.sum(value * value, axis=1, keepdims=True)

        held[:, here] = columns_to_rows(squares[0], squares[1])

    def blocks_at(step):
        @pl.loop(0, 2)
        def _(side):
            index = me - step + 2 * step * side

            @pl.when((index >= 0) & (index < n))
            def _():
                block(index, full.at[index])

    saves = [
        pltpu.make_async_copy(vqkv, full_qkv, save_sem.at[0]),
        pltpu.make_async_copy(vout, full_out, save_sem.at[1]),
    ]
    early = [r for r in range(1, chips) if len(bits_of(r)) == 1]
    late = [r for r in range(1, chips) if len(bits_of(r)) > 1]

    def next_weights():
        by_qkv.send(True)
        by_out.send(False)
        gate_copy.wait()
        by_gate.send(False)

    def qkv_here():
        by_qkv.finish()
        saves[0].start()
        block(me, x)

    def out_here():
        by_out.swap(late)
        by_out.finish()
        saves[1].start()

    hooks = {
        0: next_weights,
        3: lambda: by_qkv.swap(early),
        4: lambda: by_qkv.swap(late),
        5: qkv_here,
        6: lambda: by_out.send(True),
        7: lambda: (by_out.swap(early), by_gate.send(True)),
        8: out_here,
        9: lambda: by_gate.swap(early),
    }
    ready, number = 1, 0
    for step in range(2, n + 1):
        for c in range(CHUNKS):
            if step < n:
                gather.step(c, step)
            else:
                gather.last(c)
            if number in hooks:
                hooks.pop(number)()
            number += 1
        while number > 5 and ready < step:
            blocks_at(ready)
            ready += 1
    for hook in hooks.values():
        hook()
    while ready < n:
        blocks_at(ready)
        ready += 1
    gain_parts[at] = gains[...]
    for shift, copy in enumerate(copies, 1):
        copy.wait_recv()
        gain_parts[lax.rem(at + n_dp - shift, n_dp)] = gain_recv[shift - 1]
    by_gate.swap(late)
    q_sum, k_sum = sum_held(n, me, held, sum_recv, turned, sum_send_sem, sum_recv_sem)
    q_inv[...] = lax.rsqrt(q_sum / model_width + EPS)
    k_inv[...] = lax.rsqrt(k_sum / model_width + EPS)
    for c in range(CHUNKS):
        gather.drain(c)
    for copy in copies:
        copy.wait_send()
    by_gate.finish()
    for gathered in (by_qkv, by_out, by_gate):
        gathered.drain()
    for copy in saves:
        copy.wait()


def front(n, n_dp, block, wq, wk, wv, wo, gains, wg):
    row_count, model_width = block.shape
    rows = row_count // CHUNKS
    size = n * row_count
    width = wq.shape[1]
    chips = n_dp // 2
    column = jax.ShapeDtypeStruct((size, 1), F32)
    return pl.pallas_call(
        functools.partial(front_kernel, n, n_dp, rows, model_width),
        out_shape=(
            jax.ShapeDtypeStruct((n,) + block.shape, block.dtype),
            jax.ShapeDtypeStruct((size, 3 * width), F32),
            jax.ShapeDtypeStruct((model_width, 3 * width), BF),
            jax.ShapeDtypeStruct((width, model_width), BF),
            jax.ShapeDtypeStruct((n_dp,) + gains.shape, F32),
            column,
            column,
            jax.ShapeDtypeStruct((model_width, wg.shape[1]), BF),
        ),
        in_specs=[VMEM] * 7,
        out_specs=(HBM, VMEM, HBM, HBM, VMEM, VMEM, VMEM, HBM),
        scratch_shapes=gather_scratch(n, rows, model_width)[1:]
        + [
            pltpu.VMEM((n_dp - 1,) + gains.shape, F32),
            pltpu.SemaphoreType.DMA((n_dp - 1,)),
            pltpu.SemaphoreType.DMA((n_dp - 1,)),
            pltpu.VMEM((model_width, 3 * width), BF),
            pltpu.VMEM((width, model_width), BF),
            pltpu.SemaphoreType.DMA((2,)),
            pltpu.VMEM((row_count, model_width), BF),
            pltpu.SemaphoreType.DMA,
            pltpu.VMEM((3, row_count, 1), F32),
        ]
        + sum_scratch(n, size)
        + [pltpu.SemaphoreType.DMA]
        + plane_sems(chips) * 3,
        compiler_params=pltpu.CompilerParams(
            collective_id=0, has_side_effects=True, vmem_limit_bytes=63 * MIB
        ),
        name="front",
        cost_estimate=cost(80),
    )(block, wq, wk, wv, wo, gains, wg)


class WeightTiles:
    def __init__(self, source, held, sem, axis, size):
        self.source, self.held, self.sem, self.axis, self.size = source, held, sem, axis, size
        self.count = source.shape[axis] // size

    def at(self, ref, tile):
        span = pl.ds(pl.multiple_of(tile * self.size, self.size), self.size)
        return ref.at[:, span] if self.axis == 1 else ref.at[span]

    def copy(self, tile):
        return pltpu.make_async_copy(
            self.at(self.source, tile), self.at(self.held, tile), self.sem.at[tile]
        )

    def start(self):
        for tile in range(self.count):
            self.copy(tile).start()


def middle_kernel(
    n, n_dp, rows, att, wo, wg, wu, wd, x, upstream_in, row_valid, mlp_scale, attn_scale,
    h_full, output, dm_full, hidden_out, mlp_gain, middle_grad, da_full, attn_gain, gate_out, up_out,
    part, recv, rs_send_sem, rs_recv_sem, total, own, ag_send_sem, ag_recv_sem, local_sem,
    vg, vu, vd, wsem, in_buf, in_sem, gate_all, up_all, hidden_buf, hidden_sem, packed,
    middle, branch, mg_sem, h_buf, h_sem, extra, ready, *more,
):
    me, at = lax.axis_index("mp"), lax.axis_index("dp")
    width, hidden_width = vg.shape
    local_width = wo.shape[0]
    chips = n_dp // 2
    part_width = width // n_dp
    plane, more = more[:16], more[16:]
    v_out = more[0] if more else gate_all.at[pl.ds(0, local_width)]
    v_att = up_all.at[:, pl.ds(0, local_width)]

    def start(copies):
        for copy in copies:
            copy.start()

    def wait(copies):
        for copy in copies:
            copy.wait()

    def weight_part(owner):
        return pl.ds(pl.multiple_of(owner * part_width, part_width), part_width)

    by_up = PlaneGather(at, chips, part_width, lambda owner: vu.at[weight_part(owner)], plane[8:12])
    by_down = PlaneGather(
        at, chips, hidden_width, lambda owner: vd.at[:, weight_part(owner)], plane[12:]
    )
    own_weights = [
        pltpu.make_async_copy(wu, by_up.place(0), wsem.at[0]),
        pltpu.make_async_copy(wd, by_down.place(0), wsem.at[1]),
    ]
    gate_copy = pltpu.make_async_copy(wg, vg, wsem.at[2])
    att_copies = [
        pltpu.make_async_copy(wo, v_out, wsem.at[3]),
        pltpu.make_async_copy(att, v_att, wsem.at[4]),
    ]
    start(att_copies)
    start(own_weights)
    gate_copy.start()
    stage_barrier(me, n, at, chips)
    wait(own_weights)
    by_up.send(False)

    scatter = LineScatter(n, me, rows, part, recv, rs_send_sem, rs_recv_sem)
    gathers = [
        make_gather(n, me, rows, own, full, ag_send_sem, ag_recv_sem, local_sem)
        for full in (h_full, dm_full, da_full)
    ]

    def in_copies(phase, c):
        source = gathers[phase - 1].full
        return [
            pltpu.make_async_copy(
                source(j, c), in_buf.at[c % 2, pl.ds(j * rows, rows)], in_sem.at[c % 2, j]
            )
            for j in range(n)
        ]

    def attend_out(c):
        if c == 0:
            wait(att_copies)
        block_rows = rows * CHUNKS
        for j in range(n):
            packed[j * rows : (j + 1) * rows] = v_att[
                j * block_rows + c * rows : j * block_rows + (c + 1) * rows
            ]

        @pl.loop(0, width // TILE)
        def _(tile):
            cols = pl.ds(pl.multiple_of(tile * TILE, TILE), TILE)
            part[c, :, cols] = plain_dot(packed[...], v_out[:, cols]).astype(BF)

    def attend_rows(c):
        scatter.total(c, total)
        span = chunk_span(c, rows)
        value = total[...]
        branch[span] = value
        new = x[span].astype(F32) + value * inverse_rms(value) * attn_scale[...]
        middle[span] = new
        own[c] = new.astype(BF)

    def hidden_copies(c):
        return [
            pltpu.make_async_copy(
                hidden_buf.at[c % 2, pl.ds(j * rows, rows)],
                hidden_out.at[j, chunk_span(c, rows)],
                hidden_sem.at[c % 2, j],
            )
            for j in range(n)
        ]

    def clear(phase, c):
        scatter.drain(c)
        gathers[phase - 1].drain_sends(c)
        wait(in_copies(phase, c))

    def forward(c):
        here = pl.ds(c * n * rows, n * rows)
        slot = c % 2
        clear(1, c)
        if c == 0:
            by_up.finish()
            gate_copy.wait()
        if c >= 2:
            wait(hidden_copies(c - 2))

        @pl.loop(0, hidden_width // TILE)
        def _(tile):
            cols = pl.ds(pl.multiple_of(tile * TILE, TILE), TILE)
            gate = plain_dot(in_buf[slot], vg[:, cols])
            up = plain_dot(in_buf[slot], vu[:, cols])
            gate_all[here, cols] = gate.astype(BF)
            up_all[here, cols] = up.astype(BF)
            hidden_buf[slot, :, cols] = (gate * jax.nn.sigmoid(gate) * up).astype(BF)

        start(hidden_copies(c))
        if c == 0:
            by_down.swap(late_chips)
            by_down.finish()

        @pl.loop(0, width // TILE)
        def _(tile):
            cols = pl.ds(pl.multiple_of(tile * TILE, TILE), TILE)
            part[c, :, cols] = plain_dot(hidden_buf[slot], vd[:, cols]).astype(BF)

    def backward(c):
        here = pl.ds(c * n * rows, n * rows)
        clear(2, c)

        @pl.loop(0, hidden_width // TILE)
        def _(tile):
            cols = pl.ds(pl.multiple_of(tile * TILE, TILE), TILE)
            hidden_grad = outer_dot(in_buf[c % 2], vd[cols, :])
            gate = gate_all[here, cols].astype(F32)
            up = up_all[here, cols].astype(F32)
            sigmoid = jax.nn.sigmoid(gate)
            gate_all[here, cols] = (
                hidden_grad * up * sigmoid * (1.0 + gate * (1.0 - sigmoid))
            ).astype(BF)
            up_all[here, cols] = (hidden_grad * gate * sigmoid).astype(BF)

        @pl.loop(0, width // TILE)
        def _(tile):
            cols = pl.ds(pl.multiple_of(tile * TILE, TILE), TILE)
            part[c, :, cols] = (
                outer_dot(gate_all[here], vg[cols, :]) + outer_dot(up_all[here], vu[cols, :])
            ).astype(BF)

        if c + 1 == CHUNKS:
            for last in range(max(CHUNKS - 2, 0), CHUNKS):
                wait(hidden_copies(last))
            for gathered in (by_up, by_down):
                gathered.drain()
            start(h_copies(0))
            signal_partners(ready, at, chips)

    def mg_copy(c):
        return pltpu.make_async_copy(
            middle.at[chunk_span(c, rows)], middle_grad.at[chunk_span(c, rows)], mg_sem.at[c]
        )

    def forward_rows(c):
        scatter.total(c, total)
        span = chunk_span(c, rows)
        value = total[...]
        inverse = inverse_rms(value)
        output[span] = (middle[span] + value * inverse * mlp_scale[...]).astype(BF)
        upstream = upstream_in[span].astype(F32) * row_valid[span]
        grad, gain = norm_back(value, inverse, mlp_scale[...], upstream)
        own[c] = grad.astype(BF)
        mlp_gain[...] = gain if c == 0 else mlp_gain[...] + gain

    def backward_rows(c):
        scatter.total(c, total)
        span = chunk_span(c, rows)
        upstream = upstream_in[span].astype(F32) * row_valid[span] + total[...]
        middle[span] = upstream
        mg_copy(c).start()
        value = branch[span]
        grad, gain = norm_back(value, inverse_rms(value), attn_scale[...], upstream)
        own[c] = grad.astype(BF)
        attn_gain[...] = gain if c == 0 else attn_gain[...] + gain

    block_width = pl.ds(0, hidden_width)

    def slot_at(index):
        for ref in (vg, vu, vd):
            count = ref.shape[0] // part_width
            if index < count:
                return ref.at[pl.ds(index * part_width, part_width), block_width]
            index -= count
        for ref in (hidden_buf, in_buf):
            if index < ref.shape[0]:
                return ref.at[index, pl.ds(0, part_width), block_width]
            index -= ref.shape[0]
        return extra.at[index]

    reduces = []
    for which, out in enumerate((gate_out, up_out)):
        first = chips + 3 * chips * which
        views = (
            lambda r: slot_at(r),
            lambda r, first=first: slot_at(first + r),
            lambda r, first=first: slot_at(first + chips + r),
            lambda r, first=first: slot_at(first + 2 * chips + r - 1),
        )
        reduces.append(
            PlaneReduce(at, chips, part_width, views, plane[4 * which : 4 * which + 4], out)
        )
    order = relative_order(chips)
    jobs = [
        (which, same_core, r)
        for which in range(2)
        for same_core in (False, True)
        for r in order
    ]

    def h_copies(index):
        which, same_core, r = jobs[index]
        first = reduces[which].owner(r, same_core) * part_width
        cols = pl.ds(pl.multiple_of(first, part_width), part_width)
        return [
            pltpu.make_async_copy(
                h_full.at[j, :, cols], h_buf.at[index % 2, j], h_sem.at[index % 2, j]
            )
            for j in range(n)
        ]

    def weight_block(index):
        which, same_core, r = jobs[index]
        reduce = reduces[which]
        grad = (gate_all, up_all)[which]
        if index == 0:
            pl.semaphore_wait(ready, 1 + len(bits_of(chips - 1)))
        wait(h_copies(index))
        if index + 1 < len(jobs):
            start(h_copies(index + 1))
        if same_core:
            reduce.core_copy(r).wait_recv()
        elif which == 1:
            reduces[0].drain_core(r)
        left = jnp.concatenate(
            [
                h_buf[index % 2, j, c * rows : (c + 1) * rows]
                for c in range(CHUNKS)
                for j in range(n)
            ],
            axis=0,
        )

        @pl.loop(0, hidden_width // TILE)
        def _(tile):
            cols = pl.ds(pl.multiple_of(tile * TILE, TILE), TILE)
            block = inner_dot(left, grad[:, cols])
            if not same_core:
                reduce.core_send(r)[:, cols] = block.astype(BF)
            else:
                block = block + reduce.core_recv(r)[:, cols].astype(F32)
                if r > 0:
                    reduce.held(r)[:, cols] = block.astype(BF)
                else:
                    reduce.out[:, cols] = block

        if not same_core:
            reduce.core_copy(r).start()
        elif r > 0:
            for half in range(2):
                if not reduce.before(r, half):
                    reduce.push(r, half)

    work = []
    for index, (which, same_core, r) in enumerate(jobs):
        work.append(functools.partial(weight_block, index))
        if same_core and r == order[-1]:
            for late in order:
                for half in range(2):
                    if late > 0 and reduces[which].before(late, half):
                        work.append(functools.partial(reduces[which].push, late, half))
    pending = iter(work)

    early_chips = [r for r in range(1, chips) if len(bits_of(r)) == 1]
    late_chips = [r for r in range(1, chips) if len(bits_of(r)) > 1]
    hooks = {
        HOOKS[0]: lambda: (by_up.send(True), by_down.send(False)),
        HOOKS[1]: lambda: by_up.swap(early_chips),
        HOOKS[2]: lambda: by_up.swap(late_chips),
        HOOKS[3]: lambda: by_down.send(True),
        HOOKS[4]: lambda: by_down.swap(early_chips),
    }
    last_step = 2 * n - 2
    events = sorted(
        (
            max(PERIOD, last_step + 1) * phase + step + STAGGER * c - (0.5 if step == 0 else 0),
            phase,
            c,
            step,
        )
        for phase in range(3)
        for c in range(CHUNKS)
        for step in range(last_step + 1)
    )
    filling = False
    for number, (_, phase, c, step) in enumerate(events):
        gather = gathers[phase]
        if number in hooks:
            hooks.pop(number)()
        if step == 0:
            (attend_out, forward, backward)[phase](c)
            filling = filling or (phase == 2 and c + 1 == CHUNKS)
        if step < n - 1:
            scatter.edge(c, step)
            if step > 0:
                scatter.step(c, step)
        elif step == n - 1:
            (attend_rows, forward_rows, backward_rows)[phase](c)
            gather.step(c, 1)
        elif step < last_step:
            gather.step(c, step - n + 2)
        else:
            gather.last(c)
            if phase < 2:
                gather.local_copy(c).wait()
                start(in_copies(phase + 1, c))
        if filling:
            for _ in range(FILL):
                job = next(pending, None)
                if job is not None:
                    job()
    for job in pending:
        job()
    for c in range(CHUNKS):
        scatter.drain(c)
        gathers[2].drain(c)
    for reduce in reduces:
        reduce.finish()
        reduce.drain()
    for r in range(chips):
        reduces[1].drain_core(r)
    for c in range(CHUNKS):
        mg_copy(c).wait()


def middle(n, n_dp, attended, full_out, wg, wu, wd, x, out_grad, row_valid, mlp_scale, attn_scale):
    row_count, width = x.shape
    hidden_width = wg.shape[1]
    rows = row_count // CHUNKS
    size = n * row_count
    chips = n_dp // 2
    part_width = width // n_dp
    block = (part_width, hidden_width)
    slots = (2 * width + hidden_width) // part_width + 4
    extra = 7 * chips - 1 - slots
    by_rows = jax.ShapeDtypeStruct((n, row_count, width), BF)
    return pl.pallas_call(
        functools.partial(middle_kernel, n, n_dp, rows),
        out_shape=(
            by_rows,
            jax.ShapeDtypeStruct((row_count, width), BF),
            by_rows,
            jax.ShapeDtypeStruct((n, row_count, hidden_width), BF),
            jax.ShapeDtypeStruct((1, width), F32),
            jax.ShapeDtypeStruct((row_count, width), F32),
            by_rows,
            jax.ShapeDtypeStruct((1, width), F32),
            jax.ShapeDtypeStruct(block, F32),
            jax.ShapeDtypeStruct(block, F32),
        ),
        in_specs=[HBM] * 5 + [VMEM] * 5,
        out_specs=(HBM, VMEM, HBM, HBM, VMEM, HBM, HBM, VMEM, VMEM, VMEM),
        scratch_shapes=scatter_scratch(n, rows, width)
        + gather_scratch(n, rows, width)
        + [
            pltpu.VMEM((width, hidden_width), BF),
            pltpu.VMEM((width, hidden_width), BF),
            pltpu.VMEM((hidden_width, width), BF),
            pltpu.SemaphoreType.DMA((5,)),
            pltpu.VMEM((2, n * rows, width), BF),
            pltpu.SemaphoreType.DMA((2, n)),
            pltpu.VMEM((size, hidden_width), BF),
            pltpu.VMEM((size, hidden_width), BF),
            pltpu.VMEM((2, n * rows, hidden_width), BF),
            pltpu.SemaphoreType.DMA((2, n)),
            pltpu.VMEM((n * rows, attended.shape[1]), BF),
            pltpu.VMEM((row_count, width), F32),
            pltpu.VMEM((row_count, width), F32),
            pltpu.SemaphoreType.DMA((CHUNKS,)),
            pltpu.VMEM((2, n, row_count, part_width), BF),
            pltpu.SemaphoreType.DMA((2, n)),
            pltpu.VMEM((extra,) + block if extra > 0 else (1, 16, 128), BF),
            pltpu.SemaphoreType.REGULAR,
        ]
        + plane_sems(chips) * 4
        + ([pltpu.VMEM(full_out.shape, BF)] if hidden_width < width else []),
        compiler_params=pltpu.CompilerParams(
            collective_id=2, has_side_effects=True, vmem_limit_bytes=63 * MIB
        ),
        name="middle",
        cost_estimate=cost(350),
    )(attended, full_out, wg, wu, wd, x, out_grad, row_valid, mlp_scale, attn_scale)


def last_grads_kernel(
    n, n_dp, rows, grads, weight, base, inputs, att, da, attn_gain, mlp_gain, q_gain, k_gain,
    input_grad, qkv_out, out_out, gain_out,
    part, recv, rs_send_sem, rs_recv_sem, total, packed,
    x_buf, da_buf, load_sem,
    send_qkv, recv_qkv, held_qkv, message_qkv, send_out, recv_out, held_out, message_out,
    gains, gain_recv, gain_send_sem, gain_recv_sem, mp_recv, mp_send_sem, mp_recv_sem, *plane,
):
    me, at = lax.axis_index("mp"), lax.axis_index("dp")
    entered = peer_barrier((("mp", me, n), ("dp", at, n_dp)))
    width = weight.shape[0]
    block_rows = rows * CHUNKS
    local_width = att.shape[1]
    chips = n_dp // 2
    part_width = width // n_dp
    order = relative_order(chips)
    jobs = [(same_core, r) for same_core in (False, True) for r in order]

    def views(send, recv, held, message):
        return (
            lambda r: send.at[r],
            lambda r: recv.at[r],
            lambda r: held.at[r - 1],
            lambda r: message.at[r - 1],
        )

    by_qkv = PlaneReduce(
        at, chips, part_width, views(send_qkv, recv_qkv, held_qkv, message_qkv), plane[:4], qkv_out
    )
    by_out = PlaneReduce(
        at, chips, local_width, views(send_out, recv_out, held_out, message_out), plane[4:], out_out
    )

    def loads(k):
        same_core, r = jobs[k]
        first = by_qkv.owner(r, same_core) * part_width
        cols = pl.ds(pl.multiple_of(first, part_width), part_width)
        return [
            pltpu.make_async_copy(inputs.at[:, cols], x_buf.at[k % 2], load_sem.at[k % 2, 0]),
            pltpu.make_async_copy(da.at[:, cols], da_buf.at[k % 2], load_sem.at[k % 2, 1]),
        ]

    for copy in loads(0):
        copy.start()

    def compute(c):
        for j in range(n):
            packed[j * rows : (j + 1) * rows] = grads[
                j * block_rows + c * rows : j * block_rows + (c + 1) * rows
            ]

        @pl.loop(0, width // TILE)
        def _(tile):
            cols = pl.ds(pl.multiple_of(tile * TILE, TILE), TILE)
            part[c, :, cols] = outer_dot(packed[...], weight[cols, :]).astype(BF)

    scatter = LineScatter(n, me, rows, part, recv, rs_send_sem, rs_recv_sem)

    def row_work(c):
        scatter.total(c, total)
        span = chunk_span(c, rows)
        input_grad[span] = base[span] + total[...]

    def weight_block(k):
        same_core, r = jobs[k]
        slot = k % 2
        for copy in loads(k):
            copy.wait()
        if k + 1 < len(jobs):
            for copy in loads(k + 1):
                copy.start()
        if same_core:
            by_qkv.core_copy(r).wait_recv()
            by_out.core_copy(r).wait_recv()

        def keep(reduce, block, cols):
            if not same_core:
                reduce.core_send(r)[:, cols] = block.astype(BF)
                return
            block = block + reduce.core_recv(r)[:, cols].astype(F32)
            if r > 0:
                reduce.held(r)[:, cols] = block.astype(BF)
            else:
                reduce.out[:, cols] = block

        @pl.loop(0, 3)
        def _(tile):
            cols = pl.ds(pl.multiple_of(tile * local_width, local_width), local_width)
            keep(by_qkv, inner_dot(x_buf[slot], grads[:, cols]), cols)

        keep(by_out, inner_dot(att[...], da_buf[slot]), slice(None))
        for reduce in (by_qkv, by_out):
            if not same_core:
                reduce.core_copy(r).start()
            elif r > 0:
                for half in range(2):
                    if not reduce.before(r, half):
                        reduce.push(r, half)

    for index in range(n_dp):
        span = slice(index * part_width, (index + 1) * part_width)
        gains[index, :, :part_width] = attn_gain[:, span]
        gains[index, :, part_width : 2 * part_width] = mlp_gain[:, span]
        gains[index, :, 2 * part_width : 2 * part_width + local_width] = q_gain[...]
        gains[index, :, 2 * part_width + local_width :] = k_gain[...]
    gain_copies = exchange(
        "dp", at, n_dp, lambda peer: gains.at[peer], gain_recv, gain_send_sem, gain_recv_sem
    )
    mp_copies = exchange("mp", me, n, lambda peer: gain_out, mp_recv, mp_send_sem, mp_recv_sem)
    line = iter([(step, c) for c in range(CHUNKS) for step in range(1, n)])

    def line_steps(count):
        for _ in range(count):
            step, c = next(line, (None, None))
            if step is None:
                return
            if step < n - 1:
                scatter.step(c, step)
            else:
                row_work(c)

    def send_edges(c):
        for step in range(n - 1):
            scatter.edge(c, step)

    compute(0)
    entered()
    send_edges(0)
    for copy in gain_copies:
        copy.start()
    blocks = iter(range(len(jobs)))
    for c in range(1, CHUNKS):
        weight_block(next(blocks))
        compute(c)
        send_edges(c)
    for k in blocks:
        weight_block(k)
        line_steps(2)
    late = [(r, half) for r in order for half in range(2) if r > 0 and by_qkv.before(r, half)]
    for r, half in late:
        for reduce in (by_qkv, by_out):
            reduce.push(r, half)
        line_steps(1)
    gain_out[...] = gains[at]
    for shift, copy in enumerate(gain_copies, 1):
        copy.wait_recv()
        gain_out[...] += gain_recv[shift - 1]
    for copy in mp_copies:
        copy.start()
    line_steps(n * CHUNKS)
    for reduce in (by_qkv, by_out):
        reduce.finish()
    for copy in mp_copies:
        copy.wait_recv()
        copy.wait_send()
    lanes = lax.broadcasted_iota(jnp.int32, gain_out.shape, 1)
    shared = gain_out[...]
    for shift in range(1, n):
        shared = shared + mp_recv[shift - 1]
    gain_out[...] = jnp.where(lanes < 2 * part_width, shared, gain_out[...])
    for copy in gain_copies:
        copy.wait_send()
    for c in range(CHUNKS):
        scatter.drain(c)
    for reduce in (by_qkv, by_out):
        for r in range(chips):
            reduce.drain_core(r)
        reduce.drain()


def last_grads(n, n_dp, grads, weight, base, inputs, attended, da_full, *gains):
    row_count, width = base.shape
    rows = row_count // CHUNKS
    size, local_width = attended.shape
    part_width = width // n_dp
    chips = n_dp // 2
    qkv_block = (part_width, 3 * local_width)
    out_block = (local_width, part_width)
    gain_block = (1, 2 * part_width + 2 * local_width)
    return pl.pallas_call(
        functools.partial(last_grads_kernel, n, n_dp, rows),
        out_shape=(
            jax.ShapeDtypeStruct((row_count, width), F32),
            jax.ShapeDtypeStruct(qkv_block, F32),
            jax.ShapeDtypeStruct(out_block, F32),
            jax.ShapeDtypeStruct(gain_block, F32),
        ),
        in_specs=[VMEM, VMEM, VMEM, HBM, VMEM, HBM] + [VMEM] * 4,
        out_specs=(VMEM,) * 4,
        scratch_shapes=scatter_scratch(n, rows, width)
        + [
            pltpu.VMEM((n * rows, 3 * local_width), BF),
            pltpu.VMEM((2, size, part_width), BF),
            pltpu.VMEM((2, size, part_width), BF),
            pltpu.SemaphoreType.DMA((2, 2)),
        ]
        + [
            pltpu.VMEM((count,) + block, BF)
            for block in (qkv_block, out_block)
            for count in (chips, chips, chips - 1, chips - 1)
        ]
        + [pltpu.VMEM((n_dp,) + gain_block, F32), pltpu.VMEM((n_dp - 1,) + gain_block, F32)]
        + [pltpu.SemaphoreType.DMA((n_dp - 1,))] * 2
        + [pltpu.VMEM((n - 1,) + gain_block, F32)]
        + [pltpu.SemaphoreType.DMA((n - 1,))] * 2
        + plane_sems(chips) * 2,
        compiler_params=pltpu.CompilerParams(
            collective_id=4, has_side_effects=True, vmem_limit_bytes=63 * MIB
        ),
        name="last_grads",
        cost_estimate=cost(80),
    )(grads, weight, base, inputs, attended, da_full, *gains)


def turn(values, cos, sin):
    return values * cos + pltpu.roll(values, values.shape[1] // 2, 1) * sin


def turn_back(values, cos, sin):
    return values * cos + pltpu.roll(values * sin, values.shape[1] // 2, 1)


def allowed_keys(starts, first_row, rows, key_end):
    places = first_row + lax.broadcasted_iota(jnp.int32, (rows, key_end), 0)
    keys = lax.broadcasted_iota(jnp.int32, (rows, key_end), 1)
    return (keys <= places) & (keys >= starts)


def columns_to_rows(first, second):
    lanes = lax.broadcasted_iota(jnp.int32, (first.shape[0], 128), 1)
    return jnp.transpose(jnp.where(lanes == 0, first, second))[:8]


def sum_held(n, me, held, recv, turned, send_sem, recv_sem):
    copies = exchange("mp", me, n, lambda peer: held, recv, send_sem, recv_sem)
    for copy in copies:
        copy.start()
    total = held[...]
    for shift, copy in enumerate(copies, 1):
        copy.wait_recv()
        total = total + recv[shift - 1]
    for copy in copies:
        copy.wait_send()
    turned[...] = jnp.zeros_like(turned)
    turned[:8] = total
    back = jnp.transpose(turned[...])
    return back[:, 0:1], back[:, 1:2]


def sum_scratch(n, size):
    return [
        pltpu.VMEM((8, size), F32),
        pltpu.VMEM((n - 1, 8, size), F32),
        pltpu.VMEM((128, size), F32),
        pltpu.SemaphoreType.DMA((n - 1,)),
        pltpu.SemaphoreType.DMA((n - 1,)),
    ]


def attention_kernel(
    q_raw, k_raw, v_raw, q_inv, k_inv, q_gain, k_gain, cos, sin, starts,
    out, q_low, k_low, v_low, log_total,
):
    size, head = q_raw.shape
    score_scale = 1.0 / math.sqrt(head)
    q_low[...] = turn(q_raw[...] * q_inv[...] * q_gain[...], cos[...], sin[...]).astype(BF)
    k_low[...] = turn(k_raw[...] * k_inv[...] * k_gain[...], cos[...], sin[...]).astype(BF)
    v_low[...] = v_raw[...].astype(BF)
    rows = min(QUERY_ROWS, size)
    for first in range(0, size, rows):
        end = first + rows
        span = slice(first, end)
        scores = outer_dot(q_low[span], k_low[:end]) * score_scale
        scores = jnp.where(allowed_keys(starts[span], first, rows, end), scores, MASKED)
        row_max = jnp.max(scores, axis=1, keepdims=True)
        exponents = jnp.exp(scores - row_max)
        row_total = jnp.sum(exponents, axis=1, keepdims=True)
        probs = (exponents * (1.0 / row_total)).astype(BF)
        out[span] = plain_dot(probs, v_low[:end]).astype(BF)
        log_total[span] = row_max + jnp.log(row_total)


def head_specs(size, head, heads, count):
    return [pl.BlockSpec((size, head), lambda h, k=k: (0, k * heads + h)) for k in range(count)]


def attention(qkv_raw, q_inv, k_inv, q_gain, k_gain, cos, sin, starts, heads):
    size = qkv_raw.shape[0]
    head = cos.shape[1]
    column = pl.BlockSpec((size, 1), lambda h: (0, 0))
    table = pl.BlockSpec((size, head), lambda h: (0, 0))
    gain = pl.BlockSpec((1, head), lambda h: (0, h))
    by_head = pl.BlockSpec((size, head), lambda h: (0, h))
    low = jax.ShapeDtypeStruct((size, heads * head), BF)
    return pl.pallas_call(
        attention_kernel,
        grid=(heads,),
        out_shape=(low, low, low, low, jax.ShapeDtypeStruct((heads, size, 1), F32)),
        in_specs=head_specs(size, head, heads, 3)
        + [column, column, gain, gain, table, table, column],
        out_specs=(by_head,) * 4 + (pl.BlockSpec((None, size, 1), lambda h: (h, 0, 0)),),
        compiler_params=pltpu.CompilerParams(vmem_limit_bytes=63 * MIB),
        name="attention",
        cost_estimate=cost(18),
    )(qkv_raw, qkv_raw, qkv_raw, q_inv, k_inv, q_gain, k_gain, cos, sin, starts)


def attention_back_kernel(
    n, heads, model_width, qkv, q_low, k_low, v_low, out_grad, log_total,
    q_inv, k_inv, q_gain, k_gain, cos, sin, starts,
    grads, q_gain_grad, k_gain_grad,
    q_weighted, k_weighted, q_grad, k_sum, v_sum, q_dots, k_dots, *sums,
):
    me = lax.axis_index("mp")
    entered = peer_barrier((("mp", me, n),))
    size = qkv.shape[0]
    width = qkv.shape[1] // 3
    head = width // heads
    score_scale = 1.0 / math.sqrt(head)
    rows = min(QUERY_ROWS, size)
    q_dots[...] = jnp.zeros_like(q_dots)
    k_dots[...] = jnp.zeros_like(k_dots)

    @pl.loop(0, heads)
    def _(h):
        def cols(first):
            return pl.ds(pl.multiple_of(first + h * head, head), head)

        here = cols(0)
        for first in reversed(range(0, size, rows)):
            end = first + rows
            span = slice(first, end)
            scores = outer_dot(q_low[span, here], k_low[:end, here]) * score_scale
            scores = jnp.where(allowed_keys(starts[span], first, rows, end), scores, MASKED)
            probs = jnp.exp(scores - log_total[h, span])
            prob_grad = outer_dot(out_grad[span, here], v_low[:end, here])
            probs_low = probs.astype(BF)
            weighted = probs * prob_grad
            score_grad = (
                weighted - probs * jnp.sum(weighted, axis=1, keepdims=True)
            ).astype(BF)
            q_grad[span] = plain_dot(score_grad, k_low[:end, here]) * score_scale
            k_extra = inner_dot(score_grad, q_low[span, here])
            v_extra = inner_dot(probs_low, out_grad[span, here])
            if end == size:
                k_sum[...] = k_extra
                v_sum[...] = v_extra
            else:
                k_sum[:end] += k_extra
                v_sum[:end] += v_extra
        for first, inv, gain, grad, factor, weighted_out, dots, gain_grad in (
            (0, q_inv, q_gain, q_grad, None, q_weighted, q_dots, q_gain_grad),
            (width, k_inv, k_gain, k_sum, score_scale, k_weighted, k_dots, k_gain_grad),
        ):
            raw = qkv[:, cols(first)]
            value = grad[...] if factor is None else grad[...] * factor
            normed = turn_back(value, cos[...], sin[...])
            weighted = normed * gain[:, here]
            weighted_out[:, here] = weighted
            gain_grad[:, here] = jnp.sum(normed * raw * inv[...], axis=0, keepdims=True)
            dots[...] += jnp.sum(weighted * raw, axis=1, keepdims=True)
        grads[:, cols(2 * width)] = v_sum[...].astype(BF)

    held = sums[0]
    held[...] = columns_to_rows(q_dots[...], k_dots[...])
    entered()
    q_total, k_total = sum_held(n, me, *sums)
    for first, inv, weighted, dots in (
        (0, q_inv, q_weighted, q_total),
        (width, k_inv, k_weighted, k_total),
    ):
        scale = inv[...]
        factor = scale * scale * scale * (dots / model_width)
        grads[:, first : first + width] = (
            scale * weighted[...] - qkv[:, first : first + width] * factor
        ).astype(BF)


def attention_back(
    n, heads, model_width, qkv_raw, q_low, k_low, v_low, out_grad, log_total, q_inv, k_inv,
    q_gain, k_gain, cos, sin, starts,
):
    size, width = q_low.shape
    head = width // heads
    gains = jax.ShapeDtypeStruct((1, width), F32)
    return pl.pallas_call(
        functools.partial(attention_back_kernel, n, heads, model_width),
        out_shape=(jax.ShapeDtypeStruct((size, 3 * width), BF), gains, gains),
        in_specs=[VMEM] * 13,
        out_specs=(VMEM,) * 3,
        scratch_shapes=[pltpu.VMEM((size, width), F32)] * 2
        + [pltpu.VMEM((size, head), F32)] * 3
        + [pltpu.VMEM((size, 1), F32)] * 2
        + sum_scratch(n, size),
        compiler_params=pltpu.CompilerParams(
            collective_id=6, has_side_effects=True, vmem_limit_bytes=63 * MIB
        ),
        name="attention_back",
        cost_estimate=cost(30),
    )(
        qkv_raw, q_low, k_low, v_low, out_grad, log_total, q_inv, k_inv, q_gain, k_gain,
        cos, sin, starts,
    )


def local(
    layer_input,
    query_weight,
    key_weight,
    value_weight,
    out_weight,
    gate_weight,
    up_weight,
    down_weight,
    query_gain,
    key_gain,
    attn_gain,
    mlp_gain,
    seq_lens,
    out_grad,
):
    n = lax.axis_size("mp")
    n_dp = lax.axis_size("dp")
    me = lax.axis_index("mp")
    row_count, model_width = layer_input.shape
    group_size = row_count * n
    local_heads, gain_part = query_gain.shape
    head_size = gain_part * n_dp
    local_width = local_heads * head_size

    head_part = local_heads * gain_part
    width_part = attn_gain.shape[0]
    own_gains = jnp.concatenate(
        [attn_gain, mlp_gain, query_gain.reshape(head_part), key_gain.reshape(head_part)]
    ).astype(F32)[None]
    inputs_full, qkv_raw, full_qkv, full_out, gain_parts, query_inv, key_inv, full_gate = front(
        n, n_dp, layer_input, query_weight, key_weight, value_weight, out_weight, own_gains,
        gate_weight,
    )
    inputs_full = inputs_full.reshape(group_size, model_width)
    gain_parts = gain_parts[:, 0]

    def head_gain(first):
        piece = gain_parts[:, first : first + head_part].reshape(n_dp, local_heads, gain_part)
        return piece.transpose(1, 0, 2).reshape(1, local_width)

    query_scale = head_gain(2 * width_part)
    key_scale = head_gain(2 * width_part + head_part)
    attn_scale = gain_parts[:, :width_part].reshape(1, model_width)
    mlp_scale = gain_parts[:, width_part : 2 * width_part].reshape(1, model_width)

    starts, positions, valid = layout(seq_lens[0], group_size)
    starts = starts[:, None]
    cos_table, sin_table = rotary_tables(positions, head_size)
    row_valid = lax.dynamic_slice_in_dim(valid, me * row_count, row_count, 0).astype(F32)[:, None]

    attended, query_low, key_low, value_low, log_total = attention(
        qkv_raw, query_inv, key_inv, query_scale, key_scale, cos_table, sin_table, starts,
        local_heads,
    )
    (
        middle_full, layer_output, mlp_grad_full, hidden, mlp_gain_part, middle_grad, branch_full,
        attn_gain_part, grad_gate, grad_up,
    ) = middle(
        n, n_dp, attended, full_out, full_gate, up_weight, down_weight, layer_input, out_grad,
        row_valid, mlp_scale, attn_scale,
    )

    def flat(rows):
        return rows.reshape(group_size, rows.shape[-1])

    branch_full = flat(branch_full)
    down_part = inner_dot(flat(hidden), flat(mlp_grad_full)).astype(BF)
    branch_full, down_part = lax.optimization_barrier((branch_full, down_part))
    grad_down = lax.psum_scatter(down_part, "dp", scatter_dimension=1, tiled=True)

    mixed_grad = outer_dot(branch_full, full_out).astype(BF)
    qkv_grad, query_gain_part, key_gain_part = attention_back(
        n, local_heads, model_width, qkv_raw, query_low, key_low, value_low, mixed_grad, log_total,
        query_inv, key_inv, query_scale, key_scale, cos_table, sin_table, starts,
    )

    input_grad, grad_qkv, grad_out, gain_sums = last_grads(
        n, n_dp, qkv_grad, full_qkv, middle_grad, inputs_full, attended, branch_full,
        attn_gain_part, mlp_gain_part, query_gain_part, key_gain_part,
    )
    gain_sums = gain_sums[0]
    heads_at = 2 * width_part
    head_sums = lax.dynamic_index_in_dim(
        gain_sums[heads_at:].reshape(2, local_heads, n_dp, gain_part),
        lax.axis_index("dp"),
        2,
        keepdims=False,
    )
    return (
        layer_output,
        input_grad,
        grad_qkv[:, :local_width],
        grad_qkv[:, local_width : 2 * local_width],
        grad_qkv[:, 2 * local_width :],
        grad_out,
        grad_gate,
        grad_up,
        grad_down.astype(F32),
        head_sums[0],
        head_sums[1],
        gain_sums[:width_part],
        gain_sums[width_part:heads_at],
    )


def solution(mesh):
    return jax.shard_map(
        local,
        mesh=mesh,
        in_specs=(
            P(("dp", "mp"), None),
            P("dp", "mp"),
            P("dp", "mp"),
            P("dp", "mp"),
            P("mp", "dp"),
            P("dp", "mp"),
            P("dp", "mp"),
            P("mp", "dp"),
            P("mp", "dp"),
            P("mp", "dp"),
            P("dp"),
            P("dp"),
            P("dp", None),
            P(("dp", "mp"), None),
        ),
        out_specs=(
            P(("dp", "mp"), None),
            P(("dp", "mp"), None),
            P("dp", "mp"),
            P("dp", "mp"),
            P("dp", "mp"),
            P("mp", "dp"),
            P("dp", "mp"),
            P("dp", "mp"),
            P("mp", "dp"),
            P("mp", "dp"),
            P("mp", "dp"),
            P("dp"),
            P("dp"),
        ),
        check_vma=False,
    )
```

```python
import functools
import math

import jax
import jax.numpy as jnp
from jax import lax
from jax.experimental import pallas as pl
from jax.experimental.pallas import tpu as pltpu
from jax.sharding import PartitionSpec as P

EPS = 1e-06
THETA = 500000.0
MASKED = -1000000000.0
CHUNKS = 4
STAGGER = 2
EDGES = False
FILL = 2
PERIOD = 8
LINE_FROM = 8
HOOKS = (3, 7, 10, 13, 16)
TILE = 512
QUERY_ROWS = 256
BF = jnp.bfloat16
F32 = jnp.float32
MIB = 1 << 20
HBM = pl.BlockSpec(memory_space=pl.ANY)
VMEM = pl.BlockSpec(memory_space=pltpu.VMEM)


def cost(micros):
    return pl.CostEstimate(
        flops=micros * 1_000_000_000, bytes_accessed=micros * 3_000_000, transcendentals=0
    )


def plain_dot(former, latter):
    return jnp.dot(former, latter, preferred_element_type=F32)


def inner_dot(former, latter):
    return lax.dot_general(
        former, latter, (((0,), (0,)), ((), ())), preferred_element_type=F32
    )


def outer_dot(former, latter):
    return lax.dot_general(
        former, latter, (((1,), (1,)), ((), ())), preferred_element_type=F32
    )


def layout(lengths, group_size):
    slot_count = lengths.shape[0]
    seq_ends = jnp.cumsum(lengths, dtype=jnp.int32)
    starts = seq_ends - lengths
    places = jnp.arange(group_size, dtype=jnp.int32)
    slot_ids = jnp.arange(slot_count, dtype=jnp.int32)
    segment = jnp.sum(
        (places[:, None] >= seq_ends[None, :]).astype(jnp.int32), axis=1, dtype=jnp.int32
    )
    chosen = (segment[:, None] == slot_ids[None, :]).astype(jnp.int32)
    padded = (segment == slot_count).astype(jnp.int32)
    begins = (
        jnp.sum(chosen * starts[None, :], axis=1, dtype=jnp.int32)
        + padded * seq_ends[slot_count - 1]
    )
    return (begins, places - begins, places < seq_ends[slot_count - 1])


def rotary_tables(positions, head_size):
    half_dim = head_size // 2
    frequency = jnp.exp(jnp.arange(half_dim, dtype=F32) * (-2.0 * math.log(THETA) / head_size))
    angles = positions.astype(F32)[:, None] * frequency[None, :]
    cos_half, sin_half = jnp.cos(angles), jnp.sin(angles)
    return (
        jnp.concatenate([cos_half, cos_half], axis=1),
        jnp.concatenate([-sin_half, sin_half], axis=1),
    )


def neighbour_barrier(me, n):
    barrier = pltpu.get_barrier_semaphore()

    @pl.when(me > 0)
    def _():
        pl.semaphore_signal(barrier, inc=1, device_id={"mp": me - 1})

    @pl.when(me < n - 1)
    def _():
        pl.semaphore_signal(barrier, inc=1, device_id={"mp": me + 1})

    pl.semaphore_wait(barrier, jnp.minimum(me, 1) + jnp.minimum(n - 1 - me, 1))


class LineGather:
    def __init__(self, n, me, own, full, send_sem, recv_sem, local_sem):
        self.n, self.me, self.own, self.full = n, me, own, full
        self.send_sem, self.recv_sem, self.local_sem = send_sem, recv_sem, local_sem

    def local_copy(self, c):
        return pltpu.make_async_copy(self.own(c), self.full(self.me, c), self.local_sem.at[c])

    def copy(self, c, step, way, block, src):
        return pltpu.make_async_remote_copy(
            src_ref=src,
            dst_ref=self.full(block, c),
            send_sem=self.send_sem.at[c, step - 1, way],
            recv_sem=self.recv_sem.at[c, step - 1, way],
            device_id={"mp": self.me + (1 if way == 0 else -1)},
        )

    def sides(self):
        return ((0, self.me), (1, self.n - 1 - self.me))

    def block_at(self, way, step):
        return self.me - step if way == 0 else self.me + step

    def step(self, c, step):
        n = self.n
        if step == 1:
            self.local_copy(c).start()
        for way, place in self.sides():
            if step > 1:

                @pl.when(place >= step - 1)
                def _(way=way):
                    block = self.block_at(way, step - 1)
                    self.copy(c, step - 1, way, block, self.own(c)).wait_recv()

            @pl.when((place >= step - 1) & (place < n - 1))
            def _(way=way):
                block = self.block_at(way, step - 1)
                src = self.own(c) if step == 1 else self.full(block, c)
                self.copy(c, step, way, block, src).start()

    def last(self, c):
        n = self.n
        for way, place in self.sides():

            @pl.when(place == n - 1)
            def _(way=way):
                block = self.block_at(way, n - 1)
                self.copy(c, n - 1, way, block, self.own(c)).wait_recv()

    def drain(self, c):
        self.local_copy(c).wait()
        self.drain_sends(c)

    def drain_sends(self, c):
        for step in range(1, self.n):
            for way, place in self.sides():

                @pl.when((place >= step - 1) & (place < self.n - 1))
                def _(way=way):
                    self.copy(c, step, way, self.me, self.own(c)).wait_send()


class LineScatter:
    def __init__(self, n, me, rows, part, recv, send_sem, recv_sem):
        self.n, self.me, self.rows = n, me, rows
        self.part, self.recv = part, recv
        self.send_sem, self.recv_sem = send_sem, recv_sem

    def piece(self, c, owner):
        first = pl.multiple_of(owner * self.rows, self.rows)
        return self.part.at[c, pl.ds(first, self.rows)]

    def copy(self, c, step, way, src):
        return pltpu.make_async_remote_copy(
            src_ref=src,
            dst_ref=self.recv.at[c, step, way],
            send_sem=self.send_sem.at[c, step, way],
            recv_sem=self.recv_sem.at[c, step, way],
            device_id={"mp": self.me + (1 if way == 0 else -1)},
        )

    def sides(self):
        return ((0, self.me), (1, self.n - 1 - self.me))

    def owner(self, way, step):
        return self.n - 1 - step + self.me if way == 0 else step - (self.n - 1 - self.me)

    def edge(self, c, step):
        for way, place in self.sides():

            @pl.when(place == 0)
            def _(way=way):
                self.copy(c, step, way, self.piece(c, self.owner(way, step))).start()

    def step(self, c, step):
        for way, place in self.sides():

            @pl.when((place > 0) & (place <= min(step, self.n - 2)))
            def _(way=way):
                piece = self.piece(c, self.owner(way, step))
                self.copy(c, step - 1, way, piece).wait_recv()
                piece[...] = (
                    piece[...].astype(F32) + self.recv[c, step - 1, way].astype(F32)
                ).astype(BF)
                self.copy(c, step, way, piece).start()

    def total(self, c, out):
        n = self.n
        out[...] = self.piece(c, self.me)[...].astype(F32)
        for way, place in self.sides():

            @pl.when(place > 0)
            def _(way=way):
                self.copy(c, n - 2, way, self.recv.at[c, n - 2, way]).wait_recv()
                out[...] += self.recv[c, n - 2, way].astype(F32)

    def drain(self, c):
        n = self.n
        for step in range(n - 1):
            for way, place in self.sides():

                @pl.when(place <= min(step, n - 2))
                def _(way=way):
                    self.copy(c, step, way, self.recv.at[c, step, way]).wait_send()


def run_line(n, chunks, stagger, compute, scatter, row_work, gather, filler=None):
    last_step = 2 * n - 2 if gather is not None else n - 1
    events = sorted(
        (step + stagger * c - (0.5 if step == 0 else 0), c, step)
        for c in range(chunks)
        for step in range(last_step + 1)
    )
    computed = 0
    for _, c, step in events:
        if step == 0:
            compute(c)
            for ahead in range(n - 1 if EDGES else 1):
                scatter.edge(c, ahead)
            computed += 1
        elif step < n - 1:
            if not EDGES:
                scatter.edge(c, step)
            scatter.step(c, step)
        elif step == n - 1:
            row_work(c)
            if gather is not None:
                gather.step(c, 1)
        elif step < 2 * n - 2:
            gather.step(c, step - n + 2)
        else:
            gather.last(c)
        if filler is not None and computed == chunks:
            filler()
    for c in range(chunks):
        scatter.drain(c)
        if gather is not None:
            gather.drain(c)


def flipped(chip, bit):
    return chip + bit - 2 * bit * lax.rem(chip // bit, 2)


def bits_of(number):
    return [1 << k for k in range(number.bit_length()) if number >> k & 1]


def relative_chip(chip, relative):
    for bit in bits_of(relative):
        chip = flipped(chip, bit)
    return chip


def relative_order(chips):
    return sorted(range(chips), key=lambda r: (-len(bits_of(r)), r))


class PlaneReduce:
    def __init__(self, at, chips, rows, views, sems, out):
        self.chip, self.core = at // 2, lax.rem(at, 2)
        self.chips, self.rows, self.out = chips, rows, out
        self.core_send, self.core_recv, self.held, self.message = views
        self.core_send_sem, self.core_recv_sem, self.send_sem, self.recv_sem = sems

    def first_bit(self, relative, half):
        bits = bits_of(relative)
        return bits[0] if half == 0 else bits[-1]

    def before(self, relative, half):
        return [
            r for r in range(1, self.chips) if r - self.first_bit(r, half) == relative
        ]

    def owner(self, relative, same_core):
        return 2 * relative_chip(self.chip, relative) + (
            self.core if same_core else 1 - self.core
        )

    def half_rows(self, half):
        return pl.ds(half * (self.rows // 2), self.rows // 2)

    def core_copy(self, relative):
        return pltpu.make_async_remote_copy(
            src_ref=self.core_send(relative),
            dst_ref=self.core_recv(relative),
            send_sem=self.core_send_sem.at[relative],
            recv_sem=self.core_recv_sem.at[relative],
            device_id={"dp": 2 * self.chip + 1 - self.core},
        )

    def message_copy(self, relative, half):
        span = self.half_rows(half)
        target = flipped(self.chip, self.first_bit(relative, half))
        return pltpu.make_async_remote_copy(
            src_ref=self.held(relative).at[span],
            dst_ref=self.message(relative).at[span],
            send_sem=self.send_sem.at[relative, half],
            recv_sem=self.recv_sem.at[relative, half],
            device_id={"dp": 2 * target + self.core},
        )

    def push(self, relative, half):
        span = self.half_rows(half)
        for r in self.before(relative, half):
            self.message_copy(r, half).wait_recv()
            held = self.held(relative)
            held[span] = (
                held[span].astype(F32) + self.message(r)[span].astype(F32)
            ).astype(BF)
        self.message_copy(relative, half).start()

    def finish(self):
        for half in range(2):
            span = self.half_rows(half)
            for r in self.before(0, half):
                self.message_copy(r, half).wait_recv()
                self.out[span] += self.message(r)[span].astype(F32)

    def drain_core(self, relative):
        self.core_copy(relative).wait_send()

    def drain(self):
        for r in range(1, self.chips):
            for half in range(2):
                self.message_copy(r, half).wait_send()


def plane_sems(chips):
    return [pltpu.SemaphoreType.DMA((chips,))] * 2 + [pltpu.SemaphoreType.DMA((chips, 2))] * 2


def stage_barrier(me, n, at, chips):
    barrier = pltpu.get_barrier_semaphore()

    @pl.when(me > 0)
    def _():
        pl.semaphore_signal(barrier, inc=1, device_id={"mp": me - 1})

    @pl.when(me < n - 1)
    def _():
        pl.semaphore_signal(barrier, inc=1, device_id={"mp": me + 1})

    count = signal_partners(barrier, at, chips)
    pl.semaphore_wait(barrier, count + jnp.minimum(me, 1) + jnp.minimum(n - 1 - me, 1))


def signal_partners(sem, at, chips):
    chip, core = at // 2, lax.rem(at, 2)
    pl.semaphore_signal(sem, inc=1, device_id={"dp": 2 * chip + 1 - core})
    bits = [1 << k for k in range(chips.bit_length() - 1)]
    for bit in bits:
        pl.semaphore_signal(sem, inc=1, device_id={"dp": 2 * flipped(chip, bit) + core})
    return 1 + len(bits)


def inverse_rms(rows):
    return lax.rsqrt(jnp.mean(rows * rows, axis=1, keepdims=True) + EPS)


def norm_back(values, inverse, gain_row, upstream):
    weighted = upstream * gain_row
    mean_term = jnp.mean(weighted * values, axis=1, keepdims=True)
    grad_values = inverse * weighted - values * (inverse * inverse * inverse) * mean_term
    return (grad_values, jnp.sum(upstream * values * inverse, axis=0, keepdims=True))


def scatter_scratch(n, rows, width):
    return [
        pltpu.VMEM((CHUNKS, n * rows, width), BF),
        pltpu.VMEM((CHUNKS, n - 1, 2, rows, width), BF),
        pltpu.SemaphoreType.DMA((CHUNKS, n - 1, 2)),
        pltpu.SemaphoreType.DMA((CHUNKS, n - 1, 2)),
        pltpu.VMEM((rows, width), F32),
    ]


def gather_scratch(n, rows, width):
    return [
        pltpu.VMEM((CHUNKS, rows, width), BF),
        pltpu.SemaphoreType.DMA((CHUNKS, n - 1, 2)),
        pltpu.SemaphoreType.DMA((CHUNKS, n - 1, 2)),
        pltpu.SemaphoreType.DMA((CHUNKS,)),
    ]


def chunk_span(c, rows):
    return pl.ds(c * rows, rows)


def make_gather(n, me, rows, own, full, send_sem, recv_sem, local_sem):
    return LineGather(
        n,
        me,
        lambda c: own.at[c],
        lambda block, c: full.at[block, chunk_span(c, rows)],
        send_sem,
        recv_sem,
        local_sem,
    )


def peer_barrier(axes):
    barrier = pltpu.get_barrier_semaphore()
    count = 0
    for name, index, size in axes:
        for shift in range(1, size):
            pl.semaphore_signal(barrier, inc=1, device_id={name: lax.rem(index + shift, size)})
            count += 1
    return lambda: pl.semaphore_wait(barrier, count)


def exchange(name, index, size, src, recv, send_sem, recv_sem):
    def copy(shift):
        peer = lax.rem(index + shift, size)
        return pltpu.make_async_remote_copy(
            src_ref=src(peer),
            dst_ref=recv.at[shift - 1],
            send_sem=send_sem.at[shift - 1],
            recv_sem=recv_sem.at[shift - 1],
            device_id={name: peer},
        )

    return [copy(shift) for shift in range(1, size)]


class PlaneGather:
    def __init__(self, at, chips, rows, slot, sems):
        self.chip, self.core = at // 2, lax.rem(at, 2)
        self.chips, self.rows, self.slot = chips, rows, slot
        self.core_send_sem, self.core_recv_sem, self.send_sem, self.recv_sem = sems
        self.arrived = set()

    def last_bit(self, relative, half):
        bits = bits_of(relative)
        return bits[-1] if half == 0 else bits[0]

    def place(self, relative, same_core=True):
        return self.slot(
            2 * relative_chip(self.chip, relative) + (self.core if same_core else 1 - self.core)
        )

    def copy(self, relative, half):
        bit = self.last_bit(relative, half)
        view = self.place(relative - bit).at[pl.ds(half * (self.rows // 2), self.rows // 2)]
        return pltpu.make_async_remote_copy(
            src_ref=view,
            dst_ref=view,
            send_sem=self.send_sem.at[relative, half],
            recv_sem=self.recv_sem.at[relative, half],
            device_id={"dp": 2 * flipped(self.chip, bit) + self.core},
        )

    def core_copy(self, relative, same_core):
        view = self.place(relative, same_core)
        return pltpu.make_async_remote_copy(
            src_ref=view,
            dst_ref=view,
            send_sem=self.core_send_sem.at[relative],
            recv_sem=self.core_recv_sem.at[relative],
            device_id={"dp": 2 * self.chip + 1 - self.core},
        )

    def ensure(self, relative, half):
        if relative > 0 and (relative, half) not in self.arrived:
            self.arrived.add((relative, half))
            self.copy(relative, half).wait_recv()

    def send(self, passed_on):
        for count in range(1, self.chips.bit_length()):
            for r in range(1, self.chips):
                for half in range(2):
                    if len(bits_of(r)) == count and (count > 1) == passed_on:
                        self.ensure(r - self.last_bit(r, half), half)
                        self.copy(r, half).start()
        if not passed_on:
            self.core_copy(0, True).start()

    def swap(self, relatives):
        for r in relatives:
            for half in range(2):
                self.ensure(r, half)
            self.core_copy(r, True).start()

    def finish(self):
        for r in range(self.chips):
            self.core_copy(r, False).wait_recv()

    def drain(self):
        for r in range(self.chips):
            self.core_copy(r, True).wait_send()
            for half in range(2):
                if r > 0:
                    self.copy(r, half).wait_send()


def front_kernel(
    n, n_dp, rows, model_width, x, wq, wk, wv, wo, gains, wg,
    full, qkv, full_qkv, full_out, gain_parts, q_inv, k_inv, full_gate,
    send_sem, recv_sem, local_sem, gain_recv, gain_send_sem, gain_recv_sem,
    vqkv, vout, save_sem, x_buf, x_sem, squares,
    held, sum_recv, turned, sum_send_sem, sum_recv_sem, gate_sem, *plane,
):
    me, at = lax.axis_index("mp"), lax.axis_index("dp")
    peer_barrier((("mp", me, n), ("dp", at, n_dp)))()
    gather = LineGather(
        n,
        me,
        lambda c: x.at[chunk_span(c, rows)],
        lambda index, c: full.at[index, chunk_span(c, rows)],
        send_sem,
        recv_sem,
        local_sem,
    )
    for c in range(CHUNKS):
        gather.step(c, 1)
    chips = n_dp // 2
    part_width, width = wq.shape
    row_count = rows * CHUNKS

    def part(owner):
        return pl.ds(pl.multiple_of(owner * part_width, part_width), part_width)

    by_qkv = PlaneGather(at, chips, part_width, lambda owner: vqkv.at[part(owner)], plane[:4])
    by_out = PlaneGather(at, chips, width, lambda owner: vout.at[:, part(owner)], plane[4:8])
    by_gate = PlaneGather(
        at, chips, part_width, lambda owner: full_gate.at[part(owner)], plane[8:]
    )
    gate_copy = pltpu.make_async_copy(wg, full_gate.at[part(at)], gate_sem)
    gate_copy.start()
    for k, weight in enumerate((wq, wk, wv)):
        vqkv[part(at), k * width : (k + 1) * width] = weight[...]
    by_qkv.send(False)
    vout[:, part(at)] = wo[...]
    copies = exchange(
        "dp", at, n_dp, lambda peer: gains, gain_recv, gain_send_sem, gain_recv_sem
    )
    for copy in copies:
        copy.start()

    def block(index, source):
        load = pltpu.make_async_copy(source, x_buf, x_sem)
        load.start()
        load.wait()
        here = pl.ds(pl.multiple_of(index * row_count, row_count), row_count)

        @pl.loop(0, 3)
        def _(tile):
            cols = pl.ds(pl.multiple_of(tile * width, width), width)
            value = plain_dot(x_buf[...], vqkv[:, cols])
            qkv[here, cols] = value
            squares[tile] = jnp.sum(value * value, axis=1, keepdims=True)

        held[:, here] = columns_to_rows(squares[0], squares[1])

    def blocks_at(step):
        @pl.loop(0, 2)
        def _(side):
            index = me - step + 2 * step * side

            @pl.when((index >= 0) & (index < n))
            def _():
                block(index, full.at[index])

    saves = [
        pltpu.make_async_copy(vqkv, full_qkv, save_sem.at[0]),
        pltpu.make_async_copy(vout, full_out, save_sem.at[1]),
    ]
    early = [r for r in range(1, chips) if len(bits_of(r)) == 1]
    late = [r for r in range(1, chips) if len(bits_of(r)) > 1]

    def next_weights():
        by_qkv.send(True)
        by_out.send(False)
        gate_copy.wait()
        by_gate.send(False)

    def qkv_here():
        by_qkv.finish()
        saves[0].start()
        block(me, x)

    def out_here():
        by_out.swap(late)
        by_out.finish()
        saves[1].start()

    hooks = {
        0: next_weights,
        3: lambda: by_qkv.swap(early),
        4: lambda: by_qkv.swap(late),
        5: qkv_here,
        6: lambda: by_out.send(True),
        7: lambda: (by_out.swap(early), by_gate.send(True)),
        8: out_here,
        9: lambda: by_gate.swap(early),
    }
    ready, number = 1, 0
    for step in range(2, n + 1):
        for c in range(CHUNKS):
            if step < n:
                gather.step(c, step)
            else:
                gather.last(c)
            if number in hooks:
                hooks.pop(number)()
            number += 1
        while number > 5 and ready < step:
            blocks_at(ready)
            ready += 1
    for hook in hooks.values():
        hook()
    while ready < n:
        blocks_at(ready)
        ready += 1
    gain_parts[at] = gains[...]
    for shift, copy in enumerate(copies, 1):
        copy.wait_recv()
        gain_parts[lax.rem(at + n_dp - shift, n_dp)] = gain_recv[shift - 1]
    by_gate.swap(late)
    q_sum, k_sum = sum_held(n, me, held, sum_recv, turned, sum_send_sem, sum_recv_sem)
    q_inv[...] = lax.rsqrt(q_sum / model_width + EPS)
    k_inv[...] = lax.rsqrt(k_sum / model_width + EPS)
    for c in range(CHUNKS):
        gather.drain(c)
    for copy in copies:
        copy.wait_send()
    by_gate.finish()
    for gathered in (by_qkv, by_out, by_gate):
        gathered.drain()
    for copy in saves:
        copy.wait()


def front(n, n_dp, block, wq, wk, wv, wo, gains, wg):
    row_count, model_width = block.shape
    rows = row_count // CHUNKS
    size = n * row_count
    width = wq.shape[1]
    chips = n_dp // 2
    column = jax.ShapeDtypeStruct((size, 1), F32)
    return pl.pallas_call(
        functools.partial(front_kernel, n, n_dp, rows, model_width),
        out_shape=(
            jax.ShapeDtypeStruct((n,) + block.shape, block.dtype),
            jax.ShapeDtypeStruct((size, 3 * width), F32),
            jax.ShapeDtypeStruct((model_width, 3 * width), BF),
            jax.ShapeDtypeStruct((width, model_width), BF),
            jax.ShapeDtypeStruct((n_dp,) + gains.shape, F32),
            column,
            column,
            jax.ShapeDtypeStruct((model_width, wg.shape[1]), BF),
        ),
        in_specs=[VMEM] * 7,
        out_specs=(HBM, VMEM, HBM, HBM, VMEM, VMEM, VMEM, HBM),
        scratch_shapes=gather_scratch(n, rows, model_width)[1:]
        + [
            pltpu.VMEM((n_dp - 1,) + gains.shape, F32),
            pltpu.SemaphoreType.DMA((n_dp - 1,)),
            pltpu.SemaphoreType.DMA((n_dp - 1,)),
            pltpu.VMEM((model_width, 3 * width), BF),
            pltpu.VMEM((width, model_width), BF),
            pltpu.SemaphoreType.DMA((2,)),
            pltpu.VMEM((row_count, model_width), BF),
            pltpu.SemaphoreType.DMA,
            pltpu.VMEM((3, row_count, 1), F32),
        ]
        + sum_scratch(n, size)
        + [pltpu.SemaphoreType.DMA]
        + plane_sems(chips) * 3,
        compiler_params=pltpu.CompilerParams(
            collective_id=0, has_side_effects=True, vmem_limit_bytes=63 * MIB
        ),
        name="front",
        cost_estimate=cost(80),
    )(block, wq, wk, wv, wo, gains, wg)


class WeightTiles:
    def __init__(self, source, held, sem, axis, size):
        self.source, self.held, self.sem, self.axis, self.size = source, held, sem, axis, size
        self.count = source.shape[axis] // size

    def at(self, ref, tile):
        span = pl.ds(pl.multiple_of(tile * self.size, self.size), self.size)
        return ref.at[:, span] if self.axis == 1 else ref.at[span]

    def copy(self, tile):
        return pltpu.make_async_copy(
            self.at(self.source, tile), self.at(self.held, tile), self.sem.at[tile]
        )

    def start(self):
        for tile in range(self.count):
            self.copy(tile).start()


def middle_kernel(
    n, n_dp, rows, att, wo, wg, wu, wd, x, upstream_in, row_valid, mlp_scale, attn_scale,
    h_full, output, dm_full, hidden_out, mlp_gain, middle_grad, da_full, attn_gain, gate_out, up_out,
    part, recv, rs_send_sem, rs_recv_sem, total, own, ag_send_sem, ag_recv_sem, local_sem,
    vg, vu, vd, wsem, in_buf, in_sem, gate_all, up_all, hidden_buf, hidden_sem, packed,
    middle, branch, mg_sem, h_buf, h_sem, extra, ready, *more,
):
    me, at = lax.axis_index("mp"), lax.axis_index("dp")
    width, hidden_width = vg.shape
    local_width = wo.shape[0]
    chips = n_dp // 2
    part_width = width // n_dp
    plane, more = more[:16], more[16:]
    v_out = more[0] if more else gate_all.at[pl.ds(0, local_width)]
    v_att = up_all.at[:, pl.ds(0, local_width)]

    def start(copies):
        for copy in copies:
            copy.start()

    def wait(copies):
        for copy in copies:
            copy.wait()

    def weight_part(owner):
        return pl.ds(pl.multiple_of(owner * part_width, part_width), part_width)

    by_up = PlaneGather(at, chips, part_width, lambda owner: vu.at[weight_part(owner)], plane[8:12])
    by_down = PlaneGather(
        at, chips, hidden_width, lambda owner: vd.at[:, weight_part(owner)], plane[12:]
    )
    own_weights = [
        pltpu.make_async_copy(wu, by_up.place(0), wsem.at[0]),
        pltpu.make_async_copy(wd, by_down.place(0), wsem.at[1]),
    ]
    gate_copy = pltpu.make_async_copy(wg, vg, wsem.at[2])
    att_copies = [
        pltpu.make_async_copy(wo, v_out, wsem.at[3]),
        pltpu.make_async_copy(att, v_att, wsem.at[4]),
    ]
    start(att_copies)
    start(own_weights)
    gate_copy.start()
    stage_barrier(me, n, at, chips)
    wait(own_weights)
    by_up.send(False)

    scatter = LineScatter(n, me, rows, part, recv, rs_send_sem, rs_recv_sem)
    gathers = [
        make_gather(n, me, rows, own, full, ag_send_sem, ag_recv_sem, local_sem)
        for full in (h_full, dm_full, da_full)
    ]

    def in_copies(phase, c):
        source = gathers[phase - 1].full
        return [
            pltpu.make_async_copy(
                source(j, c), in_buf.at[c % 2, pl.ds(j * rows, rows)], in_sem.at[c % 2, j]
            )
            for j in range(n)
        ]

    def attend_out(c):
        if c == 0:
            wait(att_copies)
        block_rows = rows * CHUNKS
        for j in range(n):
            packed[j * rows : (j + 1) * rows] = v_att[
                j * block_rows + c * rows : j * block_rows + (c + 1) * rows
            ]

        @pl.loop(0, width // TILE)
        def _(tile):
            cols = pl.ds(pl.multiple_of(tile * TILE, TILE), TILE)
            part[c, :, cols] = plain_dot(packed[...], v_out[:, cols]).astype(BF)

    def attend_rows(c):
        scatter.total(c, total)
        span = chunk_span(c, rows)
        value = total[...]
        branch[span] = value
        new = x[span].astype(F32) + value * inverse_rms(value) * attn_scale[...]
        middle[span] = new
        own[c] = new.astype(BF)

    def hidden_copies(c):
        return [
            pltpu.make_async_copy(
                hidden_buf.at[c % 2, pl.ds(j * rows, rows)],
                hidden_out.at[j, chunk_span(c, rows)],
                hidden_sem.at[c % 2, j],
            )
            for j in range(n)
        ]

    def clear(phase, c):
        scatter.drain(c)
        gathers[phase - 1].drain_sends(c)
        wait(in_copies(phase, c))

    def forward(c):
        here = pl.ds(c * n * rows, n * rows)
        slot = c % 2
        clear(1, c)
        if c == 0:
            by_up.finish()
            gate_copy.wait()
        if c >= 2:
            wait(hidden_copies(c - 2))

        @pl.loop(0, hidden_width // TILE)
        def _(tile):
            cols = pl.ds(pl.multiple_of(tile * TILE, TILE), TILE)
            gate = plain_dot(in_buf[slot], vg[:, cols])
            up = plain_dot(in_buf[slot], vu[:, cols])
            gate_all[here, cols] = gate.astype(BF)
            up_all[here, cols] = up.astype(BF)
            hidden_buf[slot, :, cols] = (gate * jax.nn.sigmoid(gate) * up).astype(BF)

        start(hidden_copies(c))
        if c == 0:
            by_down.swap(late_chips)
            by_down.finish()

        @pl.loop(0, width // TILE)
        def _(tile):
            cols = pl.ds(pl.multiple_of(tile * TILE, TILE), TILE)
            part[c, :, cols] = plain_dot(hidden_buf[slot], vd[:, cols]).astype(BF)

    def backward(c):
        here = pl.ds(c * n * rows, n * rows)
        clear(2, c)

        @pl.loop(0, hidden_width // TILE)
        def _(tile):
            cols = pl.ds(pl.multiple_of(tile * TILE, TILE), TILE)
            hidden_grad = outer_dot(in_buf[c % 2], vd[cols, :])
            gate = gate_all[here, cols].astype(F32)
            up = up_all[here, cols].astype(F32)
            sigmoid = jax.nn.sigmoid(gate)
            gate_all[here, cols] = (
                hidden_grad * up * sigmoid * (1.0 + gate * (1.0 - sigmoid))
            ).astype(BF)
            up_all[here, cols] = (hidden_grad * gate * sigmoid).astype(BF)

        @pl.loop(0, width // TILE)
        def _(tile):
            cols = pl.ds(pl.multiple_of(tile * TILE, TILE), TILE)
            part[c, :, cols] = (
                outer_dot(gate_all[here], vg[cols, :]) + outer_dot(up_all[here], vu[cols, :])
            ).astype(BF)

        if c + 1 == CHUNKS:
            for last in range(max(CHUNKS - 2, 0), CHUNKS):
                wait(hidden_copies(last))
            for gathered in (by_up, by_down):
                gathered.drain()
            start(h_copies(0))
            signal_partners(ready, at, chips)

    def mg_copy(c):
        return pltpu.make_async_copy(
            middle.at[chunk_span(c, rows)], middle_grad.at[chunk_span(c, rows)], mg_sem.at[c]
        )

    def forward_rows(c):
        scatter.total(c, total)
        span = chunk_span(c, rows)
        value = total[...]
        inverse = inverse_rms(value)
        output[span] = (middle[span] + value * inverse * mlp_scale[...]).astype(BF)
        upstream = upstream_in[span].astype(F32) * row_valid[span]
        grad, gain = norm_back(value, inverse, mlp_scale[...], upstream)
        own[c] = grad.astype(BF)
        mlp_gain[...] = gain if c == 0 else mlp_gain[...] + gain

    def backward_rows(c):
        scatter.total(c, total)
        span = chunk_span(c, rows)
        upstream = upstream_in[span].astype(F32) * row_valid[span] + total[...]
        middle[span] = upstream
        mg_copy(c).start()
        value = branch[span]
        grad, gain = norm_back(value, inverse_rms(value), attn_scale[...], upstream)
        own[c] = grad.astype(BF)
        attn_gain[...] = gain if c == 0 else attn_gain[...] + gain

    block_width = pl.ds(0, hidden_width)

    def slot_at(index):
        for ref in (vg, vu, vd):
            count = ref.shape[0] // part_width
            if index < count:
                return ref.at[pl.ds(index * part_width, part_width), block_width]
            index -= count
        for ref in (hidden_buf, in_buf):
            if index < ref.shape[0]:
                return ref.at[index, pl.ds(0, part_width), block_width]
            index -= ref.shape[0]
        return extra.at[index]

    reduces = []
    for which, out in enumerate((gate_out, up_out)):
        first = chips + 3 * chips * which
        views = (
            lambda r: slot_at(r),
            lambda r, first=first: slot_at(first + r),
            lambda r, first=first: slot_at(first + chips + r),
            lambda r, first=first: slot_at(first + 2 * chips + r - 1),
        )
        reduces.append(
            PlaneReduce(at, chips, part_width, views, plane[4 * which : 4 * which + 4], out)
        )
    order = relative_order(chips)
    jobs = [
        (which, same_core, r)
        for which in range(2)
        for same_core in (False, True)
        for r in order
    ]

    def h_copies(index):
        which, same_core, r = jobs[index]
        first = reduces[which].owner(r, same_core) * part_width
        cols = pl.ds(pl.multiple_of(first, part_width), part_width)
        return [
            pltpu.make_async_copy(
                h_full.at[j, :, cols], h_buf.at[index % 2, j], h_sem.at[index % 2, j]
            )
            for j in range(n)
        ]

    def weight_block(index):
        which, same_core, r = jobs[index]
        reduce = reduces[which]
        grad = (gate_all, up_all)[which]
        if index == 0:
            pl.semaphore_wait(ready, 1 + len(bits_of(chips - 1)))
        wait(h_copies(index))
        if index + 1 < len(jobs):
            start(h_copies(index + 1))
        if same_core:
            reduce.core_copy(r).wait_recv()
        elif which == 1:
            reduces[0].drain_core(r)
        left = jnp.concatenate(
            [
                h_buf[index % 2, j, c * rows : (c + 1) * rows]
                for c in range(CHUNKS)
                for j in range(n)
            ],
            axis=0,
        )

        @pl.loop(0, hidden_width // TILE)
        def _(tile):
            cols = pl.ds(pl.multiple_of(tile * TILE, TILE), TILE)
            block = inner_dot(left, grad[:, cols])
            if not same_core:
                reduce.core_send(r)[:, cols] = block.astype(BF)
            else:
                block = block + reduce.core_recv(r)[:, cols].astype(F32)
                if r > 0:
                    reduce.held(r)[:, cols] = block.astype(BF)
                else:
                    reduce.out[:, cols] = block

        if not same_core:
            reduce.core_copy(r).start()
        elif r > 0:
            for half in range(2):
                if not reduce.before(r, half):
                    reduce.push(r, half)

    work = []
    for index, (which, same_core, r) in enumerate(jobs):
        work.append(functools.partial(weight_block, index))
        if same_core and r == order[-1]:
            for late in order:
                for half in range(2):
                    if late > 0 and reduces[which].before(late, half):
                        work.append(functools.partial(reduces[which].push, late, half))
    pending = iter(work)

    early_chips = [r for r in range(1, chips) if len(bits_of(r)) == 1]
    late_chips = [r for r in range(1, chips) if len(bits_of(r)) > 1]
    hooks = {
        HOOKS[0]: lambda: (by_up.send(True), by_down.send(False)),
        HOOKS[1]: lambda: by_up.swap(early_chips),
        HOOKS[2]: lambda: by_up.swap(late_chips),
        HOOKS[3]: lambda: by_down.send(True),
        HOOKS[4]: lambda: by_down.swap(early_chips),
    }
    last_step = 2 * n - 2
    events = sorted(
        (
            max(PERIOD, last_step + 1) * phase + step + STAGGER * c - (0.5 if step == 0 else 0),
            phase,
            c,
            step,
        )
        for phase in range(3)
        for c in range(CHUNKS)
        for step in range(last_step + 1)
    )
    filling = False
    for number, (_, phase, c, step) in enumerate(events):
        gather = gathers[phase]
        if number in hooks:
            hooks.pop(number)()
        if step == 0:
            (attend_out, forward, backward)[phase](c)
            filling = filling or (phase == 2 and c + 1 == CHUNKS)
        if step < n - 1:
            scatter.edge(c, step)
            if step > 0:
                scatter.step(c, step)
        elif step == n - 1:
            (attend_rows, forward_rows, backward_rows)[phase](c)
            gather.step(c, 1)
        elif step < last_step:
            gather.step(c, step - n + 2)
        else:
            gather.last(c)
            if phase < 2:
                gather.local_copy(c).wait()
                start(in_copies(phase + 1, c))
        if filling:
            for _ in range(FILL):
                job = next(pending, None)
                if job is not None:
                    job()
    for job in pending:
        job()
    for c in range(CHUNKS):
        scatter.drain(c)
        gathers[2].drain(c)
    for reduce in reduces:
        reduce.finish()
        reduce.drain()
    for r in range(chips):
        reduces[1].drain_core(r)
    for c in range(CHUNKS):
        mg_copy(c).wait()


def middle(n, n_dp, attended, full_out, wg, wu, wd, x, out_grad, row_valid, mlp_scale, attn_scale):
    row_count, width = x.shape
    hidden_width = wg.shape[1]
    rows = row_count // CHUNKS
    size = n * row_count
    chips = n_dp // 2
    part_width = width // n_dp
    block = (part_width, hidden_width)
    slots = (2 * width + hidden_width) // part_width + 4
    extra = 7 * chips - 1 - slots
    by_rows = jax.ShapeDtypeStruct((n, row_count, width), BF)
    return pl.pallas_call(
        functools.partial(middle_kernel, n, n_dp, rows),
        out_shape=(
            by_rows,
            jax.ShapeDtypeStruct((row_count, width), BF),
            by_rows,
            jax.ShapeDtypeStruct((n, row_count, hidden_width), BF),
            jax.ShapeDtypeStruct((1, width), F32),
            jax.ShapeDtypeStruct((row_count, width), F32),
            by_rows,
            jax.ShapeDtypeStruct((1, width), F32),
            jax.ShapeDtypeStruct(block, F32),
            jax.ShapeDtypeStruct(block, F32),
        ),
        in_specs=[HBM] * 5 + [VMEM] * 5,
        out_specs=(HBM, VMEM, HBM, HBM, VMEM, HBM, HBM, VMEM, VMEM, VMEM),
        scratch_shapes=scatter_scratch(n, rows, width)
        + gather_scratch(n, rows, width)
        + [
            pltpu.VMEM((width, hidden_width), BF),
            pltpu.VMEM((width, hidden_width), BF),
            pltpu.VMEM((hidden_width, width), BF),
            pltpu.SemaphoreType.DMA((5,)),
            pltpu.VMEM((2, n * rows, width), BF),
            pltpu.SemaphoreType.DMA((2, n)),
            pltpu.VMEM((size, hidden_width), BF),
            pltpu.VMEM((size, hidden_width), BF),
            pltpu.VMEM((2, n * rows, hidden_width), BF),
            pltpu.SemaphoreType.DMA((2, n)),
            pltpu.VMEM((n * rows, attended.shape[1]), BF),
            pltpu.VMEM((row_count, width), F32),
            pltpu.VMEM((row_count, width), F32),
            pltpu.SemaphoreType.DMA((CHUNKS,)),
            pltpu.VMEM((2, n, row_count, part_width), BF),
            pltpu.SemaphoreType.DMA((2, n)),
            pltpu.VMEM((extra,) + block if extra > 0 else (1, 16, 128), BF),
            pltpu.SemaphoreType.REGULAR,
        ]
        + plane_sems(chips) * 4
        + ([pltpu.VMEM(full_out.shape, BF)] if hidden_width < width else []),
        compiler_params=pltpu.CompilerParams(
            collective_id=2, has_side_effects=True, vmem_limit_bytes=63 * MIB
        ),
        name="middle",
        cost_estimate=cost(350),
    )(attended, full_out, wg, wu, wd, x, out_grad, row_valid, mlp_scale, attn_scale)


def last_grads_kernel(
    n, n_dp, rows, grads, weight, base, inputs, att, da, hidden, dm,
    attn_gain, mlp_gain, q_gain, k_gain,
    input_grad, qkv_out, out_out, down_out, gain_out,
    part, recv, rs_send_sem, rs_recv_sem, total, packed,
    x_buf, da_buf, dm_buf, load_sem, v_hidden, hidden_sem,
    send_qkv, recv_qkv, message_qkv, send_out, recv_out, message_out,
    send_down, recv_down, message_down,
    gains, gain_recv, gain_send_sem, gain_recv_sem, mp_recv, mp_send_sem, mp_recv_sem, *plane,
):
    me, at = lax.axis_index("mp"), lax.axis_index("dp")
    entered = peer_barrier((("mp", me, n), ("dp", at, n_dp)))
    width = weight.shape[0]
    block_rows = rows * CHUNKS
    local_width = att.shape[1]
    chips = n_dp // 2
    part_width = width // n_dp
    order = relative_order(chips)

    def views(send, recv, message):
        return (
            lambda r: send.at[r],
            lambda r: recv.at[r],
            lambda r: send.at[r],
            lambda r: message.at[r - 1],
        )

    by_qkv = PlaneReduce(
        at, chips, part_width, views(send_qkv, recv_qkv, message_qkv), plane[:4], qkv_out
    )
    by_out = PlaneReduce(
        at, chips, local_width, views(send_out, recv_out, message_out), plane[4:8], out_out
    )
    by_down = PlaneReduce(
        at, chips, part_width, views(send_down, recv_down, message_down), plane[8:], down_out
    )
    jobs = [
        (down, same_core, r)
        for down in (True, False)
        for same_core in (False, True)
        for r in order
    ]

    def loads(k):
        down, same_core, r = jobs[k]
        first = by_qkv.owner(r, same_core) * part_width
        cols = pl.ds(pl.multiple_of(first, part_width), part_width)
        pairs = ((dm, dm_buf),) if down else ((inputs, x_buf), (da, da_buf))
        return [
            pltpu.make_async_copy(source.at[:, cols], buf.at[k % 2], load_sem.at[k % 2, which])
            for which, (source, buf) in enumerate(pairs)
        ]

    load_hidden = pltpu.make_async_copy(hidden, v_hidden, hidden_sem)
    for copy in loads(0):
        copy.start()
    load_hidden.start()

    def compute(c):
        for j in range(n):
            packed[j * rows : (j + 1) * rows] = grads[
                j * block_rows + c * rows : j * block_rows + (c + 1) * rows
            ]

        @pl.loop(0, width // TILE)
        def _(tile):
            cols = pl.ds(pl.multiple_of(tile * TILE, TILE), TILE)
            part[c, :, cols] = outer_dot(packed[...], weight[cols, :]).astype(BF)

    scatter = LineScatter(n, me, rows, part, recv, rs_send_sem, rs_recv_sem)

    def row_work(c):
        scatter.total(c, total)
        span = chunk_span(c, rows)
        input_grad[span] = base[span] + total[...]

    def weight_block(k):
        down, same_core, r = jobs[k]
        slot = k % 2
        reduces = (by_down,) if down else (by_qkv, by_out)
        for copy in loads(k):
            copy.wait()
        if k + 1 < len(jobs):
            for copy in loads(k + 1):
                copy.start()
        if k == 0:
            load_hidden.wait()
        if same_core:
            for reduce in reduces:
                reduce.core_copy(r).wait_recv()
                reduce.drain_core(r)

        def keep(reduce, block, cols):
            if not same_core:
                reduce.core_send(r)[:, cols] = block.astype(BF)
                return
            block = block + reduce.core_recv(r)[:, cols].astype(F32)
            if r > 0:
                reduce.held(r)[:, cols] = block.astype(BF)
            else:
                reduce.out[:, cols] = block

        if down:

            @pl.loop(0, hidden.shape[1] // TILE)
            def _(tile):
                cols = pl.ds(pl.multiple_of(tile * TILE, TILE), TILE)
                keep(by_down, inner_dot(dm_buf[slot], v_hidden[:, cols]), cols)

        else:

            @pl.loop(0, 3)
            def _(tile):
                cols = pl.ds(pl.multiple_of(tile * local_width, local_width), local_width)
                keep(by_qkv, inner_dot(x_buf[slot], grads[:, cols]), cols)

            keep(by_out, inner_dot(att[...], da_buf[slot]), slice(None))
        for reduce in reduces:
            if not same_core:
                reduce.core_copy(r).start()
            elif r > 0:
                for half in range(2):
                    if not reduce.before(r, half):
                        reduce.push(r, half)

    def push_late(reduces):
        for r in order:
            for half in range(2):
                if r > 0 and reduces[0].before(r, half):
                    for reduce in reduces:
                        reduce.push(r, half)

    for index in range(n_dp):
        span = slice(index * part_width, (index + 1) * part_width)
        gains[index, :, :part_width] = attn_gain[:, span]
        gains[index, :, part_width : 2 * part_width] = mlp_gain[:, span]
        gains[index, :, 2 * part_width : 2 * part_width + local_width] = q_gain[...]
        gains[index, :, 2 * part_width + local_width :] = k_gain[...]
    gain_copies = exchange(
        "dp", at, n_dp, lambda peer: gains.at[peer], gain_recv, gain_send_sem, gain_recv_sem
    )
    mp_copies = exchange("mp", me, n, lambda peer: gain_out, mp_recv, mp_send_sem, mp_recv_sem)
    line = iter([(step, c) for c in range(CHUNKS) for step in range(1, n)])

    def line_steps(count):
        for _ in range(count):
            step, c = next(line, (None, None))
            if step is None:
                return
            if step < n - 1:
                scatter.step(c, step)
            else:
                row_work(c)

    def send_edges(c):
        for step in range(n - 1):
            scatter.edge(c, step)

    compute(0)
    entered()
    send_edges(0)
    for copy in gain_copies:
        copy.start()
    sent = 1
    for k in range(len(jobs)):
        weight_block(k)
        if k % 4 == 3 and sent < CHUNKS:
            compute(sent)
            send_edges(sent)
            sent += 1
        if k >= LINE_FROM:
            line_steps(1)
        if k == 3 * chips:
            push_late((by_down,))
    push_late((by_qkv, by_out))
    gain_out[...] = gains[at]
    for shift, copy in enumerate(gain_copies, 1):
        copy.wait_recv()
        gain_out[...] += gain_recv[shift - 1]
    for copy in mp_copies:
        copy.start()
    line_steps(n * CHUNKS)
    for reduce in (by_down, by_qkv, by_out):
        reduce.finish()
    for copy in mp_copies:
        copy.wait_recv()
        copy.wait_send()
    lanes = lax.broadcasted_iota(jnp.int32, gain_out.shape, 1)
    shared = gain_out[...]
    for shift in range(1, n):
        shared = shared + mp_recv[shift - 1]
    gain_out[...] = jnp.where(lanes < 2 * part_width, shared, gain_out[...])
    for copy in gain_copies:
        copy.wait_send()
    for c in range(CHUNKS):
        scatter.drain(c)
    for reduce in (by_down, by_qkv, by_out):
        reduce.drain()


def last_grads(n, n_dp, grads, weight, base, inputs, attended, da_full, hidden, dm, *gains):
    row_count, width = base.shape
    rows = row_count // CHUNKS
    size, local_width = attended.shape
    part_width = width // n_dp
    chips = n_dp // 2
    qkv_block = (part_width, 3 * local_width)
    out_block = (local_width, part_width)
    down_block = (part_width, hidden.shape[1])
    gain_block = (1, 2 * part_width + 2 * local_width)
    return pl.pallas_call(
        functools.partial(last_grads_kernel, n, n_dp, rows),
        out_shape=(
            jax.ShapeDtypeStruct((row_count, width), F32),
            jax.ShapeDtypeStruct(qkv_block, F32),
            jax.ShapeDtypeStruct(out_block, F32),
            jax.ShapeDtypeStruct(down_block, F32),
            jax.ShapeDtypeStruct(gain_block, F32),
        ),
        in_specs=[VMEM, VMEM, VMEM, HBM, VMEM, HBM, HBM, HBM] + [VMEM] * 4,
        out_specs=(VMEM,) * 5,
        scratch_shapes=scatter_scratch(n, rows, width)
        + [
            pltpu.VMEM((n * rows, 3 * local_width), BF),
            pltpu.VMEM((2, size, part_width), BF),
            pltpu.VMEM((2, size, part_width), BF),
            pltpu.VMEM((2, size, part_width), BF),
            pltpu.SemaphoreType.DMA((2, 2)),
            pltpu.VMEM(hidden.shape, BF),
            pltpu.SemaphoreType.DMA,
        ]
        + [
            pltpu.VMEM((count,) + block, BF)
            for block in (qkv_block, out_block, down_block)
            for count in (chips, chips, chips - 1)
        ]
        + [pltpu.VMEM((n_dp,) + gain_block, F32), pltpu.VMEM((n_dp - 1,) + gain_block, F32)]
        + [pltpu.SemaphoreType.DMA((n_dp - 1,))] * 2
        + [pltpu.VMEM((n - 1,) + gain_block, F32)]
        + [pltpu.SemaphoreType.DMA((n - 1,))] * 2
        + plane_sems(chips) * 3,
        compiler_params=pltpu.CompilerParams(
            collective_id=4, has_side_effects=True, vmem_limit_bytes=63 * MIB
        ),
        name="last_grads",
        cost_estimate=cost(80),
    )(grads, weight, base, inputs, attended, da_full, hidden, dm, *gains)


def turn(values, cos, sin):
    return values * cos + pltpu.roll(values, values.shape[1] // 2, 1) * sin


def turn_back(values, cos, sin):
    return values * cos + pltpu.roll(values * sin, values.shape[1] // 2, 1)


def allowed_keys(starts, first_row, rows, key_end):
    places = first_row + lax.broadcasted_iota(jnp.int32, (rows, key_end), 0)
    keys = lax.broadcasted_iota(jnp.int32, (rows, key_end), 1)
    return (keys <= places) & (keys >= starts)


def columns_to_rows(first, second):
    lanes = lax.broadcasted_iota(jnp.int32, (first.shape[0], 128), 1)
    return jnp.transpose(jnp.where(lanes == 0, first, second))[:8]


def sum_held(n, me, held, recv, turned, send_sem, recv_sem):
    copies = exchange("mp", me, n, lambda peer: held, recv, send_sem, recv_sem)
    for copy in copies:
        copy.start()
    total = held[...]
    for shift, copy in enumerate(copies, 1):
        copy.wait_recv()
        total = total + recv[shift - 1]
    for copy in copies:
        copy.wait_send()
    turned[...] = jnp.zeros_like(turned)
    turned[:8] = total
    back = jnp.transpose(turned[...])
    return back[:, 0:1], back[:, 1:2]


def sum_scratch(n, size):
    return [
        pltpu.VMEM((8, size), F32),
        pltpu.VMEM((n - 1, 8, size), F32),
        pltpu.VMEM((128, size), F32),
        pltpu.SemaphoreType.DMA((n - 1,)),
        pltpu.SemaphoreType.DMA((n - 1,)),
    ]


def attention_kernel(
    q_raw, k_raw, v_raw, q_inv, k_inv, q_gain, k_gain, cos, sin, starts,
    out, q_low, k_low, v_low, log_total,
):
    size, head = q_raw.shape
    score_scale = 1.0 / math.sqrt(head)
    q_low[...] = turn(q_raw[...] * q_inv[...] * q_gain[...], cos[...], sin[...]).astype(BF)
    k_low[...] = turn(k_raw[...] * k_inv[...] * k_gain[...], cos[...], sin[...]).astype(BF)
    v_low[...] = v_raw[...].astype(BF)
    rows = min(QUERY_ROWS, size)
    for first in range(0, size, rows):
        end = first + rows
        span = slice(first, end)
        scores = outer_dot(q_low[span], k_low[:end]) * score_scale
        scores = jnp.where(allowed_keys(starts[span], first, rows, end), scores, MASKED)
        row_max = jnp.max(scores, axis=1, keepdims=True)
        exponents = jnp.exp(scores - row_max)
        row_total = jnp.sum(exponents, axis=1, keepdims=True)
        probs = (exponents * (1.0 / row_total)).astype(BF)
        out[span] = plain_dot(probs, v_low[:end]).astype(BF)
        log_total[span] = row_max + jnp.log(row_total)


def head_specs(size, head, heads, count):
    return [pl.BlockSpec((size, head), lambda h, k=k: (0, k * heads + h)) for k in range(count)]


def attention(qkv_raw, q_inv, k_inv, q_gain, k_gain, cos, sin, starts, heads):
    size = qkv_raw.shape[0]
    head = cos.shape[1]
    column = pl.BlockSpec((size, 1), lambda h: (0, 0))
    table = pl.BlockSpec((size, head), lambda h: (0, 0))
    gain = pl.BlockSpec((1, head), lambda h: (0, h))
    by_head = pl.BlockSpec((size, head), lambda h: (0, h))
    low = jax.ShapeDtypeStruct((size, heads * head), BF)
    return pl.pallas_call(
        attention_kernel,
        grid=(heads,),
        out_shape=(low, low, low, low, jax.ShapeDtypeStruct((heads, size, 1), F32)),
        in_specs=head_specs(size, head, heads, 3)
        + [column, column, gain, gain, table, table, column],
        out_specs=(by_head,) * 4 + (pl.BlockSpec((None, size, 1), lambda h: (h, 0, 0)),),
        compiler_params=pltpu.CompilerParams(vmem_limit_bytes=63 * MIB),
        name="attention",
        cost_estimate=cost(18),
    )(qkv_raw, qkv_raw, qkv_raw, q_inv, k_inv, q_gain, k_gain, cos, sin, starts)


def attention_back_kernel(
    n, heads, model_width, qkv, q_low, k_low, v_low, out_grad, log_total,
    q_inv, k_inv, q_gain, k_gain, cos, sin, starts,
    grads, q_gain_grad, k_gain_grad,
    q_weighted, k_weighted, q_grad, k_sum, v_sum, q_dots, k_dots, *sums,
):
    me = lax.axis_index("mp")
    entered = peer_barrier((("mp", me, n),))
    size = qkv.shape[0]
    width = qkv.shape[1] // 3
    head = width // heads
    score_scale = 1.0 / math.sqrt(head)
    rows = min(QUERY_ROWS, size)
    q_dots[...] = jnp.zeros_like(q_dots)
    k_dots[...] = jnp.zeros_like(k_dots)

    @pl.loop(0, heads)
    def _(h):
        def cols(first):
            return pl.ds(pl.multiple_of(first + h * head, head), head)

        here = cols(0)
        for first in reversed(range(0, size, rows)):
            end = first + rows
            span = slice(first, end)
            scores = outer_dot(q_low[span, here], k_low[:end, here]) * score_scale
            scores = jnp.where(allowed_keys(starts[span], first, rows, end), scores, MASKED)
            probs = jnp.exp(scores - log_total[h, span])
            prob_grad = outer_dot(out_grad[span, here], v_low[:end, here])
            probs_low = probs.astype(BF)
            weighted = probs * prob_grad
            score_grad = (
                weighted - probs * jnp.sum(weighted, axis=1, keepdims=True)
            ).astype(BF)
            q_grad[span] = plain_dot(score_grad, k_low[:end, here]) * score_scale
            k_extra = inner_dot(score_grad, q_low[span, here])
            v_extra = inner_dot(probs_low, out_grad[span, here])
            if end == size:
                k_sum[...] = k_extra
                v_sum[...] = v_extra
            else:
                k_sum[:end] += k_extra
                v_sum[:end] += v_extra
        for first, inv, gain, grad, factor, weighted_out, dots, gain_grad in (
            (0, q_inv, q_gain, q_grad, None, q_weighted, q_dots, q_gain_grad),
            (width, k_inv, k_gain, k_sum, score_scale, k_weighted, k_dots, k_gain_grad),
        ):
            raw = qkv[:, cols(first)]
            value = grad[...] if factor is None else grad[...] * factor
            normed = turn_back(value, cos[...], sin[...])
            weighted = normed * gain[:, here]
            weighted_out[:, here] = weighted
            gain_grad[:, here] = jnp.sum(normed * raw * inv[...], axis=0, keepdims=True)
            dots[...] += jnp.sum(weighted * raw, axis=1, keepdims=True)
        grads[:, cols(2 * width)] = v_sum[...].astype(BF)

    held = sums[0]
    held[...] = columns_to_rows(q_dots[...], k_dots[...])
    entered()
    q_total, k_total = sum_held(n, me, *sums)
    for first, inv, weighted, dots in (
        (0, q_inv, q_weighted, q_total),
        (width, k_inv, k_weighted, k_total),
    ):
        scale = inv[...]
        factor = scale * scale * scale * (dots / model_width)
        grads[:, first : first + width] = (
            scale * weighted[...] - qkv[:, first : first + width] * factor
        ).astype(BF)


def attention_back(
    n, heads, model_width, qkv_raw, q_low, k_low, v_low, out_grad, log_total, q_inv, k_inv,
    q_gain, k_gain, cos, sin, starts,
):
    size, width = q_low.shape
    head = width // heads
    gains = jax.ShapeDtypeStruct((1, width), F32)
    return pl.pallas_call(
        functools.partial(attention_back_kernel, n, heads, model_width),
        out_shape=(jax.ShapeDtypeStruct((size, 3 * width), BF), gains, gains),
        in_specs=[VMEM] * 13,
        out_specs=(VMEM,) * 3,
        scratch_shapes=[pltpu.VMEM((size, width), F32)] * 2
        + [pltpu.VMEM((size, head), F32)] * 3
        + [pltpu.VMEM((size, 1), F32)] * 2
        + sum_scratch(n, size),
        compiler_params=pltpu.CompilerParams(
            collective_id=6, has_side_effects=True, vmem_limit_bytes=63 * MIB
        ),
        name="attention_back",
        cost_estimate=cost(30),
    )(
        qkv_raw, q_low, k_low, v_low, out_grad, log_total, q_inv, k_inv, q_gain, k_gain,
        cos, sin, starts,
    )


def local(
    layer_input,
    query_weight,
    key_weight,
    value_weight,
    out_weight,
    gate_weight,
    up_weight,
    down_weight,
    query_gain,
    key_gain,
    attn_gain,
    mlp_gain,
    seq_lens,
    out_grad,
):
    n = lax.axis_size("mp")
    n_dp = lax.axis_size("dp")
    me = lax.axis_index("mp")
    row_count, model_width = layer_input.shape
    group_size = row_count * n
    local_heads, gain_part = query_gain.shape
    head_size = gain_part * n_dp
    local_width = local_heads * head_size

    head_part = local_heads * gain_part
    width_part = attn_gain.shape[0]
    own_gains = jnp.concatenate(
        [attn_gain, mlp_gain, query_gain.reshape(head_part), key_gain.reshape(head_part)]
    ).astype(F32)[None]
    inputs_full, qkv_raw, full_qkv, full_out, gain_parts, query_inv, key_inv, full_gate = front(
        n, n_dp, layer_input, query_weight, key_weight, value_weight, out_weight, own_gains,
        gate_weight,
    )
    inputs_full = inputs_full.reshape(group_size, model_width)
    gain_parts = gain_parts[:, 0]

    def head_gain(first):
        piece = gain_parts[:, first : first + head_part].reshape(n_dp, local_heads, gain_part)
        return piece.transpose(1, 0, 2).reshape(1, local_width)

    query_scale = head_gain(2 * width_part)
    key_scale = head_gain(2 * width_part + head_part)
    attn_scale = gain_parts[:, :width_part].reshape(1, model_width)
    mlp_scale = gain_parts[:, width_part : 2 * width_part].reshape(1, model_width)

    starts, positions, valid = layout(seq_lens[0], group_size)
    starts = starts[:, None]
    cos_table, sin_table = rotary_tables(positions, head_size)
    row_valid = lax.dynamic_slice_in_dim(valid, me * row_count, row_count, 0).astype(F32)[:, None]

    attended, query_low, key_low, value_low, log_total = attention(
        qkv_raw, query_inv, key_inv, query_scale, key_scale, cos_table, sin_table, starts,
        local_heads,
    )
    (
        middle_full, layer_output, mlp_grad_full, hidden, mlp_gain_part, middle_grad, branch_full,
        attn_gain_part, grad_gate, grad_up,
    ) = middle(
        n, n_dp, attended, full_out, full_gate, up_weight, down_weight, layer_input, out_grad,
        row_valid, mlp_scale, attn_scale,
    )

    def flat(rows):
        return rows.reshape(group_size, rows.shape[-1])

    branch_full = flat(branch_full)
    mixed_grad = outer_dot(branch_full, full_out).astype(BF)
    qkv_grad, query_gain_part, key_gain_part = attention_back(
        n, local_heads, model_width, qkv_raw, query_low, key_low, value_low, mixed_grad, log_total,
        query_inv, key_inv, query_scale, key_scale, cos_table, sin_table, starts,
    )

    input_grad, grad_qkv, grad_out, grad_down, gain_sums = last_grads(
        n, n_dp, qkv_grad, full_qkv, middle_grad, inputs_full, attended, branch_full,
        flat(hidden), flat(mlp_grad_full), attn_gain_part, mlp_gain_part, query_gain_part,
        key_gain_part,
    )
    gain_sums = gain_sums[0]
    heads_at = 2 * width_part
    head_sums = lax.dynamic_index_in_dim(
        gain_sums[heads_at:].reshape(2, local_heads, n_dp, gain_part),
        lax.axis_index("dp"),
        2,
        keepdims=False,
    )
    return (
        layer_output,
        input_grad,
        grad_qkv[:, :local_width],
        grad_qkv[:, local_width : 2 * local_width],
        grad_qkv[:, 2 * local_width :],
        grad_out,
        grad_gate,
        grad_up,
        grad_down.T,
        head_sums[0],
        head_sums[1],
        gain_sums[:width_part],
        gain_sums[width_part:heads_at],
    )


def solution(mesh):
    return jax.shard_map(
        local,
        mesh=mesh,
        in_specs=(
            P(("dp", "mp"), None),
            P("dp", "mp"),
            P("dp", "mp"),
            P("dp", "mp"),
            P("mp", "dp"),
            P("dp", "mp"),
            P("dp", "mp"),
            P("mp", "dp"),
            P("mp", "dp"),
            P("mp", "dp"),
            P("dp"),
            P("dp"),
            P("dp", None),
            P(("dp", "mp"), None),
        ),
        out_specs=(
            P(("dp", "mp"), None),
            P(("dp", "mp"), None),
            P("dp", "mp"),
            P("dp", "mp"),
            P("dp", "mp"),
            P("mp", "dp"),
            P("dp", "mp"),
            P("dp", "mp"),
            P("mp", "dp"),
            P("mp", "dp"),
            P("mp", "dp"),
            P("dp"),
            P("dp"),
        ),
        check_vma=False,
    )
```

```python
import functools
import math

import jax
import jax.numpy as jnp
from jax import lax
from jax.experimental import pallas as pl
from jax.experimental.pallas import tpu as pltpu
from jax.sharding import PartitionSpec as P

EPS = 1e-06
THETA = 500000.0
MASKED = -1000000000.0
CHUNKS = 4
STAGGER = 2
EDGES = False
FILL = 2
PERIOD = 8
LINE_FROM = 11
HOOKS = (3, 7, 10, 13, 16)
TILE = 512
QUERY_ROWS = 256
BF = jnp.bfloat16
F32 = jnp.float32
MIB = 1 << 20
HBM = pl.BlockSpec(memory_space=pl.ANY)
VMEM = pl.BlockSpec(memory_space=pltpu.VMEM)


def cost(micros):
    return pl.CostEstimate(
        flops=micros * 1_000_000_000, bytes_accessed=micros * 3_000_000, transcendentals=0
    )


def plain_dot(former, latter):
    return jnp.dot(former, latter, preferred_element_type=F32)


def inner_dot(former, latter):
    return lax.dot_general(
        former, latter, (((0,), (0,)), ((), ())), preferred_element_type=F32
    )


def outer_dot(former, latter):
    return lax.dot_general(
        former, latter, (((1,), (1,)), ((), ())), preferred_element_type=F32
    )


def layout(lengths, group_size):
    slot_count = lengths.shape[0]
    seq_ends = jnp.cumsum(lengths, dtype=jnp.int32)
    starts = seq_ends - lengths
    places = jnp.arange(group_size, dtype=jnp.int32)
    slot_ids = jnp.arange(slot_count, dtype=jnp.int32)
    segment = jnp.sum(
        (places[:, None] >= seq_ends[None, :]).astype(jnp.int32), axis=1, dtype=jnp.int32
    )
    chosen = (segment[:, None] == slot_ids[None, :]).astype(jnp.int32)
    padded = (segment == slot_count).astype(jnp.int32)
    begins = (
        jnp.sum(chosen * starts[None, :], axis=1, dtype=jnp.int32)
        + padded * seq_ends[slot_count - 1]
    )
    return (begins, places - begins, places < seq_ends[slot_count - 1])


def rotary_tables(positions, head_size):
    half_dim = head_size // 2
    frequency = jnp.exp(jnp.arange(half_dim, dtype=F32) * (-2.0 * math.log(THETA) / head_size))
    angles = positions.astype(F32)[:, None] * frequency[None, :]
    cos_half, sin_half = jnp.cos(angles), jnp.sin(angles)
    return (
        jnp.concatenate([cos_half, cos_half], axis=1),
        jnp.concatenate([-sin_half, sin_half], axis=1),
    )


def neighbour_barrier(me, n):
    barrier = pltpu.get_barrier_semaphore()

    @pl.when(me > 0)
    def _():
        pl.semaphore_signal(barrier, inc=1, device_id={"mp": me - 1})

    @pl.when(me < n - 1)
    def _():
        pl.semaphore_signal(barrier, inc=1, device_id={"mp": me + 1})

    pl.semaphore_wait(barrier, jnp.minimum(me, 1) + jnp.minimum(n - 1 - me, 1))


class LineGather:
    def __init__(self, n, me, own, full, send_sem, recv_sem, local_sem):
        self.n, self.me, self.own, self.full = n, me, own, full
        self.send_sem, self.recv_sem, self.local_sem = send_sem, recv_sem, local_sem

    def local_copy(self, c):
        return pltpu.make_async_copy(self.own(c), self.full(self.me, c), self.local_sem.at[c])

    def copy(self, c, step, way, block, src):
        return pltpu.make_async_remote_copy(
            src_ref=src,
            dst_ref=self.full(block, c),
            send_sem=self.send_sem.at[c, step - 1, way],
            recv_sem=self.recv_sem.at[c, step - 1, way],
            device_id={"mp": self.me + (1 if way == 0 else -1)},
        )

    def sides(self):
        return ((0, self.me), (1, self.n - 1 - self.me))

    def block_at(self, way, step):
        return self.me - step if way == 0 else self.me + step

    def step(self, c, step):
        n = self.n
        if step == 1:
            self.local_copy(c).start()
        for way, place in self.sides():
            if step > 1:

                @pl.when(place >= step - 1)
                def _(way=way):
                    block = self.block_at(way, step - 1)
                    self.copy(c, step - 1, way, block, self.own(c)).wait_recv()

            @pl.when((place >= step - 1) & (place < n - 1))
            def _(way=way):
                block = self.block_at(way, step - 1)
                src = self.own(c) if step == 1 else self.full(block, c)
                self.copy(c, step, way, block, src).start()

    def last(self, c):
        n = self.n
        for way, place in self.sides():

            @pl.when(place == n - 1)
            def _(way=way):
                block = self.block_at(way, n - 1)
                self.copy(c, n - 1, way, block, self.own(c)).wait_recv()

    def drain(self, c):
        self.local_copy(c).wait()
        self.drain_sends(c)

    def drain_sends(self, c):
        for step in range(1, self.n):
            for way, place in self.sides():

                @pl.when((place >= step - 1) & (place < self.n - 1))
                def _(way=way):
                    self.copy(c, step, way, self.me, self.own(c)).wait_send()


class LineScatter:
    def __init__(self, n, me, rows, part, recv, send_sem, recv_sem):
        self.n, self.me, self.rows = n, me, rows
        self.part, self.recv = part, recv
        self.send_sem, self.recv_sem = send_sem, recv_sem

    def piece(self, c, owner):
        first = pl.multiple_of(owner * self.rows, self.rows)
        return self.part.at[c, pl.ds(first, self.rows)]

    def copy(self, c, step, way, src):
        return pltpu.make_async_remote_copy(
            src_ref=src,
            dst_ref=self.recv.at[c, step, way],
            send_sem=self.send_sem.at[c, step, way],
            recv_sem=self.recv_sem.at[c, step, way],
            device_id={"mp": self.me + (1 if way == 0 else -1)},
        )

    def sides(self):
        return ((0, self.me), (1, self.n - 1 - self.me))

    def owner(self, way, step):
        return self.n - 1 - step + self.me if way == 0 else step - (self.n - 1 - self.me)

    def edge(self, c, step):
        for way, place in self.sides():

            @pl.when(place == 0)
            def _(way=way):
                self.copy(c, step, way, self.piece(c, self.owner(way, step))).start()

    def step(self, c, step):
        for way, place in self.sides():

            @pl.when((place > 0) & (place <= min(step, self.n - 2)))
            def _(way=way):
                piece = self.piece(c, self.owner(way, step))
                self.copy(c, step - 1, way, piece).wait_recv()
                piece[...] = (
                    piece[...].astype(F32) + self.recv[c, step - 1, way].astype(F32)
                ).astype(BF)
                self.copy(c, step, way, piece).start()

    def total(self, c, out):
        n = self.n
        out[...] = self.piece(c, self.me)[...].astype(F32)
        for way, place in self.sides():

            @pl.when(place > 0)
            def _(way=way):
                self.copy(c, n - 2, way, self.recv.at[c, n - 2, way]).wait_recv()
                out[...] += self.recv[c, n - 2, way].astype(F32)

    def drain(self, c):
        n = self.n
        for step in range(n - 1):
            for way, place in self.sides():

                @pl.when(place <= min(step, n - 2))
                def _(way=way):
                    self.copy(c, step, way, self.recv.at[c, step, way]).wait_send()


def run_line(n, chunks, stagger, compute, scatter, row_work, gather, filler=None):
    last_step = 2 * n - 2 if gather is not None else n - 1
    events = sorted(
        (step + stagger * c - (0.5 if step == 0 else 0), c, step)
        for c in range(chunks)
        for step in range(last_step + 1)
    )
    computed = 0
    for _, c, step in events:
        if step == 0:
            compute(c)
            for ahead in range(n - 1 if EDGES else 1):
                scatter.edge(c, ahead)
            computed += 1
        elif step < n - 1:
            if not EDGES:
                scatter.edge(c, step)
            scatter.step(c, step)
        elif step == n - 1:
            row_work(c)
            if gather is not None:
                gather.step(c, 1)
        elif step < 2 * n - 2:
            gather.step(c, step - n + 2)
        else:
            gather.last(c)
        if filler is not None and computed == chunks:
            filler()
    for c in range(chunks):
        scatter.drain(c)
        if gather is not None:
            gather.drain(c)


def flipped(chip, bit):
    return chip + bit - 2 * bit * lax.rem(chip // bit, 2)


def bits_of(number):
    return [1 << k for k in range(number.bit_length()) if number >> k & 1]


def relative_chip(chip, relative):
    for bit in bits_of(relative):
        chip = flipped(chip, bit)
    return chip


def relative_order(chips):
    return sorted(range(chips), key=lambda r: (-len(bits_of(r)), r))


class PlaneReduce:
    def __init__(self, at, chips, rows, views, sems, out):
        self.chip, self.core = at // 2, lax.rem(at, 2)
        self.chips, self.rows, self.out = chips, rows, out
        self.core_send, self.core_recv, self.held, self.message = views
        self.core_send_sem, self.core_recv_sem, self.send_sem, self.recv_sem = sems

    def first_bit(self, relative, half):
        bits = bits_of(relative)
        return bits[0] if half == 0 else bits[-1]

    def before(self, relative, half):
        return [
            r for r in range(1, self.chips) if r - self.first_bit(r, half) == relative
        ]

    def owner(self, relative, same_core):
        return 2 * relative_chip(self.chip, relative) + (
            self.core if same_core else 1 - self.core
        )

    def half_rows(self, half):
        return pl.ds(half * (self.rows // 2), self.rows // 2)

    def core_copy(self, relative):
        return pltpu.make_async_remote_copy(
            src_ref=self.core_send(relative),
            dst_ref=self.core_recv(relative),
            send_sem=self.core_send_sem.at[relative],
            recv_sem=self.core_recv_sem.at[relative],
            device_id={"dp": 2 * self.chip + 1 - self.core},
        )

    def message_copy(self, relative, half):
        span = self.half_rows(half)
        target = flipped(self.chip, self.first_bit(relative, half))
        return pltpu.make_async_remote_copy(
            src_ref=self.held(relative).at[span],
            dst_ref=self.message(relative).at[span],
            send_sem=self.send_sem.at[relative, half],
            recv_sem=self.recv_sem.at[relative, half],
            device_id={"dp": 2 * target + self.core},
        )

    def push(self, relative, half):
        span = self.half_rows(half)
        for r in self.before(relative, half):
            self.message_copy(r, half).wait_recv()
            held = self.held(relative)
            held[span] = (
                held[span].astype(F32) + self.message(r)[span].astype(F32)
            ).astype(BF)
        self.message_copy(relative, half).start()

    def finish(self):
        for half in range(2):
            span = self.half_rows(half)
            for r in self.before(0, half):
                self.message_copy(r, half).wait_recv()
                self.out[span] += self.message(r)[span].astype(F32)

    def drain_core(self, relative):
        self.core_copy(relative).wait_send()

    def drain(self):
        for r in range(1, self.chips):
            for half in range(2):
                self.message_copy(r, half).wait_send()


def plane_sems(chips):
    return [pltpu.SemaphoreType.DMA((chips,))] * 2 + [pltpu.SemaphoreType.DMA((chips, 2))] * 2


def stage_barrier(me, n, at, chips):
    barrier = pltpu.get_barrier_semaphore()

    @pl.when(me > 0)
    def _():
        pl.semaphore_signal(barrier, inc=1, device_id={"mp": me - 1})

    @pl.when(me < n - 1)
    def _():
        pl.semaphore_signal(barrier, inc=1, device_id={"mp": me + 1})

    count = signal_partners(barrier, at, chips)
    pl.semaphore_wait(barrier, count + jnp.minimum(me, 1) + jnp.minimum(n - 1 - me, 1))


def signal_partners(sem, at, chips):
    chip, core = at // 2, lax.rem(at, 2)
    pl.semaphore_signal(sem, inc=1, device_id={"dp": 2 * chip + 1 - core})
    bits = [1 << k for k in range(chips.bit_length() - 1)]
    for bit in bits:
        pl.semaphore_signal(sem, inc=1, device_id={"dp": 2 * flipped(chip, bit) + core})
    return 1 + len(bits)


def inverse_rms(rows):
    return lax.rsqrt(jnp.mean(rows * rows, axis=1, keepdims=True) + EPS)


def norm_back(values, inverse, gain_row, upstream):
    weighted = upstream * gain_row
    mean_term = jnp.mean(weighted * values, axis=1, keepdims=True)
    grad_values = inverse * weighted - values * (inverse * inverse * inverse) * mean_term
    return (grad_values, jnp.sum(upstream * values * inverse, axis=0, keepdims=True))


def scatter_scratch(n, rows, width):
    return [
        pltpu.VMEM((CHUNKS, n * rows, width), BF),
        pltpu.VMEM((CHUNKS, n - 1, 2, rows, width), BF),
        pltpu.SemaphoreType.DMA((CHUNKS, n - 1, 2)),
        pltpu.SemaphoreType.DMA((CHUNKS, n - 1, 2)),
        pltpu.VMEM((rows, width), F32),
    ]


def gather_scratch(n, rows, width):
    return [
        pltpu.VMEM((CHUNKS, rows, width), BF),
        pltpu.SemaphoreType.DMA((CHUNKS, n - 1, 2)),
        pltpu.SemaphoreType.DMA((CHUNKS, n - 1, 2)),
        pltpu.SemaphoreType.DMA((CHUNKS,)),
    ]


def chunk_span(c, rows):
    return pl.ds(c * rows, rows)


def make_gather(n, me, rows, own, full, send_sem, recv_sem, local_sem):
    return LineGather(
        n,
        me,
        lambda c: own.at[c],
        lambda block, c: full.at[block, chunk_span(c, rows)],
        send_sem,
        recv_sem,
        local_sem,
    )


def peer_barrier(axes):
    barrier = pltpu.get_barrier_semaphore()
    count = 0
    for name, index, size in axes:
        for shift in range(1, size):
            pl.semaphore_signal(barrier, inc=1, device_id={name: lax.rem(index + shift, size)})
            count += 1
    return lambda: pl.semaphore_wait(barrier, count)


def exchange(name, index, size, src, recv, send_sem, recv_sem):
    def copy(shift):
        peer = lax.rem(index + shift, size)
        return pltpu.make_async_remote_copy(
            src_ref=src(peer),
            dst_ref=recv.at[shift - 1],
            send_sem=send_sem.at[shift - 1],
            recv_sem=recv_sem.at[shift - 1],
            device_id={name: peer},
        )

    return [copy(shift) for shift in range(1, size)]


class PlaneGather:
    def __init__(self, at, chips, rows, slot, sems):
        self.chip, self.core = at // 2, lax.rem(at, 2)
        self.chips, self.rows, self.slot = chips, rows, slot
        self.core_send_sem, self.core_recv_sem, self.send_sem, self.recv_sem = sems
        self.arrived = set()

    def last_bit(self, relative, half):
        bits = bits_of(relative)
        return bits[-1] if half == 0 else bits[0]

    def place(self, relative, same_core=True):
        return self.slot(
            2 * relative_chip(self.chip, relative) + (self.core if same_core else 1 - self.core)
        )

    def copy(self, relative, half):
        bit = self.last_bit(relative, half)
        view = self.place(relative - bit).at[pl.ds(half * (self.rows // 2), self.rows // 2)]
        return pltpu.make_async_remote_copy(
            src_ref=view,
            dst_ref=view,
            send_sem=self.send_sem.at[relative, half],
            recv_sem=self.recv_sem.at[relative, half],
            device_id={"dp": 2 * flipped(self.chip, bit) + self.core},
        )

    def core_copy(self, relative, same_core):
        view = self.place(relative, same_core)
        return pltpu.make_async_remote_copy(
            src_ref=view,
            dst_ref=view,
            send_sem=self.core_send_sem.at[relative],
            recv_sem=self.core_recv_sem.at[relative],
            device_id={"dp": 2 * self.chip + 1 - self.core},
        )

    def ensure(self, relative, half):
        if relative > 0 and (relative, half) not in self.arrived:
            self.arrived.add((relative, half))
            self.copy(relative, half).wait_recv()

    def send(self, passed_on):
        for count in range(1, self.chips.bit_length()):
            for r in range(1, self.chips):
                for half in range(2):
                    if len(bits_of(r)) == count and (count > 1) == passed_on:
                        self.ensure(r - self.last_bit(r, half), half)
                        self.copy(r, half).start()
        if not passed_on:
            self.core_copy(0, True).start()

    def swap(self, relatives):
        for r in relatives:
            for half in range(2):
                self.ensure(r, half)
            self.core_copy(r, True).start()

    def finish(self):
        for r in range(self.chips):
            self.core_copy(r, False).wait_recv()

    def drain(self):
        for r in range(self.chips):
            self.core_copy(r, True).wait_send()
            for half in range(2):
                if r > 0:
                    self.copy(r, half).wait_send()


def front_kernel(
    n, n_dp, rows, model_width, x, wq, wk, wv, wo, gains, wg,
    full, qkv_out, full_qkv, full_out, gain_parts, attn_scale, mlp_scale, q_inv, k_inv, full_gate,
    send_sem, recv_sem, local_sem, gain_recv, gain_send_sem, gain_recv_sem,
    vqkv, vout, qkv, save_sem, x_buf, x_sem, squares,
    held, sum_recv, turned, sum_send_sem, sum_recv_sem, gate_sem, *plane,
):
    me, at = lax.axis_index("mp"), lax.axis_index("dp")
    peer_barrier((("mp", me, n), ("dp", at, n_dp)))()
    gather = LineGather(
        n,
        me,
        lambda c: x.at[chunk_span(c, rows)],
        lambda index, c: full.at[index, chunk_span(c, rows)],
        send_sem,
        recv_sem,
        local_sem,
    )
    for c in range(CHUNKS):
        gather.step(c, 1)
    chips = n_dp // 2
    part_width, width = wq.shape
    row_count = rows * CHUNKS

    def part(owner):
        return pl.ds(pl.multiple_of(owner * part_width, part_width), part_width)

    by_qkv = PlaneGather(at, chips, part_width, lambda owner: vqkv.at[part(owner)], plane[:4])
    by_out = PlaneGather(at, chips, width, lambda owner: vout.at[:, part(owner)], plane[4:8])
    by_gate = PlaneGather(
        at, chips, part_width, lambda owner: full_gate.at[part(owner)], plane[8:]
    )
    gate_copy = pltpu.make_async_copy(wg, full_gate.at[part(at)], gate_sem)
    gate_copy.start()
    for k, weight in enumerate((wq, wk, wv)):
        vqkv[part(at), k * width : (k + 1) * width] = weight[...]
    by_qkv.send(False)
    vout[:, part(at)] = wo[...]
    copies = exchange(
        "dp", at, n_dp, lambda peer: gains, gain_recv, gain_send_sem, gain_recv_sem
    )
    for copy in copies:
        copy.start()

    def block(index, source):
        load = pltpu.make_async_copy(source, x_buf, x_sem)
        load.start()
        load.wait()
        here = pl.ds(pl.multiple_of(index * row_count, row_count), row_count)

        @pl.loop(0, 3)
        def _(tile):
            cols = pl.ds(pl.multiple_of(tile * width, width), width)
            value = plain_dot(x_buf[...], vqkv[:, cols])
            qkv[here, cols] = value
            squares[tile] = jnp.sum(value * value, axis=1, keepdims=True)

        pltpu.make_async_copy(qkv.at[here], qkv_out.at[here], save_sem.at[2]).start()
        held[:, here] = columns_to_rows(squares[0], squares[1])

    def blocks_at(step):
        @pl.loop(0, 2)
        def _(side):
            index = me - step + 2 * step * side

            @pl.when((index >= 0) & (index < n))
            def _():
                block(index, full.at[index])

    saves = [
        pltpu.make_async_copy(vqkv, full_qkv, save_sem.at[0]),
        pltpu.make_async_copy(vout, full_out, save_sem.at[1]),
        pltpu.make_async_copy(qkv, qkv_out, save_sem.at[2]),
    ]
    early = [r for r in range(1, chips) if len(bits_of(r)) == 1]
    late = [r for r in range(1, chips) if len(bits_of(r)) > 1]

    def next_weights():
        by_qkv.send(True)
        by_out.send(False)
        gate_copy.wait()
        by_gate.send(False)

    def qkv_here():
        by_qkv.finish()
        saves[0].start()
        block(me, x)

    def out_here():
        by_out.swap(late)
        by_out.finish()
        saves[1].start()

    hooks = {
        0: next_weights,
        3: lambda: by_qkv.swap(early),
        4: lambda: by_qkv.swap(late),
        5: qkv_here,
        6: lambda: by_out.send(True),
        7: lambda: (by_out.swap(early), by_gate.send(True)),
        8: out_here,
        9: lambda: by_gate.swap(early),
    }
    ready, number = 1, 0
    for step in range(2, n + 1):
        for c in range(CHUNKS):
            if step < n:
                gather.step(c, step)
            else:
                gather.last(c)
            if number in hooks:
                hooks.pop(number)()
            number += 1
        while number > 5 and ready < step:
            blocks_at(ready)
            ready += 1
    for hook in hooks.values():
        hook()
    while ready < n:
        blocks_at(ready)
        ready += 1
    def keep_gains(owner, row):
        gain_parts[owner] = row[:, 2 * part_width :]
        attn_scale[:, part(owner)] = row[:, :part_width]
        mlp_scale[:, part(owner)] = row[:, part_width : 2 * part_width]

    keep_gains(at, gains[...])
    for shift, copy in enumerate(copies, 1):
        copy.wait_recv()
        keep_gains(lax.rem(at + n_dp - shift, n_dp), gain_recv[shift - 1])
    by_gate.swap(late)
    q_sum, k_sum = sum_held(n, me, held, sum_recv, turned, sum_send_sem, sum_recv_sem)
    q_inv[...] = lax.rsqrt(q_sum / model_width + EPS)
    k_inv[...] = lax.rsqrt(k_sum / model_width + EPS)
    for c in range(CHUNKS):
        gather.drain(c)
    for copy in copies:
        copy.wait_send()
    by_gate.finish()
    for gathered in (by_qkv, by_out, by_gate):
        gathered.drain()
    for copy in saves:
        copy.wait()


def front(n, n_dp, block, wq, wk, wv, wo, gains, wg):
    row_count, model_width = block.shape
    rows = row_count // CHUNKS
    size = n * row_count
    width = wq.shape[1]
    chips = n_dp // 2
    column = jax.ShapeDtypeStruct((size, 1), F32)
    return pl.pallas_call(
        functools.partial(front_kernel, n, n_dp, rows, model_width),
        out_shape=(
            jax.ShapeDtypeStruct((n,) + block.shape, block.dtype),
            jax.ShapeDtypeStruct((size, 3 * width), F32),
            jax.ShapeDtypeStruct((model_width, 3 * width), BF),
            jax.ShapeDtypeStruct((width, model_width), BF),
            jax.ShapeDtypeStruct((n_dp, 1, gains.shape[1] - 2 * model_width // n_dp), F32),
            jax.ShapeDtypeStruct((1, model_width), F32),
            jax.ShapeDtypeStruct((1, model_width), F32),
            column,
            column,
            jax.ShapeDtypeStruct((model_width, wg.shape[1]), BF),
        ),
        in_specs=[VMEM] * 7,
        out_specs=(HBM, HBM, HBM, HBM, VMEM, VMEM, VMEM, VMEM, VMEM, HBM),
        scratch_shapes=gather_scratch(n, rows, model_width)[1:]
        + [
            pltpu.VMEM((n_dp - 1,) + gains.shape, F32),
            pltpu.SemaphoreType.DMA((n_dp - 1,)),
            pltpu.SemaphoreType.DMA((n_dp - 1,)),
            pltpu.VMEM((model_width, 3 * width), BF),
            pltpu.VMEM((width, model_width), BF),
            pltpu.VMEM((size, 3 * width), F32),
            pltpu.SemaphoreType.DMA((3,)),
            pltpu.VMEM((row_count, model_width), BF),
            pltpu.SemaphoreType.DMA,
            pltpu.VMEM((3, row_count, 1), F32),
        ]
        + sum_scratch(n, size)
        + [pltpu.SemaphoreType.DMA]
        + plane_sems(chips) * 3,
        compiler_params=pltpu.CompilerParams(
            collective_id=0, has_side_effects=True, vmem_limit_bytes=63 * MIB
        ),
        name="front",
        cost_estimate=cost(80),
    )(block, wq, wk, wv, wo, gains, wg)


class WeightTiles:
    def __init__(self, source, held, sem, axis, size):
        self.source, self.held, self.sem, self.axis, self.size = source, held, sem, axis, size
        self.count = source.shape[axis] // size

    def at(self, ref, tile):
        span = pl.ds(pl.multiple_of(tile * self.size, self.size), self.size)
        return ref.at[:, span] if self.axis == 1 else ref.at[span]

    def copy(self, tile):
        return pltpu.make_async_copy(
            self.at(self.source, tile), self.at(self.held, tile), self.sem.at[tile]
        )

    def start(self):
        for tile in range(self.count):
            self.copy(tile).start()


def middle_kernel(
    n, n_dp, rows, att, wo, wg, wu, wd, x, upstream_in, row_valid, mlp_scale, attn_scale,
    h_full, output, dm_full, hidden_out, mlp_gain, middle_grad, da_full, attn_gain, gate_out, up_out,
    part, recv, rs_send_sem, rs_recv_sem, total, own, ag_send_sem, ag_recv_sem, local_sem,
    vg, vu, vd, wsem, in_buf, in_sem, gate_all, up_all, hidden_buf, hidden_sem, packed,
    middle, branch, mg_sem, h_buf, h_sem, extra, ready, *more,
):
    me, at = lax.axis_index("mp"), lax.axis_index("dp")
    width, hidden_width = vg.shape
    local_width = wo.shape[0]
    chips = n_dp // 2
    part_width = width // n_dp
    plane, more = more[:16], more[16:]
    v_out = more[0] if more else gate_all.at[pl.ds(0, local_width)]
    v_att = up_all.at[:, pl.ds(0, local_width)]

    def start(copies):
        for copy in copies:
            copy.start()

    def wait(copies):
        for copy in copies:
            copy.wait()

    def weight_part(owner):
        return pl.ds(pl.multiple_of(owner * part_width, part_width), part_width)

    by_up = PlaneGather(at, chips, part_width, lambda owner: vu.at[weight_part(owner)], plane[8:12])
    by_down = PlaneGather(
        at, chips, hidden_width, lambda owner: vd.at[:, weight_part(owner)], plane[12:]
    )
    own_weights = [
        pltpu.make_async_copy(wu, by_up.place(0), wsem.at[0]),
        pltpu.make_async_copy(wd, by_down.place(0), wsem.at[1]),
    ]
    gate_copy = pltpu.make_async_copy(wg, vg, wsem.at[2])
    att_copies = [
        pltpu.make_async_copy(wo, v_out, wsem.at[3]),
        pltpu.make_async_copy(att, v_att, wsem.at[4]),
    ]
    start(att_copies)
    start(own_weights)
    gate_copy.start()
    stage_barrier(me, n, at, chips)
    wait(own_weights)
    by_up.send(False)

    scatter = LineScatter(n, me, rows, part, recv, rs_send_sem, rs_recv_sem)
    gathers = [
        make_gather(n, me, rows, own, full, ag_send_sem, ag_recv_sem, local_sem)
        for full in (h_full, dm_full, da_full)
    ]

    def in_copies(phase, c):
        source = gathers[phase - 1].full
        return [
            pltpu.make_async_copy(
                source(j, c), in_buf.at[c % 2, pl.ds(j * rows, rows)], in_sem.at[c % 2, j]
            )
            for j in range(n)
        ]

    def attend_out(c):
        if c == 0:
            wait(att_copies)
        block_rows = rows * CHUNKS
        for j in range(n):
            packed[j * rows : (j + 1) * rows] = v_att[
                j * block_rows + c * rows : j * block_rows + (c + 1) * rows
            ]

        @pl.loop(0, width // TILE)
        def _(tile):
            cols = pl.ds(pl.multiple_of(tile * TILE, TILE), TILE)
            part[c, :, cols] = plain_dot(packed[...], v_out[:, cols]).astype(BF)

    def attend_rows(c):
        scatter.total(c, total)
        span = chunk_span(c, rows)
        value = total[...]
        branch[span] = value
        new = x[span].astype(F32) + value * inverse_rms(value) * attn_scale[...]
        middle[span] = new
        own[c] = new.astype(BF)

    def hidden_copies(c):
        return [
            pltpu.make_async_copy(
                hidden_buf.at[c % 2, pl.ds(j * rows, rows)],
                hidden_out.at[j, chunk_span(c, rows)],
                hidden_sem.at[c % 2, j],
            )
            for j in range(n)
        ]

    def clear(phase, c):
        scatter.drain(c)
        gathers[phase - 1].drain_sends(c)
        wait(in_copies(phase, c))

    def forward(c):
        here = pl.ds(c * n * rows, n * rows)
        slot = c % 2
        clear(1, c)
        if c == 0:
            by_up.finish()
            gate_copy.wait()
        if c >= 2:
            wait(hidden_copies(c - 2))

        @pl.loop(0, hidden_width // TILE)
        def _(tile):
            cols = pl.ds(pl.multiple_of(tile * TILE, TILE), TILE)
            gate = plain_dot(in_buf[slot], vg[:, cols])
            up = plain_dot(in_buf[slot], vu[:, cols])
            gate_all[here, cols] = gate.astype(BF)
            up_all[here, cols] = up.astype(BF)
            hidden_buf[slot, :, cols] = (gate * jax.nn.sigmoid(gate) * up).astype(BF)

        start(hidden_copies(c))
        if c == 0:
            by_down.swap(late_chips)
            by_down.finish()

        @pl.loop(0, width // TILE)
        def _(tile):
            cols = pl.ds(pl.multiple_of(tile * TILE, TILE), TILE)
            part[c, :, cols] = plain_dot(hidden_buf[slot], vd[:, cols]).astype(BF)

    def backward(c):
        here = pl.ds(c * n * rows, n * rows)
        clear(2, c)

        @pl.loop(0, hidden_width // TILE)
        def _(tile):
            cols = pl.ds(pl.multiple_of(tile * TILE, TILE), TILE)
            hidden_grad = outer_dot(in_buf[c % 2], vd[cols, :])
            gate = gate_all[here, cols].astype(F32)
            up = up_all[here, cols].astype(F32)
            sigmoid = jax.nn.sigmoid(gate)
            gate_all[here, cols] = (
                hidden_grad * up * sigmoid * (1.0 + gate * (1.0 - sigmoid))
            ).astype(BF)
            up_all[here, cols] = (hidden_grad * gate * sigmoid).astype(BF)

        @pl.loop(0, width // TILE)
        def _(tile):
            cols = pl.ds(pl.multiple_of(tile * TILE, TILE), TILE)
            part[c, :, cols] = (
                outer_dot(gate_all[here], vg[cols, :]) + outer_dot(up_all[here], vu[cols, :])
            ).astype(BF)

        if c + 1 == CHUNKS:
            for last in range(max(CHUNKS - 2, 0), CHUNKS):
                wait(hidden_copies(last))
            for gathered in (by_up, by_down):
                gathered.drain()
            start(h_copies(0))
            signal_partners(ready, at, chips)

    def mg_copy(c):
        return pltpu.make_async_copy(
            middle.at[chunk_span(c, rows)], middle_grad.at[chunk_span(c, rows)], mg_sem.at[c]
        )

    def forward_rows(c):
        scatter.total(c, total)
        span = chunk_span(c, rows)
        value = total[...]
        inverse = inverse_rms(value)
        output[span] = (middle[span] + value * inverse * mlp_scale[...]).astype(BF)
        upstream = upstream_in[span].astype(F32) * row_valid[span]
        grad, gain = norm_back(value, inverse, mlp_scale[...], upstream)
        own[c] = grad.astype(BF)
        mlp_gain[...] = gain if c == 0 else mlp_gain[...] + gain

    def backward_rows(c):
        scatter.total(c, total)
        span = chunk_span(c, rows)
        upstream = upstream_in[span].astype(F32) * row_valid[span] + total[...]
        middle[span] = upstream
        mg_copy(c).start()
        value = branch[span]
        grad, gain = norm_back(value, inverse_rms(value), attn_scale[...], upstream)
        own[c] = grad.astype(BF)
        attn_gain[...] = gain if c == 0 else attn_gain[...] + gain

    block_width = pl.ds(0, hidden_width)

    def slot_at(index):
        for ref in (vg, vu, vd):
            count = ref.shape[0] // part_width
            if index < count:
                return ref.at[pl.ds(index * part_width, part_width), block_width]
            index -= count
        for ref in (hidden_buf, in_buf):
            if index < ref.shape[0]:
                return ref.at[index, pl.ds(0, part_width), block_width]
            index -= ref.shape[0]
        return extra.at[index]

    reduces = []
    for which, out in enumerate((gate_out, up_out)):
        first = chips + 3 * chips * which
        views = (
            lambda r: slot_at(r),
            lambda r, first=first: slot_at(first + r),
            lambda r, first=first: slot_at(first + chips + r),
            lambda r, first=first: slot_at(first + 2 * chips + r - 1),
        )
        reduces.append(
            PlaneReduce(at, chips, part_width, views, plane[4 * which : 4 * which + 4], out)
        )
    order = relative_order(chips)
    jobs = [
        (which, same_core, r)
        for which in range(2)
        for same_core in (False, True)
        for r in order
    ]

    def h_copies(index):
        which, same_core, r = jobs[index]
        first = reduces[which].owner(r, same_core) * part_width
        cols = pl.ds(pl.multiple_of(first, part_width), part_width)
        return [
            pltpu.make_async_copy(
                h_full.at[j, :, cols], h_buf.at[index % 2, j], h_sem.at[index % 2, j]
            )
            for j in range(n)
        ]

    def weight_block(index):
        which, same_core, r = jobs[index]
        reduce = reduces[which]
        grad = (gate_all, up_all)[which]
        if index == 0:
            pl.semaphore_wait(ready, 1 + len(bits_of(chips - 1)))
        wait(h_copies(index))
        if index + 1 < len(jobs):
            start(h_copies(index + 1))
        if same_core:
            reduce.core_copy(r).wait_recv()
        elif which == 1:
            reduces[0].drain_core(r)
        left = jnp.concatenate(
            [
                h_buf[index % 2, j, c * rows : (c + 1) * rows]
                for c in range(CHUNKS)
                for j in range(n)
            ],
            axis=0,
        )

        @pl.loop(0, hidden_width // TILE)
        def _(tile):
            cols = pl.ds(pl.multiple_of(tile * TILE, TILE), TILE)
            block = inner_dot(left, grad[:, cols])
            if not same_core:
                reduce.core_send(r)[:, cols] = block.astype(BF)
            else:
                block = block + reduce.core_recv(r)[:, cols].astype(F32)
                if r > 0:
                    reduce.held(r)[:, cols] = block.astype(BF)
                else:
                    reduce.out[:, cols] = block

        if not same_core:
            reduce.core_copy(r).start()
        elif r > 0:
            for half in range(2):
                if not reduce.before(r, half):
                    reduce.push(r, half)

    work = []
    for index, (which, same_core, r) in enumerate(jobs):
        work.append(functools.partial(weight_block, index))
        if same_core and r == order[-1]:
            for late in order:
                for half in range(2):
                    if late > 0 and reduces[which].before(late, half):
                        work.append(functools.partial(reduces[which].push, late, half))
    pending = iter(work)

    early_chips = [r for r in range(1, chips) if len(bits_of(r)) == 1]
    late_chips = [r for r in range(1, chips) if len(bits_of(r)) > 1]
    hooks = {
        HOOKS[0]: lambda: (by_up.send(True), by_down.send(False)),
        HOOKS[1]: lambda: by_up.swap(early_chips),
        HOOKS[2]: lambda: by_up.swap(late_chips),
        HOOKS[3]: lambda: by_down.send(True),
        HOOKS[4]: lambda: by_down.swap(early_chips),
    }
    last_step = 2 * n - 2
    events = sorted(
        (
            max(PERIOD, last_step + 1) * phase + step + STAGGER * c - (0.5 if step == 0 else 0),
            phase,
            c,
            step,
        )
        for phase in range(3)
        for c in range(CHUNKS)
        for step in range(last_step + 1)
    )
    filling = False
    for number, (_, phase, c, step) in enumerate(events):
        gather = gathers[phase]
        if number in hooks:
            hooks.pop(number)()
        if step == 0:
            (attend_out, forward, backward)[phase](c)
            filling = filling or (phase == 2 and c + 1 == CHUNKS)
        if step < n - 1:
            scatter.edge(c, step)
            if step > 0:
                scatter.step(c, step)
        elif step == n - 1:
            (attend_rows, forward_rows, backward_rows)[phase](c)
            gather.step(c, 1)
        elif step < last_step:
            gather.step(c, step - n + 2)
        else:
            gather.last(c)
            if phase < 2:
                gather.local_copy(c).wait()
                start(in_copies(phase + 1, c))
        if filling:
            for _ in range(FILL):
                job = next(pending, None)
                if job is not None:
                    job()
    for job in pending:
        job()
    for c in range(CHUNKS):
        scatter.drain(c)
        gathers[2].drain(c)
    for reduce in reduces:
        reduce.finish()
        reduce.drain()
    for r in range(chips):
        reduces[1].drain_core(r)
    for c in range(CHUNKS):
        mg_copy(c).wait()


def middle(n, n_dp, attended, full_out, wg, wu, wd, x, out_grad, row_valid, mlp_scale, attn_scale):
    row_count, width = x.shape
    hidden_width = wg.shape[1]
    rows = row_count // CHUNKS
    size = n * row_count
    chips = n_dp // 2
    part_width = width // n_dp
    block = (part_width, hidden_width)
    slots = (2 * width + hidden_width) // part_width + 4
    extra = 7 * chips - 1 - slots
    by_rows = jax.ShapeDtypeStruct((n, row_count, width), BF)
    return pl.pallas_call(
        functools.partial(middle_kernel, n, n_dp, rows),
        out_shape=(
            by_rows,
            jax.ShapeDtypeStruct((row_count, width), BF),
            by_rows,
            jax.ShapeDtypeStruct((n, row_count, hidden_width), BF),
            jax.ShapeDtypeStruct((1, width), F32),
            jax.ShapeDtypeStruct((row_count, width), F32),
            by_rows,
            jax.ShapeDtypeStruct((1, width), F32),
            jax.ShapeDtypeStruct(block, F32),
            jax.ShapeDtypeStruct(block, F32),
        ),
        in_specs=[HBM] * 5 + [VMEM] * 5,
        out_specs=(HBM, VMEM, HBM, HBM, VMEM, HBM, HBM, VMEM, VMEM, VMEM),
        scratch_shapes=scatter_scratch(n, rows, width)
        + gather_scratch(n, rows, width)
        + [
            pltpu.VMEM((width, hidden_width), BF),
            pltpu.VMEM((width, hidden_width), BF),
            pltpu.VMEM((hidden_width, width), BF),
            pltpu.SemaphoreType.DMA((5,)),
            pltpu.VMEM((2, n * rows, width), BF),
            pltpu.SemaphoreType.DMA((2, n)),
            pltpu.VMEM((size, hidden_width), BF),
            pltpu.VMEM((size, hidden_width), BF),
            pltpu.VMEM((2, n * rows, hidden_width), BF),
            pltpu.SemaphoreType.DMA((2, n)),
            pltpu.VMEM((n * rows, attended.shape[1]), BF),
            pltpu.VMEM((row_count, width), F32),
            pltpu.VMEM((row_count, width), F32),
            pltpu.SemaphoreType.DMA((CHUNKS,)),
            pltpu.VMEM((2, n, row_count, part_width), BF),
            pltpu.SemaphoreType.DMA((2, n)),
            pltpu.VMEM((extra,) + block if extra > 0 else (1, 16, 128), BF),
            pltpu.SemaphoreType.REGULAR,
        ]
        + plane_sems(chips) * 4
        + ([pltpu.VMEM(full_out.shape, BF)] if hidden_width < width else []),
        compiler_params=pltpu.CompilerParams(
            collective_id=2, has_side_effects=True, vmem_limit_bytes=63 * MIB
        ),
        name="middle",
        cost_estimate=cost(350),
    )(attended, full_out, wg, wu, wd, x, out_grad, row_valid, mlp_scale, attn_scale)


def last_grads_kernel(
    n, n_dp, rows, grads, weight, base, inputs, att, da, hidden, dm,
    attn_gain, mlp_gain, q_gain, k_gain,
    input_grad, qkv_out, out_out, down_out, gain_out,
    part, recv, rs_send_sem, rs_recv_sem, total, packed,
    x_buf, da_buf, dm_buf, load_sem, v_hidden, hidden_sem,
    send_qkv, recv_qkv, message_qkv, send_out, recv_out, message_out,
    send_down, recv_down, message_down,
    gains, gain_recv, gain_send_sem, gain_recv_sem, mp_recv, mp_send_sem, mp_recv_sem, *plane,
):
    me, at = lax.axis_index("mp"), lax.axis_index("dp")
    entered = peer_barrier((("mp", me, n), ("dp", at, n_dp)))
    width = weight.shape[0]
    block_rows = rows * CHUNKS
    local_width = att.shape[1]
    chips = n_dp // 2
    part_width = width // n_dp
    order = relative_order(chips)

    def views(send, recv, message):
        return (
            lambda r: send.at[r],
            lambda r: recv.at[r],
            lambda r: send.at[r],
            lambda r: message.at[r - 1],
        )

    by_qkv = PlaneReduce(
        at, chips, part_width, views(send_qkv, recv_qkv, message_qkv), plane[:4], qkv_out
    )
    by_out = PlaneReduce(
        at, chips, local_width, views(send_out, recv_out, message_out), plane[4:8], out_out
    )
    by_down = PlaneReduce(
        at, chips, part_width, views(send_down, recv_down, message_down), plane[8:], down_out
    )
    jobs = [
        (down, same_core, r)
        for down in (True, False)
        for same_core in (False, True)
        for r in order
    ]

    def loads(k):
        down, same_core, r = jobs[k]
        first = by_qkv.owner(r, same_core) * part_width
        cols = pl.ds(pl.multiple_of(first, part_width), part_width)
        pairs = ((dm, dm_buf),) if down else ((inputs, x_buf), (da, da_buf))
        return [
            pltpu.make_async_copy(source.at[:, cols], buf.at[k % 2], load_sem.at[k % 2, which])
            for which, (source, buf) in enumerate(pairs)
        ]

    load_hidden = pltpu.make_async_copy(hidden, v_hidden, hidden_sem)
    for copy in loads(0):
        copy.start()
    load_hidden.start()

    def compute(c):
        for j in range(n):
            packed[j * rows : (j + 1) * rows] = grads[
                j * block_rows + c * rows : j * block_rows + (c + 1) * rows
            ]

        @pl.loop(0, width // TILE)
        def _(tile):
            cols = pl.ds(pl.multiple_of(tile * TILE, TILE), TILE)
            part[c, :, cols] = outer_dot(packed[...], weight[cols, :]).astype(BF)

    scatter = LineScatter(n, me, rows, part, recv, rs_send_sem, rs_recv_sem)

    def row_work(c):
        scatter.total(c, total)
        span = chunk_span(c, rows)
        input_grad[span] = base[span] + total[...]

    def weight_block(k):
        down, same_core, r = jobs[k]
        slot = k % 2
        reduces = (by_down,) if down else (by_qkv, by_out)
        for copy in loads(k):
            copy.wait()
        if k + 1 < len(jobs):
            for copy in loads(k + 1):
                copy.start()
        if k == 0:
            load_hidden.wait()
        if same_core:
            for reduce in reduces:
                reduce.core_copy(r).wait_recv()
                reduce.drain_core(r)

        def keep(reduce, block, cols):
            if not same_core:
                reduce.core_send(r)[:, cols] = block.astype(BF)
                return
            block = block + reduce.core_recv(r)[:, cols].astype(F32)
            if r > 0:
                reduce.held(r)[:, cols] = block.astype(BF)
            else:
                reduce.out[:, cols] = block

        if down:

            @pl.loop(0, hidden.shape[1] // TILE)
            def _(tile):
                cols = pl.ds(pl.multiple_of(tile * TILE, TILE), TILE)
                keep(by_down, inner_dot(dm_buf[slot], v_hidden[:, cols]), cols)

        else:

            @pl.loop(0, 3)
            def _(tile):
                cols = pl.ds(pl.multiple_of(tile * local_width, local_width), local_width)
                keep(by_qkv, inner_dot(x_buf[slot], grads[:, cols]), cols)

            keep(by_out, inner_dot(att[...], da_buf[slot]), slice(None))
        for reduce in reduces:
            if not same_core:
                reduce.core_copy(r).start()
            elif r > 0:
                for half in range(2):
                    if not reduce.before(r, half):
                        reduce.push(r, half)

    def push_late(reduces):
        for r in order:
            for half in range(2):
                if r > 0 and reduces[0].before(r, half):
                    for reduce in reduces:
                        reduce.push(r, half)

    for index in range(n_dp):
        span = slice(index * part_width, (index + 1) * part_width)
        gains[index, :, :part_width] = attn_gain[:, span]
        gains[index, :, part_width : 2 * part_width] = mlp_gain[:, span]
        gains[index, :, 2 * part_width : 2 * part_width + local_width] = q_gain[...]
        gains[index, :, 2 * part_width + local_width :] = k_gain[...]
    gain_copies = exchange(
        "dp", at, n_dp, lambda peer: gains.at[peer], gain_recv, gain_send_sem, gain_recv_sem
    )
    mp_copies = exchange("mp", me, n, lambda peer: gain_out, mp_recv, mp_send_sem, mp_recv_sem)
    line = iter([(step, c) for c in range(CHUNKS) for step in range(1, n)])

    def line_steps(count):
        for _ in range(count):
            step, c = next(line, (None, None))
            if step is None:
                return
            if step < n - 1:
                scatter.step(c, step)
            else:
                row_work(c)

    def send_edges(c):
        for step in range(n - 1):
            scatter.edge(c, step)

    compute(0)
    entered()
    send_edges(0)
    for copy in gain_copies:
        copy.start()
    sent = 1
    for k in range(len(jobs)):
        weight_block(k)
        if k % 4 == 3 and sent < CHUNKS:
            compute(sent)
            send_edges(sent)
            sent += 1
        if k >= LINE_FROM:
            line_steps(1)
        if k == 3 * chips:
            push_late((by_down,))
    push_late((by_qkv, by_out))
    gain_out[...] = gains[at]
    for shift, copy in enumerate(gain_copies, 1):
        copy.wait_recv()
        gain_out[...] += gain_recv[shift - 1]
    for copy in mp_copies:
        copy.start()
    line_steps(n * CHUNKS)
    for reduce in (by_down, by_qkv, by_out):
        reduce.finish()
    for copy in mp_copies:
        copy.wait_recv()
        copy.wait_send()
    lanes = lax.broadcasted_iota(jnp.int32, gain_out.shape, 1)
    shared = gain_out[...]
    for shift in range(1, n):
        shared = shared + mp_recv[shift - 1]
    gain_out[...] = jnp.where(lanes < 2 * part_width, shared, gain_out[...])
    for copy in gain_copies:
        copy.wait_send()
    for c in range(CHUNKS):
        scatter.drain(c)
    for reduce in (by_down, by_qkv, by_out):
        reduce.drain()


def last_grads(n, n_dp, grads, weight, base, inputs, attended, da_full, hidden, dm, *gains):
    row_count, width = base.shape
    rows = row_count // CHUNKS
    size, local_width = attended.shape
    part_width = width // n_dp
    chips = n_dp // 2
    qkv_block = (part_width, 3 * local_width)
    out_block = (local_width, part_width)
    down_block = (part_width, hidden.shape[1])
    gain_block = (1, 2 * part_width + 2 * local_width)
    return pl.pallas_call(
        functools.partial(last_grads_kernel, n, n_dp, rows),
        out_shape=(
            jax.ShapeDtypeStruct((row_count, width), F32),
            jax.ShapeDtypeStruct(qkv_block, F32),
            jax.ShapeDtypeStruct(out_block, F32),
            jax.ShapeDtypeStruct(down_block, F32),
            jax.ShapeDtypeStruct(gain_block, F32),
        ),
        in_specs=[VMEM, VMEM, VMEM, HBM, VMEM, HBM, HBM, HBM] + [VMEM] * 4,
        out_specs=(VMEM,) * 5,
        scratch_shapes=scatter_scratch(n, rows, width)
        + [
            pltpu.VMEM((n * rows, 3 * local_width), BF),
            pltpu.VMEM((2, size, part_width), BF),
            pltpu.VMEM((2, size, part_width), BF),
            pltpu.VMEM((2, size, part_width), BF),
            pltpu.SemaphoreType.DMA((2, 2)),
            pltpu.VMEM(hidden.shape, BF),
            pltpu.SemaphoreType.DMA,
        ]
        + [
            pltpu.VMEM((count,) + block, BF)
            for block in (qkv_block, out_block, down_block)
            for count in (chips, chips, chips - 1)
        ]
        + [pltpu.VMEM((n_dp,) + gain_block, F32), pltpu.VMEM((n_dp - 1,) + gain_block, F32)]
        + [pltpu.SemaphoreType.DMA((n_dp - 1,))] * 2
        + [pltpu.VMEM((n - 1,) + gain_block, F32)]
        + [pltpu.SemaphoreType.DMA((n - 1,))] * 2
        + plane_sems(chips) * 3,
        compiler_params=pltpu.CompilerParams(
            collective_id=4, has_side_effects=True, vmem_limit_bytes=63 * MIB
        ),
        name="last_grads",
        cost_estimate=cost(80),
    )(grads, weight, base, inputs, attended, da_full, hidden, dm, *gains)


def turn(values, cos, sin):
    return values * cos + pltpu.roll(values, values.shape[1] // 2, 1) * sin


def turn_back(values, cos, sin):
    return values * cos + pltpu.roll(values * sin, values.shape[1] // 2, 1)


def allowed_keys(starts, first_row, rows, key_end):
    places = first_row + lax.broadcasted_iota(jnp.int32, (rows, key_end), 0)
    keys = lax.broadcasted_iota(jnp.int32, (rows, key_end), 1)
    return (keys <= places) & (keys >= starts)


def columns_to_rows(first, second):
    lanes = lax.broadcasted_iota(jnp.int32, (first.shape[0], 128), 1)
    return jnp.transpose(jnp.where(lanes == 0, first, second))[:8]


def sum_held(n, me, held, recv, turned, send_sem, recv_sem):
    copies = exchange("mp", me, n, lambda peer: held, recv, send_sem, recv_sem)
    for copy in copies:
        copy.start()
    total = held[...]
    for shift, copy in enumerate(copies, 1):
        copy.wait_recv()
        total = total + recv[shift - 1]
    for copy in copies:
        copy.wait_send()
    turned[...] = jnp.zeros_like(turned)
    turned[:8] = total
    back = jnp.transpose(turned[...])
    return back[:, 0:1], back[:, 1:2]


def sum_scratch(n, size):
    return [
        pltpu.VMEM((8, size), F32),
        pltpu.VMEM((n - 1, 8, size), F32),
        pltpu.VMEM((128, size), F32),
        pltpu.SemaphoreType.DMA((n - 1,)),
        pltpu.SemaphoreType.DMA((n - 1,)),
    ]


def attention_kernel(
    q_raw, k_raw, v_raw, q_inv, k_inv, q_gain, k_gain, cos, sin, starts,
    out, q_low, k_low, v_low, log_total,
):
    size, head = q_raw.shape
    score_scale = 1.0 / math.sqrt(head)
    q_low[...] = turn(q_raw[...] * q_inv[...] * q_gain[...], cos[...], sin[...]).astype(BF)
    k_low[...] = turn(k_raw[...] * k_inv[...] * k_gain[...], cos[...], sin[...]).astype(BF)
    v_low[...] = v_raw[...].astype(BF)
    rows = min(QUERY_ROWS, size)
    for first in range(0, size, rows):
        end = first + rows
        span = slice(first, end)
        scores = outer_dot(q_low[span], k_low[:end]) * score_scale
        scores = jnp.where(allowed_keys(starts[span], first, rows, end), scores, MASKED)
        row_max = jnp.max(scores, axis=1, keepdims=True)
        exponents = jnp.exp(scores - row_max)
        row_total = jnp.sum(exponents, axis=1, keepdims=True)
        probs = (exponents * (1.0 / row_total)).astype(BF)
        out[span] = plain_dot(probs, v_low[:end]).astype(BF)
        log_total[span] = row_max + jnp.log(row_total)


def head_specs(size, head, heads, count):
    return [pl.BlockSpec((size, head), lambda h, k=k: (0, k * heads + h)) for k in range(count)]


def attention(qkv_raw, q_inv, k_inv, q_gain, k_gain, cos, sin, starts, heads):
    size = qkv_raw.shape[0]
    head = cos.shape[1]
    column = pl.BlockSpec((size, 1), lambda h: (0, 0))
    table = pl.BlockSpec((size, head), lambda h: (0, 0))
    gain = pl.BlockSpec((1, head), lambda h: (0, h))
    by_head = pl.BlockSpec((size, head), lambda h: (0, h))
    low = jax.ShapeDtypeStruct((size, heads * head), BF)
    return pl.pallas_call(
        attention_kernel,
        grid=(heads,),
        out_shape=(low, low, low, low, jax.ShapeDtypeStruct((heads, size, 1), F32)),
        in_specs=head_specs(size, head, heads, 3)
        + [column, column, gain, gain, table, table, column],
        out_specs=(by_head,) * 4 + (pl.BlockSpec((None, size, 1), lambda h: (h, 0, 0)),),
        compiler_params=pltpu.CompilerParams(vmem_limit_bytes=63 * MIB),
        name="attention",
        cost_estimate=cost(18),
    )(qkv_raw, qkv_raw, qkv_raw, q_inv, k_inv, q_gain, k_gain, cos, sin, starts)


def attention_back_kernel(
    n, heads, model_width, qkv, q_low, k_low, v_low, out_grad, log_total,
    q_inv, k_inv, q_gain, k_gain, cos, sin, starts,
    grads, q_gain_grad, k_gain_grad,
    q_weighted, k_weighted, q_grad, k_sum, v_sum, q_dots, k_dots, *sums,
):
    me = lax.axis_index("mp")
    entered = peer_barrier((("mp", me, n),))
    size = qkv.shape[0]
    width = qkv.shape[1] // 3
    head = width // heads
    score_scale = 1.0 / math.sqrt(head)
    rows = min(QUERY_ROWS, size)
    q_dots[...] = jnp.zeros_like(q_dots)
    k_dots[...] = jnp.zeros_like(k_dots)

    @pl.loop(0, heads)
    def _(h):
        def cols(first):
            return pl.ds(pl.multiple_of(first + h * head, head), head)

        here = cols(0)
        for first in reversed(range(0, size, rows)):
            end = first + rows
            span = slice(first, end)
            scores = outer_dot(q_low[span, here], k_low[:end, here]) * score_scale
            scores = jnp.where(allowed_keys(starts[span], first, rows, end), scores, MASKED)
            probs = jnp.exp(scores - log_total[h, span])
            prob_grad = outer_dot(out_grad[span, here], v_low[:end, here])
            probs_low = probs.astype(BF)
            weighted = probs * prob_grad
            score_grad = (
                weighted - probs * jnp.sum(weighted, axis=1, keepdims=True)
            ).astype(BF)
            q_grad[span] = plain_dot(score_grad, k_low[:end, here]) * score_scale
            k_extra = inner_dot(score_grad, q_low[span, here])
            v_extra = inner_dot(probs_low, out_grad[span, here])
            if end == size:
                k_sum[...] = k_extra
                v_sum[...] = v_extra
            else:
                k_sum[:end] += k_extra
                v_sum[:end] += v_extra
        for first, inv, gain, grad, factor, weighted_out, dots, gain_grad in (
            (0, q_inv, q_gain, q_grad, None, q_weighted, q_dots, q_gain_grad),
            (width, k_inv, k_gain, k_sum, score_scale, k_weighted, k_dots, k_gain_grad),
        ):
            raw = qkv[:, cols(first)]
            value = grad[...] if factor is None else grad[...] * factor
            normed = turn_back(value, cos[...], sin[...])
            weighted = normed * gain[:, here]
            weighted_out[:, here] = weighted
            gain_grad[:, here] = jnp.sum(normed * raw * inv[...], axis=0, keepdims=True)
            dots[...] += jnp.sum(weighted * raw, axis=1, keepdims=True)
        grads[:, cols(2 * width)] = v_sum[...].astype(BF)

    held = sums[0]
    held[...] = columns_to_rows(q_dots[...], k_dots[...])
    entered()
    q_total, k_total = sum_held(n, me, *sums)
    for first, inv, weighted, dots in (
        (0, q_inv, q_weighted, q_total),
        (width, k_inv, k_weighted, k_total),
    ):
        scale = inv[...]
        factor = scale * scale * scale * (dots / model_width)
        grads[:, first : first + width] = (
            scale * weighted[...] - qkv[:, first : first + width] * factor
        ).astype(BF)


def attention_back(
    n, heads, model_width, qkv_raw, q_low, k_low, v_low, out_grad, log_total, q_inv, k_inv,
    q_gain, k_gain, cos, sin, starts,
):
    size, width = q_low.shape
    head = width // heads
    gains = jax.ShapeDtypeStruct((1, width), F32)
    return pl.pallas_call(
        functools.partial(attention_back_kernel, n, heads, model_width),
        out_shape=(jax.ShapeDtypeStruct((size, 3 * width), BF), gains, gains),
        in_specs=[VMEM] * 13,
        out_specs=(VMEM,) * 3,
        scratch_shapes=[pltpu.VMEM((size, width), F32)] * 2
        + [pltpu.VMEM((size, head), F32)] * 3
        + [pltpu.VMEM((size, 1), F32)] * 2
        + sum_scratch(n, size),
        compiler_params=pltpu.CompilerParams(
            collective_id=6, has_side_effects=True, vmem_limit_bytes=63 * MIB
        ),
        name="attention_back",
        cost_estimate=cost(30),
    )(
        qkv_raw, q_low, k_low, v_low, out_grad, log_total, q_inv, k_inv, q_gain, k_gain,
        cos, sin, starts,
    )


def local(
    layer_input,
    query_weight,
    key_weight,
    value_weight,
    out_weight,
    gate_weight,
    up_weight,
    down_weight,
    query_gain,
    key_gain,
    attn_gain,
    mlp_gain,
    seq_lens,
    out_grad,
):
    n = lax.axis_size("mp")
    n_dp = lax.axis_size("dp")
    me = lax.axis_index("mp")
    row_count, model_width = layer_input.shape
    group_size = row_count * n
    local_heads, gain_part = query_gain.shape
    head_size = gain_part * n_dp
    local_width = local_heads * head_size

    head_part = local_heads * gain_part
    width_part = attn_gain.shape[0]
    own_gains = jnp.concatenate(
        [attn_gain, mlp_gain, query_gain.reshape(head_part), key_gain.reshape(head_part)]
    ).astype(F32)[None]
    (
        inputs_full, qkv_raw, full_qkv, full_out, gain_parts, attn_scale, mlp_scale, query_inv,
        key_inv, full_gate,
    ) = front(
        n, n_dp, layer_input, query_weight, key_weight, value_weight, out_weight, own_gains,
        gate_weight,
    )
    inputs_full = inputs_full.reshape(group_size, model_width)
    gain_parts = gain_parts[:, 0]

    def head_gain(first):
        piece = gain_parts[:, first : first + head_part].reshape(n_dp, local_heads, gain_part)
        return piece.transpose(1, 0, 2).reshape(1, local_width)

    query_scale = head_gain(0)
    key_scale = head_gain(head_part)

    starts, positions, valid = layout(seq_lens[0], group_size)
    starts = starts[:, None]
    cos_table, sin_table = rotary_tables(positions, head_size)
    row_valid = lax.dynamic_slice_in_dim(valid, me * row_count, row_count, 0).astype(F32)[:, None]

    attended, query_low, key_low, value_low, log_total = attention(
        qkv_raw, query_inv, key_inv, query_scale, key_scale, cos_table, sin_table, starts,
        local_heads,
    )
    (
        middle_full, layer_output, mlp_grad_full, hidden, mlp_gain_part, middle_grad, branch_full,
        attn_gain_part, grad_gate, grad_up,
    ) = middle(
        n, n_dp, attended, full_out, full_gate, up_weight, down_weight, layer_input, out_grad,
        row_valid, mlp_scale, attn_scale,
    )

    def flat(rows):
        return rows.reshape(group_size, rows.shape[-1])

    branch_full = flat(branch_full)
    mixed_grad = outer_dot(branch_full, full_out).astype(BF)
    qkv_grad, query_gain_part, key_gain_part = attention_back(
        n, local_heads, model_width, qkv_raw, query_low, key_low, value_low, mixed_grad, log_total,
        query_inv, key_inv, query_scale, key_scale, cos_table, sin_table, starts,
    )

    input_grad, grad_qkv, grad_out, grad_down, gain_sums = last_grads(
        n, n_dp, qkv_grad, full_qkv, middle_grad, inputs_full, attended, branch_full,
        flat(hidden), flat(mlp_grad_full), attn_gain_part, mlp_gain_part, query_gain_part,
        key_gain_part,
    )
    gain_sums = gain_sums[0]
    heads_at = 2 * width_part
    head_sums = lax.dynamic_index_in_dim(
        gain_sums[heads_at:].reshape(2, local_heads, n_dp, gain_part),
        lax.axis_index("dp"),
        2,
        keepdims=False,
    )
    return (
        layer_output,
        input_grad,
        grad_qkv[:, :local_width],
        grad_qkv[:, local_width : 2 * local_width],
        grad_qkv[:, 2 * local_width :],
        grad_out,
        grad_gate,
        grad_up,
        grad_down.T,
        head_sums[0],
        head_sums[1],
        gain_sums[:width_part],
        gain_sums[width_part:heads_at],
    )


def solution(mesh):
    return jax.shard_map(
        local,
        mesh=mesh,
        in_specs=(
            P(("dp", "mp"), None),
            P("dp", "mp"),
            P("dp", "mp"),
            P("dp", "mp"),
            P("mp", "dp"),
            P("dp", "mp"),
            P("dp", "mp"),
            P("mp", "dp"),
            P("mp", "dp"),
            P("mp", "dp"),
            P("dp"),
            P("dp"),
            P("dp", None),
            P(("dp", "mp"), None),
        ),
        out_specs=(
            P(("dp", "mp"), None),
            P(("dp", "mp"), None),
            P("dp", "mp"),
            P("dp", "mp"),
            P("dp", "mp"),
            P("mp", "dp"),
            P("dp", "mp"),
            P("dp", "mp"),
            P("mp", "dp"),
            P("mp", "dp"),
            P("mp", "dp"),
            P("dp"),
            P("dp"),
        ),
        check_vma=False,
    )
```

```python
import functools
import math

import jax
import jax.numpy as jnp
from jax import lax
from jax.experimental import pallas as pl
from jax.experimental.pallas import tpu as pltpu
from jax.sharding import PartitionSpec as P

EPS = 1e-06
THETA = 500000.0
MASKED = -1000000000.0
CHUNKS = 4
STAGGER = 2
EDGES = False
FILL = 2
PERIOD = 8
LINE_FROM = 11
HOOKS = (3, 7, 10, 13, 16)
TILE = 512
QUERY_ROWS = 512
BACK_ROWS = 256
BF = jnp.bfloat16
F32 = jnp.float32
MIB = 1 << 20
HBM = pl.BlockSpec(memory_space=pl.ANY)
VMEM = pl.BlockSpec(memory_space=pltpu.VMEM)


def cost(micros):
    return pl.CostEstimate(
        flops=micros * 1_000_000_000, bytes_accessed=micros * 3_000_000, transcendentals=0
    )


def plain_dot(former, latter):
    return jnp.dot(former, latter, preferred_element_type=F32)


def inner_dot(former, latter):
    return lax.dot_general(
        former, latter, (((0,), (0,)), ((), ())), preferred_element_type=F32
    )


def outer_dot(former, latter):
    return lax.dot_general(
        former, latter, (((1,), (1,)), ((), ())), preferred_element_type=F32
    )


def layout(lengths, group_size):
    slot_count = lengths.shape[0]
    seq_ends = jnp.cumsum(lengths, dtype=jnp.int32)
    starts = seq_ends - lengths
    places = jnp.arange(group_size, dtype=jnp.int32)
    slot_ids = jnp.arange(slot_count, dtype=jnp.int32)
    segment = jnp.sum(
        (places[:, None] >= seq_ends[None, :]).astype(jnp.int32), axis=1, dtype=jnp.int32
    )
    chosen = (segment[:, None] == slot_ids[None, :]).astype(jnp.int32)
    padded = (segment == slot_count).astype(jnp.int32)
    begins = (
        jnp.sum(chosen * starts[None, :], axis=1, dtype=jnp.int32)
        + padded * seq_ends[slot_count - 1]
    )
    return (begins, places - begins, places < seq_ends[slot_count - 1])


def rotary_tables(positions, head_size):
    half_dim = head_size // 2
    frequency = jnp.exp(jnp.arange(half_dim, dtype=F32) * (-2.0 * math.log(THETA) / head_size))
    angles = positions.astype(F32)[:, None] * frequency[None, :]
    cos_half, sin_half = jnp.cos(angles), jnp.sin(angles)
    return (
        jnp.concatenate([cos_half, cos_half], axis=1),
        jnp.concatenate([-sin_half, sin_half], axis=1),
    )


def neighbour_barrier(me, n):
    barrier = pltpu.get_barrier_semaphore()

    @pl.when(me > 0)
    def _():
        pl.semaphore_signal(barrier, inc=1, device_id={"mp": me - 1})

    @pl.when(me < n - 1)
    def _():
        pl.semaphore_signal(barrier, inc=1, device_id={"mp": me + 1})

    pl.semaphore_wait(barrier, jnp.minimum(me, 1) + jnp.minimum(n - 1 - me, 1))


class LineGather:
    def __init__(self, n, me, own, full, send_sem, recv_sem, local_sem):
        self.n, self.me, self.own, self.full = n, me, own, full
        self.send_sem, self.recv_sem, self.local_sem = send_sem, recv_sem, local_sem

    def local_copy(self, c):
        return pltpu.make_async_copy(self.own(c), self.full(self.me, c), self.local_sem.at[c])

    def copy(self, c, step, way, block, src):
        return pltpu.make_async_remote_copy(
            src_ref=src,
            dst_ref=self.full(block, c),
            send_sem=self.send_sem.at[c, step - 1, way],
            recv_sem=self.recv_sem.at[c, step - 1, way],
            device_id={"mp": self.me + (1 if way == 0 else -1)},
        )

    def sides(self):
        return ((0, self.me), (1, self.n - 1 - self.me))

    def block_at(self, way, step):
        return self.me - step if way == 0 else self.me + step

    def step(self, c, step):
        n = self.n
        if step == 1:
            self.local_copy(c).start()
        for way, place in self.sides():
            if step > 1:

                @pl.when(place >= step - 1)
                def _(way=way):
                    block = self.block_at(way, step - 1)
                    self.copy(c, step - 1, way, block, self.own(c)).wait_recv()

            @pl.when((place >= step - 1) & (place < n - 1))
            def _(way=way):
                block = self.block_at(way, step - 1)
                src = self.own(c) if step == 1 else self.full(block, c)
                self.copy(c, step, way, block, src).start()

    def last(self, c):
        n = self.n
        for way, place in self.sides():

            @pl.when(place == n - 1)
            def _(way=way):
                block = self.block_at(way, n - 1)
                self.copy(c, n - 1, way, block, self.own(c)).wait_recv()

    def drain(self, c):
        self.local_copy(c).wait()
        self.drain_sends(c)

    def drain_sends(self, c):
        for step in range(1, self.n):
            for way, place in self.sides():

                @pl.when((place >= step - 1) & (place < self.n - 1))
                def _(way=way):
                    self.copy(c, step, way, self.me, self.own(c)).wait_send()


class LineScatter:
    def __init__(self, n, me, rows, part, recv, send_sem, recv_sem):
        self.n, self.me, self.rows = n, me, rows
        self.part, self.recv = part, recv
        self.send_sem, self.recv_sem = send_sem, recv_sem

    def piece(self, c, owner):
        first = pl.multiple_of(owner * self.rows, self.rows)
        return self.part.at[c, pl.ds(first, self.rows)]

    def copy(self, c, step, way, src):
        return pltpu.make_async_remote_copy(
            src_ref=src,
            dst_ref=self.recv.at[c, step, way],
            send_sem=self.send_sem.at[c, step, way],
            recv_sem=self.recv_sem.at[c, step, way],
            device_id={"mp": self.me + (1 if way == 0 else -1)},
        )

    def sides(self):
        return ((0, self.me), (1, self.n - 1 - self.me))

    def owner(self, way, step):
        return self.n - 1 - step + self.me if way == 0 else step - (self.n - 1 - self.me)

    def edge(self, c, step):
        for way, place in self.sides():

            @pl.when(place == 0)
            def _(way=way):
                self.copy(c, step, way, self.piece(c, self.owner(way, step))).start()

    def step(self, c, step):
        for way, place in self.sides():

            @pl.when((place > 0) & (place <= min(step, self.n - 2)))
            def _(way=way):
                piece = self.piece(c, self.owner(way, step))
                self.copy(c, step - 1, way, piece).wait_recv()
                piece[...] = (
                    piece[...].astype(F32) + self.recv[c, step - 1, way].astype(F32)
                ).astype(BF)
                self.copy(c, step, way, piece).start()

    def total(self, c, out):
        n = self.n
        out[...] = self.piece(c, self.me)[...].astype(F32)
        for way, place in self.sides():

            @pl.when(place > 0)
            def _(way=way):
                self.copy(c, n - 2, way, self.recv.at[c, n - 2, way]).wait_recv()
                out[...] += self.recv[c, n - 2, way].astype(F32)

    def drain(self, c):
        n = self.n
        for step in range(n - 1):
            for way, place in self.sides():

                @pl.when(place <= min(step, n - 2))
                def _(way=way):
                    self.copy(c, step, way, self.recv.at[c, step, way]).wait_send()


def run_line(n, chunks, stagger, compute, scatter, row_work, gather, filler=None):
    last_step = 2 * n - 2 if gather is not None else n - 1
    events = sorted(
        (step + stagger * c - (0.5 if step == 0 else 0), c, step)
        for c in range(chunks)
        for step in range(last_step + 1)
    )
    computed = 0
    for _, c, step in events:
        if step == 0:
            compute(c)
            for ahead in range(n - 1 if EDGES else 1):
                scatter.edge(c, ahead)
            computed += 1
        elif step < n - 1:
            if not EDGES:
                scatter.edge(c, step)
            scatter.step(c, step)
        elif step == n - 1:
            row_work(c)
            if gather is not None:
                gather.step(c, 1)
        elif step < 2 * n - 2:
            gather.step(c, step - n + 2)
        else:
            gather.last(c)
        if filler is not None and computed == chunks:
            filler()
    for c in range(chunks):
        scatter.drain(c)
        if gather is not None:
            gather.drain(c)


def flipped(chip, bit):
    return chip + bit - 2 * bit * lax.rem(chip // bit, 2)


def bits_of(number):
    return [1 << k for k in range(number.bit_length()) if number >> k & 1]


def relative_chip(chip, relative):
    for bit in bits_of(relative):
        chip = flipped(chip, bit)
    return chip


def relative_order(chips):
    return sorted(range(chips), key=lambda r: (-len(bits_of(r)), r))


class PlaneReduce:
    def __init__(self, at, chips, rows, views, sems, out):
        self.chip, self.core = at // 2, lax.rem(at, 2)
        self.chips, self.rows, self.out = chips, rows, out
        self.core_send, self.core_recv, self.held, self.message = views
        self.core_send_sem, self.core_recv_sem, self.send_sem, self.recv_sem = sems

    def first_bit(self, relative, half):
        bits = bits_of(relative)
        return bits[0] if half == 0 else bits[-1]

    def before(self, relative, half):
        return [
            r for r in range(1, self.chips) if r - self.first_bit(r, half) == relative
        ]

    def owner(self, relative, same_core):
        return 2 * relative_chip(self.chip, relative) + (
            self.core if same_core else 1 - self.core
        )

    def half_rows(self, half):
        return pl.ds(half * (self.rows // 2), self.rows // 2)

    def core_copy(self, relative):
        return pltpu.make_async_remote_copy(
            src_ref=self.core_send(relative),
            dst_ref=self.core_recv(relative),
            send_sem=self.core_send_sem.at[relative],
            recv_sem=self.core_recv_sem.at[relative],
            device_id={"dp": 2 * self.chip + 1 - self.core},
        )

    def message_copy(self, relative, half):
        span = self.half_rows(half)
        target = flipped(self.chip, self.first_bit(relative, half))
        return pltpu.make_async_remote_copy(
            src_ref=self.held(relative).at[span],
            dst_ref=self.message(relative).at[span],
            send_sem=self.send_sem.at[relative, half],
            recv_sem=self.recv_sem.at[relative, half],
            device_id={"dp": 2 * target + self.core},
        )

    def push(self, relative, half):
        span = self.half_rows(half)
        for r in self.before(relative, half):
            self.message_copy(r, half).wait_recv()
            held = self.held(relative)
            held[span] = (
                held[span].astype(F32) + self.message(r)[span].astype(F32)
            ).astype(BF)
        self.message_copy(relative, half).start()

    def finish(self):
        for half in range(2):
            span = self.half_rows(half)
            for r in self.before(0, half):
                self.message_copy(r, half).wait_recv()
                self.out[span] += self.message(r)[span].astype(F32)

    def drain_core(self, relative):
        self.core_copy(relative).wait_send()

    def drain(self):
        for r in range(1, self.chips):
            for half in range(2):
                self.message_copy(r, half).wait_send()


def plane_sems(chips):
    return [pltpu.SemaphoreType.DMA((chips,))] * 2 + [pltpu.SemaphoreType.DMA((chips, 2))] * 2


def stage_barrier(me, n, at, chips):
    barrier = pltpu.get_barrier_semaphore()

    @pl.when(me > 0)
    def _():
        pl.semaphore_signal(barrier, inc=1, device_id={"mp": me - 1})

    @pl.when(me < n - 1)
    def _():
        pl.semaphore_signal(barrier, inc=1, device_id={"mp": me + 1})

    count = signal_partners(barrier, at, chips)
    pl.semaphore_wait(barrier, count + jnp.minimum(me, 1) + jnp.minimum(n - 1 - me, 1))


def signal_partners(sem, at, chips):
    chip, core = at // 2, lax.rem(at, 2)
    pl.semaphore_signal(sem, inc=1, device_id={"dp": 2 * chip + 1 - core})
    bits = [1 << k for k in range(chips.bit_length() - 1)]
    for bit in bits:
        pl.semaphore_signal(sem, inc=1, device_id={"dp": 2 * flipped(chip, bit) + core})
    return 1 + len(bits)


def inverse_rms(rows):
    return lax.rsqrt(jnp.mean(rows * rows, axis=1, keepdims=True) + EPS)


def norm_back(values, inverse, gain_row, upstream):
    weighted = upstream * gain_row
    mean_term = jnp.mean(weighted * values, axis=1, keepdims=True)
    grad_values = inverse * weighted - values * (inverse * inverse * inverse) * mean_term
    return (grad_values, jnp.sum(upstream * values * inverse, axis=0, keepdims=True))


def scatter_scratch(n, rows, width):
    return [
        pltpu.VMEM((CHUNKS, n * rows, width), BF),
        pltpu.VMEM((CHUNKS, n - 1, 2, rows, width), BF),
        pltpu.SemaphoreType.DMA((CHUNKS, n - 1, 2)),
        pltpu.SemaphoreType.DMA((CHUNKS, n - 1, 2)),
        pltpu.VMEM((rows, width), F32),
    ]


def gather_scratch(n, rows, width):
    return [
        pltpu.VMEM((CHUNKS, rows, width), BF),
        pltpu.SemaphoreType.DMA((CHUNKS, n - 1, 2)),
        pltpu.SemaphoreType.DMA((CHUNKS, n - 1, 2)),
        pltpu.SemaphoreType.DMA((CHUNKS,)),
    ]


def chunk_span(c, rows):
    return pl.ds(c * rows, rows)


def make_gather(n, me, rows, own, full, send_sem, recv_sem, local_sem):
    return LineGather(
        n,
        me,
        lambda c: own.at[c],
        lambda block, c: full.at[block, chunk_span(c, rows)],
        send_sem,
        recv_sem,
        local_sem,
    )


def peer_barrier(axes):
    barrier = pltpu.get_barrier_semaphore()
    count = 0
    for name, index, size in axes:
        for shift in range(1, size):
            pl.semaphore_signal(barrier, inc=1, device_id={name: lax.rem(index + shift, size)})
            count += 1
    return lambda: pl.semaphore_wait(barrier, count)


def exchange(name, index, size, src, recv, send_sem, recv_sem):
    def copy(shift):
        peer = lax.rem(index + shift, size)
        return pltpu.make_async_remote_copy(
            src_ref=src(peer),
            dst_ref=recv.at[shift - 1],
            send_sem=send_sem.at[shift - 1],
            recv_sem=recv_sem.at[shift - 1],
            device_id={name: peer},
        )

    return [copy(shift) for shift in range(1, size)]


class PlaneGather:
    def __init__(self, at, chips, rows, slot, sems):
        self.chip, self.core = at // 2, lax.rem(at, 2)
        self.chips, self.rows, self.slot = chips, rows, slot
        self.core_send_sem, self.core_recv_sem, self.send_sem, self.recv_sem = sems
        self.arrived = set()

    def last_bit(self, relative, half):
        bits = bits_of(relative)
        return bits[-1] if half == 0 else bits[0]

    def place(self, relative, same_core=True):
        return self.slot(
            2 * relative_chip(self.chip, relative) + (self.core if same_core else 1 - self.core)
        )

    def copy(self, relative, half):
        bit = self.last_bit(relative, half)
        view = self.place(relative - bit).at[pl.ds(half * (self.rows // 2), self.rows // 2)]
        return pltpu.make_async_remote_copy(
            src_ref=view,
            dst_ref=view,
            send_sem=self.send_sem.at[relative, half],
            recv_sem=self.recv_sem.at[relative, half],
            device_id={"dp": 2 * flipped(self.chip, bit) + self.core},
        )

    def core_copy(self, relative, same_core):
        view = self.place(relative, same_core)
        return pltpu.make_async_remote_copy(
            src_ref=view,
            dst_ref=view,
            send_sem=self.core_send_sem.at[relative],
            recv_sem=self.core_recv_sem.at[relative],
            device_id={"dp": 2 * self.chip + 1 - self.core},
        )

    def ensure(self, relative, half):
        if relative > 0 and (relative, half) not in self.arrived:
            self.arrived.add((relative, half))
            self.copy(relative, half).wait_recv()

    def send(self, passed_on):
        for count in range(1, self.chips.bit_length()):
            for r in range(1, self.chips):
                for half in range(2):
                    if len(bits_of(r)) == count and (count > 1) == passed_on:
                        self.ensure(r - self.last_bit(r, half), half)
                        self.copy(r, half).start()
        if not passed_on:
            self.core_copy(0, True).start()

    def swap(self, relatives):
        for r in relatives:
            for half in range(2):
                self.ensure(r, half)
            self.core_copy(r, True).start()

    def finish(self):
        for r in range(self.chips):
            self.core_copy(r, False).wait_recv()

    def drain(self):
        for r in range(self.chips):
            self.core_copy(r, True).wait_send()
            for half in range(2):
                if r > 0:
                    self.copy(r, half).wait_send()


def front_kernel(
    n, n_dp, rows, model_width, x, wq, wk, wv, wo, gains, wg,
    full, qkv_out, full_qkv, full_out, gain_parts, attn_scale, mlp_scale, q_inv, k_inv, full_gate,
    send_sem, recv_sem, local_sem, gain_recv, gain_send_sem, gain_recv_sem,
    vqkv, vout, qkv, save_sem, x_buf, x_sem, squares,
    held, sum_recv, turned, sum_send_sem, sum_recv_sem, gate_sem, *plane,
):
    me, at = lax.axis_index("mp"), lax.axis_index("dp")
    peer_barrier((("mp", me, n), ("dp", at, n_dp)))()
    gather = LineGather(
        n,
        me,
        lambda c: x.at[chunk_span(c, rows)],
        lambda index, c: full.at[index, chunk_span(c, rows)],
        send_sem,
        recv_sem,
        local_sem,
    )
    for c in range(CHUNKS):
        gather.step(c, 1)
    chips = n_dp // 2
    part_width, width = wq.shape
    row_count = rows * CHUNKS

    def part(owner):
        return pl.ds(pl.multiple_of(owner * part_width, part_width), part_width)

    by_qkv = PlaneGather(at, chips, part_width, lambda owner: vqkv.at[part(owner)], plane[:4])
    by_out = PlaneGather(at, chips, width, lambda owner: vout.at[:, part(owner)], plane[4:8])
    by_gate = PlaneGather(
        at, chips, part_width, lambda owner: full_gate.at[part(owner)], plane[8:]
    )
    gate_copy = pltpu.make_async_copy(wg, full_gate.at[part(at)], gate_sem)
    gate_copy.start()
    for k, weight in enumerate((wq, wk, wv)):
        vqkv[part(at), k * width : (k + 1) * width] = weight[...]
    by_qkv.send(False)
    vout[:, part(at)] = wo[...]
    copies = exchange(
        "dp", at, n_dp, lambda peer: gains, gain_recv, gain_send_sem, gain_recv_sem
    )
    for copy in copies:
        copy.start()

    def block(index, source):
        load = pltpu.make_async_copy(source, x_buf, x_sem)
        load.start()
        load.wait()
        here = pl.ds(pl.multiple_of(index * row_count, row_count), row_count)

        @pl.loop(0, 3)
        def _(tile):
            cols = pl.ds(pl.multiple_of(tile * width, width), width)
            value = plain_dot(x_buf[...], vqkv[:, cols])
            qkv[here, cols] = value
            squares[tile] = jnp.sum(value * value, axis=1, keepdims=True)

        pltpu.make_async_copy(qkv.at[here], qkv_out.at[here], save_sem.at[2]).start()
        held[:, here] = columns_to_rows(squares[0], squares[1])

    def blocks_at(step):
        @pl.loop(0, 2)
        def _(side):
            index = me - step + 2 * step * side

            @pl.when((index >= 0) & (index < n))
            def _():
                block(index, full.at[index])

    saves = [
        pltpu.make_async_copy(vqkv, full_qkv, save_sem.at[0]),
        pltpu.make_async_copy(vout, full_out, save_sem.at[1]),
        pltpu.make_async_copy(qkv, qkv_out, save_sem.at[2]),
    ]
    early = [r for r in range(1, chips) if len(bits_of(r)) == 1]
    late = [r for r in range(1, chips) if len(bits_of(r)) > 1]

    def next_weights():
        by_qkv.send(True)
        by_out.send(False)
        gate_copy.wait()
        by_gate.send(False)

    def qkv_here():
        by_qkv.finish()
        saves[0].start()
        block(me, x)

    def out_here():
        by_out.swap(late)
        by_out.finish()
        saves[1].start()

    hooks = {
        0: next_weights,
        3: lambda: by_qkv.swap(early),
        4: lambda: by_qkv.swap(late),
        5: qkv_here,
        6: lambda: by_out.send(True),
        7: lambda: (by_out.swap(early), by_gate.send(True)),
        8: out_here,
        9: lambda: by_gate.swap(early),
    }
    ready, number = 1, 0
    for step in range(2, n + 1):
        for c in range(CHUNKS):
            if step < n:
                gather.step(c, step)
            else:
                gather.last(c)
            if number in hooks:
                hooks.pop(number)()
            number += 1
        while number > 5 and ready < step:
            blocks_at(ready)
            ready += 1
    for hook in hooks.values():
        hook()
    while ready < n:
        blocks_at(ready)
        ready += 1
    def keep_gains(owner, row):
        gain_parts[owner] = row[:, 2 * part_width :]
        attn_scale[:, part(owner)] = row[:, :part_width]
        mlp_scale[:, part(owner)] = row[:, part_width : 2 * part_width]

    keep_gains(at, gains[...])
    for shift, copy in enumerate(copies, 1):
        copy.wait_recv()
        keep_gains(lax.rem(at + n_dp - shift, n_dp), gain_recv[shift - 1])
    by_gate.swap(late)
    q_sum, k_sum = sum_held(n, me, held, sum_recv, turned, sum_send_sem, sum_recv_sem)
    q_inv[...] = lax.rsqrt(q_sum / model_width + EPS)
    k_inv[...] = lax.rsqrt(k_sum / model_width + EPS)
    for c in range(CHUNKS):
        gather.drain(c)
    for copy in copies:
        copy.wait_send()
    by_gate.finish()
    for gathered in (by_qkv, by_out, by_gate):
        gathered.drain()
    for copy in saves:
        copy.wait()


def front(n, n_dp, block, wq, wk, wv, wo, gains, wg):
    row_count, model_width = block.shape
    rows = row_count // CHUNKS
    size = n * row_count
    width = wq.shape[1]
    chips = n_dp // 2
    column = jax.ShapeDtypeStruct((size, 1), F32)
    return pl.pallas_call(
        functools.partial(front_kernel, n, n_dp, rows, model_width),
        out_shape=(
            jax.ShapeDtypeStruct((n,) + block.shape, block.dtype),
            jax.ShapeDtypeStruct((size, 3 * width), F32),
            jax.ShapeDtypeStruct((model_width, 3 * width), BF),
            jax.ShapeDtypeStruct((width, model_width), BF),
            jax.ShapeDtypeStruct((n_dp, 1, gains.shape[1] - 2 * model_width // n_dp), F32),
            jax.ShapeDtypeStruct((1, model_width), F32),
            jax.ShapeDtypeStruct((1, model_width), F32),
            column,
            column,
            jax.ShapeDtypeStruct((model_width, wg.shape[1]), BF),
        ),
        in_specs=[VMEM] * 7,
        out_specs=(HBM, HBM, HBM, HBM, VMEM, VMEM, VMEM, VMEM, VMEM, HBM),
        scratch_shapes=gather_scratch(n, rows, model_width)[1:]
        + [
            pltpu.VMEM((n_dp - 1,) + gains.shape, F32),
            pltpu.SemaphoreType.DMA((n_dp - 1,)),
            pltpu.SemaphoreType.DMA((n_dp - 1,)),
            pltpu.VMEM((model_width, 3 * width), BF),
            pltpu.VMEM((width, model_width), BF),
            pltpu.VMEM((size, 3 * width), F32),
            pltpu.SemaphoreType.DMA((3,)),
            pltpu.VMEM((row_count, model_width), BF),
            pltpu.SemaphoreType.DMA,
            pltpu.VMEM((3, row_count, 1), F32),
        ]
        + sum_scratch(n, size)
        + [pltpu.SemaphoreType.DMA]
        + plane_sems(chips) * 3,
        compiler_params=pltpu.CompilerParams(
            collective_id=0, has_side_effects=True, vmem_limit_bytes=63 * MIB
        ),
        name="front",
        cost_estimate=cost(80),
    )(block, wq, wk, wv, wo, gains, wg)


class WeightTiles:
    def __init__(self, source, held, sem, axis, size):
        self.source, self.held, self.sem, self.axis, self.size = source, held, sem, axis, size
        self.count = source.shape[axis] // size

    def at(self, ref, tile):
        span = pl.ds(pl.multiple_of(tile * self.size, self.size), self.size)
        return ref.at[:, span] if self.axis == 1 else ref.at[span]

    def copy(self, tile):
        return pltpu.make_async_copy(
            self.at(self.source, tile), self.at(self.held, tile), self.sem.at[tile]
        )

    def start(self):
        for tile in range(self.count):
            self.copy(tile).start()


def middle_kernel(
    n, n_dp, rows, att, wo, wg, wu, wd, x, upstream_in, row_valid, mlp_scale, attn_scale,
    h_full, output, dm_full, hidden_out, mlp_gain, middle_grad, da_full, attn_gain, gate_out, up_out,
    part, recv, rs_send_sem, rs_recv_sem, total, own, ag_send_sem, ag_recv_sem, local_sem,
    vg, vu, vd, wsem, in_buf, in_sem, gate_all, up_all, hidden_buf, hidden_sem, packed,
    middle, branch, mg_sem, h_buf, h_sem, extra, ready, *more,
):
    me, at = lax.axis_index("mp"), lax.axis_index("dp")
    width, hidden_width = vg.shape
    local_width = wo.shape[0]
    chips = n_dp // 2
    part_width = width // n_dp
    plane, more = more[:16], more[16:]
    v_out = more[0] if more else gate_all.at[pl.ds(0, local_width)]
    v_att = up_all.at[:, pl.ds(0, local_width)]

    def start(copies):
        for copy in copies:
            copy.start()

    def wait(copies):
        for copy in copies:
            copy.wait()

    def weight_part(owner):
        return pl.ds(pl.multiple_of(owner * part_width, part_width), part_width)

    by_up = PlaneGather(at, chips, part_width, lambda owner: vu.at[weight_part(owner)], plane[8:12])
    by_down = PlaneGather(
        at, chips, hidden_width, lambda owner: vd.at[:, weight_part(owner)], plane[12:]
    )
    own_weights = [
        pltpu.make_async_copy(wu, by_up.place(0), wsem.at[0]),
        pltpu.make_async_copy(wd, by_down.place(0), wsem.at[1]),
    ]
    gate_copy = pltpu.make_async_copy(wg, vg, wsem.at[2])
    att_copies = [
        pltpu.make_async_copy(wo, v_out, wsem.at[3]),
        pltpu.make_async_copy(att, v_att, wsem.at[4]),
    ]
    start(att_copies)
    start(own_weights)
    gate_copy.start()
    stage_barrier(me, n, at, chips)
    wait(own_weights)
    by_up.send(False)

    scatter = LineScatter(n, me, rows, part, recv, rs_send_sem, rs_recv_sem)
    gathers = [
        make_gather(n, me, rows, own, full, ag_send_sem, ag_recv_sem, local_sem)
        for full in (h_full, dm_full, da_full)
    ]

    def in_copies(phase, c):
        source = gathers[phase - 1].full
        return [
            pltpu.make_async_copy(
                source(j, c), in_buf.at[c % 2, pl.ds(j * rows, rows)], in_sem.at[c % 2, j]
            )
            for j in range(n)
        ]

    def attend_out(c):
        if c == 0:
            wait(att_copies)
        block_rows = rows * CHUNKS
        for j in range(n):
            packed[j * rows : (j + 1) * rows] = v_att[
                j * block_rows + c * rows : j * block_rows + (c + 1) * rows
            ]

        @pl.loop(0, width // TILE)
        def _(tile):
            cols = pl.ds(pl.multiple_of(tile * TILE, TILE), TILE)
            part[c, :, cols] = plain_dot(packed[...], v_out[:, cols]).astype(BF)

    def attend_rows(c):
        scatter.total(c, total)
        span = chunk_span(c, rows)
        value = total[...]
        branch[span] = value
        new = x[span].astype(F32) + value * inverse_rms(value) * attn_scale[...]
        middle[span] = new
        own[c] = new.astype(BF)

    def hidden_copies(c):
        return [
            pltpu.make_async_copy(
                hidden_buf.at[c % 2, pl.ds(j * rows, rows)],
                hidden_out.at[j, chunk_span(c, rows)],
                hidden_sem.at[c % 2, j],
            )
            for j in range(n)
        ]

    def clear(phase, c):
        scatter.drain(c)
        gathers[phase - 1].drain_sends(c)
        wait(in_copies(phase, c))

    def forward(c):
        here = pl.ds(c * n * rows, n * rows)
        slot = c % 2
        clear(1, c)
        if c == 0:
            by_up.finish()
            gate_copy.wait()
        if c >= 2:
            wait(hidden_copies(c - 2))

        @pl.loop(0, hidden_width // TILE)
        def _(tile):
            cols = pl.ds(pl.multiple_of(tile * TILE, TILE), TILE)
            gate = plain_dot(in_buf[slot], vg[:, cols])
            up = plain_dot(in_buf[slot], vu[:, cols])
            gate_all[here, cols] = gate.astype(BF)
            up_all[here, cols] = up.astype(BF)
            hidden_buf[slot, :, cols] = (gate * jax.nn.sigmoid(gate) * up).astype(BF)

        start(hidden_copies(c))
        if c == 0:
            by_down.swap(late_chips)
            by_down.finish()

        @pl.loop(0, width // TILE)
        def _(tile):
            cols = pl.ds(pl.multiple_of(tile * TILE, TILE), TILE)
            part[c, :, cols] = plain_dot(hidden_buf[slot], vd[:, cols]).astype(BF)

    def backward(c):
        here = pl.ds(c * n * rows, n * rows)
        clear(2, c)

        @pl.loop(0, hidden_width // TILE)
        def _(tile):
            cols = pl.ds(pl.multiple_of(tile * TILE, TILE), TILE)
            hidden_grad = outer_dot(in_buf[c % 2], vd[cols, :])
            gate = gate_all[here, cols].astype(F32)
            up = up_all[here, cols].astype(F32)
            sigmoid = jax.nn.sigmoid(gate)
            gate_all[here, cols] = (
                hidden_grad * up * sigmoid * (1.0 + gate * (1.0 - sigmoid))
            ).astype(BF)
            up_all[here, cols] = (hidden_grad * gate * sigmoid).astype(BF)

        @pl.loop(0, width // TILE)
        def _(tile):
            cols = pl.ds(pl.multiple_of(tile * TILE, TILE), TILE)
            part[c, :, cols] = (
                outer_dot(gate_all[here], vg[cols, :]) + outer_dot(up_all[here], vu[cols, :])
            ).astype(BF)

        if c + 1 == CHUNKS:
            for last in range(max(CHUNKS - 2, 0), CHUNKS):
                wait(hidden_copies(last))
            for gathered in (by_up, by_down):
                gathered.drain()
            start(h_copies(0))
            signal_partners(ready, at, chips)

    def mg_copy(c):
        return pltpu.make_async_copy(
            middle.at[chunk_span(c, rows)], middle_grad.at[chunk_span(c, rows)], mg_sem.at[c]
        )

    def forward_rows(c):
        scatter.total(c, total)
        span = chunk_span(c, rows)
        value = total[...]
        inverse = inverse_rms(value)
        output[span] = (middle[span] + value * inverse * mlp_scale[...]).astype(BF)
        upstream = upstream_in[span].astype(F32) * row_valid[span]
        grad, gain = norm_back(value, inverse, mlp_scale[...], upstream)
        own[c] = grad.astype(BF)
        mlp_gain[...] = gain if c == 0 else mlp_gain[...] + gain

    def backward_rows(c):
        scatter.total(c, total)
        span = chunk_span(c, rows)
        upstream = upstream_in[span].astype(F32) * row_valid[span] + total[...]
        middle[span] = upstream
        mg_copy(c).start()
        value = branch[span]
        grad, gain = norm_back(value, inverse_rms(value), attn_scale[...], upstream)
        own[c] = grad.astype(BF)
        attn_gain[...] = gain if c == 0 else attn_gain[...] + gain

    block_width = pl.ds(0, hidden_width)

    def slot_at(index):
        for ref in (vg, vu, vd):
            count = ref.shape[0] // part_width
            if index < count:
                return ref.at[pl.ds(index * part_width, part_width), block_width]
            index -= count
        for ref in (hidden_buf, in_buf):
            if index < ref.shape[0]:
                return ref.at[index, pl.ds(0, part_width), block_width]
            index -= ref.shape[0]
        return extra.at[index]

    reduces = []
    for which, out in enumerate((gate_out, up_out)):
        first = chips + 3 * chips * which
        views = (
            lambda r: slot_at(r),
            lambda r, first=first: slot_at(first + r),
            lambda r, first=first: slot_at(first + chips + r),
            lambda r, first=first: slot_at(first + 2 * chips + r - 1),
        )
        reduces.append(
            PlaneReduce(at, chips, part_width, views, plane[4 * which : 4 * which + 4], out)
        )
    order = relative_order(chips)
    jobs = [
        (which, same_core, r)
        for which in range(2)
        for same_core in (False, True)
        for r in order
    ]

    def h_copies(index):
        which, same_core, r = jobs[index]
        first = reduces[which].owner(r, same_core) * part_width
        cols = pl.ds(pl.multiple_of(first, part_width), part_width)
        return [
            pltpu.make_async_copy(
                h_full.at[j, :, cols], h_buf.at[index % 2, j], h_sem.at[index % 2, j]
            )
            for j in range(n)
        ]

    def weight_block(index):
        which, same_core, r = jobs[index]
        reduce = reduces[which]
        grad = (gate_all, up_all)[which]
        if index == 0:
            pl.semaphore_wait(ready, 1 + len(bits_of(chips - 1)))
        wait(h_copies(index))
        if index + 1 < len(jobs):
            start(h_copies(index + 1))
        if same_core:
            reduce.core_copy(r).wait_recv()
        elif which == 1:
            reduces[0].drain_core(r)
        left = jnp.concatenate(
            [
                h_buf[index % 2, j, c * rows : (c + 1) * rows]
                for c in range(CHUNKS)
                for j in range(n)
            ],
            axis=0,
        )

        @pl.loop(0, hidden_width // TILE)
        def _(tile):
            cols = pl.ds(pl.multiple_of(tile * TILE, TILE), TILE)
            block = inner_dot(left, grad[:, cols])
            if not same_core:
                reduce.core_send(r)[:, cols] = block.astype(BF)
            else:
                block = block + reduce.core_recv(r)[:, cols].astype(F32)
                if r > 0:
                    reduce.held(r)[:, cols] = block.astype(BF)
                else:
                    reduce.out[:, cols] = block

        if not same_core:
            reduce.core_copy(r).start()
        elif r > 0:
            for half in range(2):
                if not reduce.before(r, half):
                    reduce.push(r, half)

    work = []
    for index, (which, same_core, r) in enumerate(jobs):
        work.append(functools.partial(weight_block, index))
        if same_core and r == order[-1]:
            for late in order:
                for half in range(2):
                    if late > 0 and reduces[which].before(late, half):
                        work.append(functools.partial(reduces[which].push, late, half))
    pending = iter(work)

    early_chips = [r for r in range(1, chips) if len(bits_of(r)) == 1]
    late_chips = [r for r in range(1, chips) if len(bits_of(r)) > 1]
    hooks = {
        HOOKS[0]: lambda: (by_up.send(True), by_down.send(False)),
        HOOKS[1]: lambda: by_up.swap(early_chips),
        HOOKS[2]: lambda: by_up.swap(late_chips),
        HOOKS[3]: lambda: by_down.send(True),
        HOOKS[4]: lambda: by_down.swap(early_chips),
    }
    last_step = 2 * n - 2
    events = sorted(
        (
            max(PERIOD, last_step + 1) * phase + step + STAGGER * c - (0.5 if step == 0 else 0),
            phase,
            c,
            step,
        )
        for phase in range(3)
        for c in range(CHUNKS)
        for step in range(last_step + 1)
    )
    filling = False
    for number, (_, phase, c, step) in enumerate(events):
        gather = gathers[phase]
        if number in hooks:
            hooks.pop(number)()
        if step == 0:
            (attend_out, forward, backward)[phase](c)
            filling = filling or (phase == 2 and c + 1 == CHUNKS)
        if step < n - 1:
            scatter.edge(c, step)
            if step > 0:
                scatter.step(c, step)
        elif step == n - 1:
            (attend_rows, forward_rows, backward_rows)[phase](c)
            gather.step(c, 1)
        elif step < last_step:
            gather.step(c, step - n + 2)
        else:
            gather.last(c)
            if phase < 2:
                gather.local_copy(c).wait()
                start(in_copies(phase + 1, c))
        if filling:
            for _ in range(FILL):
                job = next(pending, None)
                if job is not None:
                    job()
    for job in pending:
        job()
    for c in range(CHUNKS):
        scatter.drain(c)
        gathers[2].drain(c)
    for reduce in reduces:
        reduce.finish()
        reduce.drain()
    for r in range(chips):
        reduces[1].drain_core(r)
    for c in range(CHUNKS):
        mg_copy(c).wait()


def middle(n, n_dp, attended, full_out, wg, wu, wd, x, out_grad, row_valid, mlp_scale, attn_scale):
    row_count, width = x.shape
    hidden_width = wg.shape[1]
    rows = row_count // CHUNKS
    size = n * row_count
    chips = n_dp // 2
    part_width = width // n_dp
    block = (part_width, hidden_width)
    slots = (2 * width + hidden_width) // part_width + 4
    extra = 7 * chips - 1 - slots
    by_rows = jax.ShapeDtypeStruct((n, row_count, width), BF)
    return pl.pallas_call(
        functools.partial(middle_kernel, n, n_dp, rows),
        out_shape=(
            by_rows,
            jax.ShapeDtypeStruct((row_count, width), BF),
            by_rows,
            jax.ShapeDtypeStruct((n, row_count, hidden_width), BF),
            jax.ShapeDtypeStruct((1, width), F32),
            jax.ShapeDtypeStruct((row_count, width), F32),
            by_rows,
            jax.ShapeDtypeStruct((1, width), F32),
            jax.ShapeDtypeStruct(block, F32),
            jax.ShapeDtypeStruct(block, F32),
        ),
        in_specs=[HBM] * 5 + [VMEM] * 5,
        out_specs=(HBM, VMEM, HBM, HBM, VMEM, HBM, HBM, VMEM, VMEM, VMEM),
        scratch_shapes=scatter_scratch(n, rows, width)
        + gather_scratch(n, rows, width)
        + [
            pltpu.VMEM((width, hidden_width), BF),
            pltpu.VMEM((width, hidden_width), BF),
            pltpu.VMEM((hidden_width, width), BF),
            pltpu.SemaphoreType.DMA((5,)),
            pltpu.VMEM((2, n * rows, width), BF),
            pltpu.SemaphoreType.DMA((2, n)),
            pltpu.VMEM((size, hidden_width), BF),
            pltpu.VMEM((size, hidden_width), BF),
            pltpu.VMEM((2, n * rows, hidden_width), BF),
            pltpu.SemaphoreType.DMA((2, n)),
            pltpu.VMEM((n * rows, attended.shape[1]), BF),
            pltpu.VMEM((row_count, width), F32),
            pltpu.VMEM((row_count, width), F32),
            pltpu.SemaphoreType.DMA((CHUNKS,)),
            pltpu.VMEM((2, n, row_count, part_width), BF),
            pltpu.SemaphoreType.DMA((2, n)),
            pltpu.VMEM((extra,) + block if extra > 0 else (1, 16, 128), BF),
            pltpu.SemaphoreType.REGULAR,
        ]
        + plane_sems(chips) * 4
        + ([pltpu.VMEM(full_out.shape, BF)] if hidden_width < width else []),
        compiler_params=pltpu.CompilerParams(
            collective_id=2, has_side_effects=True, vmem_limit_bytes=63 * MIB
        ),
        name="middle",
        cost_estimate=cost(350),
    )(attended, full_out, wg, wu, wd, x, out_grad, row_valid, mlp_scale, attn_scale)


def last_grads_kernel(
    n, n_dp, rows, grads, weight, base, inputs, att, da, hidden, dm,
    attn_gain, mlp_gain, q_gain, k_gain,
    input_grad, qkv_out, out_out, down_out, gain_out,
    part, recv, rs_send_sem, rs_recv_sem, total, packed,
    x_buf, da_buf, dm_buf, load_sem, v_hidden, hidden_sem,
    send_qkv, recv_qkv, message_qkv, send_out, recv_out, message_out,
    send_down, recv_down, message_down,
    gains, gain_recv, gain_send_sem, gain_recv_sem, mp_recv, mp_send_sem, mp_recv_sem, *plane,
):
    me, at = lax.axis_index("mp"), lax.axis_index("dp")
    entered = peer_barrier((("mp", me, n), ("dp", at, n_dp)))
    width = weight.shape[0]
    block_rows = rows * CHUNKS
    local_width = att.shape[1]
    chips = n_dp // 2
    part_width = width // n_dp
    order = relative_order(chips)

    def views(send, recv, message):
        return (
            lambda r: send.at[r],
            lambda r: recv.at[r],
            lambda r: send.at[r],
            lambda r: message.at[r - 1],
        )

    by_qkv = PlaneReduce(
        at, chips, part_width, views(send_qkv, recv_qkv, message_qkv), plane[:4], qkv_out
    )
    by_out = PlaneReduce(
        at, chips, local_width, views(send_out, recv_out, message_out), plane[4:8], out_out
    )
    by_down = PlaneReduce(
        at, chips, part_width, views(send_down, recv_down, message_down), plane[8:], down_out
    )
    jobs = [
        (down, same_core, r)
        for down in (True, False)
        for same_core in (False, True)
        for r in order
    ]

    def loads(k):
        down, same_core, r = jobs[k]
        first = by_qkv.owner(r, same_core) * part_width
        cols = pl.ds(pl.multiple_of(first, part_width), part_width)
        pairs = ((dm, dm_buf),) if down else ((inputs, x_buf), (da, da_buf))
        return [
            pltpu.make_async_copy(source.at[:, cols], buf.at[k % 2], load_sem.at[k % 2, which])
            for which, (source, buf) in enumerate(pairs)
        ]

    load_hidden = pltpu.make_async_copy(hidden, v_hidden, hidden_sem)
    for copy in loads(0):
        copy.start()
    load_hidden.start()

    def compute(c):
        for j in range(n):
            packed[j * rows : (j + 1) * rows] = grads[
                j * block_rows + c * rows : j * block_rows + (c + 1) * rows
            ]

        @pl.loop(0, width // TILE)
        def _(tile):
            cols = pl.ds(pl.multiple_of(tile * TILE, TILE), TILE)
            part[c, :, cols] = outer_dot(packed[...], weight[cols, :]).astype(BF)

    scatter = LineScatter(n, me, rows, part, recv, rs_send_sem, rs_recv_sem)

    def row_work(c):
        scatter.total(c, total)
        span = chunk_span(c, rows)
        input_grad[span] = base[span] + total[...]

    def weight_block(k):
        down, same_core, r = jobs[k]
        slot = k % 2
        reduces = (by_down,) if down else (by_qkv, by_out)
        for copy in loads(k):
            copy.wait()
        if k + 1 < len(jobs):
            for copy in loads(k + 1):
                copy.start()
        if k == 0:
            load_hidden.wait()
        if same_core:
            for reduce in reduces:
                reduce.core_copy(r).wait_recv()
                reduce.drain_core(r)

        def keep(reduce, block, cols):
            if not same_core:
                reduce.core_send(r)[:, cols] = block.astype(BF)
                return
            block = block + reduce.core_recv(r)[:, cols].astype(F32)
            if r > 0:
                reduce.held(r)[:, cols] = block.astype(BF)
            else:
                reduce.out[:, cols] = block

        if down:

            @pl.loop(0, hidden.shape[1] // TILE)
            def _(tile):
                cols = pl.ds(pl.multiple_of(tile * TILE, TILE), TILE)
                keep(by_down, inner_dot(dm_buf[slot], v_hidden[:, cols]), cols)

        else:

            @pl.loop(0, 3)
            def _(tile):
                cols = pl.ds(pl.multiple_of(tile * local_width, local_width), local_width)
                keep(by_qkv, inner_dot(x_buf[slot], grads[:, cols]), cols)

            keep(by_out, inner_dot(att[...], da_buf[slot]), slice(None))
        for reduce in reduces:
            if not same_core:
                reduce.core_copy(r).start()
            elif r > 0:
                for half in range(2):
                    if not reduce.before(r, half):
                        reduce.push(r, half)

    def push_late(reduces):
        for r in order:
            for half in range(2):
                if r > 0 and reduces[0].before(r, half):
                    for reduce in reduces:
                        reduce.push(r, half)

    for index in range(n_dp):
        span = slice(index * part_width, (index + 1) * part_width)
        gains[index, :, :part_width] = attn_gain[:, span]
        gains[index, :, part_width : 2 * part_width] = mlp_gain[:, span]
        gains[index, :, 2 * part_width : 2 * part_width + local_width] = q_gain[...]
        gains[index, :, 2 * part_width + local_width :] = k_gain[...]
    gain_copies = exchange(
        "dp", at, n_dp, lambda peer: gains.at[peer], gain_recv, gain_send_sem, gain_recv_sem
    )
    mp_copies = exchange("mp", me, n, lambda peer: gain_out, mp_recv, mp_send_sem, mp_recv_sem)
    line = iter([(step, c) for c in range(CHUNKS) for step in range(1, n)])

    def line_steps(count):
        for _ in range(count):
            step, c = next(line, (None, None))
            if step is None:
                return
            if step < n - 1:
                scatter.step(c, step)
            else:
                row_work(c)

    def send_edges(c):
        for step in range(n - 1):
            scatter.edge(c, step)

    compute(0)
    entered()
    send_edges(0)
    for copy in gain_copies:
        copy.start()
    sent = 1
    for k in range(len(jobs)):
        weight_block(k)
        if k % 4 == 3 and sent < CHUNKS:
            compute(sent)
            send_edges(sent)
            sent += 1
        if k >= LINE_FROM:
            line_steps(1)
        if k == 3 * chips:
            push_late((by_down,))
    push_late((by_qkv, by_out))
    gain_out[...] = gains[at]
    for shift, copy in enumerate(gain_copies, 1):
        copy.wait_recv()
        gain_out[...] += gain_recv[shift - 1]
    for copy in mp_copies:
        copy.start()
    line_steps(n * CHUNKS)
    for reduce in (by_down, by_qkv, by_out):
        reduce.finish()
    for copy in mp_copies:
        copy.wait_recv()
        copy.wait_send()
    lanes = lax.broadcasted_iota(jnp.int32, gain_out.shape, 1)
    shared = gain_out[...]
    for shift in range(1, n):
        shared = shared + mp_recv[shift - 1]
    gain_out[...] = jnp.where(lanes < 2 * part_width, shared, gain_out[...])
    for copy in gain_copies:
        copy.wait_send()
    for c in range(CHUNKS):
        scatter.drain(c)
    for reduce in (by_down, by_qkv, by_out):
        reduce.drain()


def last_grads(n, n_dp, grads, weight, base, inputs, attended, da_full, hidden, dm, *gains):
    row_count, width = base.shape
    rows = row_count // CHUNKS
    size, local_width = attended.shape
    part_width = width // n_dp
    chips = n_dp // 2
    qkv_block = (part_width, 3 * local_width)
    out_block = (local_width, part_width)
    down_block = (part_width, hidden.shape[1])
    gain_block = (1, 2 * part_width + 2 * local_width)
    return pl.pallas_call(
        functools.partial(last_grads_kernel, n, n_dp, rows),
        out_shape=(
            jax.ShapeDtypeStruct((row_count, width), F32),
            jax.ShapeDtypeStruct(qkv_block, F32),
            jax.ShapeDtypeStruct(out_block, F32),
            jax.ShapeDtypeStruct(down_block, F32),
            jax.ShapeDtypeStruct(gain_block, F32),
        ),
        in_specs=[VMEM, VMEM, VMEM, HBM, VMEM, HBM, HBM, HBM] + [VMEM] * 4,
        out_specs=(VMEM,) * 5,
        scratch_shapes=scatter_scratch(n, rows, width)
        + [
            pltpu.VMEM((n * rows, 3 * local_width), BF),
            pltpu.VMEM((2, size, part_width), BF),
            pltpu.VMEM((2, size, part_width), BF),
            pltpu.VMEM((2, size, part_width), BF),
            pltpu.SemaphoreType.DMA((2, 2)),
            pltpu.VMEM(hidden.shape, BF),
            pltpu.SemaphoreType.DMA,
        ]
        + [
            pltpu.VMEM((count,) + block, BF)
            for block in (qkv_block, out_block, down_block)
            for count in (chips, chips, chips - 1)
        ]
        + [pltpu.VMEM((n_dp,) + gain_block, F32), pltpu.VMEM((n_dp - 1,) + gain_block, F32)]
        + [pltpu.SemaphoreType.DMA((n_dp - 1,))] * 2
        + [pltpu.VMEM((n - 1,) + gain_block, F32)]
        + [pltpu.SemaphoreType.DMA((n - 1,))] * 2
        + plane_sems(chips) * 3,
        compiler_params=pltpu.CompilerParams(
            collective_id=4, has_side_effects=True, vmem_limit_bytes=63 * MIB
        ),
        name="last_grads",
        cost_estimate=cost(80),
    )(grads, weight, base, inputs, attended, da_full, hidden, dm, *gains)


def turn(values, cos, sin):
    return values * cos + pltpu.roll(values, values.shape[1] // 2, 1) * sin


def turn_back(values, cos, sin):
    return values * cos + pltpu.roll(values * sin, values.shape[1] // 2, 1)


def allowed_keys(starts, first_row, rows, key_end):
    places = first_row + lax.broadcasted_iota(jnp.int32, (rows, key_end), 0)
    keys = lax.broadcasted_iota(jnp.int32, (rows, key_end), 1)
    return (keys <= places) & (keys >= starts)


def columns_to_rows(first, second):
    lanes = lax.broadcasted_iota(jnp.int32, (first.shape[0], 128), 1)
    return jnp.transpose(jnp.where(lanes == 0, first, second))[:8]


def sum_held(n, me, held, recv, turned, send_sem, recv_sem):
    copies = exchange("mp", me, n, lambda peer: held, recv, send_sem, recv_sem)
    for copy in copies:
        copy.start()
    total = held[...]
    for shift, copy in enumerate(copies, 1):
        copy.wait_recv()
        total = total + recv[shift - 1]
    for copy in copies:
        copy.wait_send()
    turned[...] = jnp.zeros_like(turned)
    turned[:8] = total
    back = jnp.transpose(turned[...])
    return back[:, 0:1], back[:, 1:2]


def sum_scratch(n, size):
    return [
        pltpu.VMEM((8, size), F32),
        pltpu.VMEM((n - 1, 8, size), F32),
        pltpu.VMEM((128, size), F32),
        pltpu.SemaphoreType.DMA((n - 1,)),
        pltpu.SemaphoreType.DMA((n - 1,)),
    ]


def attention_kernel(
    q_raw, k_raw, v_raw, q_inv, k_inv, q_gain, k_gain, cos, sin, starts,
    out, q_low, k_low, v_low, log_total,
):
    size, head = q_raw.shape
    score_scale = 1.0 / math.sqrt(head)
    q_low[...] = turn(q_raw[...] * q_inv[...] * q_gain[...], cos[...], sin[...]).astype(BF)
    k_low[...] = turn(k_raw[...] * k_inv[...] * k_gain[...], cos[...], sin[...]).astype(BF)
    v_low[...] = v_raw[...].astype(BF)
    rows = min(QUERY_ROWS, size)
    for first in range(0, size, rows):
        end = first + rows
        span = slice(first, end)
        scores = outer_dot(q_low[span], k_low[:end]) * score_scale
        scores = jnp.where(allowed_keys(starts[span], first, rows, end), scores, MASKED)
        row_max = jnp.max(scores, axis=1, keepdims=True)
        exponents = jnp.exp(scores - row_max)
        row_total = jnp.sum(exponents, axis=1, keepdims=True)
        probs = (exponents * (1.0 / row_total)).astype(BF)
        out[span] = plain_dot(probs, v_low[:end]).astype(BF)
        log_total[span] = row_max + jnp.log(row_total)


def head_specs(size, head, heads, count):
    return [pl.BlockSpec((size, head), lambda h, k=k: (0, k * heads + h)) for k in range(count)]


def attention(qkv_raw, q_inv, k_inv, q_gain, k_gain, cos, sin, starts, heads):
    size = qkv_raw.shape[0]
    head = cos.shape[1]
    column = pl.BlockSpec((size, 1), lambda h: (0, 0))
    table = pl.BlockSpec((size, head), lambda h: (0, 0))
    gain = pl.BlockSpec((1, head), lambda h: (0, h))
    by_head = pl.BlockSpec((size, head), lambda h: (0, h))
    low = jax.ShapeDtypeStruct((size, heads * head), BF)
    return pl.pallas_call(
        attention_kernel,
        grid=(heads,),
        out_shape=(low, low, low, low, jax.ShapeDtypeStruct((heads, size, 1), F32)),
        in_specs=head_specs(size, head, heads, 3)
        + [column, column, gain, gain, table, table, column],
        out_specs=(by_head,) * 4 + (pl.BlockSpec((None, size, 1), lambda h: (h, 0, 0)),),
        compiler_params=pltpu.CompilerParams(vmem_limit_bytes=63 * MIB),
        name="attention",
        cost_estimate=cost(18),
    )(qkv_raw, qkv_raw, qkv_raw, q_inv, k_inv, q_gain, k_gain, cos, sin, starts)


def attention_back_kernel(
    n, heads, model_width, qkv, q_low, k_low, v_low, out_grad, log_total,
    q_inv, k_inv, q_gain, k_gain, cos, sin, starts,
    grads, q_gain_grad, k_gain_grad,
    q_weighted, k_weighted, q_grad, k_sum, v_sum, q_dots, k_dots, *sums,
):
    me = lax.axis_index("mp")
    entered = peer_barrier((("mp", me, n),))
    size = qkv.shape[0]
    width = qkv.shape[1] // 3
    head = width // heads
    score_scale = 1.0 / math.sqrt(head)
    rows = min(BACK_ROWS, size)
    q_dots[...] = jnp.zeros_like(q_dots)
    k_dots[...] = jnp.zeros_like(k_dots)

    @pl.loop(0, heads)
    def _(h):
        def cols(first):
            return pl.ds(pl.multiple_of(first + h * head, head), head)

        here = cols(0)
        for first in reversed(range(0, size, rows)):
            end = first + rows
            span = slice(first, end)
            scores = outer_dot(q_low[span, here], k_low[:end, here]) * score_scale
            scores = jnp.where(allowed_keys(starts[span], first, rows, end), scores, MASKED)
            probs = jnp.exp(scores - log_total[h, span])
            prob_grad = outer_dot(out_grad[span, here], v_low[:end, here])
            probs_low = probs.astype(BF)
            weighted = probs * prob_grad
            score_grad = (
                weighted - probs * jnp.sum(weighted, axis=1, keepdims=True)
            ).astype(BF)
            q_grad[span] = plain_dot(score_grad, k_low[:end, here]) * score_scale
            k_extra = inner_dot(score_grad, q_low[span, here])
            v_extra = inner_dot(probs_low, out_grad[span, here])
            if end == size:
                k_sum[...] = k_extra
                v_sum[...] = v_extra
            else:
                k_sum[:end] += k_extra
                v_sum[:end] += v_extra
        for first, inv, gain, grad, factor, weighted_out, dots, gain_grad in (
            (0, q_inv, q_gain, q_grad, None, q_weighted, q_dots, q_gain_grad),
            (width, k_inv, k_gain, k_sum, score_scale, k_weighted, k_dots, k_gain_grad),
        ):
            raw = qkv[:, cols(first)]
            value = grad[...] if factor is None else grad[...] * factor
            normed = turn_back(value, cos[...], sin[...])
            weighted = normed * gain[:, here]
            weighted_out[:, here] = weighted
            gain_grad[:, here] = jnp.sum(normed * raw * inv[...], axis=0, keepdims=True)
            dots[...] += jnp.sum(weighted * raw, axis=1, keepdims=True)
        grads[:, cols(2 * width)] = v_sum[...].astype(BF)

    held = sums[0]
    held[...] = columns_to_rows(q_dots[...], k_dots[...])
    entered()
    q_total, k_total = sum_held(n, me, *sums)
    for first, inv, weighted, dots in (
        (0, q_inv, q_weighted, q_total),
        (width, k_inv, k_weighted, k_total),
    ):
        scale = inv[...]
        factor = scale * scale * scale * (dots / model_width)
        grads[:, first : first + width] = (
            scale * weighted[...] - qkv[:, first : first + width] * factor
        ).astype(BF)


def attention_back(
    n, heads, model_width, qkv_raw, q_low, k_low, v_low, out_grad, log_total, q_inv, k_inv,
    q_gain, k_gain, cos, sin, starts,
):
    size, width = q_low.shape
    head = width // heads
    gains = jax.ShapeDtypeStruct((1, width), F32)
    return pl.pallas_call(
        functools.partial(attention_back_kernel, n, heads, model_width),
        out_shape=(jax.ShapeDtypeStruct((size, 3 * width), BF), gains, gains),
        in_specs=[VMEM] * 13,
        out_specs=(VMEM,) * 3,
        scratch_shapes=[pltpu.VMEM((size, width), F32)] * 2
        + [pltpu.VMEM((size, head), F32)] * 3
        + [pltpu.VMEM((size, 1), F32)] * 2
        + sum_scratch(n, size),
        compiler_params=pltpu.CompilerParams(
            collective_id=6, has_side_effects=True, vmem_limit_bytes=63 * MIB
        ),
        name="attention_back",
        cost_estimate=cost(30),
    )(
        qkv_raw, q_low, k_low, v_low, out_grad, log_total, q_inv, k_inv, q_gain, k_gain,
        cos, sin, starts,
    )


def local(
    layer_input,
    query_weight,
    key_weight,
    value_weight,
    out_weight,
    gate_weight,
    up_weight,
    down_weight,
    query_gain,
    key_gain,
    attn_gain,
    mlp_gain,
    seq_lens,
    out_grad,
):
    n = lax.axis_size("mp")
    n_dp = lax.axis_size("dp")
    me = lax.axis_index("mp")
    row_count, model_width = layer_input.shape
    group_size = row_count * n
    local_heads, gain_part = query_gain.shape
    head_size = gain_part * n_dp
    local_width = local_heads * head_size

    head_part = local_heads * gain_part
    width_part = attn_gain.shape[0]
    own_gains = jnp.concatenate(
        [attn_gain, mlp_gain, query_gain.reshape(head_part), key_gain.reshape(head_part)]
    ).astype(F32)[None]
    (
        inputs_full, qkv_raw, full_qkv, full_out, gain_parts, attn_scale, mlp_scale, query_inv,
        key_inv, full_gate,
    ) = front(
        n, n_dp, layer_input, query_weight, key_weight, value_weight, out_weight, own_gains,
        gate_weight,
    )
    inputs_full = inputs_full.reshape(group_size, model_width)
    gain_parts = gain_parts[:, 0]

    def head_gain(first):
        piece = gain_parts[:, first : first + head_part].reshape(n_dp, local_heads, gain_part)
        return piece.transpose(1, 0, 2).reshape(1, local_width)

    query_scale = head_gain(0)
    key_scale = head_gain(head_part)

    starts, positions, valid = layout(seq_lens[0], group_size)
    starts = starts[:, None]
    cos_table, sin_table = rotary_tables(positions, head_size)
    row_valid = lax.dynamic_slice_in_dim(valid, me * row_count, row_count, 0).astype(F32)[:, None]

    attended, query_low, key_low, value_low, log_total = attention(
        qkv_raw, query_inv, key_inv, query_scale, key_scale, cos_table, sin_table, starts,
        local_heads,
    )
    (
        middle_full, layer_output, mlp_grad_full, hidden, mlp_gain_part, middle_grad, branch_full,
        attn_gain_part, grad_gate, grad_up,
    ) = middle(
        n, n_dp, attended, full_out, full_gate, up_weight, down_weight, layer_input, out_grad,
        row_valid, mlp_scale, attn_scale,
    )

    def flat(rows):
        return rows.reshape(group_size, rows.shape[-1])

    branch_full = flat(branch_full)
    mixed_grad = outer_dot(branch_full, full_out).astype(BF)
    qkv_grad, query_gain_part, key_gain_part = attention_back(
        n, local_heads, model_width, qkv_raw, query_low, key_low, value_low, mixed_grad, log_total,
        query_inv, key_inv, query_scale, key_scale, cos_table, sin_table, starts,
    )

    input_grad, grad_qkv, grad_out, grad_down, gain_sums = last_grads(
        n, n_dp, qkv_grad, full_qkv, middle_grad, inputs_full, attended, branch_full,
        flat(hidden), flat(mlp_grad_full), attn_gain_part, mlp_gain_part, query_gain_part,
        key_gain_part,
    )
    gain_sums = gain_sums[0]
    heads_at = 2 * width_part
    head_sums = lax.dynamic_index_in_dim(
        gain_sums[heads_at:].reshape(2, local_heads, n_dp, gain_part),
        lax.axis_index("dp"),
        2,
        keepdims=False,
    )
    return (
        layer_output,
        input_grad,
        grad_qkv[:, :local_width],
        grad_qkv[:, local_width : 2 * local_width],
        grad_qkv[:, 2 * local_width :],
        grad_out,
        grad_gate,
        grad_up,
        grad_down.T,
        head_sums[0],
        head_sums[1],
        gain_sums[:width_part],
        gain_sums[width_part:heads_at],
    )


def solution(mesh):
    return jax.shard_map(
        local,
        mesh=mesh,
        in_specs=(
            P(("dp", "mp"), None),
            P("dp", "mp"),
            P("dp", "mp"),
            P("dp", "mp"),
            P("mp", "dp"),
            P("dp", "mp"),
            P("dp", "mp"),
            P("mp", "dp"),
            P("mp", "dp"),
            P("mp", "dp"),
            P("dp"),
            P("dp"),
            P("dp", None),
            P(("dp", "mp"), None),
        ),
        out_specs=(
            P(("dp", "mp"), None),
            P(("dp", "mp"), None),
            P("dp", "mp"),
            P("dp", "mp"),
            P("dp", "mp"),
            P("mp", "dp"),
            P("dp", "mp"),
            P("dp", "mp"),
            P("mp", "dp"),
            P("mp", "dp"),
            P("mp", "dp"),
            P("dp"),
            P("dp"),
        ),
        check_vma=False,
    )
```

```python
import functools
import math

import jax
import jax.numpy as jnp
from jax import lax
from jax.experimental import pallas as pl
from jax.experimental.pallas import tpu as pltpu
from jax.sharding import PartitionSpec as P

EPS = 1e-06
THETA = 500000.0
MASKED = -1000000000.0
CHUNKS = 4
STAGGER = 2
EDGES = False
FILL = 2
PERIOD = 8
LINE_FROM = 11
HOOKS = (4, 8, 11, 14, 17)
TILE = 512
QUERY_ROWS = 512
BACK_ROWS = 256
BF = jnp.bfloat16
F32 = jnp.float32
MIB = 1 << 20
HBM = pl.BlockSpec(memory_space=pl.ANY)
VMEM = pl.BlockSpec(memory_space=pltpu.VMEM)


def cost(micros):
    return pl.CostEstimate(
        flops=micros * 1_000_000_000, bytes_accessed=micros * 3_000_000, transcendentals=0
    )


def plain_dot(former, latter):
    return jnp.dot(former, latter, preferred_element_type=F32)


def inner_dot(former, latter):
    return lax.dot_general(
        former, latter, (((0,), (0,)), ((), ())), preferred_element_type=F32
    )


def outer_dot(former, latter):
    return lax.dot_general(
        former, latter, (((1,), (1,)), ((), ())), preferred_element_type=F32
    )


def layout(lengths, group_size):
    slot_count = lengths.shape[0]
    seq_ends = jnp.cumsum(lengths, dtype=jnp.int32)
    starts = seq_ends - lengths
    places = jnp.arange(group_size, dtype=jnp.int32)
    slot_ids = jnp.arange(slot_count, dtype=jnp.int32)
    segment = jnp.sum(
        (places[:, None] >= seq_ends[None, :]).astype(jnp.int32), axis=1, dtype=jnp.int32
    )
    chosen = (segment[:, None] == slot_ids[None, :]).astype(jnp.int32)
    padded = (segment == slot_count).astype(jnp.int32)
    begins = (
        jnp.sum(chosen * starts[None, :], axis=1, dtype=jnp.int32)
        + padded * seq_ends[slot_count - 1]
    )
    return (begins, places - begins, places < seq_ends[slot_count - 1])


def rotary_tables(positions, head_size):
    half_dim = head_size // 2
    frequency = jnp.exp(jnp.arange(half_dim, dtype=F32) * (-2.0 * math.log(THETA) / head_size))
    angles = positions.astype(F32)[:, None] * frequency[None, :]
    cos_half, sin_half = jnp.cos(angles), jnp.sin(angles)
    return (
        jnp.concatenate([cos_half, cos_half], axis=1),
        jnp.concatenate([-sin_half, sin_half], axis=1),
    )


def neighbour_barrier(me, n):
    barrier = pltpu.get_barrier_semaphore()

    @pl.when(me > 0)
    def _():
        pl.semaphore_signal(barrier, inc=1, device_id={"mp": me - 1})

    @pl.when(me < n - 1)
    def _():
        pl.semaphore_signal(barrier, inc=1, device_id={"mp": me + 1})

    pl.semaphore_wait(barrier, jnp.minimum(me, 1) + jnp.minimum(n - 1 - me, 1))


class LineGather:
    def __init__(self, n, me, own, full, send_sem, recv_sem, local_sem):
        self.n, self.me, self.own, self.full = n, me, own, full
        self.send_sem, self.recv_sem, self.local_sem = send_sem, recv_sem, local_sem

    def local_copy(self, c):
        return pltpu.make_async_copy(self.own(c), self.full(self.me, c), self.local_sem.at[c])

    def copy(self, c, step, way, block, src):
        return pltpu.make_async_remote_copy(
            src_ref=src,
            dst_ref=self.full(block, c),
            send_sem=self.send_sem.at[c, step - 1, way],
            recv_sem=self.recv_sem.at[c, step - 1, way],
            device_id={"mp": self.me + (1 if way == 0 else -1)},
        )

    def sides(self):
        return ((0, self.me), (1, self.n - 1 - self.me))

    def block_at(self, way, step):
        return self.me - step if way == 0 else self.me + step

    def step(self, c, step):
        n = self.n
        if step == 1:
            self.local_copy(c).start()
        for way, place in self.sides():
            if step > 1:

                @pl.when(place >= step - 1)
                def _(way=way):
                    block = self.block_at(way, step - 1)
                    self.copy(c, step - 1, way, block, self.own(c)).wait_recv()

            @pl.when((place >= step - 1) & (place < n - 1))
            def _(way=way):
                block = self.block_at(way, step - 1)
                src = self.own(c) if step == 1 else self.full(block, c)
                self.copy(c, step, way, block, src).start()

    def last(self, c):
        n = self.n
        for way, place in self.sides():

            @pl.when(place == n - 1)
            def _(way=way):
                block = self.block_at(way, n - 1)
                self.copy(c, n - 1, way, block, self.own(c)).wait_recv()

    def drain(self, c):
        self.local_copy(c).wait()
        self.drain_sends(c)

    def drain_sends(self, c):
        for step in range(1, self.n):
            for way, place in self.sides():

                @pl.when((place >= step - 1) & (place < self.n - 1))
                def _(way=way):
                    self.copy(c, step, way, self.me, self.own(c)).wait_send()


class LineScatter:
    def __init__(self, n, me, rows, part, recv, send_sem, recv_sem):
        self.n, self.me, self.rows = n, me, rows
        self.part, self.recv = part, recv
        self.send_sem, self.recv_sem = send_sem, recv_sem

    def piece(self, c, owner):
        first = pl.multiple_of(owner * self.rows, self.rows)
        return self.part.at[c, pl.ds(first, self.rows)]

    def copy(self, c, step, way, src):
        return pltpu.make_async_remote_copy(
            src_ref=src,
            dst_ref=self.recv.at[c, step, way],
            send_sem=self.send_sem.at[c, step, way],
            recv_sem=self.recv_sem.at[c, step, way],
            device_id={"mp": self.me + (1 if way == 0 else -1)},
        )

    def sides(self):
        return ((0, self.me), (1, self.n - 1 - self.me))

    def owner(self, way, step):
        return self.n - 1 - step + self.me if way == 0 else step - (self.n - 1 - self.me)

    def edge(self, c, step):
        for way, place in self.sides():

            @pl.when(place == 0)
            def _(way=way):
                self.copy(c, step, way, self.piece(c, self.owner(way, step))).start()

    def step(self, c, step):
        for way, place in self.sides():

            @pl.when((place > 0) & (place <= min(step, self.n - 2)))
            def _(way=way):
                piece = self.piece(c, self.owner(way, step))
                self.copy(c, step - 1, way, piece).wait_recv()
                piece[...] = (
                    piece[...].astype(F32) + self.recv[c, step - 1, way].astype(F32)
                ).astype(BF)
                self.copy(c, step, way, piece).start()

    def total(self, c, out):
        n = self.n
        out[...] = self.piece(c, self.me)[...].astype(F32)
        for way, place in self.sides():

            @pl.when(place > 0)
            def _(way=way):
                self.copy(c, n - 2, way, self.recv.at[c, n - 2, way]).wait_recv()
                out[...] += self.recv[c, n - 2, way].astype(F32)

    def drain(self, c):
        n = self.n
        for step in range(n - 1):
            for way, place in self.sides():

                @pl.when(place <= min(step, n - 2))
                def _(way=way):
                    self.copy(c, step, way, self.recv.at[c, step, way]).wait_send()


def run_line(n, chunks, stagger, compute, scatter, row_work, gather, filler=None):
    last_step = 2 * n - 2 if gather is not None else n - 1
    events = sorted(
        (step + stagger * c - (0.5 if step == 0 else 0), c, step)
        for c in range(chunks)
        for step in range(last_step + 1)
    )
    computed = 0
    for _, c, step in events:
        if step == 0:
            compute(c)
            for ahead in range(n - 1 if EDGES else 1):
                scatter.edge(c, ahead)
            computed += 1
        elif step < n - 1:
            if not EDGES:
                scatter.edge(c, step)
            scatter.step(c, step)
        elif step == n - 1:
            row_work(c)
            if gather is not None:
                gather.step(c, 1)
        elif step < 2 * n - 2:
            gather.step(c, step - n + 2)
        else:
            gather.last(c)
        if filler is not None and computed == chunks:
            filler()
    for c in range(chunks):
        scatter.drain(c)
        if gather is not None:
            gather.drain(c)


def flipped(chip, bit):
    return chip + bit - 2 * bit * lax.rem(chip // bit, 2)


def bits_of(number):
    return [1 << k for k in range(number.bit_length()) if number >> k & 1]


def relative_chip(chip, relative):
    for bit in bits_of(relative):
        chip = flipped(chip, bit)
    return chip


def relative_order(chips):
    return sorted(range(chips), key=lambda r: (-len(bits_of(r)), r))


class PlaneReduce:
    def __init__(self, at, chips, rows, views, sems, out):
        self.chip, self.core = at // 2, lax.rem(at, 2)
        self.chips, self.rows, self.out = chips, rows, out
        self.core_send, self.core_recv, self.held, self.message = views
        self.core_send_sem, self.core_recv_sem, self.send_sem, self.recv_sem = sems

    def first_bit(self, relative, half):
        bits = bits_of(relative)
        return bits[0] if half == 0 else bits[-1]

    def before(self, relative, half):
        return [
            r for r in range(1, self.chips) if r - self.first_bit(r, half) == relative
        ]

    def owner(self, relative, same_core):
        return 2 * relative_chip(self.chip, relative) + (
            self.core if same_core else 1 - self.core
        )

    def half_rows(self, half):
        return pl.ds(half * (self.rows // 2), self.rows // 2)

    def core_copy(self, relative):
        return pltpu.make_async_remote_copy(
            src_ref=self.core_send(relative),
            dst_ref=self.core_recv(relative),
            send_sem=self.core_send_sem.at[relative],
            recv_sem=self.core_recv_sem.at[relative],
            device_id={"dp": 2 * self.chip + 1 - self.core},
        )

    def message_copy(self, relative, half):
        span = self.half_rows(half)
        target = flipped(self.chip, self.first_bit(relative, half))
        return pltpu.make_async_remote_copy(
            src_ref=self.held(relative).at[span],
            dst_ref=self.message(relative).at[span],
            send_sem=self.send_sem.at[relative, half],
            recv_sem=self.recv_sem.at[relative, half],
            device_id={"dp": 2 * target + self.core},
        )

    def push(self, relative, half):
        span = self.half_rows(half)
        for r in self.before(relative, half):
            self.message_copy(r, half).wait_recv()
            held = self.held(relative)
            held[span] = (
                held[span].astype(F32) + self.message(r)[span].astype(F32)
            ).astype(BF)
        self.message_copy(relative, half).start()

    def finish(self):
        for half in range(2):
            span = self.half_rows(half)
            for r in self.before(0, half):
                self.message_copy(r, half).wait_recv()
                self.out[span] += self.message(r)[span].astype(F32)

    def drain_core(self, relative):
        self.core_copy(relative).wait_send()

    def drain(self):
        for r in range(1, self.chips):
            for half in range(2):
                self.message_copy(r, half).wait_send()


def plane_sems(chips):
    return [pltpu.SemaphoreType.DMA((chips,))] * 2 + [pltpu.SemaphoreType.DMA((chips, 2))] * 2


def stage_barrier(me, n, at, chips):
    barrier = pltpu.get_barrier_semaphore()

    @pl.when(me > 0)
    def _():
        pl.semaphore_signal(barrier, inc=1, device_id={"mp": me - 1})

    @pl.when(me < n - 1)
    def _():
        pl.semaphore_signal(barrier, inc=1, device_id={"mp": me + 1})

    count = signal_partners(barrier, at, chips)
    pl.semaphore_wait(barrier, count + jnp.minimum(me, 1) + jnp.minimum(n - 1 - me, 1))


def signal_partners(sem, at, chips):
    chip, core = at // 2, lax.rem(at, 2)
    pl.semaphore_signal(sem, inc=1, device_id={"dp": 2 * chip + 1 - core})
    bits = [1 << k for k in range(chips.bit_length() - 1)]
    for bit in bits:
        pl.semaphore_signal(sem, inc=1, device_id={"dp": 2 * flipped(chip, bit) + core})
    return 1 + len(bits)


def inverse_rms(rows):
    return lax.rsqrt(jnp.mean(rows * rows, axis=1, keepdims=True) + EPS)


def norm_back(values, inverse, gain_row, upstream):
    weighted = upstream * gain_row
    mean_term = jnp.mean(weighted * values, axis=1, keepdims=True)
    grad_values = inverse * weighted - values * (inverse * inverse * inverse) * mean_term
    return (grad_values, jnp.sum(upstream * values * inverse, axis=0, keepdims=True))


def scatter_scratch(n, rows, width):
    return [
        pltpu.VMEM((CHUNKS, n * rows, width), BF),
        pltpu.VMEM((CHUNKS, n - 1, 2, rows, width), BF),
        pltpu.SemaphoreType.DMA((CHUNKS, n - 1, 2)),
        pltpu.SemaphoreType.DMA((CHUNKS, n - 1, 2)),
        pltpu.VMEM((rows, width), F32),
    ]


def gather_scratch(n, rows, width):
    return [
        pltpu.VMEM((CHUNKS, rows, width), BF),
        pltpu.SemaphoreType.DMA((CHUNKS, n - 1, 2)),
        pltpu.SemaphoreType.DMA((CHUNKS, n - 1, 2)),
        pltpu.SemaphoreType.DMA((CHUNKS,)),
    ]


def chunk_span(c, rows):
    return pl.ds(c * rows, rows)


def make_gather(n, me, rows, own, full, send_sem, recv_sem, local_sem):
    return LineGather(
        n,
        me,
        lambda c: own.at[c],
        lambda block, c: full.at[block, chunk_span(c, rows)],
        send_sem,
        recv_sem,
        local_sem,
    )


def peer_barrier(axes):
    barrier = pltpu.get_barrier_semaphore()
    count = 0
    for name, index, size in axes:
        for shift in range(1, size):
            pl.semaphore_signal(barrier, inc=1, device_id={name: lax.rem(index + shift, size)})
            count += 1
    return lambda: pl.semaphore_wait(barrier, count)


def exchange(name, index, size, src, recv, send_sem, recv_sem):
    def copy(shift):
        peer = lax.rem(index + shift, size)
        return pltpu.make_async_remote_copy(
            src_ref=src(peer),
            dst_ref=recv.at[shift - 1],
            send_sem=send_sem.at[shift - 1],
            recv_sem=recv_sem.at[shift - 1],
            device_id={name: peer},
        )

    return [copy(shift) for shift in range(1, size)]


class PlaneGather:
    def __init__(self, at, chips, rows, slot, sems):
        self.chip, self.core = at // 2, lax.rem(at, 2)
        self.chips, self.rows, self.slot = chips, rows, slot
        self.core_send_sem, self.core_recv_sem, self.send_sem, self.recv_sem = sems
        self.arrived = set()

    def last_bit(self, relative, half):
        bits = bits_of(relative)
        return bits[-1] if half == 0 else bits[0]

    def place(self, relative, same_core=True):
        return self.slot(
            2 * relative_chip(self.chip, relative) + (self.core if same_core else 1 - self.core)
        )

    def copy(self, relative, half):
        bit = self.last_bit(relative, half)
        view = self.place(relative - bit).at[pl.ds(half * (self.rows // 2), self.rows // 2)]
        return pltpu.make_async_remote_copy(
            src_ref=view,
            dst_ref=view,
            send_sem=self.send_sem.at[relative, half],
            recv_sem=self.recv_sem.at[relative, half],
            device_id={"dp": 2 * flipped(self.chip, bit) + self.core},
        )

    def core_copy(self, relative, same_core):
        view = self.place(relative, same_core)
        return pltpu.make_async_remote_copy(
            src_ref=view,
            dst_ref=view,
            send_sem=self.core_send_sem.at[relative],
            recv_sem=self.core_recv_sem.at[relative],
            device_id={"dp": 2 * self.chip + 1 - self.core},
        )

    def ensure(self, relative, half):
        if relative > 0 and (relative, half) not in self.arrived:
            self.arrived.add((relative, half))
            self.copy(relative, half).wait_recv()

    def send(self, passed_on):
        for count in range(1, self.chips.bit_length()):
            for r in range(1, self.chips):
                for half in range(2):
                    if len(bits_of(r)) == count and (count > 1) == passed_on:
                        self.ensure(r - self.last_bit(r, half), half)
                        self.copy(r, half).start()
        if not passed_on:
            self.core_copy(0, True).start()

    def swap(self, relatives):
        for r in relatives:
            for half in range(2):
                self.ensure(r, half)
            self.core_copy(r, True).start()

    def finish(self):
        for r in range(self.chips):
            self.core_copy(r, False).wait_recv()

    def drain(self):
        for r in range(self.chips):
            self.core_copy(r, True).wait_send()
            for half in range(2):
                if r > 0:
                    self.copy(r, half).wait_send()


def front_kernel(
    n, n_dp, rows, model_width, x, wq, wk, wv, wo, gains, wg,
    full, qkv_out, full_qkv, full_out, gain_parts, attn_scale, mlp_scale, q_inv, k_inv, full_gate,
    send_sem, recv_sem, local_sem, gain_recv, gain_send_sem, gain_recv_sem,
    vqkv, vout, qkv, save_sem, x_buf, x_sem, squares,
    held, sum_recv, turned, sum_send_sem, sum_recv_sem, gate_sem, *plane,
):
    me, at = lax.axis_index("mp"), lax.axis_index("dp")
    peer_barrier((("mp", me, n), ("dp", at, n_dp)))()
    gather = LineGather(
        n,
        me,
        lambda c: x.at[chunk_span(c, rows)],
        lambda index, c: full.at[index, chunk_span(c, rows)],
        send_sem,
        recv_sem,
        local_sem,
    )
    for c in range(CHUNKS):
        gather.step(c, 1)
    chips = n_dp // 2
    part_width, width = wq.shape
    row_count = rows * CHUNKS

    def part(owner):
        return pl.ds(pl.multiple_of(owner * part_width, part_width), part_width)

    by_qkv = PlaneGather(at, chips, part_width, lambda owner: vqkv.at[part(owner)], plane[:4])
    by_out = PlaneGather(at, chips, width, lambda owner: vout.at[:, part(owner)], plane[4:8])
    by_gate = PlaneGather(
        at, chips, part_width, lambda owner: full_gate.at[part(owner)], plane[8:]
    )
    gate_copy = pltpu.make_async_copy(wg, full_gate.at[part(at)], gate_sem)
    gate_copy.start()
    for k, weight in enumerate((wq, wk, wv)):
        vqkv[part(at), k * width : (k + 1) * width] = weight[...]
    by_qkv.send(False)
    vout[:, part(at)] = wo[...]
    copies = exchange(
        "dp", at, n_dp, lambda peer: gains, gain_recv, gain_send_sem, gain_recv_sem
    )
    for copy in copies:
        copy.start()

    def block(index, source):
        load = pltpu.make_async_copy(source, x_buf, x_sem)
        load.start()
        load.wait()
        here = pl.ds(pl.multiple_of(index * row_count, row_count), row_count)

        @pl.loop(0, 3)
        def _(tile):
            cols = pl.ds(pl.multiple_of(tile * width, width), width)
            value = plain_dot(x_buf[...], vqkv[:, cols])
            qkv[here, cols] = value
            squares[tile] = jnp.sum(value * value, axis=1, keepdims=True)

        pltpu.make_async_copy(qkv.at[here], qkv_out.at[here], save_sem.at[2]).start()
        held[:, here] = columns_to_rows(squares[0], squares[1])

    def blocks_at(step):
        @pl.loop(0, 2)
        def _(side):
            index = me - step + 2 * step * side

            @pl.when((index >= 0) & (index < n))
            def _():
                block(index, full.at[index])

    saves = [
        pltpu.make_async_copy(vqkv, full_qkv, save_sem.at[0]),
        pltpu.make_async_copy(vout, full_out, save_sem.at[1]),
        pltpu.make_async_copy(qkv, qkv_out, save_sem.at[2]),
    ]
    early = [r for r in range(1, chips) if len(bits_of(r)) == 1]
    late = [r for r in range(1, chips) if len(bits_of(r)) > 1]

    def next_weights():
        by_qkv.send(True)
        by_out.send(False)
        gate_copy.wait()
        by_gate.send(False)

    def qkv_here():
        by_qkv.finish()
        saves[0].start()
        block(me, x)

    def out_here():
        by_out.swap(late)
        by_out.finish()
        saves[1].start()

    hooks = {
        0: next_weights,
        3: lambda: by_qkv.swap(early),
        4: lambda: by_qkv.swap(late),
        5: qkv_here,
        6: lambda: by_out.send(True),
        7: lambda: (by_out.swap(early), by_gate.send(True)),
        8: out_here,
        9: lambda: by_gate.swap(early),
    }
    ready, number = 1, 0
    for step in range(2, n + 1):
        for c in range(CHUNKS):
            if step < n:
                gather.step(c, step)
            else:
                gather.last(c)
            if number in hooks:
                hooks.pop(number)()
            number += 1
        while number > 5 and ready < step:
            blocks_at(ready)
            ready += 1
    for hook in hooks.values():
        hook()
    while ready < n:
        blocks_at(ready)
        ready += 1
    def keep_gains(owner, row):
        gain_parts[owner] = row[:, 2 * part_width :]
        attn_scale[:, part(owner)] = row[:, :part_width]
        mlp_scale[:, part(owner)] = row[:, part_width : 2 * part_width]

    keep_gains(at, gains[...])
    for shift, copy in enumerate(copies, 1):
        copy.wait_recv()
        keep_gains(lax.rem(at + n_dp - shift, n_dp), gain_recv[shift - 1])
    by_gate.swap(late)
    q_sum, k_sum = sum_held(n, me, held, sum_recv, turned, sum_send_sem, sum_recv_sem)
    q_inv[...] = lax.rsqrt(q_sum / model_width + EPS)
    k_inv[...] = lax.rsqrt(k_sum / model_width + EPS)
    for c in range(CHUNKS):
        gather.drain(c)
    for copy in copies:
        copy.wait_send()
    by_gate.finish()
    for gathered in (by_qkv, by_out, by_gate):
        gathered.drain()
    for copy in saves:
        copy.wait()


def front(n, n_dp, block, wq, wk, wv, wo, gains, wg):
    row_count, model_width = block.shape
    rows = row_count // CHUNKS
    size = n * row_count
    width = wq.shape[1]
    chips = n_dp // 2
    column = jax.ShapeDtypeStruct((size, 1), F32)
    return pl.pallas_call(
        functools.partial(front_kernel, n, n_dp, rows, model_width),
        out_shape=(
            jax.ShapeDtypeStruct((n,) + block.shape, block.dtype),
            jax.ShapeDtypeStruct((size, 3 * width), F32),
            jax.ShapeDtypeStruct((model_width, 3 * width), BF),
            jax.ShapeDtypeStruct((width, model_width), BF),
            jax.ShapeDtypeStruct((n_dp, 1, gains.shape[1] - 2 * model_width // n_dp), F32),
            jax.ShapeDtypeStruct((1, model_width), F32),
            jax.ShapeDtypeStruct((1, model_width), F32),
            column,
            column,
            jax.ShapeDtypeStruct((model_width, wg.shape[1]), BF),
        ),
        in_specs=[VMEM] * 7,
        out_specs=(HBM, HBM, HBM, HBM, VMEM, VMEM, VMEM, VMEM, VMEM, HBM),
        scratch_shapes=gather_scratch(n, rows, model_width)[1:]
        + [
            pltpu.VMEM((n_dp - 1,) + gains.shape, F32),
            pltpu.SemaphoreType.DMA((n_dp - 1,)),
            pltpu.SemaphoreType.DMA((n_dp - 1,)),
            pltpu.VMEM((model_width, 3 * width), BF),
            pltpu.VMEM((width, model_width), BF),
            pltpu.VMEM((size, 3 * width), F32),
            pltpu.SemaphoreType.DMA((3,)),
            pltpu.VMEM((row_count, model_width), BF),
            pltpu.SemaphoreType.DMA,
            pltpu.VMEM((3, row_count, 1), F32),
        ]
        + sum_scratch(n, size)
        + [pltpu.SemaphoreType.DMA]
        + plane_sems(chips) * 3,
        compiler_params=pltpu.CompilerParams(
            collective_id=0, has_side_effects=True, vmem_limit_bytes=63 * MIB
        ),
        name="front",
        cost_estimate=cost(80),
    )(block, wq, wk, wv, wo, gains, wg)


class WeightTiles:
    def __init__(self, source, held, sem, axis, size):
        self.source, self.held, self.sem, self.axis, self.size = source, held, sem, axis, size
        self.count = source.shape[axis] // size

    def at(self, ref, tile):
        span = pl.ds(pl.multiple_of(tile * self.size, self.size), self.size)
        return ref.at[:, span] if self.axis == 1 else ref.at[span]

    def copy(self, tile):
        return pltpu.make_async_copy(
            self.at(self.source, tile), self.at(self.held, tile), self.sem.at[tile]
        )

    def start(self):
        for tile in range(self.count):
            self.copy(tile).start()


def middle_kernel(
    n, n_dp, rows, att, wo, wg, wu, wd, x, upstream_in, row_valid, mlp_scale, attn_scale,
    h_full, output, dm_full, hidden_out, mlp_gain, middle_grad, da_full, attn_gain, gate_out, up_out,
    part, recv, rs_send_sem, rs_recv_sem, total, own, ag_send_sem, ag_recv_sem, local_sem,
    vg, vu, vd, wsem, in_buf, in_sem, gate_all, up_all, hidden_buf, hidden_sem, packed,
    middle, branch, mg_sem, h_buf, h_sem, extra, ready, *more,
):
    me, at = lax.axis_index("mp"), lax.axis_index("dp")
    width, hidden_width = vg.shape
    local_width = wo.shape[0]
    chips = n_dp // 2
    part_width = width // n_dp
    plane, more = more[:16], more[16:]
    v_out = more[0] if more else gate_all.at[pl.ds(0, local_width)]
    v_att = up_all.at[:, pl.ds(0, local_width)]

    def start(copies):
        for copy in copies:
            copy.start()

    def wait(copies):
        for copy in copies:
            copy.wait()

    def weight_part(owner):
        return pl.ds(pl.multiple_of(owner * part_width, part_width), part_width)

    by_up = PlaneGather(at, chips, part_width, lambda owner: vu.at[weight_part(owner)], plane[8:12])
    by_down = PlaneGather(
        at, chips, hidden_width, lambda owner: vd.at[:, weight_part(owner)], plane[12:]
    )
    own_weights = [
        pltpu.make_async_copy(wu, by_up.place(0), wsem.at[0]),
        pltpu.make_async_copy(wd, by_down.place(0), wsem.at[1]),
    ]
    gate_copy = pltpu.make_async_copy(wg, vg, wsem.at[2])
    att_copies = [
        pltpu.make_async_copy(wo, v_out, wsem.at[3]),
        pltpu.make_async_copy(att, v_att, wsem.at[4]),
    ]
    start(att_copies)
    start(own_weights)
    gate_copy.start()
    stage_barrier(me, n, at, chips)
    wait(own_weights)
    by_up.send(False)

    scatter = LineScatter(n, me, rows, part, recv, rs_send_sem, rs_recv_sem)
    gathers = [
        make_gather(n, me, rows, own, full, ag_send_sem, ag_recv_sem, local_sem)
        for full in (h_full, dm_full, da_full)
    ]

    def in_copies(phase, c):
        source = gathers[phase - 1].full
        return [
            pltpu.make_async_copy(
                source(j, c), in_buf.at[c % 2, pl.ds(j * rows, rows)], in_sem.at[c % 2, j]
            )
            for j in range(n)
        ]

    def attend_out(c):
        if c == 0:
            wait(att_copies)
        block_rows = rows * CHUNKS
        for j in range(n):
            packed[j * rows : (j + 1) * rows] = v_att[
                j * block_rows + c * rows : j * block_rows + (c + 1) * rows
            ]

        @pl.loop(0, width // TILE)
        def _(tile):
            cols = pl.ds(pl.multiple_of(tile * TILE, TILE), TILE)
            part[c, :, cols] = plain_dot(packed[...], v_out[:, cols]).astype(BF)

    def attend_rows(c):
        scatter.total(c, total)
        span = chunk_span(c, rows)
        value = total[...]
        branch[span] = value
        new = x[span].astype(F32) + value * inverse_rms(value) * attn_scale[...]
        middle[span] = new
        own[c] = new.astype(BF)

    def hidden_copies(c):
        return [
            pltpu.make_async_copy(
                hidden_buf.at[c % 2, pl.ds(j * rows, rows)],
                hidden_out.at[j, chunk_span(c, rows)],
                hidden_sem.at[c % 2, j],
            )
            for j in range(n)
        ]

    def clear(phase, c):
        scatter.drain(c)
        gathers[phase - 1].drain_sends(c)
        wait(in_copies(phase, c))

    def forward(c):
        here = pl.ds(c * n * rows, n * rows)
        slot = c % 2
        clear(1, c)
        if c == 0:
            by_up.finish()
            gate_copy.wait()
        if c >= 2:
            wait(hidden_copies(c - 2))

        @pl.loop(0, hidden_width // TILE)
        def _(tile):
            cols = pl.ds(pl.multiple_of(tile * TILE, TILE), TILE)
            gate = plain_dot(in_buf[slot], vg[:, cols])
            up = plain_dot(in_buf[slot], vu[:, cols])
            gate_all[here, cols] = gate.astype(BF)
            up_all[here, cols] = up.astype(BF)
            hidden_buf[slot, :, cols] = (gate * jax.nn.sigmoid(gate) * up).astype(BF)

        start(hidden_copies(c))
        if c == 0:
            by_down.swap(late_chips)
            by_down.finish()

        @pl.loop(0, width // TILE)
        def _(tile):
            cols = pl.ds(pl.multiple_of(tile * TILE, TILE), TILE)
            part[c, :, cols] = plain_dot(hidden_buf[slot], vd[:, cols]).astype(BF)

    def backward(c):
        here = pl.ds(c * n * rows, n * rows)
        clear(2, c)

        @pl.loop(0, hidden_width // TILE)
        def _(tile):
            cols = pl.ds(pl.multiple_of(tile * TILE, TILE), TILE)
            hidden_grad = outer_dot(in_buf[c % 2], vd[cols, :])
            gate = gate_all[here, cols].astype(F32)
            up = up_all[here, cols].astype(F32)
            sigmoid = jax.nn.sigmoid(gate)
            gate_all[here, cols] = (
                hidden_grad * up * sigmoid * (1.0 + gate * (1.0 - sigmoid))
            ).astype(BF)
            up_all[here, cols] = (hidden_grad * gate * sigmoid).astype(BF)

        @pl.loop(0, width // TILE)
        def _(tile):
            cols = pl.ds(pl.multiple_of(tile * TILE, TILE), TILE)
            part[c, :, cols] = (
                outer_dot(gate_all[here], vg[cols, :]) + outer_dot(up_all[here], vu[cols, :])
            ).astype(BF)

        if c + 1 == CHUNKS:
            for last in range(max(CHUNKS - 2, 0), CHUNKS):
                wait(hidden_copies(last))
            for gathered in (by_up, by_down):
                gathered.drain()
            start(h_copies(0))
            signal_partners(ready, at, chips)

    def mg_copy(c):
        return pltpu.make_async_copy(
            middle.at[chunk_span(c, rows)], middle_grad.at[chunk_span(c, rows)], mg_sem.at[c]
        )

    def forward_rows(c):
        scatter.total(c, total)
        span = chunk_span(c, rows)
        value = total[...]
        inverse = inverse_rms(value)
        output[span] = (middle[span] + value * inverse * mlp_scale[...]).astype(BF)
        upstream = upstream_in[span].astype(F32) * row_valid[span]
        grad, gain = norm_back(value, inverse, mlp_scale[...], upstream)
        own[c] = grad.astype(BF)
        mlp_gain[...] = gain if c == 0 else mlp_gain[...] + gain

    def backward_rows(c):
        scatter.total(c, total)
        span = chunk_span(c, rows)
        upstream = upstream_in[span].astype(F32) * row_valid[span] + total[...]
        middle[span] = upstream
        mg_copy(c).start()
        value = branch[span]
        grad, gain = norm_back(value, inverse_rms(value), attn_scale[...], upstream)
        own[c] = grad.astype(BF)
        attn_gain[...] = gain if c == 0 else attn_gain[...] + gain

    block_width = pl.ds(0, hidden_width)

    def slot_at(index):
        for ref in (vg, vu, vd):
            count = ref.shape[0] // part_width
            if index < count:
                return ref.at[pl.ds(index * part_width, part_width), block_width]
            index -= count
        for ref in (hidden_buf, in_buf):
            if index < ref.shape[0]:
                return ref.at[index, pl.ds(0, part_width), block_width]
            index -= ref.shape[0]
        return extra.at[index]

    reduces = []
    for which, out in enumerate((gate_out, up_out)):
        first = chips + 3 * chips * which
        views = (
            lambda r: slot_at(r),
            lambda r, first=first: slot_at(first + r),
            lambda r, first=first: slot_at(first + chips + r),
            lambda r, first=first: slot_at(first + 2 * chips + r - 1),
        )
        reduces.append(
            PlaneReduce(at, chips, part_width, views, plane[4 * which : 4 * which + 4], out)
        )
    order = relative_order(chips)
    jobs = [
        (which, same_core, r)
        for which in range(2)
        for same_core in (False, True)
        for r in order
    ]

    def h_copies(index):
        which, same_core, r = jobs[index]
        first = reduces[which].owner(r, same_core) * part_width
        cols = pl.ds(pl.multiple_of(first, part_width), part_width)
        return [
            pltpu.make_async_copy(
                h_full.at[j, :, cols], h_buf.at[index % 2, j], h_sem.at[index % 2, j]
            )
            for j in range(n)
        ]

    def weight_block(index):
        which, same_core, r = jobs[index]
        reduce = reduces[which]
        grad = (gate_all, up_all)[which]
        if index == 0:
            pl.semaphore_wait(ready, 1 + len(bits_of(chips - 1)))
        wait(h_copies(index))
        if index + 1 < len(jobs):
            start(h_copies(index + 1))
        if same_core:
            reduce.core_copy(r).wait_recv()
        elif which == 1:
            reduces[0].drain_core(r)
        left = jnp.concatenate(
            [
                h_buf[index % 2, j, c * rows : (c + 1) * rows]
                for c in range(CHUNKS)
                for j in range(n)
            ],
            axis=0,
        )

        @pl.loop(0, hidden_width // TILE)
        def _(tile):
            cols = pl.ds(pl.multiple_of(tile * TILE, TILE), TILE)
            block = inner_dot(left, grad[:, cols])
            if not same_core:
                reduce.core_send(r)[:, cols] = block.astype(BF)
            else:
                block = block + reduce.core_recv(r)[:, cols].astype(F32)
                if r > 0:
                    reduce.held(r)[:, cols] = block.astype(BF)
                else:
                    reduce.out[:, cols] = block

        if not same_core:
            reduce.core_copy(r).start()
        elif r > 0:
            for half in range(2):
                if not reduce.before(r, half):
                    reduce.push(r, half)

    work = []
    for index, (which, same_core, r) in enumerate(jobs):
        work.append(functools.partial(weight_block, index))
        if same_core and r == order[-1]:
            for late in order:
                for half in range(2):
                    if late > 0 and reduces[which].before(late, half):
                        work.append(functools.partial(reduces[which].push, late, half))
    pending = iter(work)

    early_chips = [r for r in range(1, chips) if len(bits_of(r)) == 1]
    late_chips = [r for r in range(1, chips) if len(bits_of(r)) > 1]
    hooks = {
        HOOKS[0]: lambda: (by_up.send(True), by_down.send(False)),
        HOOKS[1]: lambda: by_up.swap(early_chips),
        HOOKS[2]: lambda: by_up.swap(late_chips),
        HOOKS[3]: lambda: by_down.send(True),
        HOOKS[4]: lambda: by_down.swap(early_chips),
    }
    last_step = 2 * n - 2
    events = sorted(
        (
            max(PERIOD, last_step + 1) * phase + step + STAGGER * c - (0.5 if step == 0 else 0),
            phase,
            c,
            step,
        )
        for phase in range(3)
        for c in range(CHUNKS)
        for step in range(last_step + 1)
    )
    filling = False
    for number, (_, phase, c, step) in enumerate(events):
        gather = gathers[phase]
        if number in hooks:
            hooks.pop(number)()
        if step == 0:
            (attend_out, forward, backward)[phase](c)
            filling = filling or (phase == 2 and c + 1 == CHUNKS)
        if step < n - 1:
            scatter.edge(c, step)
            if step > 0:
                scatter.step(c, step)
        elif step == n - 1:
            (attend_rows, forward_rows, backward_rows)[phase](c)
            gather.step(c, 1)
        elif step < last_step:
            gather.step(c, step - n + 2)
        else:
            gather.last(c)
            if phase < 2:
                gather.local_copy(c).wait()
                start(in_copies(phase + 1, c))
        if filling:
            for _ in range(FILL):
                job = next(pending, None)
                if job is not None:
                    job()
    for job in pending:
        job()
    for c in range(CHUNKS):
        scatter.drain(c)
        gathers[2].drain(c)
    for reduce in reduces:
        reduce.finish()
        reduce.drain()
    for r in range(chips):
        reduces[1].drain_core(r)
    for c in range(CHUNKS):
        mg_copy(c).wait()


def middle(n, n_dp, attended, full_out, wg, wu, wd, x, out_grad, row_valid, mlp_scale, attn_scale):
    row_count, width = x.shape
    hidden_width = wg.shape[1]
    rows = row_count // CHUNKS
    size = n * row_count
    chips = n_dp // 2
    part_width = width // n_dp
    block = (part_width, hidden_width)
    slots = (2 * width + hidden_width) // part_width + 4
    extra = 7 * chips - 1 - slots
    by_rows = jax.ShapeDtypeStruct((n, row_count, width), BF)
    return pl.pallas_call(
        functools.partial(middle_kernel, n, n_dp, rows),
        out_shape=(
            by_rows,
            jax.ShapeDtypeStruct((row_count, width), BF),
            by_rows,
            jax.ShapeDtypeStruct((n, row_count, hidden_width), BF),
            jax.ShapeDtypeStruct((1, width), F32),
            jax.ShapeDtypeStruct((row_count, width), F32),
            by_rows,
            jax.ShapeDtypeStruct((1, width), F32),
            jax.ShapeDtypeStruct(block, F32),
            jax.ShapeDtypeStruct(block, F32),
        ),
        in_specs=[HBM] * 5 + [VMEM] * 5,
        out_specs=(HBM, VMEM, HBM, HBM, VMEM, HBM, HBM, VMEM, VMEM, VMEM),
        scratch_shapes=scatter_scratch(n, rows, width)
        + gather_scratch(n, rows, width)
        + [
            pltpu.VMEM((width, hidden_width), BF),
            pltpu.VMEM((width, hidden_width), BF),
            pltpu.VMEM((hidden_width, width), BF),
            pltpu.SemaphoreType.DMA((5,)),
            pltpu.VMEM((2, n * rows, width), BF),
            pltpu.SemaphoreType.DMA((2, n)),
            pltpu.VMEM((size, hidden_width), BF),
            pltpu.VMEM((size, hidden_width), BF),
            pltpu.VMEM((2, n * rows, hidden_width), BF),
            pltpu.SemaphoreType.DMA((2, n)),
            pltpu.VMEM((n * rows, attended.shape[1]), BF),
            pltpu.VMEM((row_count, width), F32),
            pltpu.VMEM((row_count, width), F32),
            pltpu.SemaphoreType.DMA((CHUNKS,)),
            pltpu.VMEM((2, n, row_count, part_width), BF),
            pltpu.SemaphoreType.DMA((2, n)),
            pltpu.VMEM((extra,) + block if extra > 0 else (1, 16, 128), BF),
            pltpu.SemaphoreType.REGULAR,
        ]
        + plane_sems(chips) * 4
        + ([pltpu.VMEM(full_out.shape, BF)] if hidden_width < width else []),
        compiler_params=pltpu.CompilerParams(
            collective_id=2, has_side_effects=True, vmem_limit_bytes=63 * MIB
        ),
        name="middle",
        cost_estimate=cost(350),
    )(attended, full_out, wg, wu, wd, x, out_grad, row_valid, mlp_scale, attn_scale)


def last_grads_kernel(
    n, n_dp, rows, grads, weight, base, inputs, att, da, hidden, dm,
    attn_gain, mlp_gain, q_gain, k_gain,
    input_grad, qkv_out, out_out, down_out, gain_out,
    part, recv, rs_send_sem, rs_recv_sem, total, packed,
    x_buf, da_buf, dm_buf, load_sem, v_hidden, hidden_sem,
    send_qkv, recv_qkv, message_qkv, send_out, recv_out, message_out,
    send_down, recv_down, message_down,
    gains, gain_recv, gain_send_sem, gain_recv_sem, mp_recv, mp_send_sem, mp_recv_sem, *plane,
):
    me, at = lax.axis_index("mp"), lax.axis_index("dp")
    entered = peer_barrier((("mp", me, n), ("dp", at, n_dp)))
    width = weight.shape[0]
    block_rows = rows * CHUNKS
    local_width = att.shape[1]
    chips = n_dp // 2
    part_width = width // n_dp
    order = relative_order(chips)

    def views(send, recv, message):
        return (
            lambda r: send.at[r],
            lambda r: recv.at[r],
            lambda r: send.at[r],
            lambda r: message.at[r - 1],
        )

    by_qkv = PlaneReduce(
        at, chips, part_width, views(send_qkv, recv_qkv, message_qkv), plane[:4], qkv_out
    )
    by_out = PlaneReduce(
        at, chips, local_width, views(send_out, recv_out, message_out), plane[4:8], out_out
    )
    by_down = PlaneReduce(
        at, chips, part_width, views(send_down, recv_down, message_down), plane[8:], down_out
    )
    jobs = [
        (down, same_core, r)
        for down in (True, False)
        for same_core in (False, True)
        for r in order
    ]

    def loads(k):
        down, same_core, r = jobs[k]
        first = by_qkv.owner(r, same_core) * part_width
        cols = pl.ds(pl.multiple_of(first, part_width), part_width)
        pairs = ((dm, dm_buf),) if down else ((inputs, x_buf), (da, da_buf))
        return [
            pltpu.make_async_copy(source.at[:, cols], buf.at[k % 2], load_sem.at[k % 2, which])
            for which, (source, buf) in enumerate(pairs)
        ]

    load_hidden = pltpu.make_async_copy(hidden, v_hidden, hidden_sem)
    for copy in loads(0):
        copy.start()
    load_hidden.start()

    def compute(c):
        for j in range(n):
            packed[j * rows : (j + 1) * rows] = grads[
                j * block_rows + c * rows : j * block_rows + (c + 1) * rows
            ]

        @pl.loop(0, width // TILE)
        def _(tile):
            cols = pl.ds(pl.multiple_of(tile * TILE, TILE), TILE)
            part[c, :, cols] = outer_dot(packed[...], weight[cols, :]).astype(BF)

    scatter = LineScatter(n, me, rows, part, recv, rs_send_sem, rs_recv_sem)

    def row_work(c):
        scatter.total(c, total)
        span = chunk_span(c, rows)
        input_grad[span] = base[span] + total[...]

    def weight_block(k):
        down, same_core, r = jobs[k]
        slot = k % 2
        reduces = (by_down,) if down else (by_qkv, by_out)
        for copy in loads(k):
            copy.wait()
        if k + 1 < len(jobs):
            for copy in loads(k + 1):
                copy.start()
        if k == 0:
            load_hidden.wait()
        if same_core:
            for reduce in reduces:
                reduce.core_copy(r).wait_recv()
                reduce.drain_core(r)

        def keep(reduce, block, cols):
            if not same_core:
                reduce.core_send(r)[:, cols] = block.astype(BF)
                return
            block = block + reduce.core_recv(r)[:, cols].astype(F32)
            if r > 0:
                reduce.held(r)[:, cols] = block.astype(BF)
            else:
                reduce.out[:, cols] = block

        if down:

            @pl.loop(0, hidden.shape[1] // TILE)
            def _(tile):
                cols = pl.ds(pl.multiple_of(tile * TILE, TILE), TILE)
                keep(by_down, inner_dot(dm_buf[slot], v_hidden[:, cols]), cols)

        else:

            @pl.loop(0, 3)
            def _(tile):
                cols = pl.ds(pl.multiple_of(tile * local_width, local_width), local_width)
                keep(by_qkv, inner_dot(x_buf[slot], grads[:, cols]), cols)

            keep(by_out, inner_dot(att[...], da_buf[slot]), slice(None))
        for reduce in reduces:
            if not same_core:
                reduce.core_copy(r).start()
            elif r > 0:
                for half in range(2):
                    if not reduce.before(r, half):
                        reduce.push(r, half)

    def push_late(reduces):
        for r in order:
            for half in range(2):
                if r > 0 and reduces[0].before(r, half):
                    for reduce in reduces:
                        reduce.push(r, half)

    for index in range(n_dp):
        span = slice(index * part_width, (index + 1) * part_width)
        gains[index, :, :part_width] = attn_gain[:, span]
        gains[index, :, part_width : 2 * part_width] = mlp_gain[:, span]
        gains[index, :, 2 * part_width : 2 * part_width + local_width] = q_gain[...]
        gains[index, :, 2 * part_width + local_width :] = k_gain[...]
    gain_copies = exchange(
        "dp", at, n_dp, lambda peer: gains.at[peer], gain_recv, gain_send_sem, gain_recv_sem
    )
    mp_copies = exchange("mp", me, n, lambda peer: gain_out, mp_recv, mp_send_sem, mp_recv_sem)
    line = iter([(step, c) for c in range(CHUNKS) for step in range(1, n)])

    def line_steps(count):
        for _ in range(count):
            step, c = next(line, (None, None))
            if step is None:
                return
            if step < n - 1:
                scatter.step(c, step)
            else:
                row_work(c)

    def send_edges(c):
        for step in range(n - 1):
            scatter.edge(c, step)

    compute(0)
    entered()
    send_edges(0)
    for copy in gain_copies:
        copy.start()
    sent = 1
    for k in range(len(jobs)):
        weight_block(k)
        if k % 4 == 3 and sent < CHUNKS:
            compute(sent)
            send_edges(sent)
            sent += 1
        if k >= LINE_FROM:
            line_steps(1)
        if k == 3 * chips:
            push_late((by_down,))
    push_late((by_qkv, by_out))
    gain_out[...] = gains[at]
    for shift, copy in enumerate(gain_copies, 1):
        copy.wait_recv()
        gain_out[...] += gain_recv[shift - 1]
    for copy in mp_copies:
        copy.start()
    line_steps(n * CHUNKS)
    for reduce in (by_down, by_qkv, by_out):
        reduce.finish()
    for copy in mp_copies:
        copy.wait_recv()
        copy.wait_send()
    lanes = lax.broadcasted_iota(jnp.int32, gain_out.shape, 1)
    shared = gain_out[...]
    for shift in range(1, n):
        shared = shared + mp_recv[shift - 1]
    gain_out[...] = jnp.where(lanes < 2 * part_width, shared, gain_out[...])
    for copy in gain_copies:
        copy.wait_send()
    for c in range(CHUNKS):
        scatter.drain(c)
    for reduce in (by_down, by_qkv, by_out):
        reduce.drain()


def last_grads(n, n_dp, grads, weight, base, inputs, attended, da_full, hidden, dm, *gains):
    row_count, width = base.shape
    rows = row_count // CHUNKS
    size, local_width = attended.shape
    part_width = width // n_dp
    chips = n_dp // 2
    qkv_block = (part_width, 3 * local_width)
    out_block = (local_width, part_width)
    down_block = (part_width, hidden.shape[1])
    gain_block = (1, 2 * part_width + 2 * local_width)
    return pl.pallas_call(
        functools.partial(last_grads_kernel, n, n_dp, rows),
        out_shape=(
            jax.ShapeDtypeStruct((row_count, width), F32),
            jax.ShapeDtypeStruct(qkv_block, F32),
            jax.ShapeDtypeStruct(out_block, F32),
            jax.ShapeDtypeStruct(down_block, F32),
            jax.ShapeDtypeStruct(gain_block, F32),
        ),
        in_specs=[VMEM, VMEM, VMEM, HBM, VMEM, HBM, HBM, HBM] + [VMEM] * 4,
        out_specs=(VMEM,) * 5,
        scratch_shapes=scatter_scratch(n, rows, width)
        + [
            pltpu.VMEM((n * rows, 3 * local_width), BF),
            pltpu.VMEM((2, size, part_width), BF),
            pltpu.VMEM((2, size, part_width), BF),
            pltpu.VMEM((2, size, part_width), BF),
            pltpu.SemaphoreType.DMA((2, 2)),
            pltpu.VMEM(hidden.shape, BF),
            pltpu.SemaphoreType.DMA,
        ]
        + [
            pltpu.VMEM((count,) + block, BF)
            for block in (qkv_block, out_block, down_block)
            for count in (chips, chips, chips - 1)
        ]
        + [pltpu.VMEM((n_dp,) + gain_block, F32), pltpu.VMEM((n_dp - 1,) + gain_block, F32)]
        + [pltpu.SemaphoreType.DMA((n_dp - 1,))] * 2
        + [pltpu.VMEM((n - 1,) + gain_block, F32)]
        + [pltpu.SemaphoreType.DMA((n - 1,))] * 2
        + plane_sems(chips) * 3,
        compiler_params=pltpu.CompilerParams(
            collective_id=4, has_side_effects=True, vmem_limit_bytes=63 * MIB
        ),
        name="last_grads",
        cost_estimate=cost(80),
    )(grads, weight, base, inputs, attended, da_full, hidden, dm, *gains)


def turn(values, cos, sin):
    return values * cos + pltpu.roll(values, values.shape[1] // 2, 1) * sin


def turn_back(values, cos, sin):
    return values * cos + pltpu.roll(values * sin, values.shape[1] // 2, 1)


def allowed_keys(starts, first_row, rows, key_end):
    places = first_row + lax.broadcasted_iota(jnp.int32, (rows, key_end), 0)
    keys = lax.broadcasted_iota(jnp.int32, (rows, key_end), 1)
    return (keys <= places) & (keys >= starts)


def columns_to_rows(first, second):
    lanes = lax.broadcasted_iota(jnp.int32, (first.shape[0], 128), 1)
    return jnp.transpose(jnp.where(lanes == 0, first, second))[:8]


def sum_held(n, me, held, recv, turned, send_sem, recv_sem):
    copies = exchange("mp", me, n, lambda peer: held, recv, send_sem, recv_sem)
    for copy in copies:
        copy.start()
    total = held[...]
    for shift, copy in enumerate(copies, 1):
        copy.wait_recv()
        total = total + recv[shift - 1]
    for copy in copies:
        copy.wait_send()
    turned[...] = jnp.zeros_like(turned)
    turned[:8] = total
    back = jnp.transpose(turned[...])
    return back[:, 0:1], back[:, 1:2]


def sum_scratch(n, size):
    return [
        pltpu.VMEM((8, size), F32),
        pltpu.VMEM((n - 1, 8, size), F32),
        pltpu.VMEM((128, size), F32),
        pltpu.SemaphoreType.DMA((n - 1,)),
        pltpu.SemaphoreType.DMA((n - 1,)),
    ]


def attention_kernel(
    q_raw, k_raw, v_raw, q_inv, k_inv, q_gain, k_gain, cos, sin, starts,
    out, q_low, k_low, v_low, log_total,
):
    size, head = q_raw.shape
    score_scale = 1.0 / math.sqrt(head)
    q_low[...] = turn(q_raw[...] * q_inv[...] * q_gain[...], cos[...], sin[...]).astype(BF)
    k_low[...] = turn(k_raw[...] * k_inv[...] * k_gain[...], cos[...], sin[...]).astype(BF)
    v_low[...] = v_raw[...].astype(BF)
    rows = min(QUERY_ROWS, size)
    for first in range(0, size, rows):
        end = first + rows
        span = slice(first, end)
        scores = outer_dot(q_low[span], k_low[:end]) * score_scale
        scores = jnp.where(allowed_keys(starts[span], first, rows, end), scores, MASKED)
        row_max = jnp.max(scores, axis=1, keepdims=True)
        exponents = jnp.exp(scores - row_max)
        row_total = jnp.sum(exponents, axis=1, keepdims=True)
        probs = (exponents * (1.0 / row_total)).astype(BF)
        out[span] = plain_dot(probs, v_low[:end]).astype(BF)
        log_total[span] = row_max + jnp.log(row_total)


def head_specs(size, head, heads, count):
    return [pl.BlockSpec((size, head), lambda h, k=k: (0, k * heads + h)) for k in range(count)]


def attention(qkv_raw, q_inv, k_inv, q_gain, k_gain, cos, sin, starts, heads):
    size = qkv_raw.shape[0]
    head = cos.shape[1]
    column = pl.BlockSpec((size, 1), lambda h: (0, 0))
    table = pl.BlockSpec((size, head), lambda h: (0, 0))
    gain = pl.BlockSpec((1, head), lambda h: (0, h))
    by_head = pl.BlockSpec((size, head), lambda h: (0, h))
    low = jax.ShapeDtypeStruct((size, heads * head), BF)
    return pl.pallas_call(
        attention_kernel,
        grid=(heads,),
        out_shape=(low, low, low, low, jax.ShapeDtypeStruct((heads, size, 1), F32)),
        in_specs=head_specs(size, head, heads, 3)
        + [column, column, gain, gain, table, table, column],
        out_specs=(by_head,) * 4 + (pl.BlockSpec((None, size, 1), lambda h: (h, 0, 0)),),
        compiler_params=pltpu.CompilerParams(vmem_limit_bytes=63 * MIB),
        name="attention",
        cost_estimate=cost(18),
    )(qkv_raw, qkv_raw, qkv_raw, q_inv, k_inv, q_gain, k_gain, cos, sin, starts)


def attention_back_kernel(
    n, heads, model_width, qkv, q_low, k_low, v_low, out_grad, log_total,
    q_inv, k_inv, q_gain, k_gain, cos, sin, starts,
    grads, q_gain_grad, k_gain_grad,
    q_weighted, k_weighted, q_grad, k_sum, v_sum, q_dots, k_dots, *sums,
):
    me = lax.axis_index("mp")
    entered = peer_barrier((("mp", me, n),))
    size = qkv.shape[0]
    width = qkv.shape[1] // 3
    head = width // heads
    score_scale = 1.0 / math.sqrt(head)
    rows = min(BACK_ROWS, size)
    q_dots[...] = jnp.zeros_like(q_dots)
    k_dots[...] = jnp.zeros_like(k_dots)

    @pl.loop(0, heads)
    def _(h):
        def cols(first):
            return pl.ds(pl.multiple_of(first + h * head, head), head)

        here = cols(0)
        for first in reversed(range(0, size, rows)):
            end = first + rows
            span = slice(first, end)
            scores = outer_dot(q_low[span, here], k_low[:end, here]) * score_scale
            scores = jnp.where(allowed_keys(starts[span], first, rows, end), scores, MASKED)
            probs = jnp.exp(scores - log_total[h, span])
            prob_grad = outer_dot(out_grad[span, here], v_low[:end, here])
            probs_low = probs.astype(BF)
            weighted = probs * prob_grad
            score_grad = (
                weighted - probs * jnp.sum(weighted, axis=1, keepdims=True)
            ).astype(BF)
            q_grad[span] = plain_dot(score_grad, k_low[:end, here]) * score_scale
            k_extra = inner_dot(score_grad, q_low[span, here])
            v_extra = inner_dot(probs_low, out_grad[span, here])
            if end == size:
                k_sum[...] = k_extra
                v_sum[...] = v_extra
            else:
                k_sum[:end] += k_extra
                v_sum[:end] += v_extra
        for first, inv, gain, grad, factor, weighted_out, dots, gain_grad in (
            (0, q_inv, q_gain, q_grad, None, q_weighted, q_dots, q_gain_grad),
            (width, k_inv, k_gain, k_sum, score_scale, k_weighted, k_dots, k_gain_grad),
        ):
            raw = qkv[:, cols(first)]
            value = grad[...] if factor is None else grad[...] * factor
            normed = turn_back(value, cos[...], sin[...])
            weighted = normed * gain[:, here]
            weighted_out[:, here] = weighted
            gain_grad[:, here] = jnp.sum(normed * raw * inv[...], axis=0, keepdims=True)
            dots[...] += jnp.sum(weighted * raw, axis=1, keepdims=True)
        grads[:, cols(2 * width)] = v_sum[...].astype(BF)

    held = sums[0]
    held[...] = columns_to_rows(q_dots[...], k_dots[...])
    entered()
    q_total, k_total = sum_held(n, me, *sums)
    for first, inv, weighted, dots in (
        (0, q_inv, q_weighted, q_total),
        (width, k_inv, k_weighted, k_total),
    ):
        scale = inv[...]
        factor = scale * scale * scale * (dots / model_width)
        grads[:, first : first + width] = (
            scale * weighted[...] - qkv[:, first : first + width] * factor
        ).astype(BF)


def attention_back(
    n, heads, model_width, qkv_raw, q_low, k_low, v_low, out_grad, log_total, q_inv, k_inv,
    q_gain, k_gain, cos, sin, starts,
):
    size, width = q_low.shape
    head = width // heads
    gains = jax.ShapeDtypeStruct((1, width), F32)
    return pl.pallas_call(
        functools.partial(attention_back_kernel, n, heads, model_width),
        out_shape=(jax.ShapeDtypeStruct((size, 3 * width), BF), gains, gains),
        in_specs=[VMEM] * 13,
        out_specs=(VMEM,) * 3,
        scratch_shapes=[pltpu.VMEM((size, width), F32)] * 2
        + [pltpu.VMEM((size, head), F32)] * 3
        + [pltpu.VMEM((size, 1), F32)] * 2
        + sum_scratch(n, size),
        compiler_params=pltpu.CompilerParams(
            collective_id=6, has_side_effects=True, vmem_limit_bytes=63 * MIB
        ),
        name="attention_back",
        cost_estimate=cost(30),
    )(
        qkv_raw, q_low, k_low, v_low, out_grad, log_total, q_inv, k_inv, q_gain, k_gain,
        cos, sin, starts,
    )


def local(
    layer_input,
    query_weight,
    key_weight,
    value_weight,
    out_weight,
    gate_weight,
    up_weight,
    down_weight,
    query_gain,
    key_gain,
    attn_gain,
    mlp_gain,
    seq_lens,
    out_grad,
):
    n = lax.axis_size("mp")
    n_dp = lax.axis_size("dp")
    me = lax.axis_index("mp")
    row_count, model_width = layer_input.shape
    group_size = row_count * n
    local_heads, gain_part = query_gain.shape
    head_size = gain_part * n_dp
    local_width = local_heads * head_size

    head_part = local_heads * gain_part
    width_part = attn_gain.shape[0]
    own_gains = jnp.concatenate(
        [attn_gain, mlp_gain, query_gain.reshape(head_part), key_gain.reshape(head_part)]
    ).astype(F32)[None]
    (
        inputs_full, qkv_raw, full_qkv, full_out, gain_parts, attn_scale, mlp_scale, query_inv,
        key_inv, full_gate,
    ) = front(
        n, n_dp, layer_input, query_weight, key_weight, value_weight, out_weight, own_gains,
        gate_weight,
    )
    inputs_full = inputs_full.reshape(group_size, model_width)
    gain_parts = gain_parts[:, 0]

    def head_gain(first):
        piece = gain_parts[:, first : first + head_part].reshape(n_dp, local_heads, gain_part)
        return piece.transpose(1, 0, 2).reshape(1, local_width)

    query_scale = head_gain(0)
    key_scale = head_gain(head_part)

    starts, positions, valid = layout(seq_lens[0], group_size)
    starts = starts[:, None]
    cos_table, sin_table = rotary_tables(positions, head_size)
    row_valid = lax.dynamic_slice_in_dim(valid, me * row_count, row_count, 0).astype(F32)[:, None]

    attended, query_low, key_low, value_low, log_total = attention(
        qkv_raw, query_inv, key_inv, query_scale, key_scale, cos_table, sin_table, starts,
        local_heads,
    )
    (
        middle_full, layer_output, mlp_grad_full, hidden, mlp_gain_part, middle_grad, branch_full,
        attn_gain_part, grad_gate, grad_up,
    ) = middle(
        n, n_dp, attended, full_out, full_gate, up_weight, down_weight, layer_input, out_grad,
        row_valid, mlp_scale, attn_scale,
    )

    def flat(rows):
        return rows.reshape(group_size, rows.shape[-1])

    branch_full = flat(branch_full)
    mixed_grad = outer_dot(branch_full, full_out).astype(BF)
    qkv_grad, query_gain_part, key_gain_part = attention_back(
        n, local_heads, model_width, qkv_raw, query_low, key_low, value_low, mixed_grad, log_total,
        query_inv, key_inv, query_scale, key_scale, cos_table, sin_table, starts,
    )

    input_grad, grad_qkv, grad_out, grad_down, gain_sums = last_grads(
        n, n_dp, qkv_grad, full_qkv, middle_grad, inputs_full, attended, branch_full,
        flat(hidden), flat(mlp_grad_full), attn_gain_part, mlp_gain_part, query_gain_part,
        key_gain_part,
    )
    gain_sums = gain_sums[0]
    heads_at = 2 * width_part
    head_sums = lax.dynamic_index_in_dim(
        gain_sums[heads_at:].reshape(2, local_heads, n_dp, gain_part),
        lax.axis_index("dp"),
        2,
        keepdims=False,
    )
    return (
        layer_output,
        input_grad,
        grad_qkv[:, :local_width],
        grad_qkv[:, local_width : 2 * local_width],
        grad_qkv[:, 2 * local_width :],
        grad_out,
        grad_gate,
        grad_up,
        grad_down.T,
        head_sums[0],
        head_sums[1],
        gain_sums[:width_part],
        gain_sums[width_part:heads_at],
    )


def solution(mesh):
    return jax.shard_map(
        local,
        mesh=mesh,
        in_specs=(
            P(("dp", "mp"), None),
            P("dp", "mp"),
            P("dp", "mp"),
            P("dp", "mp"),
            P("mp", "dp"),
            P("dp", "mp"),
            P("dp", "mp"),
            P("mp", "dp"),
            P("mp", "dp"),
            P("mp", "dp"),
            P("dp"),
            P("dp"),
            P("dp", None),
            P(("dp", "mp"), None),
        ),
        out_specs=(
            P(("dp", "mp"), None),
            P(("dp", "mp"), None),
            P("dp", "mp"),
            P("dp", "mp"),
            P("dp", "mp"),
            P("mp", "dp"),
            P("dp", "mp"),
            P("dp", "mp"),
            P("mp", "dp"),
            P("mp", "dp"),
            P("mp", "dp"),
            P("dp"),
            P("dp"),
        ),
        check_vma=False,
    )
```
